128 devices in a mesh: dp: 16 (over y, x), tensor: 8 (over z, core).
Axes of the slice: x: 4, y: 4, z: 4, core: 2. Of those that a mesh axis runs over, the one named last changes fastest.
Arguments:
- tokens: bfloat16 [16384, 1536], P('dp'), may hold values from -6 to 6
- teacher_feats: bfloat16 [16384, 256], P('dp'), may hold values from -12 to 12
- masks: int32 [64, 256], P('dp'), may hold values from 0 to 1, as said below
- w_in: bfloat16 [1536, 2048], P('dp'), may hold values from -0.15625 to 0.15625
- w_out: bfloat16 [2048, 256], P('dp'), may hold values from -0.125 to 0.125
- proto_student: bfloat16 [256, 131072], P(None, ('dp', 'tensor')), may hold values from -0.375 to 0.375
- proto_teacher: bfloat16 [256, 131072], P(None, ('dp', 'tensor')), may hold values from -1 to 1
Outputs:
- d_tokens: bfloat16 [16384, 1536], P('dp')
- grad_in: float32 [1536, 2048], P('dp')
- grad_out: float32 [2048, 256], P('dp')
- grad_proto: float32 [256, 131072], P(None, ('dp', 'tensor'))
- crop_loss: float32 [64], P('dp')
The draws below stay inside these ranges and needn't reach their ends.
Inputs may be any that keep to these rules, and one draw needn't show every extreme that they name: `masks`: the crops of one index of dp hold 256 or fewer masked patches together, exactly 256 on some index; a crop holds at most 129.
All inputs are finite; a program needn't handle non-finite values.
Results may differ from the reference program's by a relative error of at most 0.02.
Values may be sent and summed in bfloat16 or wider, within the bound.
No kernel may reach another device: no remote copies, remote signals or barrier semaphores. Data moves between devices by JAX's collectives and lax.ppermute only.
A program may use at most 192 MiB of HBM per device.

```python
import math
import jax
import jax.numpy as jnp
from jax import lax

D = 1536
HID = 2048
BOT = 256
PROTOS = 131072
PATCHES = 256
ROUNDS = 3
CROPS_DEV = 4
CAP = 256
CROPS = 64
N_DP = 16
N_TENSOR = 8


def draw_masks(key, part):
    crops = CROPS_DEV * N_DP
    base_key = jax.random.fold_in(key, 4241)
    key_total, key_full, key_move, key_perm = jax.random.split(base_key, 4)
    totals = jax.random.randint(key_total, (N_DP,), CAP // 4, CAP + 1)
    fullest = jax.random.randint(key_full, (), 0, N_DP)
    totals = jnp.where(jnp.arange(N_DP) == fullest, CAP, totals)
    base = totals // CROPS_DEV
    extra = totals % CROPS_DEV
    counts = base[:, None] + (jnp.arange(CROPS_DEV)[None, :] < extra[:, None]).astype(jnp.int32)
    pairs = counts.reshape(N_DP, CROPS_DEV // 2, 2)
    moved = jax.random.randint(key_move, (N_DP, CROPS_DEV // 2), 0, base[:, None] + 1)
    pairs = pairs + jnp.stack([moved, -moved], axis=-1)
    counts = pairs.reshape(crops)
    orders = jax.vmap(lambda sub: jax.random.permutation(sub, PATCHES))(jax.random.split(key_perm, crops))
    return (orders < counts[:, None]).astype(jnp.int32)


def cluster_layout(key, spread):
    cluster_total = 24
    base_key = jax.random.fold_in(key, 7001)
    key_dir, key_rows, key_cols = jax.random.split(base_key, 3)
    centres = jax.random.normal(key_dir, (cluster_total, BOT), jnp.float32)
    centres = centres / jnp.sqrt(jnp.sum(centres * centres, axis=1, keepdims=True))
    ladder = jnp.arange(cluster_total).astype(jnp.float32) / (cluster_total - 1.0)
    row_logits = spread * jnp.take(ladder, jax.random.permutation(key_rows, cluster_total))
    col_logits = spread * jnp.take(ladder, jax.random.permutation(key_cols, cluster_total))
    return (centres, row_logits, col_logits)


def draw_teacher_feats(key, part):
    patch_total = CROPS_DEV * N_DP * PATCHES
    spread = math.log(10.0)
    centres, row_logits, col_logits = cluster_layout(key, spread)
    own_key = jax.random.fold_in(key, 7103)
    key_pick, key_noise = jax.random.split(own_key, 2)
    chosen = jax.random.categorical(key_pick, row_logits, shape=(patch_total,))
    root_bot = math.sqrt(BOT)
    noise = jax.random.normal(key_noise, (patch_total, BOT), jnp.float32)
    values = jnp.take(centres, chosen, axis=0) * root_bot + 1.1 * noise
    return jnp.clip(values, -12.0, 12.0).astype(jnp.bfloat16)


def draw_proto_teacher(key, part):
    spread = math.log(10.0)
    centres, row_logits, col_logits = cluster_layout(key, spread)
    own_key = jax.random.fold_in(key, 7207)
    key_pick, key_noise = jax.random.split(own_key, 2)
    shard_cols = PROTOS // (N_DP * N_TENSOR)
    owner = jnp.arange(PROTOS) // shard_cols % N_TENSOR
    tied = (jnp.arange(24)[None, :] % N_TENSOR == owner[:, None]).astype(jnp.float32)
    logits = col_logits[None, :] + 4.0 * tied
    chosen = jax.random.categorical(key_pick, logits, axis=1)
    root_bot = math.sqrt(BOT)
    noise = jax.random.normal(key_noise, (BOT, PROTOS), jnp.float32)
    values = (jnp.take(centres, chosen, axis=0).T * root_bot + 1.1 * noise) / root_bot
    return jnp.clip(values, -1.0, 1.0).astype(jnp.bfloat16)


def spiked(drawn, key, source, target, blocks, factor):
    owner, partner = [(jnp.arange(drawn.shape[axis_at]) // (drawn.shape[axis_at] // blocks)).reshape([-1 if axis == axis_at else 1 for axis in range(drawn.ndim)]) for axis_at in (source, target)]
    chosen = jax.random.permutation(key, blocks)[partner]
    strong = (owner == chosen) | (owner == (partner + blocks // 2) % blocks)
    return jnp.where(strong, factor * drawn, drawn)


def block_scale(stream_key, shape, cuts, least, top_value):
    def one(position, blocks):
        steps = jax.random.uniform(jax.random.fold_in(jax.random.fold_in(stream_key, 6), position), (blocks,), jnp.float32, least / len(cuts), top_value / len(cuts))
        return jnp.repeat(jnp.exp(steps), shape[position] // blocks).reshape((-1,) + (1,) * (len(shape) - position - 1))

    gain = one(*cuts[0])
    for cut in cuts[1:]:
        gain = gain * one(*cut)
    return gain


def gaussian(key, extent, scale, bound, cuts=(), dtype=jnp.bfloat16):
    values = jax.random.normal(key, extent, jnp.float32) * scale
    if len(cuts) > 0:
        values = block_scale(key, extent, cuts, -0.22, 0.18) * values
    return jnp.clip(values, min=-bound, max=bound).astype(dtype)


def noise_with(stream_key, shape, deviation, reach, cuts, heavy, held_as=jnp.bfloat16):
    result = deviation * jax.random.normal(stream_key, shape, jnp.float32)
    if cuts:
        result = result * block_scale(stream_key, shape, cuts, -0.22, 0.18)
    return jnp.clip(spiked(result, jax.random.fold_in(stream_key, 3), *heavy), -reach, reach).astype(held_as)


def setup_inputs(seed: int = 0) -> dict:
    streams_of = jax.random.split(jax.random.key(seed), 8)
    return {
        "tokens": noise_with(streams_of[0], (CROPS * PATCHES, D), 1.0, 6.0, ((0, 16),), (0, 1, 16, 2.0)),
        "teacher_feats": draw_teacher_feats(jax.random.fold_in(streams_of[7], 71), 0),
        "masks": draw_masks(jax.random.fold_in(streams_of[7], 71), 0),
        "w_in": gaussian(streams_of[3], (D, HID), D ** -0.5, 0.15625, ((0, 16),)),
        "w_out": gaussian(streams_of[4], (HID, BOT), HID ** -0.5, 0.125, ((0, 16),)),
        "proto_student": gaussian(streams_of[5], (BOT, PROTOS), BOT ** -0.5, 0.375, ((1, 128),)),
        "proto_teacher": draw_proto_teacher(jax.random.fold_in(streams_of[7], 71), 0),
    }


TEACHER_TEMP = 0.07
STUDENT_TEMP = 0.1
EPS = 1e-06
GRAD_SCALE = 65536.0

def gelu_parts(pre):
    cdf = 0.5 * (1.0 + lax.erf(pre * 0.7071067811865476))
    pdf = jnp.exp(-0.5 * pre * pre) * 0.3989422804014327
    return (pre * cdf, cdf + pre * pdf)

def unit_rows(feats):
    inverse = lax.rsqrt(lax.optimization_barrier(jnp.sum(feats * feats, axis=1, keepdims=True)) + EPS)
    return (feats * inverse, inverse)

def unit_columns(protos):
    wide = protos.astype(jnp.float32)
    norms = jnp.sqrt(lax.optimization_barrier(jnp.sum(wide * wide, axis=0, keepdims=True)) + EPS)
    return (wide / norms, norms)

def matmul(left, right):
    return jnp.dot(left.astype(jnp.float32), right.astype(jnp.float32), precision=lax.Precision.HIGHEST)

def rounded(value):
    return lax.optimization_barrier(value.astype(jnp.bfloat16)).astype(jnp.float32)

def reference(tokens, teacher_feats, masks, w_in, w_out, proto_student, proto_teacher):
    groups = N_DP
    per_dev = CROPS_DEV * PATCHES
    total = groups * CAP
    flat = masks.reshape(groups, per_dev)

    def pick(bits):
        return jnp.nonzero(bits, size=CAP, fill_value=0)[0].astype(jnp.int32)
    index = jax.vmap(pick)(flat)
    count = lax.optimization_barrier(jnp.sum(flat, axis=1))
    livef = (jnp.arange(CAP)[None, :] < count[:, None]).astype(jnp.float32)
    crop_count = lax.optimization_barrier(jnp.sum(masks, axis=1)).reshape(groups, CROPS_DEV)
    inverse = 1.0 / jnp.maximum(crop_count, 1).astype(jnp.float32)
    member = (index[:, :, None] // PATCHES == jnp.arange(CROPS_DEV)[None, None, :]).astype(jnp.float32) * livef[:, :, None]
    weight = (GRAD_SCALE * lax.optimization_barrier(jnp.sum(member * inverse[:, None, :], axis=2))).astype(jnp.bfloat16)

    def take_rows(table, idx):
        return table[idx]
    rows = jax.vmap(take_rows)(tokens.reshape(groups, per_dev, D), index).reshape(total, D)
    teacher_pick = jax.vmap(take_rows)(teacher_feats.reshape(groups, per_dev, BOT), index).reshape(total, BOT)
    live_all = livef.reshape(total)
    weight_all = weight.reshape(total).astype(jnp.float32)
    pre = matmul(rows, w_in)
    act, slope = gelu_parts(pre)
    hidden = act.astype(jnp.bfloat16)
    feats = matmul(hidden, w_out)
    unit, inv = unit_rows(feats)
    student_rows = unit.astype(jnp.bfloat16).astype(jnp.float32)
    teacher_rows = unit_rows(teacher_pick.astype(jnp.float32))[0].astype(jnp.bfloat16).astype(jnp.float32)
    s_cols, s_norm = unit_columns(proto_student)
    t_cols, _ = unit_columns(proto_teacher)
    width = min(8192, PROTOS)
    count_blocks = PROTOS // width

    def blocks(matrix):
        return matrix.reshape(BOT, count_blocks, width).transpose(1, 0, 2)
    s_blocks = blocks(s_cols.astype(jnp.bfloat16).astype(jnp.float32))
    t_blocks = blocks(t_cols.astype(jnp.bfloat16).astype(jnp.float32))

    def teacher_exp(tcol):
        return jnp.exp(matmul(teacher_rows, tcol) / TEACHER_TEMP) * live_all[:, None]
    scale_row = live_all
    for turn in range(ROUNDS - 1):

        def step(acc, tcol):
            expo = teacher_exp(tcol)
            col_scale = 1.0 / lax.optimization_barrier(jnp.sum(expo * scale_row[:, None], axis=0))
            return (acc + lax.optimization_barrier(jnp.sum(expo * col_scale[None, :], axis=1)), col_scale)
        row_sum, _ = lax.scan(step, jnp.zeros((total,), jnp.float32), t_blocks)
        scale_row = live_all / (row_sum + 1.0 - live_all)

    def last_step(acc, both):
        tcol, scol = both
        expo = teacher_exp(tcol)
        col_scale = 1.0 / lax.optimization_barrier(jnp.sum(expo * scale_row[:, None], axis=0))
        balanced = expo * col_scale[None, :]
        scores = matmul(student_rows, scol) / STUDENT_TEMP
        acc = (acc[0] + lax.optimization_barrier(jnp.sum(balanced, axis=1)), acc[1] + lax.optimization_barrier(jnp.sum(jnp.exp(scores), axis=1)), acc[2] + lax.optimization_barrier(jnp.sum(balanced * scores, axis=1)))
        return (acc, col_scale)
    zero = jnp.zeros((total,), jnp.float32)
    (row_sum, norm_sum, cross), col_last = lax.scan(last_step, (zero, zero, zero), (t_blocks, s_blocks))
    scale_last = live_all / (row_sum + 1.0 - live_all)
    row_loss = jnp.log(norm_sum) - scale_last * cross
    crop_loss = (lax.optimization_barrier(jnp.sum(member * row_loss.reshape(groups, CAP)[:, :, None], axis=1)) * inverse).reshape(groups * CROPS_DEV)

    def back_step(grad_acc, three):
        tcol, scol, col_scale = three
        expo = teacher_exp(tcol)
        balanced = expo * col_scale[None, :]
        target = balanced * scale_last[:, None]
        scores = matmul(student_rows, scol) / STUDENT_TEMP
        probs = jnp.exp(scores) / norm_sum[:, None]
        grad_score = (weight_all[:, None] * (probs - target) / STUDENT_TEMP).astype(jnp.bfloat16).astype(jnp.float32)
        grad_acc = grad_acc + matmul(grad_score, scol.T)
        parts = jnp.einsum('grb,grk->gbk', student_rows.reshape(groups, CAP, BOT), grad_score.reshape(groups, CAP, width), precision=lax.Precision.HIGHEST)
        return (grad_acc, lax.optimization_barrier(jnp.sum(rounded(parts), axis=0)))
    grad_unit, grad_blocks = lax.scan(back_step, jnp.zeros((total, BOT), jnp.float32), (t_blocks, s_blocks, col_last))
    grad_cols = grad_blocks.transpose(1, 0, 2).reshape(BOT, PROTOS)
    grad_proto = (grad_cols - s_cols * lax.optimization_barrier(jnp.sum(s_cols * grad_cols, axis=0, keepdims=True))) / s_norm
    inner = lax.optimization_barrier(jnp.sum(unit * grad_unit, axis=1, keepdims=True))
    grad_feats = (inv * (grad_unit - unit * inner)).astype(jnp.bfloat16).astype(jnp.float32)
    hidden_wide = hidden.astype(jnp.float32)
    out_parts = jnp.einsum('grh,grb->ghb', hidden_wide.reshape(groups, CAP, HID), grad_feats.reshape(groups, CAP, BOT), precision=lax.Precision.HIGHEST)
    grad_out = lax.optimization_barrier(jnp.sum(rounded(out_parts), axis=0))
    grad_pre = (matmul(grad_feats, w_out.T) * slope).astype(jnp.bfloat16).astype(jnp.float32)
    in_parts = jnp.einsum('grd,grh->gdh', rows.astype(jnp.float32).reshape(groups, CAP, D), grad_pre.reshape(groups, CAP, HID), precision=lax.Precision.HIGHEST)
    grad_in = lax.optimization_barrier(jnp.sum(rounded(in_parts), axis=0))
    grad_rows = (matmul(grad_pre, w_in.T) * live_all[:, None]).reshape(groups, CAP, D)

    def place(idx, values):
        return jnp.zeros((per_dev, D), jnp.float32).at[idx].add(values)
    d_tokens = jax.vmap(place)(index, grad_rows).reshape(groups * per_dev, D).astype(jnp.bfloat16)
    return (d_tokens, grad_in, grad_out, grad_proto, crop_loss)
```

```python
import jax
import jax.numpy as jnp
from jax import lax
from jax.experimental import pallas as pl
from jax.experimental.pallas import tpu as pltpu
from jax.sharding import PartitionSpec as P

ROUNDS = 3
CAP = 256
TEACHER_TEMP = 0.07
STUDENT_TEMP = 0.1
EPS = 1e-06
GRAD_SCALE = 65536.0
INTERPRET = False
f32, bf16 = (jnp.float32, jnp.bfloat16)
VMEM = pl.BlockSpec(memory_space=pltpu.VMEM)
HBM = pl.BlockSpec(memory_space=pl.ANY)
SMEM = pl.BlockSpec(memory_space=pltpu.SMEM)
NT = (((1,), (1,)), ((), ()))
TN = (((0,), (0,)), ((), ()))
EXTRA = 16


def mm(a, b, dims=None):
    if dims is None:
        return jnp.dot(a, b, preferred_element_type=f32)
    return lax.dot_general(a, b, dims, preferred_element_type=f32)


def call(body, outs, ins, out_specs=None, in_specs=None, scratch=(), name=None):
    outs = tuple(jax.ShapeDtypeStruct(s, d) for s, d in outs)
    return pl.pallas_call(
        body,
        out_shape=outs,
        in_specs=in_specs or [VMEM] * len(ins),
        out_specs=tuple(out_specs or [VMEM] * len(outs)),
        scratch_shapes=list(scratch),
        interpret=INTERPRET,
        name=name,
        compiler_params=pltpu.CompilerParams(vmem_limit_bytes=48 << 20),
    )(*ins)


def iota(shape, dim):
    return lax.broadcasted_iota(jnp.int32, shape, dim)


def select_body(mask_ref, feats_ref, sel_ref, pack_ref, member_ref):
    crops, patches = mask_ref.shape
    mask = mask_ref[...].astype(f32)
    upto = (iota((patches, patches), 0) <= iota((patches, patches), 1)).astype(f32).astype(bf16)
    rank = mm(mask.astype(bf16), upto)
    count = jnp.sum(mask, axis=1, keepdims=True)
    total = jnp.sum(count, axis=0, keepdims=True)
    slot = iota((CAP, patches), 0).astype(f32)
    lane = iota((1, CAP), 1).astype(f32)
    start = jnp.zeros((1, 1), f32)
    weight = jnp.zeros((1, CAP), f32)
    first = iota((CAP, patches), 1) == 0
    member_ref[...] = jnp.zeros_like(member_ref)
    for c in range(crops):
        hit = jnp.where((rank[c : c + 1] + start == slot + 1.0) & (mask[c : c + 1] > 0.0), 1.0, 0.0)
        if c == 0:
            hit = jnp.where(first & (slot >= total), 1.0, hit)
        sel_ref[:, c * patches : (c + 1) * patches] = hit.astype(bf16)
        own = count[c : c + 1]
        inside = jnp.where((lane >= start) & (lane < start + own), 1.0, 0.0)
        part = inside * (1.0 / jnp.maximum(own, 1.0))
        member_ref[c : c + 1, :] = part
        weight = weight + part
        start = start + own
    live = jnp.where(lane < total, 1.0, 0.0)
    picked = mm(sel_ref[...], feats_ref[...])
    scale = lax.rsqrt(jnp.sum(picked * picked, axis=1, keepdims=True) + EPS)
    pack_ref[0:CAP, :] = (picked * scale).astype(bf16)
    at = iota((EXTRA, CAP), 0)
    tail = jnp.where(at == 0, live, jnp.where(at == 1, weight * GRAD_SCALE, 0.0))
    pack_ref[CAP : CAP + EXTRA, :] = tail.astype(bf16)


def columns_body(student_ref, teacher_ref, cols_ref, student_t_ref, teacher_t_ref, norm_ref):
    width = student_ref.shape[1]
    step = min(256, width)
    for at in range(0, width, step):
        part = slice(at, at + step)
        wide = student_ref[:, part].astype(f32)
        norm = jnp.sqrt(jnp.sum(wide * wide, axis=0, keepdims=True) + EPS)
        norm_ref[:, part] = norm
        unit = wide / norm
        cols_ref[:, part] = unit.astype(bf16)
        student_t_ref[part, :] = unit.T.astype(bf16)
        wide = teacher_ref[:, part].astype(f32)
        norm = jnp.sqrt(jnp.sum(wide * wide, axis=0, keepdims=True) + EPS)
        teacher_t_ref[part, :] = (wide / norm).T.astype(bf16)


def weights_body(at_ref, w_in_ref, w_out_ref, pack_ref):
    rows, hid = w_in_ref.shape
    per = w_out_ref.shape[0]
    own = at_ref[0]
    chunk = per * 8
    row = iota((chunk, per), 0)
    col = iota((chunk, per), 1)
    pick = (row == (col // 16) * per + own * 16 + col % 16).astype(f32).astype(bf16)
    for m in range(hid // chunk):
        part = mm(w_in_ref[:, m * chunk : (m + 1) * chunk], pick)
        pack_ref[0:rows, m * per : (m + 1) * per] = part.astype(bf16)
    pack_ref[rows : rows + 16, :] = w_out_ref[pl.ds(pl.multiple_of(own * 16, 16), 16), :]


def forward_body(sel_ref, tokens_ref, pack_ref, rows_ref, hidden_ref, slope_ref, feats_ref, w_in_ref, w_out_ref):
    peers, lines, width = pack_ref.shape
    per = lines - 16
    for g in range(peers):
        w_in_ref[g * per : (g + 1) * per, :] = pack_ref[g, 0:per, :]
        w_out_ref[g * 16 : (g + 1) * 16, :] = pack_ref[g, per:lines, :]
    rows = mm(sel_ref[...], tokens_ref[...]).astype(bf16)
    rows_ref[...] = rows
    pre = mm(rows, w_in_ref[...])
    cdf = 0.5 * (1.0 + lax.erf(pre * 0.7071067811865476))
    slope_ref[...] = cdf + pre * (jnp.exp(-0.5 * pre * pre) * 0.3989422804014327)
    hidden = (pre * cdf).astype(bf16)
    hidden_ref[...] = hidden
    feats_ref[...] = mm(hidden, w_out_ref[...])


def unit_body(feats_ref, unit_ref, inv_ref, rows_ref):
    feats = feats_ref[...]
    inv = lax.rsqrt(jnp.sum(feats * feats, axis=1, keepdims=True) + EPS)
    unit = feats * inv
    unit_ref[...] = unit.T
    inv_ref[...] = jnp.broadcast_to(inv, feats.shape).T[0:8]
    rows_ref[...] = unit.astype(bf16)


def chunks_of(width):
    step = min(256, width)
    return [slice(at, at + step) for at in range(0, width, step)]


def row_of(ref, g):
    return ref[pl.ds(g, 1), :]


def fold(x):
    return x.reshape(x.shape[0] // 8, 8, x.shape[1]).sum(axis=0)


def expo_body(cols_ref, pack_ref, expo_hbm, part_ref, live_ref, weight_ref, expo_ref, total_ref, sems):
    peers = pack_ref.shape[0]
    width = cols_ref.shape[0]
    total_ref[...] = jnp.zeros_like(total_ref)

    def first(g, _):
        rows = pack_ref[g, 0:CAP, :]
        tail = pack_ref[g, CAP : CAP + EXTRA, :].astype(f32)
        live = tail[0:1]
        live_ref[pl.ds(g, 1), :] = live
        weight_ref[pl.ds(g, 1), :] = tail[1:2]
        for part in chunks_of(width):
            cos = mm(cols_ref[part, :], rows, NT)
            expo = jnp.exp(cos * (1.0 / TEACHER_TEMP)) * live
            expo_ref[g, part, :] = expo.astype(bf16)
            total_ref[part, :] += expo[:, 0:128] + expo[:, 128:256]
        pltpu.make_async_copy(expo_ref.at[g], expo_hbm.at[g], sems.at[g]).start()
        return 0

    lax.fori_loop(0, peers, first, 0)
    spread_scale(total_ref)
    lax.fori_loop(0, peers, lambda g, _: row_part(g, expo_ref, total_ref, part_ref), 0)

    def last(g, _):
        pltpu.make_async_copy(expo_ref.at[g], expo_hbm.at[g], sems.at[g]).wait()
        return 0

    lax.fori_loop(0, peers, last, 0)


def spread_scale(total_ref):
    for part in chunks_of(total_ref.shape[0]):
        sums = jnp.sum(total_ref[part, :], axis=1, keepdims=True)
        total_ref[part, :] = jnp.broadcast_to(1.0 / sums, sums.shape[:1] + (128,))


def scaled(expo, scale):
    return jnp.concatenate([expo[:, 0:128] * scale, expo[:, 128:256] * scale], axis=1)


def row_part(g, expo_ref, scale_ref, part_ref):
    acc = jnp.zeros((8, CAP), f32)
    for part in chunks_of(scale_ref.shape[0]):
        acc = acc + fold(scaled(expo_ref[g, part, :].astype(f32), scale_ref[part, :]))
    part_ref[pl.ds(g, 1), :] = jnp.sum(acc, axis=0, keepdims=True)
    return 0


def load_expo(expo_hbm, expo_ref, sems, peers):
    def begin(g, _):
        pltpu.make_async_copy(expo_hbm.at[g], expo_ref.at[g], sems.at[g]).start()
        return 0

    lax.fori_loop(0, peers, begin, 0)


def column_sums(expo_hbm, expo_ref, sems, scale, total_ref, peers):
    def step(g, _):
        pltpu.make_async_copy(expo_hbm.at[g], expo_ref.at[g], sems.at[g]).wait()
        row = row_of(scale, g)
        for part in chunks_of(total_ref.shape[0]):
            expo = expo_ref[g, part, :].astype(f32)
            total_ref[part, :] += expo[:, 0:128] * row[:, 0:128] + expo[:, 128:256] * row[:, 128:256]
        return 0

    lax.fori_loop(0, peers, step, 0)


def balance_body(expo_hbm, sums_ref, live_ref, part_ref, expo_ref, total_ref, scale_ref, sems):
    peers = live_ref.shape[0]
    load_expo(expo_hbm, expo_ref, sems, peers)
    live = live_ref[...]
    scale_ref[...] = live / (sums_ref[...] + 1.0 - live)
    total_ref[...] = jnp.zeros_like(total_ref)
    column_sums(expo_hbm, expo_ref, sems, scale_ref, total_ref, peers)
    spread_scale(total_ref)
    lax.fori_loop(0, peers, lambda g, _: row_part(g, expo_ref, total_ref, part_ref), 0)


def last_body(expo_hbm, sums_ref, live_ref, cols_ref, part_ref, pull_ref, total_ref, expo_ref, scale_ref, sems):
    peers = live_ref.shape[0]
    load_expo(expo_hbm, expo_ref, sems, peers)
    live = live_ref[...]
    scale_ref[...] = live / (sums_ref[...] + 1.0 - live)
    total_ref[...] = jnp.zeros_like(total_ref)
    column_sums(expo_hbm, expo_ref, sems, scale_ref, total_ref, peers)
    spread_scale(total_ref)

    def step(g, _):
        acc = jnp.zeros((8, CAP), f32)
        pull = jnp.zeros((cols_ref.shape[0], CAP), f32)
        for part in chunks_of(total_ref.shape[0]):
            balanced = scaled(expo_ref[g, part, :].astype(f32), total_ref[part, :])
            acc = acc + fold(balanced)
            pull = pull + mm(cols_ref[:, part], balanced.astype(bf16))
        part_ref[pl.ds(g, 1), :] = jnp.sum(acc, axis=0, keepdims=True)
        pull_ref[g] = pull.astype(bf16)
        return 0

    lax.fori_loop(0, peers, step, 0)


def student_body(cols_t_ref, cols_ref, rows_ref, raised_hbm, part_ref, pull_ref, raised_ref, sems):
    peers = rows_ref.shape[0]
    width = cols_t_ref.shape[0]

    def step(g, _):
        rows = rows_ref[g]
        acc = jnp.zeros((8, CAP), f32)
        pull = jnp.zeros((cols_ref.shape[0], CAP), f32)
        for part in chunks_of(width):
            raised = jnp.exp(mm(cols_t_ref[part, :], rows, NT) * (1.0 / STUDENT_TEMP))
            acc = acc + fold(raised)
            raised = raised.astype(bf16)
            raised_ref[g, part, :] = raised
            pull = pull + mm(cols_ref[:, part], raised)
        part_ref[pl.ds(g, 1), :] = jnp.sum(acc, axis=0, keepdims=True)
        pull_ref[g] = pull.astype(bf16)
        pltpu.make_async_copy(raised_ref.at[g], raised_hbm.at[g], sems.at[g]).start()
        return 0

    lax.fori_loop(0, peers, step, 0)

    def last(g, _):
        pltpu.make_async_copy(raised_ref.at[g], raised_hbm.at[g], sems.at[g]).wait()
        return 0

    lax.fori_loop(0, peers, last, 0)


def columns_grad_body(
    expo_hbm, raised_hbm, scale_ref, norm_sum_ref, sums_ref, live_ref, weight_ref, rows_ref, proto_ref, norm_ref,
    grad_ref, expo_ref, raised_ref, acc_ref, alpha_ref, beta_ref, esems, rsems,
):
    peers = live_ref.shape[0]
    load_expo(expo_hbm, expo_ref, esems, peers)
    load_expo(raised_hbm, raised_ref, rsems, peers)
    live = live_ref[...]
    weight = weight_ref[...] * (1.0 / STUDENT_TEMP)
    alpha_ref[...] = weight / norm_sum_ref[...]
    beta_ref[...] = weight * (live / (sums_ref[...] + 1.0 - live))
    acc_ref[...] = jnp.zeros_like(acc_ref)

    def step(g, _):
        pltpu.make_async_copy(expo_hbm.at[g], expo_ref.at[g], esems.at[g]).wait()
        pltpu.make_async_copy(raised_hbm.at[g], raised_ref.at[g], rsems.at[g]).wait()
        alpha, beta = (row_of(alpha_ref, g), row_of(beta_ref, g))
        rows = rows_ref[g]
        for part in chunks_of(acc_ref.shape[0]):
            balanced = scaled(expo_ref[g, part, :].astype(f32), scale_ref[part, :])
            score = raised_ref[g, part, :].astype(f32) * alpha - balanced * beta
            acc_ref[part, :] += mm(score.astype(bf16), rows)
        return 0

    lax.fori_loop(0, peers, step, 0)
    for part in chunks_of(acc_ref.shape[0]):
        grad = acc_ref[part, :].T
        norm = norm_ref[:, part]
        unit = proto_ref[:, part].astype(f32) / norm
        grad_ref[:, part] = (grad - unit * jnp.sum(unit * grad, axis=0, keepdims=True)) / norm


def backward_body(
    push_ref, pull_ref, norm_sum_ref, sums_ref, pack_ref, member_ref, unit_ref, inv_ref, rows_ref, hidden_ref, slope_ref,
    w_ref, send_ref, grad_rows_ref, loss_ref, w_in_ref, w_out_ref,
):
    peers, lines, width = w_ref.shape
    per = lines - 16
    for g in range(peers):
        w_in_ref[g * per : (g + 1) * per, :] = w_ref[g, 0:per, :]
        w_out_ref[g * 16 : (g + 1) * 16, :] = w_ref[g, per:lines, :]
    tail = pack_ref[CAP : CAP + EXTRA, :].astype(f32)
    live, weight = (tail[0:1], tail[1:2])
    norm_sum = norm_sum_ref[...]
    scale = live / (sums_ref[...] + 1.0 - live)
    pull = pull_ref[...]
    unit = unit_ref[...]
    cross = jnp.sum(unit.astype(bf16).astype(f32) * pull, axis=0, keepdims=True) * (1.0 / STUDENT_TEMP)
    row_loss = jnp.log(norm_sum) - scale * cross
    loss = jnp.sum(member_ref[...] * row_loss, axis=1, keepdims=True)
    loss_ref[...] = jnp.broadcast_to(loss, loss_ref.shape)
    grad_unit = (weight * (1.0 / STUDENT_TEMP)) * (push_ref[...] / norm_sum - scale * pull)
    inner = jnp.sum(unit * grad_unit, axis=0, keepdims=True)
    grad_feats = (inv_ref[0:1] * (grad_unit - unit * inner)).T.astype(bf16)
    hidden = hidden_ref[...]
    grad_out = mm(hidden, grad_feats, TN).astype(bf16)
    grad_pre = (mm(grad_feats, w_out_ref[...], NT) * slope_ref[...]).astype(bf16)
    grad_in = mm(rows_ref[...], grad_pre, TN).astype(bf16)
    for g in range(peers):
        send_ref[g, 0:per, :] = grad_in[g * per : (g + 1) * per, :]
        send_ref[g, per:lines, :] = grad_out[g * 16 : (g + 1) * 16, :]
    grad_rows_ref[...] = mm(grad_pre, w_in_ref[...], NT).astype(bf16)


def place_body(sel_ref, rows_ref, out_ref):
    out_ref[...] = mm(sel_ref[...], rows_ref[...], TN).astype(bf16)


def weight_grads_body(parts_ref, grad_in_ref, grad_out_ref):
    peers, lines, width = parts_ref.shape
    per = lines - 16
    wide = peers * 128
    row = iota((wide, wide), 0)
    col = iota((wide, wide), 1)
    goes = (col // 128) * 16 + ((col % 128) // 16) * 128 + col % 16
    order = (row == goes).astype(f32).astype(bf16)
    for m in range(width // 128):
        block = jnp.concatenate([parts_ref[t, 0:per, m * 128 : (m + 1) * 128] for t in range(peers)], axis=1)
        grad_in_ref[:, m * wide : (m + 1) * wide] = mm(block, order)
    for t in range(peers):
        grad_out_ref[t * 16 : (t + 1) * 16, :] = parts_ref[t, per:lines, :].astype(f32)


def exchange(x, axis):
    return lax.all_to_all(x, axis, split_axis=0, concat_axis=0, tiled=True)


def spread(x, axis):
    return exchange(jnp.broadcast_to(x, (lax.axis_size(axis), *x.shape)), axis)


def total(x):
    return x.astype(f32).sum(axis=0)


def everywhere(x):
    return total(spread(total(spread(x, "tensor")), "dp"))


def shards(tokens, teacher_feats, masks, w_in, w_out, proto_student, proto_teacher):
    dim = tokens.shape[1]
    hid = w_in.shape[1]
    bot, width = proto_student.shape
    dp, tensor = (lax.axis_size("dp"), lax.axis_size("tensor"))
    per = w_in.shape[0]
    lines = per + 16
    me = lax.axis_index("dp")
    own = lax.axis_index("tensor").astype(jnp.int32).reshape(1)
    part_hid = hid // tensor

    sel, pack, member = call(
        select_body,
        [((CAP, tokens.shape[0]), bf16), ((CAP + EXTRA, bot), bf16), ((8, CAP), f32)],
        (masks, teacher_feats),
        name="select",
    )
    packs = spread(pack, "dp")
    (w_pack,) = call(
        weights_body, [((lines, part_hid), bf16)], (own, w_in, w_out), in_specs=[SMEM, VMEM, VMEM], name="weights"
    )
    w_packs = spread(w_pack, "dp")
    cols, student_t, teacher_t, norm = call(
        columns_body,
        [((bot, width), bf16), ((width, bot), bf16), ((width, bot), bf16), ((1, width), f32)],
        (proto_student, proto_teacher),
        name="columns",
    )
    big = ((dp, width, CAP), bf16)
    small = ((dp, CAP), f32)
    held = pltpu.VMEM(*big)
    sems = pltpu.SemaphoreType.DMA((dp,))
    sums = pltpu.VMEM((width, 128), f32)
    expo, part, live, weight = call(
        expo_body,
        [big, small, small, small],
        (teacher_t, packs),
        out_specs=[HBM, VMEM, VMEM, VMEM],
        scratch=[held, sums, sems],
        name="expo",
    )
    rows, hidden, slope, feats_part = call(
        forward_body,
        [((CAP, dim), bf16), ((CAP, part_hid), bf16), ((CAP, part_hid), f32), ((CAP, bot), f32)],
        (sel, tokens, w_packs),
        scratch=[pltpu.VMEM((dim, part_hid), bf16), pltpu.VMEM((part_hid, bot), bf16)],
        name="forward",
    )
    feats = total(exchange(feats_part.reshape(tensor, CAP // tensor, bot), "tensor"))
    feats = spread(feats, "tensor").reshape(CAP, bot)
    unit, inv, student_rows = call(
        unit_body, [((bot, CAP), f32), ((8, CAP), f32), ((CAP, bot), bf16)], (feats,), name="unit"
    )
    all_rows = spread(student_rows, "dp")
    row_sum = everywhere(part)
    raised, norm_part, push = call(
        student_body,
        [big, small, ((dp, bot, CAP), bf16)],
        (student_t, cols, all_rows),
        out_specs=[HBM, VMEM, VMEM],
        scratch=[held, sems],
        name="student",
    )
    (part,) = call(
        balance_body,
        [small],
        (expo, row_sum, live),
        in_specs=[HBM, VMEM, VMEM],
        scratch=[held, sums, pltpu.VMEM(*small), sems],
        name="balance",
    )
    both = everywhere(jnp.concatenate([part, norm_part], axis=0))
    row_sum, norm_sum = (both[:dp], both[dp:])
    push_own = total(spread(total(exchange(push, "dp")).astype(bf16), "tensor"))
    part, pull, scale = call(
        last_body,
        [small, ((dp, bot, CAP), bf16), ((width, 128), f32)],
        (expo, row_sum, live, cols),
        in_specs=[HBM, VMEM, VMEM, VMEM],
        scratch=[held, pltpu.VMEM(*small), sems],
        name="last",
    )
    row_sum = everywhere(part)
    pull_own = total(spread(total(exchange(pull, "dp")).astype(bf16), "tensor"))
    (grad_proto,) = call(
        columns_grad_body,
        [((bot, width), f32)],
        (expo, raised, scale, norm_sum, row_sum, live, weight, all_rows, proto_student, norm),
        in_specs=[HBM, HBM] + [VMEM] * 8,
        scratch=[held, held, pltpu.VMEM((width, bot), f32), pltpu.VMEM(*small), pltpu.VMEM(*small), sems, sems],
        name="columns_grad",
    )
    mine = lambda x: lax.dynamic_slice_in_dim(x, me, 1, axis=0)
    send, grad_rows, loss = call(
        backward_body,
        [((dp, lines, part_hid), bf16), ((CAP, dim), bf16), ((8, 128), f32)],
        (push_own, pull_own, mine(norm_sum), mine(row_sum), pack, member, unit, inv, rows, hidden, slope, w_packs),
        scratch=[pltpu.VMEM((dim, part_hid), bf16), pltpu.VMEM((part_hid, bot), bf16)],
        name="backward",
    )
    weight_part = total(exchange(send, "dp")).astype(bf16)
    rows_part = total(exchange(grad_rows.reshape(tensor, CAP // tensor, dim), "tensor")).astype(bf16)
    weight_parts = spread(weight_part, "tensor")
    rows_full = spread(rows_part, "tensor").reshape(CAP, dim)
    grad_in, grad_out = call(
        weight_grads_body,
        [((per, hid), f32), ((w_out.shape[0], bot), f32)],
        (weight_parts,),
        name="weight_grads",
    )
    (d_tokens,) = call(place_body, [(tokens.shape, bf16)], (sel, rows_full), name="place")
    return (d_tokens, grad_in, grad_out, grad_proto, loss[: masks.shape[0], 0])


def solution(mesh):
    placed = (
        P("dp", None),
        P("dp", None),
        P("dp", None),
        P("dp", None),
        P("dp", None),
        P(None, ("dp", "tensor")),
        P(None, ("dp", "tensor")),
    )
    return jax.shard_map(
        shards,
        mesh=mesh,
        in_specs=placed,
        out_specs=(P("dp", None), P("dp", None), P("dp", None), P(None, ("dp", "tensor")), P("dp")),
        check_vma=False,
    )
```

```python
import jax
import jax.numpy as jnp
from jax import lax
from jax.experimental import pallas as pl
from jax.experimental.pallas import tpu as pltpu
from jax.sharding import PartitionSpec as P

ROUNDS = 3
CAP = 256
TEACHER_TEMP = 0.07
STUDENT_TEMP = 0.1
EPS = 1e-06
GRAD_SCALE = 65536.0
INTERPRET = False
f32, bf16 = (jnp.float32, jnp.bfloat16)
VMEM = pl.BlockSpec(memory_space=pltpu.VMEM)
HBM = pl.BlockSpec(memory_space=pl.ANY)
SMEM = pl.BlockSpec(memory_space=pltpu.SMEM)
NT = (((1,), (1,)), ((), ()))
TN = (((0,), (0,)), ((), ()))
EXTRA = 16
HALF = CAP // 2
LINES = CAP + EXTRA


def mm(a, b, dims=None):
    if dims is None:
        return jnp.dot(a, b, preferred_element_type=f32)
    return lax.dot_general(a, b, dims, preferred_element_type=f32)


def call(body, outs, ins, out_specs=None, in_specs=None, scratch=(), name=None):
    outs = tuple(jax.ShapeDtypeStruct(s, d) for s, d in outs)
    return pl.pallas_call(
        body,
        out_shape=outs,
        in_specs=in_specs or [VMEM] * len(ins),
        out_specs=tuple(out_specs or [VMEM] * len(outs)),
        scratch_shapes=list(scratch),
        interpret=INTERPRET,
        name=name,
        compiler_params=pltpu.CompilerParams(vmem_limit_bytes=48 << 20),
    )(*ins)


def iota(shape, dim):
    return lax.broadcasted_iota(jnp.int32, shape, dim)


def copies(pairs, sems):
    return [pltpu.make_async_copy(a, b, sems.at[i]) for i, (a, b) in enumerate(pairs)]


def start_all(peers, make):
    def go(g, _):
        make(g).start()
        return 0

    lax.fori_loop(0, peers, go, 0)


def wait_all(peers, make):
    def go(g, _):
        make(g).wait()
        return 0

    lax.fori_loop(0, peers, go, 0)


def select_body(at_ref, mask_ref, feats_ref, sel_ref, send_hbm, member_ref, mine_ref, unit_ref, pack_ref, sems):
    crops, patches = mask_ref.shape
    mask = mask_ref[...].astype(f32)
    upto = (iota((patches, patches), 0) <= iota((patches, patches), 1)).astype(f32).astype(bf16)
    rank = mm(mask.astype(bf16), upto)
    count = jnp.sum(mask, axis=1, keepdims=True)
    total = jnp.sum(count, axis=0, keepdims=True)
    slot = iota((CAP, patches), 0).astype(f32)
    lane = iota((1, CAP), 1).astype(f32)
    start = jnp.zeros((1, 1), f32)
    weight = jnp.zeros((1, CAP), f32)
    first = iota((CAP, patches), 1) == 0
    member_ref[...] = jnp.zeros_like(member_ref)
    for c in range(crops):
        hit = jnp.where((rank[c : c + 1] + start == slot + 1.0) & (mask[c : c + 1] > 0.0), 1.0, 0.0)
        if c == 0:
            hit = jnp.where(first & (slot >= total), 1.0, hit)
        sel_ref[:, c * patches : (c + 1) * patches] = hit.astype(bf16)
        own = count[c : c + 1]
        inside = jnp.where((lane >= start) & (lane < start + own), 1.0, 0.0)
        part = inside * (1.0 / jnp.maximum(own, 1.0))
        member_ref[c : c + 1, :] = part
        weight = weight + part
        start = start + own
    live = jnp.where(lane < total, 1.0, 0.0)
    picked = mm(sel_ref[...], feats_ref[...])
    scale = lax.rsqrt(jnp.sum(picked * picked, axis=1, keepdims=True) + EPS)
    unit_ref[...] = (picked * scale).astype(bf16)
    at = iota((EXTRA, CAP), 0)
    tail = jnp.where(at == 0, live, jnp.where(at == 1, weight * GRAD_SCALE, 0.0)).astype(bf16)
    mine_ref[...] = tail
    pack_ref[0:HALF, :] = unit_ref[pl.ds(pl.multiple_of(at_ref[0] * HALF, HALF), HALF), :]
    pack_ref[HALF : HALF + EXTRA, :] = tail
    peers = send_hbm.shape[0]
    make = lambda g: pltpu.make_async_copy(pack_ref, send_hbm.at[g], sems.at[g])
    start_all(peers, make)
    wait_all(peers, make)


def columns_body(student_ref, teacher_ref, cols_ref, student_t_ref, teacher_t_ref, norm_ref):
    for part in chunks_of(student_ref.shape[1]):
        wide = student_ref[:, part].astype(f32)
        norm = jnp.sqrt(jnp.sum(wide * wide, axis=0, keepdims=True) + EPS)
        norm_ref[:, part] = norm
        unit = wide / norm
        cols_ref[:, part] = unit.astype(bf16)
        student_t_ref[part, :] = unit.T.astype(bf16)
        wide = teacher_ref[:, part].astype(f32)
        norm = jnp.sqrt(jnp.sum(wide * wide, axis=0, keepdims=True) + EPS)
        teacher_t_ref[part, :] = (wide / norm).T.astype(bf16)


def weights_body(at_ref, w_in_ref, w_out_ref, pack_ref):
    rows, hid = w_in_ref.shape
    half = hid // 2
    bot = w_out_ref.shape[1]
    lines = w_out_ref.shape[0] * bot // half
    pack_ref[0:rows, :] = w_in_ref[:, pl.ds(pl.multiple_of(at_ref[0] * half, half), half)]
    for q in range(half // bot):
        pack_ref[rows : rows + lines, q * bot : (q + 1) * bot] = w_out_ref[q * lines : (q + 1) * lines, :]


def weight_loads(at_ref, w_hbm, w_in_ref, w_out_ref, sems):
    peers = w_hbm.shape[0]
    rows = w_in_ref.shape[0] // peers
    lines = w_hbm.shape[1] - rows
    bot = w_out_ref.shape[1]
    quarters = w_hbm.shape[2] // bot
    pairs = [(w_hbm.at[g, 0:rows, :], w_in_ref.at[g * rows : (g + 1) * rows, :]) for g in range(peers)]
    for i in range(peers // 2):
        for q in range(quarters):
            source = w_hbm.at[at_ref[0] * (peers // 2) + i, rows : rows + lines, q * bot : (q + 1) * bot]
            at = (i * quarters + q) * lines
            pairs.append((source, w_out_ref.at[at : at + lines, :]))
    return copies(pairs, sems)


def forward_body(
    at_ref, sel_ref, tokens_hbm, w_hbm, rows_ref, hidden_ref, slope_ref, feats_ref, tokens_ref, w_in_ref, w_out_ref, sems, tsem
):
    tokens = pltpu.make_async_copy(tokens_hbm, tokens_ref, tsem)
    tokens.start()
    loads = weight_loads(at_ref, w_hbm, w_in_ref, w_out_ref, sems)
    for load in loads:
        load.start()
    tokens.wait()
    rows = mm(sel_ref[...], tokens_ref[...]).astype(bf16)
    rows_ref[...] = rows
    for load in loads:
        load.wait()
    feats = jnp.zeros(feats_ref.shape, f32)
    for part in chunks_of(hidden_ref.shape[1]):
        pre = mm(rows, w_in_ref[:, part])
        cdf = 0.5 * (1.0 + lax.erf(pre * 0.7071067811865476))
        slope_ref[:, part] = cdf + pre * (jnp.exp(-0.5 * pre * pre) * 0.3989422804014327)
        hidden = (pre * cdf).astype(bf16)
        hidden_ref[:, part] = hidden
        feats = feats + mm(hidden, w_out_ref[part, :])
    feats_ref[...] = feats


def unit_body(feats_ref, other_ref, unit_ref, inv_ref, rows_ref):
    feats = feats_ref[...] + other_ref[...]
    inv = lax.rsqrt(jnp.sum(feats * feats, axis=1, keepdims=True) + EPS)
    unit = feats * inv
    unit_ref[...] = unit.T
    inv_ref[...] = jnp.broadcast_to(inv, feats.shape).T[0:8]
    rows_ref[...] = unit.astype(bf16)


def chunks_of(width):
    step = min(256, width)
    return [slice(at, at + step) for at in range(0, width, step)]


def row_of(ref, g):
    return ref[pl.ds(g, 1), :]


def fold(x):
    return x.reshape(x.shape[0] // 8, 8, x.shape[1]).sum(axis=0)


def expo_body(
    at_ref, cols_ref, own_hbm, other_hbm, expo_hbm, part_ref, live_ref, weight_ref,
    own_ref, other_ref, expo_ref, total_ref, sums_ref, sems, own_sems, other_sems,
):
    peers = own_hbm.shape[0]
    width = cols_ref.shape[0]
    load_own = lambda g: pltpu.make_async_copy(own_hbm.at[g], own_ref.at[g], own_sems.at[g])
    load_other = lambda g: pltpu.make_async_copy(other_hbm.at[g], other_ref.at[g], other_sems.at[g])
    store = lambda g: pltpu.make_async_copy(expo_ref.at[g], expo_hbm.at[g], sems.at[g])
    start_all(peers, load_own)
    start_all(peers, load_other)
    total_ref[...] = jnp.zeros_like(total_ref)
    low = at_ref[0] == 0

    def first(g, _):
        load_own(g).wait()
        load_other(g).wait()
        own = own_ref[g, 0:HALF, :]
        other = other_ref[g, 0:HALF, :]
        rows = jnp.concatenate([jnp.where(low, own, other), jnp.where(low, other, own)], axis=0)
        tail = own_ref[g, HALF : HALF + EXTRA, :].astype(f32)
        live = tail[0:1]
        live_ref[pl.ds(g, 1), :] = live
        weight_ref[pl.ds(g, 1), :] = tail[1:2]
        for part in chunks_of(width):
            cos = mm(cols_ref[part, :], rows, NT)
            expo = jnp.exp(cos * (1.0 / TEACHER_TEMP)) * live
            expo_ref[g, part, :] = expo.astype(bf16)
            total_ref[part, :] += expo[:, 0:128] + expo[:, 128:256]
        store(g).start()
        return 0

    lax.fori_loop(0, peers, first, 0)
    spread_scale(total_ref)
    row_parts(expo_ref, total_ref, sums_ref, part_ref)
    wait_all(peers, store)


def spread_scale(total_ref):
    for part in chunks_of(total_ref.shape[0]):
        sums = jnp.sum(total_ref[part, :], axis=1, keepdims=True)
        total_ref[part, :] = jnp.broadcast_to(1.0 / sums, sums.shape[:1] + (128,))


def scaled(expo, scale):
    return jnp.concatenate([expo[:, 0:128] * scale, expo[:, 128:256] * scale], axis=1)


def row_parts(expo_ref, scale_ref, sums_ref, part_ref):
    def step(g, _):
        acc = jnp.zeros((8, CAP), f32)
        for part in chunks_of(scale_ref.shape[0]):
            acc = acc + fold(scaled(expo_ref[g, part, :].astype(f32), scale_ref[part, :]))
        sums_ref[pl.ds(g, 1), :] = jnp.sum(acc, axis=0, keepdims=True)
        return 0

    lax.fori_loop(0, expo_ref.shape[0], step, 0)
    sums = sums_ref[...].astype(bf16)
    for t in range(part_ref.shape[0]):
        part_ref[t] = sums


def relay_body(parts_ref, out_ref):
    sums = parts_ref[0].astype(f32)
    for t in range(1, parts_ref.shape[0]):
        sums = sums + parts_ref[t].astype(f32)
    sums = sums.astype(bf16)
    for g in range(out_ref.shape[0]):
        out_ref[g] = sums


def scales_from(parts_ref, live_ref, scale_ref):
    sums = parts_ref[0].astype(f32)
    for g in range(1, parts_ref.shape[0]):
        sums = sums + parts_ref[g].astype(f32)
    live = live_ref[...]
    scale_ref[...] = live / (sums + 1.0 - live)


def column_sums(load, expo_ref, scale_ref, total_ref):
    total_ref[...] = jnp.zeros_like(total_ref)

    def step(g, _):
        load(g).wait()
        row = row_of(scale_ref, g)
        for part in chunks_of(total_ref.shape[0]):
            expo = expo_ref[g, part, :].astype(f32)
            total_ref[part, :] += expo[:, 0:128] * row[:, 0:128] + expo[:, 128:256] * row[:, 128:256]
        return 0

    lax.fori_loop(0, expo_ref.shape[0], step, 0)
    spread_scale(total_ref)


def balance_body(expo_hbm, parts_ref, live_ref, part_ref, expo_ref, total_ref, sums_ref, scale_ref, sems):
    load = lambda g: pltpu.make_async_copy(expo_hbm.at[g], expo_ref.at[g], sems.at[g])
    start_all(expo_ref.shape[0], load)
    scales_from(parts_ref, live_ref, scale_ref)
    column_sums(load, expo_ref, scale_ref, total_ref)
    row_parts(expo_ref, total_ref, sums_ref, part_ref)


def divide_up(low, g, acc, pull, keep_ref, give_ref):
    rows = jnp.sum(acc, axis=0, keepdims=True)
    rows = jnp.where(iota((EXTRA, CAP), 0) == 0, rows, 0.0).astype(bf16)
    pull = pull.astype(bf16)
    for at, block in ((slice(0, CAP), pull), (slice(CAP, LINES), rows)):
        left, right = (block[:, 0:HALF], block[:, HALF:CAP])
        keep_ref[g, at, :] = jnp.where(low, left, right)
        give_ref[g, at, :] = jnp.where(low, right, left)


def last_body(
    at_ref, expo_hbm, parts_ref, live_ref, cols_ref, keep_hbm, give_hbm, total_ref,
    expo_ref, scale_ref, keep_ref, give_ref, sems, keep_sems, give_sems,
):
    peers = expo_ref.shape[0]
    load = lambda g: pltpu.make_async_copy(expo_hbm.at[g], expo_ref.at[g], sems.at[g])
    keep = lambda g: pltpu.make_async_copy(keep_ref.at[g], keep_hbm.at[g], keep_sems.at[g])
    give = lambda g: pltpu.make_async_copy(give_ref.at[g], give_hbm.at[g], give_sems.at[g])
    start_all(peers, load)
    scales_from(parts_ref, live_ref, scale_ref)
    column_sums(load, expo_ref, scale_ref, total_ref)
    low = at_ref[0] == 0

    def step(g, _):
        acc = jnp.zeros((8, CAP), f32)
        pull = jnp.zeros((cols_ref.shape[0], CAP), f32)
        for part in chunks_of(total_ref.shape[0]):
            balanced = scaled(expo_ref[g, part, :].astype(f32), total_ref[part, :])
            acc = acc + fold(balanced)
            pull = pull + mm(cols_ref[:, part], balanced.astype(bf16))
        divide_up(low, g, acc, pull, keep_ref, give_ref)
        give(g).start()
        keep(g).start()
        return 0

    lax.fori_loop(0, peers, step, 0)
    wait_all(peers, give)
    wait_all(peers, keep)


def student_body(
    at_ref, cols_t_ref, cols_ref, rows_ref, raised_hbm, keep_hbm, give_hbm,
    raised_ref, keep_ref, give_ref, sems, keep_sems, give_sems,
):
    peers = rows_ref.shape[0]
    width = cols_t_ref.shape[0]
    store = lambda g: pltpu.make_async_copy(raised_ref.at[g], raised_hbm.at[g], sems.at[g])
    keep = lambda g: pltpu.make_async_copy(keep_ref.at[g], keep_hbm.at[g], keep_sems.at[g])
    give = lambda g: pltpu.make_async_copy(give_ref.at[g], give_hbm.at[g], give_sems.at[g])
    low = at_ref[0] == 0

    def step(g, _):
        rows = rows_ref[g]
        acc = jnp.zeros((8, CAP), f32)
        pull = jnp.zeros((cols_ref.shape[0], CAP), f32)
        for part in chunks_of(width):
            raised = jnp.exp(mm(cols_t_ref[part, :], rows, NT) * (1.0 / STUDENT_TEMP))
            acc = acc + fold(raised)
            raised = raised.astype(bf16)
            raised_ref[g, part, :] = raised
            pull = pull + mm(cols_ref[:, part], raised)
        divide_up(low, g, acc, pull, keep_ref, give_ref)
        store(g).start()
        give(g).start()
        keep(g).start()
        return 0

    lax.fori_loop(0, peers, step, 0)
    wait_all(peers, give)
    wait_all(peers, keep)
    wait_all(peers, store)


def columns_grad_body(
    expo_hbm, raised_hbm, scale_ref, got_ref, rows_ref, proto_ref, norm_ref,
    grad_ref, expo_ref, raised_ref, acc_ref, esems, rsems,
):
    peers = expo_ref.shape[0]
    load = lambda g: pltpu.make_async_copy(expo_hbm.at[g], expo_ref.at[g], esems.at[g])
    load_raised = lambda g: pltpu.make_async_copy(raised_hbm.at[g], raised_ref.at[g], rsems.at[g])
    start_all(peers, load)
    start_all(peers, load_raised)
    acc_ref[...] = jnp.zeros_like(acc_ref)
    lines = got_ref.shape[1] - EXTRA

    def step(g, _):
        load(g).wait()
        load_raised(g).wait()
        tail = got_ref[g, lines : lines + EXTRA, :].astype(f32)
        alpha = tail[0:1] + tail[1:2]
        beta = tail[2:3] + tail[3:4]
        rows = rows_ref[g]
        for part in chunks_of(acc_ref.shape[0]):
            balanced = scaled(expo_ref[g, part, :].astype(f32), scale_ref[part, :])
            score = raised_ref[g, part, :].astype(f32) * alpha - balanced * beta
            acc_ref[part, :] += mm(score.astype(bf16), rows)
        return 0

    lax.fori_loop(0, peers, step, 0)
    for part in chunks_of(acc_ref.shape[0]):
        grad = acc_ref[part, :].T
        norm = norm_ref[:, part]
        unit = proto_ref[:, part].astype(f32) / norm
        grad_ref[:, part] = (grad - unit * jnp.sum(unit * grad, axis=0, keepdims=True)) / norm


def join(parts_ref):
    halves = []
    for c in range(2):
        acc = parts_ref[c].astype(f32)
        for t in range(c + 2, parts_ref.shape[0], 2):
            acc = acc + parts_ref[t].astype(f32)
        halves.append(acc)
    return jnp.concatenate(halves, axis=1)


def two_parts(x):
    high = x.astype(bf16)
    return (high.astype(f32), x - high.astype(f32))


def backward_body(
    at_ref, push_ref, pull_ref, mine_ref, member_ref, unit_ref, inv_ref, rows_ref, hidden_ref, slope_ref, w_hbm,
    send_hbm, grad_rows_ref, loss_ref, w_in_ref, w_out_ref, send_ref, pre_ref, out_ref, sems, send_sems,
):
    peers = w_hbm.shape[0]
    loads = weight_loads(at_ref, w_hbm, w_in_ref, w_out_ref, sems)
    for load in loads:
        load.start()
    tail = mine_ref[...].astype(f32)
    live, weight = (tail[0:1], tail[1:2] * (1.0 / STUDENT_TEMP))
    push = join(push_ref)
    pull = join(pull_ref)
    norm_sum = push[CAP : CAP + 1]
    push = push[0:CAP]
    scale = live / (pull[CAP : CAP + 1] + 1.0 - live)
    pull = pull[0:CAP]
    unit = unit_ref[...]
    cross = jnp.sum(unit.astype(bf16).astype(f32) * pull, axis=0, keepdims=True) * (1.0 / STUDENT_TEMP)
    row_loss = jnp.log(norm_sum) - scale * cross
    loss = jnp.sum(member_ref[...] * row_loss, axis=1, keepdims=True)
    loss_ref[...] = jnp.broadcast_to(loss, loss_ref.shape)
    alpha = weight / norm_sum
    beta = weight * scale
    grad_unit = push * alpha - pull * beta
    inner = jnp.sum(unit * grad_unit, axis=0, keepdims=True)
    grad_feats = (inv_ref[0:1] * (grad_unit - unit * inner)).T.astype(bf16)
    for load in loads:
        load.wait()
    width = send_ref.shape[2]
    grad_rows = jnp.zeros(grad_rows_ref.shape, f32)
    for part in chunks_of(hidden_ref.shape[1]):
        grad_pre = (mm(grad_feats, w_out_ref[part, :], NT) * slope_ref[:, part]).astype(bf16)
        pre_ref[:, part] = grad_pre
        grad_rows = grad_rows + mm(grad_pre, w_in_ref[:, part], NT)
        out_ref[part, :] = mm(hidden_ref[:, part], grad_feats, TN).astype(bf16)
    grad_rows_ref[...] = grad_rows.astype(bf16)
    core, level = (at_ref[0], at_ref[1])
    own = pre_ref[:, pl.ds(pl.multiple_of(level * width, width), width)]
    grad_in = mm(rows_ref[...], own, TN).astype(bf16)
    per = grad_in.shape[0] // peers
    block = out_ref.shape[0] // (peers // 2)
    share = block // 4
    at = iota((EXTRA, CAP), 0)
    rows = jnp.zeros((EXTRA, CAP), f32)
    for i, x in enumerate(two_parts(alpha) + two_parts(beta)):
        rows = jnp.where(at == i, x, rows)
    rows = rows.astype(bf16)
    store = lambda g: pltpu.make_async_copy(send_ref.at[g], send_hbm.at[g], send_sems.at[g])
    for g in range(peers):
        send_ref[g, 0:per, :] = grad_in[g * per : (g + 1) * per, :]
        start = pl.multiple_of((g % (peers // 2)) * block + level * share, share)
        out = out_ref[pl.ds(start, share), :]
        send_ref[g, per : per + share, :] = jnp.where(core == g // (peers // 2), out, jnp.zeros_like(out))
        send_ref[g, per + share : per + share + EXTRA, :] = rows
        store(g).start()
    wait_all(peers, store)


def place_body(sel_ref, rows_ref, other_ref, out_hbm, out_ref, sems):
    rows = (rows_ref[...].astype(f32) + other_ref[...].astype(f32)).astype(bf16)
    pieces = out_ref.shape[0]
    size = out_ref.shape[1]
    store = lambda i: pltpu.make_async_copy(out_ref.at[i], out_hbm.at[i], sems.at[i])
    for i in range(pieces):
        out_ref[i] = mm(sel_ref[:, i * size : (i + 1) * size], rows, TN).astype(bf16)
        store(i).start()
    wait_all(pieces, store)


def gather_grads_body(got_ref, send_ref):
    peers = got_ref.shape[0]
    lines = send_ref.shape[1]
    acc = got_ref[0, 0:lines, :].astype(f32)
    for g in range(1, peers):
        acc = acc + got_ref[g, 0:lines, :].astype(f32)
    acc = acc.astype(bf16)
    for t in range(send_ref.shape[0]):
        send_ref[t] = acc


def weight_grads_body(at_ref, parts_ref, grad_in_ref, grad_out_ref):
    peers, lines, width = parts_ref.shape
    per = grad_in_ref.shape[0]
    share = lines - per
    for t in range(peers):
        to = ((t % 2) * (peers // 2) + t // 2) * width
        grad_in_ref[:, to : to + width] = parts_ref[t, 0:per, :].astype(f32)
    for z in range(peers // 2):
        grad_out_ref[z * share : (z + 1) * share, :] = parts_ref[2 * z + at_ref[2], per:lines, :].astype(f32)


def exchange(x, axis):
    return lax.all_to_all(x, axis, split_axis=0, concat_axis=0, tiled=True)


def sibling(x):
    peers = lax.axis_size("tensor")
    return lax.ppermute(x, "tensor", [(i, i ^ 1) for i in range(peers)])


def everywhere(part, small):
    got = exchange(part, "tensor")
    (sums,) = call(relay_body, [((small[0], *small), bf16)], (got,), name="relay")
    return exchange(sums, "dp")


def reduced(keep, give):
    both = (keep.astype(f32) + sibling(give).astype(f32)).astype(bf16)
    got = exchange(both, "dp")
    part = got.astype(f32).sum(axis=0).astype(bf16)
    return exchange(jnp.broadcast_to(part, (lax.axis_size("tensor"), *part.shape)), "tensor")


def shards(tokens, teacher_feats, masks, w_in, w_out, proto_student, proto_teacher):
    dim = tokens.shape[1]
    hid = w_in.shape[1]
    bot, width = proto_student.shape
    dp, tensor = (lax.axis_size("dp"), lax.axis_size("tensor"))
    per = w_in.shape[0]
    half = hid // 2
    share = w_out.shape[0] // 4
    t = lax.axis_index("tensor").astype(jnp.int32)
    g = lax.axis_index("dp").astype(jnp.int32)
    at = jnp.stack([t % 2, t // 2, g // (dp // 2)])

    lines = per + w_out.shape[0] * bot // half
    (w_pack,) = call(weights_body, [((lines, half), bf16)], (at, w_in, w_out), in_specs=[SMEM, VMEM, VMEM], name="weights")
    w_all = lax.all_gather(w_pack, "dp", axis=0, tiled=True).reshape(dp, lines, half)
    dma = pltpu.SemaphoreType.DMA
    sems = dma((dp,))
    sel, send, member, mine = call(
        select_body,
        [((CAP, tokens.shape[0]), bf16), ((dp, HALF + EXTRA, bot), bf16), ((8, CAP), f32), ((EXTRA, CAP), bf16)],
        (at, masks, teacher_feats),
        in_specs=[SMEM, VMEM, VMEM],
        out_specs=[VMEM, HBM, VMEM, VMEM],
        scratch=[pltpu.VMEM((CAP, bot), bf16), pltpu.VMEM((HALF + EXTRA, bot), bf16), sems],
        name="select",
    )
    packs = exchange(send, "dp")
    others = sibling(packs)
    cols, student_t, teacher_t, norm = call(
        columns_body,
        [((bot, width), bf16), ((width, bot), bf16), ((width, bot), bf16), ((1, width), f32)],
        (proto_student, proto_teacher),
        name="columns",
    )
    big = ((dp, width, CAP), bf16)
    small = ((dp, CAP), f32)
    part_out = ((tensor, dp, CAP), bf16)
    held = pltpu.VMEM(*big)
    sums = pltpu.VMEM((width, 128), f32)
    pack_held = pltpu.VMEM((dp, HALF + EXTRA, bot), bf16)
    expo, part, live, weight = call(
        expo_body,
        [big, part_out, small, small],
        (at, teacher_t, packs, others),
        in_specs=[SMEM, VMEM, HBM, HBM],
        out_specs=[HBM, VMEM, VMEM, VMEM],
        scratch=[pack_held, pack_held, held, sums, pltpu.VMEM(*small), sems, sems, sems],
        name="expo",
    )
    loads = dma((dp + 2 * dp,))
    w_held = [pltpu.VMEM((dim, half), bf16), pltpu.VMEM((half, bot), bf16)]
    rows, hidden, slope, feats = call(
        forward_body,
        [((CAP, dim), bf16), ((CAP, half), bf16), ((CAP, half), f32), ((CAP, bot), f32)],
        (at, sel, tokens, w_all),
        in_specs=[SMEM, VMEM, HBM, HBM],
        scratch=[pltpu.VMEM(tokens.shape, bf16), *w_held, loads, dma(())],
        name="forward",
    )
    unit, inv, student_rows = call(
        unit_body, [((bot, CAP), f32), ((8, CAP), f32), ((CAP, bot), bf16)], (feats, sibling(feats)), name="unit"
    )
    all_rows = lax.all_gather(student_rows, "dp", axis=0, tiled=True).reshape(dp, CAP, bot)
    got = everywhere(part, small[0])
    (part,) = call(
        balance_body,
        [part_out],
        (expo, got, live),
        in_specs=[HBM, VMEM, VMEM],
        scratch=[held, sums, pltpu.VMEM(*small), pltpu.VMEM(*small), sems],
        name="balance",
    )
    got = everywhere(part, small[0])
    halves = ((dp, LINES, HALF), bf16)
    half_held = pltpu.VMEM(*halves)
    keep, give, scale = call(
        last_body,
        [halves, halves, ((width, 128), f32)],
        (at, expo, got, live, cols),
        in_specs=[SMEM, HBM, VMEM, VMEM, VMEM],
        out_specs=[HBM, HBM, VMEM],
        scratch=[held, pltpu.VMEM(*small), half_held, half_held, sems, sems, sems],
        name="last",
    )
    pull = reduced(keep, give)
    raised, keep, give = call(
        student_body,
        [big, halves, halves],
        (at, student_t, cols, all_rows),
        in_specs=[SMEM, VMEM, VMEM, VMEM],
        out_specs=[HBM, HBM, HBM],
        scratch=[held, half_held, half_held, sems, sems, sems],
        name="student",
    )
    push = reduced(keep, give)
    back_lines = per + share + EXTRA
    send, grad_rows, loss = call(
        backward_body,
        [((dp, back_lines, bot), bf16), ((CAP, dim), bf16), ((8, 128), f32)],
        (at, push, pull, mine, member, unit, inv, rows, hidden, slope, w_all),
        in_specs=[SMEM] + [VMEM] * 9 + [HBM],
        out_specs=[HBM, VMEM, VMEM],
        scratch=[
            *w_held,
            pltpu.VMEM((dp, back_lines, bot), bf16),
            pltpu.VMEM((CAP, half), bf16),
            pltpu.VMEM((half, bot), bf16),
            loads,
            sems,
        ],
        name="backward",
    )
    got = exchange(send, "dp")
    (sent,) = call(gather_grads_body, [((tensor, per + share, bot), bf16)], (got,), name="gather_grads")
    parts = exchange(sent, "tensor")
    (grad_proto,) = call(
        columns_grad_body,
        [((bot, width), f32)],
        (expo, raised, scale, got, all_rows, proto_student, norm),
        in_specs=[HBM, HBM] + [VMEM] * 5,
        scratch=[held, held, pltpu.VMEM((width, bot), f32), sems, sems],
        name="columns_grad",
    )
    pieces = 4
    d_shape = (pieces, tokens.shape[0] // pieces, dim)
    (d_tokens,) = call(
        place_body,
        [(d_shape, bf16)],
        (sel, grad_rows, sibling(grad_rows)),
        out_specs=[HBM],
        scratch=[pltpu.VMEM(d_shape, bf16), dma((pieces,))],
        name="place",
    )
    grad_in, grad_out = call(
        weight_grads_body,
        [((per, hid), f32), ((w_out.shape[0], bot), f32)],
        (at, parts),
        in_specs=[SMEM, VMEM],
        name="weight_grads",
    )
    return (d_tokens.reshape(tokens.shape), grad_in, grad_out, grad_proto, loss[: masks.shape[0], 0])


def solution(mesh):
    placed = (
        P("dp", None),
        P("dp", None),
        P("dp", None),
        P("dp", None),
        P("dp", None),
        P(None, ("dp", "tensor")),
        P(None, ("dp", "tensor")),
    )
    return jax.shard_map(
        shards,
        mesh=mesh,
        in_specs=placed,
        out_specs=(P("dp", None), P("dp", None), P("dp", None), P(None, ("dp", "tensor")), P("dp")),
        check_vma=False,
    )
```

```python
import jax
import jax.numpy as jnp
from jax import lax
from jax.experimental import pallas as pl
from jax.experimental.pallas import tpu as pltpu
from jax.sharding import PartitionSpec as P

ROUNDS = 3
CAP = 256
TEACHER_TEMP = 0.07
STUDENT_TEMP = 0.1
EPS = 1e-06
GRAD_SCALE = 65536.0
INTERPRET = False
f32, bf16 = (jnp.float32, jnp.bfloat16)
VMEM = pl.BlockSpec(memory_space=pltpu.VMEM)
HBM = pl.BlockSpec(memory_space=pl.ANY)
SMEM = pl.BlockSpec(memory_space=pltpu.SMEM)
NT = (((1,), (1,)), ((), ()))
TN = (((0,), (0,)), ((), ()))
EXTRA = 16
HALF = CAP // 2
LINES = CAP + EXTRA


def mm(a, b, dims=None):
    if dims is None:
        return jnp.dot(a, b, preferred_element_type=f32)
    return lax.dot_general(a, b, dims, preferred_element_type=f32)


def call(body, outs, ins, out_specs=None, in_specs=None, scratch=(), name=None):
    outs = tuple(jax.ShapeDtypeStruct(s, d) for s, d in outs)
    return pl.pallas_call(
        body,
        out_shape=outs,
        in_specs=in_specs or [VMEM] * len(ins),
        out_specs=tuple(out_specs or [VMEM] * len(outs)),
        scratch_shapes=list(scratch),
        interpret=INTERPRET,
        name=name,
        compiler_params=pltpu.CompilerParams(vmem_limit_bytes=48 << 20),
    )(*ins)


def iota(shape, dim):
    return lax.broadcasted_iota(jnp.int32, shape, dim)


def copies(pairs, sems):
    return [pltpu.make_async_copy(a, b, sems.at[i]) for i, (a, b) in enumerate(pairs)]


def start_all(peers, make):
    def go(g, _):
        make(g).start()
        return 0

    lax.fori_loop(0, peers, go, 0)


def wait_all(peers, make):
    def go(g, _):
        make(g).wait()
        return 0

    lax.fori_loop(0, peers, go, 0)


def select_body(at_ref, mask_ref, feats_ref, sel_ref, send_hbm, member_ref, mine_ref, unit_ref, pack_ref, sems):
    crops, patches = mask_ref.shape
    mask = mask_ref[...].astype(f32)
    upto = (iota((patches, patches), 0) <= iota((patches, patches), 1)).astype(f32).astype(bf16)
    rank = mm(mask.astype(bf16), upto)
    count = jnp.sum(mask, axis=1, keepdims=True)
    total = jnp.sum(count, axis=0, keepdims=True)
    slot = iota((CAP, patches), 0).astype(f32)
    lane = iota((1, CAP), 1).astype(f32)
    start = jnp.zeros((1, 1), f32)
    weight = jnp.zeros((1, CAP), f32)
    first = iota((CAP, patches), 1) == 0
    member_ref[...] = jnp.zeros_like(member_ref)
    for c in range(crops):
        hit = jnp.where((rank[c : c + 1] + start == slot + 1.0) & (mask[c : c + 1] > 0.0), 1.0, 0.0)
        if c == 0:
            hit = jnp.where(first & (slot >= total), 1.0, hit)
        sel_ref[:, c * patches : (c + 1) * patches] = hit.astype(bf16)
        own = count[c : c + 1]
        inside = jnp.where((lane >= start) & (lane < start + own), 1.0, 0.0)
        part = inside * (1.0 / jnp.maximum(own, 1.0))
        member_ref[c : c + 1, :] = part
        weight = weight + part
        start = start + own
    live = jnp.where(lane < total, 1.0, 0.0)
    picked = mm(sel_ref[...], feats_ref[...])
    scale = lax.rsqrt(jnp.sum(picked * picked, axis=1, keepdims=True) + EPS)
    unit_ref[...] = (picked * scale).astype(bf16)
    at = iota((EXTRA, CAP), 0)
    tail = jnp.where(at == 0, live, jnp.where(at == 1, weight * GRAD_SCALE, 0.0)).astype(bf16)
    mine_ref[...] = tail
    pack_ref[0:HALF, :] = unit_ref[pl.ds(pl.multiple_of(at_ref[0] * HALF, HALF), HALF), :]
    pack_ref[HALF : HALF + EXTRA, :] = tail
    peers = send_hbm.shape[0]
    make = lambda g: pltpu.make_async_copy(pack_ref, send_hbm.at[g], sems.at[g])
    start_all(peers, make)
    wait_all(peers, make)


def columns_body(student_ref, teacher_ref, cols_ref, student_t_ref, teacher_t_ref, norm_ref):
    for part in chunks_of(student_ref.shape[1]):
        wide = student_ref[:, part].astype(f32)
        norm = jnp.sqrt(jnp.sum(wide * wide, axis=0, keepdims=True) + EPS)
        norm_ref[:, part] = norm
        unit = wide / norm
        cols_ref[:, part] = unit.astype(bf16)
        student_t_ref[part, :] = unit.T.astype(bf16)
        wide = teacher_ref[:, part].astype(f32)
        norm = jnp.sqrt(jnp.sum(wide * wide, axis=0, keepdims=True) + EPS)
        teacher_t_ref[part, :] = (wide / norm).T.astype(bf16)


def weights_body(at_ref, w_in_ref, w_out_ref, pack_ref):
    rows, hid = w_in_ref.shape
    half = hid // 2
    bot = w_out_ref.shape[1]
    lines = w_out_ref.shape[0] * bot // half
    pack_ref[0:rows, :] = w_in_ref[:, pl.ds(pl.multiple_of(at_ref[0] * half, half), half)]
    for q in range(half // bot):
        pack_ref[rows : rows + lines, q * bot : (q + 1) * bot] = w_out_ref[q * lines : (q + 1) * lines, :]


def weight_loads(at_ref, w_hbm, w_in_ref, w_out_ref, sems):
    peers = w_hbm.shape[0]
    rows = w_in_ref.shape[0] // peers
    lines = w_hbm.shape[1] - rows
    bot = w_out_ref.shape[1]
    quarters = w_hbm.shape[2] // bot
    pairs = [(w_hbm.at[g, 0:rows, :], w_in_ref.at[g * rows : (g + 1) * rows, :]) for g in range(peers)]
    for i in range(peers // 2):
        for q in range(quarters):
            source = w_hbm.at[at_ref[0] * (peers // 2) + i, rows : rows + lines, q * bot : (q + 1) * bot]
            at = (i * quarters + q) * lines
            pairs.append((source, w_out_ref.at[at : at + lines, :]))
    return copies(pairs, sems)


def forward_body(
    at_ref, sel_ref, tokens_hbm, w_hbm, rows_ref, hidden_ref, slope_ref, feats_ref, tokens_ref, w_in_ref, w_out_ref, sems, tsem
):
    tokens = pltpu.make_async_copy(tokens_hbm, tokens_ref, tsem)
    tokens.start()
    loads = weight_loads(at_ref, w_hbm, w_in_ref, w_out_ref, sems)
    for load in loads:
        load.start()
    tokens.wait()
    rows = mm(sel_ref[...], tokens_ref[...]).astype(bf16)
    rows_ref[...] = rows
    for load in loads:
        load.wait()
    feats = jnp.zeros(feats_ref.shape, f32)
    for part in chunks_of(hidden_ref.shape[1]):
        pre = mm(rows, w_in_ref[:, part])
        cdf = 0.5 * (1.0 + lax.erf(pre * 0.7071067811865476))
        slope_ref[:, part] = cdf + pre * (jnp.exp(-0.5 * pre * pre) * 0.3989422804014327)
        hidden = (pre * cdf).astype(bf16)
        hidden_ref[:, part] = hidden
        feats = feats + mm(hidden, w_out_ref[part, :])
    feats_ref[...] = feats


def unit_body(feats_ref, other_ref, unit_ref, inv_ref, rows_ref):
    feats = feats_ref[...] + other_ref[...]
    inv = lax.rsqrt(jnp.sum(feats * feats, axis=1, keepdims=True) + EPS)
    unit = feats * inv
    unit_ref[...] = unit.T
    inv_ref[...] = jnp.broadcast_to(inv, feats.shape).T[0:8]
    rows_ref[...] = unit.astype(bf16)


def chunks_of(width):
    step = min(256, width)
    return [slice(at, at + step) for at in range(0, width, step)]


def row_of(ref, g):
    return ref[pl.ds(g, 1), :]


def fold(x):
    return x.reshape(x.shape[0] // 8, 8, x.shape[1]).sum(axis=0)


def expo_body(
    at_ref, cols_ref, own_hbm, other_hbm, expo_hbm, part_ref, live_ref, weight_ref,
    rows_ref, tail_ref, expo_ref, total_ref, sums_ref, sems, own_sems, other_sems, tail_sems,
):
    peers = own_hbm.shape[0]
    width = cols_ref.shape[0]
    half = slice(0, HALF)
    core = at_ref[0]
    load_own = lambda g: pltpu.make_async_copy(own_hbm.at[g, half, :], rows_ref.at[g, core], own_sems.at[g])
    load_other = lambda g: pltpu.make_async_copy(other_hbm.at[g, half, :], rows_ref.at[g, 1 - core], other_sems.at[g])
    load_tail = lambda g: pltpu.make_async_copy(own_hbm.at[g, HALF : HALF + EXTRA, :], tail_ref.at[g], tail_sems.at[g])
    store = lambda g: pltpu.make_async_copy(expo_ref.at[g], expo_hbm.at[g], sems.at[g])
    start_all(peers, load_own)
    start_all(peers, load_other)
    start_all(peers, load_tail)
    total_ref[...] = jnp.zeros_like(total_ref)

    def first(g, _):
        load_own(g).wait()
        load_other(g).wait()
        load_tail(g).wait()
        rows = rows_ref[g].reshape(CAP, rows_ref.shape[3])
        tail = tail_ref[g].astype(f32)
        live = tail[0:1]
        live_ref[pl.ds(g, 1), :] = live
        weight_ref[pl.ds(g, 1), :] = tail[1:2]
        for part in chunks_of(width):
            cos = mm(cols_ref[part, :], rows, NT)
            expo = jnp.exp(cos * (1.0 / TEACHER_TEMP)) * live
            expo_ref[g, part, :] = expo.astype(bf16)
            total_ref[part, :] += expo[:, 0:128] + expo[:, 128:256]
        store(g).start()
        return 0

    lax.fori_loop(0, peers, first, 0)
    spread_scale(total_ref)
    row_parts(expo_ref, total_ref, sums_ref, part_ref)
    wait_all(peers, store)


def spread_scale(total_ref):
    for part in chunks_of(total_ref.shape[0]):
        sums = jnp.sum(total_ref[part, :], axis=1, keepdims=True)
        total_ref[part, :] = jnp.broadcast_to(1.0 / sums, sums.shape[:1] + (128,))


def scaled(expo, scale):
    return jnp.concatenate([expo[:, 0:128] * scale, expo[:, 128:256] * scale], axis=1)


def row_parts(expo_ref, scale_ref, sums_ref, part_ref):
    def step(g, _):
        acc = jnp.zeros((8, CAP), f32)
        for part in chunks_of(scale_ref.shape[0]):
            acc = acc + fold(scaled(expo_ref[g, part, :].astype(f32), scale_ref[part, :]))
        sums_ref[pl.ds(g, 1), :] = jnp.sum(acc, axis=0, keepdims=True)
        return 0

    lax.fori_loop(0, expo_ref.shape[0], step, 0)
    sums = sums_ref[...].astype(bf16)
    for t in range(part_ref.shape[0]):
        part_ref[t] = sums


def relay_body(parts_ref, out_ref):
    sums = parts_ref[0].astype(f32)
    for t in range(1, parts_ref.shape[0]):
        sums = sums + parts_ref[t].astype(f32)
    sums = sums.astype(bf16)
    for g in range(out_ref.shape[0]):
        out_ref[g] = sums


def scales_from(parts_ref, live_ref, scale_ref):
    sums = parts_ref[0].astype(f32)
    for g in range(1, parts_ref.shape[0]):
        sums = sums + parts_ref[g].astype(f32)
    live = live_ref[...]
    scale_ref[...] = live / (sums + 1.0 - live)


def column_sums(load, expo_ref, scale_ref, total_ref):
    total_ref[...] = jnp.zeros_like(total_ref)

    def step(g, _):
        load(g).wait()
        row = row_of(scale_ref, g)
        for part in chunks_of(total_ref.shape[0]):
            expo = expo_ref[g, part, :].astype(f32)
            total_ref[part, :] += expo[:, 0:128] * row[:, 0:128] + expo[:, 128:256] * row[:, 128:256]
        return 0

    lax.fori_loop(0, expo_ref.shape[0], step, 0)
    spread_scale(total_ref)


def balance_body(expo_hbm, parts_ref, live_ref, part_ref, expo_ref, total_ref, sums_ref, scale_ref, sems):
    load = lambda g: pltpu.make_async_copy(expo_hbm.at[g], expo_ref.at[g], sems.at[g])
    start_all(expo_ref.shape[0], load)
    scales_from(parts_ref, live_ref, scale_ref)
    column_sums(load, expo_ref, scale_ref, total_ref)
    row_parts(expo_ref, total_ref, sums_ref, part_ref)


def divide_up(g, acc, pull, halves_ref):
    rows = jnp.sum(acc, axis=0, keepdims=True)
    rows = jnp.where(iota((EXTRA, CAP), 0) == 0, rows, 0.0).astype(bf16)
    pull = pull.astype(bf16)
    for at, block in ((slice(0, CAP), pull), (slice(CAP, LINES), rows)):
        halves_ref[0, g, at, :] = block[:, 0:HALF]
        halves_ref[1, g, at, :] = block[:, HALF:CAP]


def last_body(
    at_ref, expo_hbm, parts_ref, live_ref, cols_ref, keep_hbm, give_hbm, total_ref,
    expo_ref, scale_ref, halves_ref, sems, keep_sems, give_sems,
):
    peers = expo_ref.shape[0]
    core = at_ref[0]
    load = lambda g: pltpu.make_async_copy(expo_hbm.at[g], expo_ref.at[g], sems.at[g])
    keep = lambda g: pltpu.make_async_copy(halves_ref.at[core, g], keep_hbm.at[g], keep_sems.at[g])
    give = lambda g: pltpu.make_async_copy(halves_ref.at[1 - core, g], give_hbm.at[g], give_sems.at[g])
    start_all(peers, load)
    scales_from(parts_ref, live_ref, scale_ref)
    column_sums(load, expo_ref, scale_ref, total_ref)

    def step(g, _):
        acc = jnp.zeros((8, CAP), f32)
        pull = jnp.zeros((cols_ref.shape[0], CAP), f32)
        for part in chunks_of(total_ref.shape[0]):
            balanced = scaled(expo_ref[g, part, :].astype(f32), total_ref[part, :])
            acc = acc + fold(balanced)
            pull = pull + mm(cols_ref[:, part], balanced.astype(bf16))
        divide_up(g, acc, pull, halves_ref)
        give(g).start()
        keep(g).start()
        return 0

    lax.fori_loop(0, peers, step, 0)
    wait_all(peers, give)
    wait_all(peers, keep)


def student_body(
    at_ref, cols_t_ref, cols_ref, rows_hbm, raised_hbm, keep_hbm, give_hbm,
    rows_ref, raised_ref, halves_ref, row_sems, sems, keep_sems, give_sems,
):
    peers = rows_ref.shape[0]
    load = lambda g: pltpu.make_async_copy(rows_hbm.at[g], rows_ref.at[g], row_sems.at[g])
    start_all(peers, load)
    core = at_ref[0]
    width = cols_t_ref.shape[0]
    store = lambda g: pltpu.make_async_copy(raised_ref.at[g], raised_hbm.at[g], sems.at[g])
    keep = lambda g: pltpu.make_async_copy(halves_ref.at[core, g], keep_hbm.at[g], keep_sems.at[g])
    give = lambda g: pltpu.make_async_copy(halves_ref.at[1 - core, g], give_hbm.at[g], give_sems.at[g])

    def step(g, _):
        load(g).wait()
        rows = rows_ref[g]
        acc = jnp.zeros((8, CAP), f32)
        pull = jnp.zeros((cols_ref.shape[0], CAP), f32)
        for part in chunks_of(width):
            raised = jnp.exp(mm(cols_t_ref[part, :], rows, NT) * (1.0 / STUDENT_TEMP))
            acc = acc + fold(raised)
            raised = raised.astype(bf16)
            raised_ref[g, part, :] = raised
            pull = pull + mm(cols_ref[:, part], raised)
        divide_up(g, acc, pull, halves_ref)
        store(g).start()
        give(g).start()
        keep(g).start()
        return 0

    lax.fori_loop(0, peers, step, 0)
    wait_all(peers, give)
    wait_all(peers, keep)
    wait_all(peers, store)


def columns_grad_body(
    expo_hbm, raised_hbm, scale_ref, got_hbm, rows_hbm, proto_ref, norm_ref,
    grad_ref, expo_ref, raised_ref, acc_ref, tail_ref, rows_ref, esems, rsems, tail_sems, row_sems,
):
    peers = expo_ref.shape[0]
    load = lambda g: pltpu.make_async_copy(expo_hbm.at[g], expo_ref.at[g], esems.at[g])
    load_raised = lambda g: pltpu.make_async_copy(raised_hbm.at[g], raised_ref.at[g], rsems.at[g])
    lines = got_hbm.shape[1] - EXTRA
    load_tail = lambda g: pltpu.make_async_copy(got_hbm.at[g, lines : lines + EXTRA, :], tail_ref.at[g], tail_sems.at[g])
    load_rows = lambda g: pltpu.make_async_copy(rows_hbm.at[g], rows_ref.at[g], row_sems.at[g])

    def begin(g, _):
        for make in (load_tail, load_rows, load, load_raised):
            make(g).start()
        return 0

    lax.fori_loop(0, peers, begin, 0)
    acc_ref[...] = jnp.zeros_like(acc_ref)

    def step(g, _):
        for make in (load_tail, load_rows, load, load_raised):
            make(g).wait()
        tail = tail_ref[g].astype(f32)
        alpha = tail[0:1] + tail[1:2]
        beta = tail[2:3] + tail[3:4]
        rows = rows_ref[g]
        for part in chunks_of(acc_ref.shape[0]):
            balanced = scaled(expo_ref[g, part, :].astype(f32), scale_ref[part, :])
            score = raised_ref[g, part, :].astype(f32) * alpha - balanced * beta
            acc_ref[part, :] += mm(score.astype(bf16), rows)
        return 0

    lax.fori_loop(0, peers, step, 0)
    for part in chunks_of(acc_ref.shape[0]):
        grad = acc_ref[part, :].T
        norm = norm_ref[:, part]
        unit = proto_ref[:, part].astype(f32) / norm
        grad_ref[:, part] = (grad - unit * jnp.sum(unit * grad, axis=0, keepdims=True)) / norm


def join(core, both_ref, other_ref, at):
    own, other = (both_ref[at], other_ref[at])
    low = core == 0
    return jnp.concatenate([jnp.where(low, own, other), jnp.where(low, other, own)], axis=1)


def two_parts(x):
    high = x.astype(bf16)
    return (high.astype(f32), x - high.astype(f32))


def backward_body(
    at_ref, both_ref, other_ref, mine_ref, member_ref, unit_ref, inv_ref, rows_ref, hidden_ref, slope_ref, w_hbm,
    send_hbm, grad_rows_ref, loss_ref, w_in_ref, w_out_ref, send_ref, pre_ref, out_ref, sems, send_sems,
):
    peers = w_hbm.shape[0]
    loads = weight_loads(at_ref, w_hbm, w_in_ref, w_out_ref, sems)
    for load in loads:
        load.start()
    tail = mine_ref[...].astype(f32)
    live, weight = (tail[0:1], tail[1:2] * (1.0 / STUDENT_TEMP))
    pull = join(at_ref[0], both_ref, other_ref, 0)
    push = join(at_ref[0], both_ref, other_ref, 1)
    norm_sum = push[CAP : CAP + 1]
    push = push[0:CAP]
    scale = live / (pull[CAP : CAP + 1] + 1.0 - live)
    pull = pull[0:CAP]
    unit = unit_ref[...]
    cross = jnp.sum(unit.astype(bf16).astype(f32) * pull, axis=0, keepdims=True) * (1.0 / STUDENT_TEMP)
    row_loss = jnp.log(norm_sum) - scale * cross
    loss = jnp.sum(member_ref[...] * row_loss, axis=1, keepdims=True)
    loss_ref[...] = jnp.broadcast_to(loss, loss_ref.shape)
    alpha = weight / norm_sum
    beta = weight * scale
    grad_unit = push * alpha - pull * beta
    inner = jnp.sum(unit * grad_unit, axis=0, keepdims=True)
    grad_feats = (inv_ref[0:1] * (grad_unit - unit * inner)).T.astype(bf16)
    for load in loads:
        load.wait()
    width = send_ref.shape[2]
    grad_rows = jnp.zeros(grad_rows_ref.shape, f32)
    for part in chunks_of(hidden_ref.shape[1]):
        grad_pre = (mm(grad_feats, w_out_ref[part, :], NT) * slope_ref[:, part]).astype(bf16)
        pre_ref[:, part] = grad_pre
        grad_rows = grad_rows + mm(grad_pre, w_in_ref[:, part], NT)
        out_ref[part, :] = mm(hidden_ref[:, part], grad_feats, TN).astype(bf16)
    grad_rows_ref[...] = grad_rows.astype(bf16)
    core, level = (at_ref[0], at_ref[1])
    own = pre_ref[:, pl.ds(pl.multiple_of(level * width, width), width)]
    grad_in = mm(rows_ref[...], own, TN).astype(bf16)
    per = grad_in.shape[0] // peers
    block = out_ref.shape[0] // (peers // 2)
    share = block // 4
    at = iota((EXTRA, CAP), 0)
    rows = jnp.zeros((EXTRA, CAP), f32)
    for i, x in enumerate(two_parts(alpha) + two_parts(beta)):
        rows = jnp.where(at == i, x, rows)
    rows = rows.astype(bf16)
    store = lambda g: pltpu.make_async_copy(send_ref.at[g], send_hbm.at[g], send_sems.at[g])
    for g in range(peers):
        send_ref[g, 0:per, :] = grad_in[g * per : (g + 1) * per, :]
        start = pl.multiple_of((g % (peers // 2)) * block + level * share, share)
        out = out_ref[pl.ds(start, share), :]
        send_ref[g, per : per + share, :] = jnp.where(core == g // (peers // 2), out, jnp.zeros_like(out))
        send_ref[g, per + share : per + share + EXTRA, :] = rows
        store(g).start()
    wait_all(peers, store)


def place_body(sel_ref, rows_ref, other_ref, out_hbm, out_ref, sems):
    rows = (rows_ref[...].astype(f32) + other_ref[...].astype(f32)).astype(bf16)
    pieces = out_ref.shape[0]
    size = out_ref.shape[1]
    store = lambda i: pltpu.make_async_copy(out_ref.at[i], out_hbm.at[i], sems.at[i])
    for i in range(pieces):
        out_ref[i] = mm(sel_ref[:, i * size : (i + 1) * size], rows, TN).astype(bf16)
        store(i).start()
    wait_all(pieces, store)


def gather_grads_body(got_ref, send_ref):
    peers = got_ref.shape[0]
    lines = send_ref.shape[1]
    acc = got_ref[0, 0:lines, :].astype(f32)
    for g in range(1, peers):
        acc = acc + got_ref[g, 0:lines, :].astype(f32)
    acc = acc.astype(bf16)
    for t in range(send_ref.shape[0]):
        send_ref[t] = acc


def weight_grads_body(at_ref, parts_ref, grad_in_ref, grad_out_ref):
    peers, lines, width = parts_ref.shape
    per = grad_in_ref.shape[0]
    share = lines - per
    for t in range(peers):
        to = ((t % 2) * (peers // 2) + t // 2) * width
        grad_in_ref[:, to : to + width] = parts_ref[t, 0:per, :].astype(f32)
    for z in range(peers // 2):
        grad_out_ref[z * share : (z + 1) * share, :] = parts_ref[2 * z + at_ref[2], per:lines, :].astype(f32)


def exchange(x, axis):
    return lax.all_to_all(x, axis, split_axis=0, concat_axis=0, tiled=True)


def sibling(x):
    peers = lax.axis_size("tensor")
    return lax.ppermute(x, "tensor", [(i, i ^ 1) for i in range(peers)])


def everywhere(part, small):
    got = exchange(part, "tensor")
    (sums,) = call(relay_body, [((small[0], *small), bf16)], (got,), name="relay")
    return exchange(sums, "dp")


def levels(x, by):
    peers = lax.axis_size("tensor")
    return lax.ppermute(x, "tensor", [(i, i ^ (2 * by)) for i in range(peers)])


def paired(keep, give):
    return (keep.astype(f32) + sibling(give).astype(f32)).astype(bf16)


def slot_sums_body(parts_hbm, out_ref, parts_ref, sems):
    peers = parts_hbm.shape[0]
    load = lambda g: pltpu.make_async_copy(parts_hbm.at[g], parts_ref.at[g], sems.at[g])
    start_all(peers, load)
    load(0).wait()
    acc = parts_ref[0].astype(f32)
    for g in range(1, peers):
        load(g).wait()
        acc = acc + parts_ref[g].astype(f32)
    out_ref[...] = acc.astype(bf16)


def slot_sums(parts):
    out = parts.shape[1:]
    scratch = [pltpu.VMEM(parts.shape, bf16), pltpu.SemaphoreType.DMA((parts.shape[0],))]
    return call(slot_sums_body, [(out, bf16)], (parts,), in_specs=[HBM], scratch=scratch, name="slot_sums")[0]


def after(x, earlier):
    return lax.optimization_barrier((x, earlier))[0]


def shards(tokens, teacher_feats, masks, w_in, w_out, proto_student, proto_teacher):
    dim = tokens.shape[1]
    hid = w_in.shape[1]
    bot, width = proto_student.shape
    dp, tensor = (lax.axis_size("dp"), lax.axis_size("tensor"))
    per = w_in.shape[0]
    half = hid // 2
    share = w_out.shape[0] // 4
    t = lax.axis_index("tensor").astype(jnp.int32)
    g = lax.axis_index("dp").astype(jnp.int32)
    at = jnp.stack([t % 2, t // 2, g // (dp // 2)])

    lines = per + w_out.shape[0] * bot // half
    (w_pack,) = call(weights_body, [((lines, half), bf16)], (at, w_in, w_out), in_specs=[SMEM, VMEM, VMEM], name="weights")
    w_all = lax.all_gather(w_pack, "dp", axis=0, tiled=True).reshape(dp, lines, half)
    dma = pltpu.SemaphoreType.DMA
    sems = dma((dp,))
    sel, send, member, mine = call(
        select_body,
        [((CAP, tokens.shape[0]), bf16), ((dp, HALF + EXTRA, bot), bf16), ((8, CAP), f32), ((EXTRA, CAP), bf16)],
        (at, masks, teacher_feats),
        in_specs=[SMEM, VMEM, VMEM],
        out_specs=[VMEM, HBM, VMEM, VMEM],
        scratch=[pltpu.VMEM((CAP, bot), bf16), pltpu.VMEM((HALF + EXTRA, bot), bf16), sems],
        name="select",
    )
    packs = exchange(send, "dp")
    others = sibling(packs)
    cols, student_t, teacher_t, norm = call(
        columns_body,
        [((bot, width), bf16), ((width, bot), bf16), ((width, bot), bf16), ((1, width), f32)],
        (proto_student, proto_teacher),
        name="columns",
    )
    big = ((dp, width, CAP), bf16)
    small = ((dp, CAP), f32)
    part_out = ((tensor, dp, CAP), bf16)
    held = pltpu.VMEM(*big)
    sums = pltpu.VMEM((width, 128), f32)
    expo, part, live, weight = call(
        expo_body,
        [big, part_out, small, small],
        (at, teacher_t, packs, others),
        in_specs=[SMEM, VMEM, HBM, HBM],
        out_specs=[HBM, VMEM, VMEM, VMEM],
        scratch=[
            pltpu.VMEM((dp, 2, HALF, bot), bf16),
            pltpu.VMEM((dp, EXTRA, bot), bf16),
            held,
            sums,
            pltpu.VMEM(*small),
            sems,
            sems,
            sems,
            sems,
        ],
        name="expo",
    )
    loads = dma((dp + 2 * dp,))
    w_held = [pltpu.VMEM((dim, half), bf16), pltpu.VMEM((half, bot), bf16)]
    rows, hidden, slope, feats = call(
        forward_body,
        [((CAP, dim), bf16), ((CAP, half), bf16), ((CAP, half), f32), ((CAP, bot), f32)],
        (at, sel, tokens, after(w_all, part)),
        in_specs=[SMEM, VMEM, HBM, HBM],
        scratch=[pltpu.VMEM(tokens.shape, bf16), *w_held, loads, dma(())],
        name="forward",
    )
    unit, inv, student_rows = call(
        unit_body, [((bot, CAP), f32), ((8, CAP), f32), ((CAP, bot), bf16)], (feats, sibling(feats)), name="unit"
    )
    all_rows = lax.all_gather(student_rows, "dp", axis=0, tiled=True).reshape(dp, CAP, bot)
    got = everywhere(part, small[0])
    (part,) = call(
        balance_body,
        [part_out],
        (expo, got, live),
        in_specs=[HBM, VMEM, VMEM],
        scratch=[held, sums, pltpu.VMEM(*small), pltpu.VMEM(*small), sems],
        name="balance",
    )
    got = everywhere(part, small[0])
    halves = ((dp, LINES, HALF), bf16)
    half_held = pltpu.VMEM((2, *halves[0]), bf16)
    keep, give, scale = call(
        last_body,
        [halves, halves, ((width, 128), f32)],
        (at, expo, got, live, cols),
        in_specs=[SMEM, HBM, VMEM, VMEM, VMEM],
        out_specs=[HBM, HBM, VMEM],
        scratch=[held, pltpu.VMEM(*small), half_held, sems, sems, sems],
        name="last",
    )
    pull = paired(keep, give)
    pull_got = exchange(pull, "dp")
    all_rows = after(all_rows, pull)
    raised, keep, give = call(
        student_body,
        [big, halves, halves],
        (at, student_t, cols, all_rows),
        in_specs=[SMEM, VMEM, VMEM, HBM],
        out_specs=[HBM, HBM, HBM],
        scratch=[pltpu.VMEM((dp, CAP, bot), bf16), held, half_held, sems, sems, sems, sems],
        name="student",
    )
    push_got = exchange(paired(keep, give), "dp")
    both = jnp.stack([slot_sums(pull_got), slot_sums(push_got)])
    near, far, last = (levels(both, by) for by in (1, 2, 3))
    wide = lambda x: x.astype(f32)
    both = (wide(both) + wide(near)) + (wide(far) + wide(last))
    back_lines = per + share + EXTRA
    send, grad_rows, loss = call(
        backward_body,
        [((dp, back_lines, bot), bf16), ((CAP, dim), bf16), ((8, 128), f32)],
        (at, both, sibling(both), mine, member, unit, inv, rows, hidden, slope, w_all),
        in_specs=[SMEM] + [VMEM] * 9 + [HBM],
        out_specs=[HBM, VMEM, VMEM],
        scratch=[
            *w_held,
            pltpu.VMEM((dp, back_lines, bot), bf16),
            pltpu.VMEM((CAP, half), bf16),
            pltpu.VMEM((half, bot), bf16),
            loads,
            sems,
        ],
        name="backward",
    )
    got = exchange(send, "dp")
    pieces = 4
    d_shape = (pieces, tokens.shape[0] // pieces, dim)
    (d_tokens,) = call(
        place_body,
        [(d_shape, bf16)],
        (sel, grad_rows, sibling(grad_rows)),
        out_specs=[HBM],
        scratch=[pltpu.VMEM(d_shape, bf16), dma((pieces,))],
        name="place",
    )
    got, d_tokens = lax.optimization_barrier((got, d_tokens))
    (sent,) = call(gather_grads_body, [((tensor, per + share, bot), bf16)], (got,), name="gather_grads")
    parts = exchange(sent, "tensor")
    (grad_proto,) = call(
        columns_grad_body,
        [((bot, width), f32)],
        (expo, raised, scale, got, all_rows, proto_student, norm),
        in_specs=[HBM, HBM, VMEM, HBM, HBM, VMEM, VMEM],
        scratch=[
            held,
            held,
            pltpu.VMEM((width, bot), f32),
            pltpu.VMEM((dp, EXTRA, CAP), bf16),
            pltpu.VMEM((dp, CAP, bot), bf16),
            sems,
            sems,
            sems,
            sems,
        ],
        name="columns_grad",
    )
    grad_in, grad_out = call(
        weight_grads_body,
        [((per, hid), f32), ((w_out.shape[0], bot), f32)],
        (at, parts),
        in_specs=[SMEM, VMEM],
        name="weight_grads",
    )
    return (d_tokens.reshape(tokens.shape), grad_in, grad_out, grad_proto, loss[: masks.shape[0], 0])


def solution(mesh):
    placed = (
        P("dp", None),
        P("dp", None),
        P("dp", None),
        P("dp", None),
        P("dp", None),
        P(None, ("dp", "tensor")),
        P(None, ("dp", "tensor")),
    )
    return jax.shard_map(
        shards,
        mesh=mesh,
        in_specs=placed,
        out_specs=(P("dp", None), P("dp", None), P("dp", None), P(None, ("dp", "tensor")), P("dp")),
        check_vma=False,
    )
```

```python
import jax
import jax.numpy as jnp
from jax import lax
from jax.experimental import pallas as pl
from jax.experimental.pallas import tpu as pltpu
from jax.sharding import PartitionSpec as P

CAP = 256
TEACHER_TEMP = 0.07
STUDENT_TEMP = 0.1
EPS = 1e-06
GRAD_SCALE = 65536.0
INTERPRET = False
f32, bf16 = (jnp.float32, jnp.bfloat16)
VMEM = pl.BlockSpec(memory_space=pltpu.VMEM)
HBM = pl.BlockSpec(memory_space=pl.ANY)
SMEM = pl.BlockSpec(memory_space=pltpu.SMEM)
NT = (((1,), (1,)), ((), ()))
TN = (((0,), (0,)), ((), ()))
EXTRA = 16
HALF = CAP // 2
LINES = CAP + EXTRA


def mm(a, b, dims=None):
    if dims is None:
        return jnp.dot(a, b, preferred_element_type=f32)
    return lax.dot_general(a, b, dims, preferred_element_type=f32)


def call(body, outs, ins, out_specs=None, in_specs=None, scratch=()):
    outs = tuple(jax.ShapeDtypeStruct(s, d) for s, d in outs)
    return pl.pallas_call(
        body,
        out_shape=outs,
        in_specs=in_specs or [VMEM] * len(ins),
        out_specs=tuple(out_specs or [VMEM] * len(outs)),
        scratch_shapes=list(scratch),
        interpret=INTERPRET,
        compiler_params=pltpu.CompilerParams(vmem_limit_bytes=48 << 20),
    )(*ins)


def iota(shape, dim):
    return lax.broadcasted_iota(jnp.int32, shape, dim)


def copies(pairs, sems):
    return [pltpu.make_async_copy(a, b, sems.at[i]) for i, (a, b) in enumerate(pairs)]


GROUP = 4
UNROLL = 4


def group(ref, q):
    return ref.at[pl.ds(q * GROUP, GROUP)]


def start_all(number, make):
    def go(i, _):
        make(i).start()
        return 0

    lax.fori_loop(0, number, go, 0)


def wait_all(number, make):
    def go(i, _):
        make(i).wait()
        return 0

    lax.fori_loop(0, number, go, 0)


def over_groups(peers, step, loads=(), stores=(), unroll=1):
    def go(q, _):
        for make in loads:
            make(q).wait()
        lax.fori_loop(0, GROUP, lambda i, _: step(q * GROUP + i), 0, unroll=unroll)
        for make in stores:
            make(q).start()
        return 0

    lax.fori_loop(0, peers // GROUP, go, 0)


def select_body(at_ref, mask_ref, feats_ref, sel_ref, send_hbm, member_ref, mine_ref, unit_ref, pack_ref, sems):
    crops, patches = mask_ref.shape
    mask = mask_ref[...].astype(f32)
    upto = (iota((patches, patches), 0) <= iota((patches, patches), 1)).astype(f32).astype(bf16)
    rank = mm(mask.astype(bf16), upto)
    count = jnp.sum(mask, axis=1, keepdims=True)
    total = jnp.sum(count, axis=0, keepdims=True)
    slot = iota((CAP, patches), 0).astype(f32)
    lane = iota((1, CAP), 1).astype(f32)
    start = jnp.zeros((1, 1), f32)
    weight = jnp.zeros((1, CAP), f32)
    first = iota((CAP, patches), 1) == 0
    member_ref[...] = jnp.zeros_like(member_ref)
    for c in range(crops):
        hit = jnp.where((rank[c : c + 1] + start == slot + 1.0) & (mask[c : c + 1] > 0.0), 1.0, 0.0)
        if c == 0:
            hit = jnp.where(first & (slot >= total), 1.0, hit)
        sel_ref[:, c * patches : (c + 1) * patches] = hit.astype(bf16)
        own = count[c : c + 1]
        inside = jnp.where((lane >= start) & (lane < start + own), 1.0, 0.0)
        part = inside * (1.0 / jnp.maximum(own, 1.0))
        member_ref[c : c + 1, :] = part
        weight = weight + part
        start = start + own
    live = jnp.where(lane < total, 1.0, 0.0)
    picked = mm(sel_ref[...], feats_ref[...])
    scale = lax.rsqrt(jnp.sum(picked * picked, axis=1, keepdims=True) + EPS)
    unit_ref[...] = (picked * scale).astype(bf16)
    at = iota((EXTRA, CAP), 0)
    tail = jnp.where(at == 0, live, jnp.where(at == 1, weight * GRAD_SCALE, 0.0)).astype(bf16)
    mine_ref[...] = tail
    pack_ref[0:HALF, :] = unit_ref[pl.ds(pl.multiple_of(at_ref[0] * HALF, HALF), HALF), :]
    pack_ref[HALF : HALF + EXTRA, :] = tail
    peers = send_hbm.shape[0]
    make = lambda g: pltpu.make_async_copy(pack_ref, send_hbm.at[g], sems.at[g])
    start_all(peers, make)
    wait_all(peers, make)


def columns_body(student_ref, teacher_ref, cols_ref, student_t_ref, teacher_t_ref, norm_ref):
    for part in chunks_of(student_ref.shape[1]):
        wide = student_ref[:, part].astype(f32)
        norm = jnp.sqrt(jnp.sum(wide * wide, axis=0, keepdims=True) + EPS)
        norm_ref[:, part] = norm
        unit = wide / norm
        cols_ref[:, part] = unit.astype(bf16)
        student_t_ref[part, :] = unit.T.astype(bf16)
        wide = teacher_ref[:, part].astype(f32)
        norm = jnp.sqrt(jnp.sum(wide * wide, axis=0, keepdims=True) + EPS)
        teacher_t_ref[part, :] = (wide / norm).T.astype(bf16)


def weights_body(at_ref, w_in_ref, w_out_ref, pack_ref):
    rows, hid = w_in_ref.shape
    half = hid // 2
    bot = w_out_ref.shape[1]
    lines = w_out_ref.shape[0] * bot // half
    pack_ref[0:rows, :] = w_in_ref[:, pl.ds(pl.multiple_of(at_ref[0] * half, half), half)]
    for q in range(half // bot):
        pack_ref[rows : rows + lines, q * bot : (q + 1) * bot] = w_out_ref[q * lines : (q + 1) * lines, :]


def weight_loads(at_ref, w_hbm, w_in_ref, w_out_ref, sems):
    peers = w_hbm.shape[0]
    rows = w_in_ref.shape[0] // peers
    lines = w_hbm.shape[1] - rows
    bot = w_out_ref.shape[1]
    quarters = w_hbm.shape[2] // bot
    pairs = [(w_hbm.at[g, 0:rows, :], w_in_ref.at[g * rows : (g + 1) * rows, :]) for g in range(peers)]
    for i in range(peers // 2):
        for q in range(quarters):
            source = w_hbm.at[at_ref[0] * (peers // 2) + i, rows : rows + lines, q * bot : (q + 1) * bot]
            at = (i * quarters + q) * lines
            pairs.append((source, w_out_ref.at[at : at + lines, :]))
    return copies(pairs, sems)


def forward_body(
    at_ref, sel_ref, tokens_hbm, w_hbm, rows_ref, hidden_ref, slope_ref, feats_ref, tokens_ref, w_in_ref, w_out_ref, sems, tsem
):
    tokens = pltpu.make_async_copy(tokens_hbm, tokens_ref, tsem)
    tokens.start()
    loads = weight_loads(at_ref, w_hbm, w_in_ref, w_out_ref, sems)
    for load in loads:
        load.start()
    tokens.wait()
    rows = mm(sel_ref[...], tokens_ref[...]).astype(bf16)
    rows_ref[...] = rows
    for load in loads:
        load.wait()
    feats = jnp.zeros(feats_ref.shape, f32)
    for part in chunks_of(hidden_ref.shape[1]):
        pre = mm(rows, w_in_ref[:, part])
        cdf = 0.5 * (1.0 + lax.erf(pre * 0.7071067811865476))
        slope_ref[:, part] = cdf + pre * (jnp.exp(-0.5 * pre * pre) * 0.3989422804014327)
        hidden = (pre * cdf).astype(bf16)
        hidden_ref[:, part] = hidden
        feats = feats + mm(hidden, w_out_ref[part, :])
    feats_ref[...] = feats


def unit_body(feats_ref, other_ref, unit_ref, inv_ref, rows_ref):
    feats = feats_ref[...] + other_ref[...]
    inv = lax.rsqrt(jnp.sum(feats * feats, axis=1, keepdims=True) + EPS)
    unit = feats * inv
    unit_ref[...] = unit.T
    inv_ref[...] = jnp.broadcast_to(inv, feats.shape).T[0:8]
    rows_ref[...] = unit.astype(bf16)


def chunks_of(width):
    step = min(256, width)
    return [slice(at, at + step) for at in range(0, width, step)]


def row_of(ref, g):
    return ref[pl.ds(g, 1), :]


def fold(x):
    return x.reshape(x.shape[0] // 8, 8, x.shape[1]).sum(axis=0)


def expo_body(
    at_ref, cols_ref, own_hbm, other_hbm, expo_hbm, part_ref, live_ref, weight_ref,
    rows_ref, tail_ref, expo_ref, total_ref, sums_ref, sems, own_sems, other_sems, tail_sems,
):
    peers = own_hbm.shape[0]
    width = cols_ref.shape[0]
    core = at_ref[0]
    number = peers // GROUP
    rows_of = lambda ref, q: ref.at[pl.ds(q * GROUP, GROUP), 0:HALF, :]
    rows_at = lambda q, c: rows_ref.at[pl.ds(q * GROUP, GROUP), c]
    load_own = lambda q: pltpu.make_async_copy(rows_of(own_hbm, q), rows_at(q, core), own_sems.at[q])
    load_other = lambda q: pltpu.make_async_copy(rows_of(other_hbm, q), rows_at(q, 1 - core), other_sems.at[q])
    load_tail = pltpu.make_async_copy(own_hbm.at[:, HALF : HALF + EXTRA, :], tail_ref, tail_sems.at[0])
    store = lambda q: pltpu.make_async_copy(group(expo_ref, q), group(expo_hbm, q), sems.at[q])
    load_tail.start()
    start_all(number, load_own)
    start_all(number, load_other)
    total_ref[...] = jnp.zeros_like(total_ref)
    load_tail.wait()

    def first(g):
        rows = rows_ref[g].reshape(CAP, rows_ref.shape[3])
        tail = tail_ref[g].astype(f32)
        live = tail[0:1]
        live_ref[pl.ds(g, 1), :] = live
        weight_ref[pl.ds(g, 1), :] = tail[1:2]
        for part in chunks_of(width):
            cos = mm(cols_ref[part, :], rows, NT)
            expo = jnp.exp(cos * (1.0 / TEACHER_TEMP)) * live
            expo_ref[g, part, :] = expo.astype(bf16)
            total_ref[part, :] += expo[:, 0:128] + expo[:, 128:256]
        return 0

    over_groups(peers, first, (load_own, load_other), (store,), UNROLL)
    spread_scale(total_ref)
    row_parts(expo_ref, total_ref, sums_ref, part_ref)
    wait_all(number, store)


def spread_scale(total_ref):
    for part in chunks_of(total_ref.shape[0]):
        sums = jnp.sum(total_ref[part, :], axis=1, keepdims=True)
        total_ref[part, :] = jnp.broadcast_to(1.0 / sums, sums.shape[:1] + (128,))


def scaled(expo, scale):
    return jnp.concatenate([expo[:, 0:128] * scale, expo[:, 128:256] * scale], axis=1)


def row_parts(expo_ref, scale_ref, sums_ref, part_ref):
    def step(g):
        acc = jnp.zeros((8, CAP), f32)
        for part in chunks_of(scale_ref.shape[0]):
            acc = acc + fold(scaled(expo_ref[g, part, :].astype(f32), scale_ref[part, :]))
        sums_ref[pl.ds(g, 1), :] = jnp.sum(acc, axis=0, keepdims=True)
        return 0

    over_groups(expo_ref.shape[0], step, unroll=UNROLL)
    sums = sums_ref[...].astype(bf16)
    for t in range(part_ref.shape[0]):
        part_ref[t] = sums


def relay_body(parts_ref, out_ref):
    sums = parts_ref[0].astype(f32)
    for t in range(1, parts_ref.shape[0]):
        sums = sums + parts_ref[t].astype(f32)
    sums = sums.astype(bf16)
    for g in range(out_ref.shape[0]):
        out_ref[g] = sums


def scales_from(parts_ref, live_ref, scale_ref):
    sums = parts_ref[0].astype(f32)
    for g in range(1, parts_ref.shape[0]):
        sums = sums + parts_ref[g].astype(f32)
    live = live_ref[...]
    scale_ref[...] = live / (sums + 1.0 - live)


def column_sums(load, expo_ref, scale_ref, total_ref):
    total_ref[...] = jnp.zeros_like(total_ref)

    def step(g):
        row = row_of(scale_ref, g)
        for part in chunks_of(total_ref.shape[0]):
            expo = expo_ref[g, part, :].astype(f32)
            total_ref[part, :] += expo[:, 0:128] * row[:, 0:128] + expo[:, 128:256] * row[:, 128:256]
        return 0

    over_groups(expo_ref.shape[0], step, (load,), unroll=UNROLL)
    spread_scale(total_ref)


def balance_body(expo_hbm, parts_ref, live_ref, part_ref, expo_ref, total_ref, sums_ref, scale_ref, sems):
    load = lambda q: pltpu.make_async_copy(group(expo_hbm, q), group(expo_ref, q), sems.at[q])
    start_all(expo_ref.shape[0] // GROUP, load)
    scales_from(parts_ref, live_ref, scale_ref)
    column_sums(load, expo_ref, scale_ref, total_ref)
    row_parts(expo_ref, total_ref, sums_ref, part_ref)


def divide_up(g, acc, pull, halves_ref):
    rows = jnp.sum(acc, axis=0, keepdims=True)
    rows = jnp.where(iota((EXTRA, CAP), 0) == 0, rows, 0.0).astype(bf16)
    pull = pull.astype(bf16)
    for at, block in ((slice(0, CAP), pull), (slice(CAP, LINES), rows)):
        halves_ref[0, g, at, :] = block[:, 0:HALF]
        halves_ref[1, g, at, :] = block[:, HALF:CAP]


def last_body(
    at_ref, expo_hbm, parts_ref, live_ref, cols_ref, keep_hbm, give_hbm, total_ref,
    expo_ref, scale_ref, halves_ref, sems, keep_sems, give_sems,
):
    peers = expo_ref.shape[0]
    core = at_ref[0]
    load = lambda q: pltpu.make_async_copy(group(expo_hbm, q), group(expo_ref, q), sems.at[q])
    half_at = lambda c, q: halves_ref.at[c, pl.ds(q * GROUP, GROUP)]
    keep = lambda q: pltpu.make_async_copy(half_at(core, q), group(keep_hbm, q), keep_sems.at[q])
    give = lambda q: pltpu.make_async_copy(half_at(1 - core, q), group(give_hbm, q), give_sems.at[q])
    number = peers // GROUP
    start_all(number, load)
    scales_from(parts_ref, live_ref, scale_ref)
    column_sums(load, expo_ref, scale_ref, total_ref)

    def step(g):
        acc = jnp.zeros((8, CAP), f32)
        pull = jnp.zeros((cols_ref.shape[0], CAP), f32)
        for part in chunks_of(total_ref.shape[0]):
            balanced = scaled(expo_ref[g, part, :].astype(f32), total_ref[part, :])
            acc = acc + fold(balanced)
            pull = pull + mm(cols_ref[:, part], balanced.astype(bf16))
        divide_up(g, acc, pull, halves_ref)
        return 0

    over_groups(peers, step, (), (give, keep), UNROLL)
    wait_all(number, give)
    wait_all(number, keep)


def student_body(
    at_ref, cols_t_ref, cols_ref, rows_hbm, raised_hbm, keep_hbm, give_hbm,
    rows_ref, raised_ref, halves_ref, row_sems, sems, keep_sems, give_sems,
):
    peers = rows_ref.shape[0]
    load = lambda q: pltpu.make_async_copy(group(rows_hbm, q), group(rows_ref, q), row_sems.at[q])
    start_all(peers // GROUP, load)
    core = at_ref[0]
    width = cols_t_ref.shape[0]
    store = lambda q: pltpu.make_async_copy(group(raised_ref, q), group(raised_hbm, q), sems.at[q])
    half_at = lambda c, q: halves_ref.at[c, pl.ds(q * GROUP, GROUP)]
    keep = lambda q: pltpu.make_async_copy(half_at(core, q), group(keep_hbm, q), keep_sems.at[q])
    give = lambda q: pltpu.make_async_copy(half_at(1 - core, q), group(give_hbm, q), give_sems.at[q])
    number = peers // GROUP

    def step(g):
        rows = rows_ref[g]
        acc = jnp.zeros((8, CAP), f32)
        pull = jnp.zeros((cols_ref.shape[0], CAP), f32)
        for part in chunks_of(width):
            raised = jnp.exp(mm(cols_t_ref[part, :], rows, NT) * (1.0 / STUDENT_TEMP))
            acc = acc + fold(raised)
            raised = raised.astype(bf16)
            raised_ref[g, part, :] = raised
            pull = pull + mm(cols_ref[:, part], raised)
        divide_up(g, acc, pull, halves_ref)
        return 0

    over_groups(peers, step, (load,), (store, give, keep), UNROLL)
    for make in (give, keep, store):
        wait_all(number, make)


def columns_grad_body(
    expo_hbm, raised_hbm, scale_ref, got_hbm, rows_hbm, proto_ref, norm_ref,
    grad_ref, expo_ref, raised_ref, acc_ref, tail_ref, rows_ref, esems, rsems, tail_sems, row_sems,
):
    peers = expo_ref.shape[0]
    load = lambda q: pltpu.make_async_copy(group(expo_hbm, q), group(expo_ref, q), esems.at[q])
    load_raised = lambda q: pltpu.make_async_copy(group(raised_hbm, q), group(raised_ref, q), rsems.at[q])
    load_rows = lambda q: pltpu.make_async_copy(group(rows_hbm, q), group(rows_ref, q), row_sems.at[q])
    lines = got_hbm.shape[1] - EXTRA
    load_tail = pltpu.make_async_copy(got_hbm.at[:, lines : lines + EXTRA, :], tail_ref, tail_sems.at[0])
    load_tail.start()

    def begin(q, _):
        for make in (load_rows, load, load_raised):
            make(q).start()
        return 0

    lax.fori_loop(0, peers // GROUP, begin, 0)
    acc_ref[...] = jnp.zeros_like(acc_ref)
    load_tail.wait()

    def step(g):
        tail = tail_ref[g].astype(f32)
        alpha = tail[0:1] + tail[1:2]
        beta = tail[2:3] + tail[3:4]
        rows = rows_ref[g]
        for part in chunks_of(acc_ref.shape[0]):
            balanced = scaled(expo_ref[g, part, :].astype(f32), scale_ref[part, :])
            score = raised_ref[g, part, :].astype(f32) * alpha - balanced * beta
            acc_ref[part, :] += mm(score.astype(bf16), rows)
        return 0

    over_groups(peers, step, (load_rows, load, load_raised), (), UNROLL)
    for part in chunks_of(acc_ref.shape[0]):
        grad = acc_ref[part, :].T
        norm = norm_ref[:, part]
        unit = proto_ref[:, part].astype(f32) / norm
        grad_ref[:, part] = (grad - unit * jnp.sum(unit * grad, axis=0, keepdims=True)) / norm


def join(core, both_ref, other_ref, at):
    own, other = (both_ref[at], other_ref[at])
    low = core == 0
    return jnp.concatenate([jnp.where(low, own, other), jnp.where(low, other, own)], axis=1)


def two_parts(x):
    high = x.astype(bf16)
    return (high.astype(f32), x - high.astype(f32))


def backward_body(
    at_ref, both_ref, other_ref, mine_ref, member_ref, unit_ref, inv_ref, rows_ref, hidden_ref, slope_ref, w_hbm,
    send_hbm, grad_rows_ref, loss_ref, w_in_ref, w_out_ref, send_ref, pre_ref, out_ref, sems, send_sems,
):
    peers = w_hbm.shape[0]
    loads = weight_loads(at_ref, w_hbm, w_in_ref, w_out_ref, sems)
    for load in loads:
        load.start()
    tail = mine_ref[...].astype(f32)
    live, weight = (tail[0:1], tail[1:2] * (1.0 / STUDENT_TEMP))
    pull = join(at_ref[0], both_ref, other_ref, 0)
    push = join(at_ref[0], both_ref, other_ref, 1)
    norm_sum = push[CAP : CAP + 1]
    push = push[0:CAP]
    scale = live / (pull[CAP : CAP + 1] + 1.0 - live)
    pull = pull[0:CAP]
    unit = unit_ref[...]
    cross = jnp.sum(unit.astype(bf16).astype(f32) * pull, axis=0, keepdims=True) * (1.0 / STUDENT_TEMP)
    row_loss = jnp.log(norm_sum) - scale * cross
    loss = jnp.sum(member_ref[...] * row_loss, axis=1, keepdims=True)
    loss_ref[...] = jnp.broadcast_to(loss, loss_ref.shape)
    alpha = weight / norm_sum
    beta = weight * scale
    grad_unit = push * alpha - pull * beta
    inner = jnp.sum(unit * grad_unit, axis=0, keepdims=True)
    grad_feats = (inv_ref[0:1] * (grad_unit - unit * inner)).T.astype(bf16)
    for load in loads:
        load.wait()
    width = send_ref.shape[2]
    grad_rows = jnp.zeros(grad_rows_ref.shape, f32)
    for part in chunks_of(hidden_ref.shape[1]):
        grad_pre = (mm(grad_feats, w_out_ref[part, :], NT) * slope_ref[:, part]).astype(bf16)
        pre_ref[:, part] = grad_pre
        grad_rows = grad_rows + mm(grad_pre, w_in_ref[:, part], NT)
        out_ref[part, :] = mm(hidden_ref[:, part], grad_feats, TN).astype(bf16)
    grad_rows_ref[...] = grad_rows.astype(bf16)
    core, level = (at_ref[0], at_ref[1])
    own = pre_ref[:, pl.ds(pl.multiple_of(level * width, width), width)]
    grad_in = mm(rows_ref[...], own, TN).astype(bf16)
    per = grad_in.shape[0] // peers
    block = out_ref.shape[0] // (peers // 2)
    share = block // 4
    at = iota((EXTRA, CAP), 0)
    rows = jnp.zeros((EXTRA, CAP), f32)
    for i, x in enumerate(two_parts(alpha) + two_parts(beta)):
        rows = jnp.where(at == i, x, rows)
    rows = rows.astype(bf16)
    store = lambda g: pltpu.make_async_copy(send_ref.at[g], send_hbm.at[g], send_sems.at[g])
    for g in range(peers):
        send_ref[g, 0:per, :] = grad_in[g * per : (g + 1) * per, :]
        start = pl.multiple_of((g % (peers // 2)) * block + level * share, share)
        out = out_ref[pl.ds(start, share), :]
        send_ref[g, per : per + share, :] = jnp.where(core == g // (peers // 2), out, jnp.zeros_like(out))
        send_ref[g, per + share : per + share + EXTRA, :] = rows
        store(g).start()
    wait_all(peers, store)


def place_body(sel_ref, rows_ref, other_ref, out_hbm, out_ref, sems):
    rows = (rows_ref[...].astype(f32) + other_ref[...].astype(f32)).astype(bf16)
    pieces = out_ref.shape[0]
    size = out_ref.shape[1]
    store = lambda i: pltpu.make_async_copy(out_ref.at[i], out_hbm.at[i], sems.at[i])
    for i in range(pieces):
        out_ref[i] = mm(sel_ref[:, i * size : (i + 1) * size], rows, TN).astype(bf16)
        store(i).start()
    wait_all(pieces, store)


def gather_grads_body(got_ref, send_ref):
    peers = got_ref.shape[0]
    lines = send_ref.shape[1]
    acc = got_ref[0, 0:lines, :].astype(f32)
    for g in range(1, peers):
        acc = acc + got_ref[g, 0:lines, :].astype(f32)
    acc = acc.astype(bf16)
    for t in range(send_ref.shape[0]):
        send_ref[t] = acc


def weight_grads_body(at_ref, parts_ref, grad_in_ref, grad_out_ref):
    peers, lines, width = parts_ref.shape
    per = grad_in_ref.shape[0]
    share = lines - per
    for t in range(peers):
        to = ((t % 2) * (peers // 2) + t // 2) * width
        grad_in_ref[:, to : to + width] = parts_ref[t, 0:per, :].astype(f32)
    for z in range(peers // 2):
        grad_out_ref[z * share : (z + 1) * share, :] = parts_ref[2 * z + at_ref[2], per:lines, :].astype(f32)


def sem(number):
    return pltpu.SemaphoreType.DMA((number,))


def run_expo(at, cols_t, own, other, tensor):
    dp, (width, bot) = (own.shape[0], cols_t.shape)
    big, small = ((dp, width, CAP), (dp, CAP))
    return call(
        expo_body,
        [(big, bf16), ((tensor, *small), bf16), (small, f32), (small, f32)],
        (at, cols_t, own, other),
        in_specs=[SMEM, VMEM, HBM, HBM],
        out_specs=[HBM, VMEM, VMEM, VMEM],
        scratch=[
            pltpu.VMEM((dp, 2, HALF, bot), bf16),
            pltpu.VMEM((dp, EXTRA, bot), bf16),
            pltpu.VMEM(big, bf16),
            pltpu.VMEM((width, 128), f32),
            pltpu.VMEM(small, f32),
            *[sem(dp // GROUP)] * 4,
        ],
    )


def run_balance(expo, got, live, tensor):
    dp, width, _ = expo.shape
    small = pltpu.VMEM(live.shape, f32)
    return call(
        balance_body,
        [((tensor, *live.shape), bf16)],
        (expo, got, live),
        in_specs=[HBM, VMEM, VMEM],
        scratch=[pltpu.VMEM(expo.shape, bf16), pltpu.VMEM((width, 128), f32), small, small, sem(dp // GROUP)],
    )[0]


def run_last(at, expo, got, live, cols):
    dp, width, _ = expo.shape
    halves = (dp, LINES, HALF)
    return call(
        last_body,
        [(halves, bf16), (halves, bf16), ((width, 128), f32)],
        (at, expo, got, live, cols),
        in_specs=[SMEM, HBM, VMEM, VMEM, VMEM],
        out_specs=[HBM, HBM, VMEM],
        scratch=[
            pltpu.VMEM(expo.shape, bf16),
            pltpu.VMEM(live.shape, f32),
            pltpu.VMEM((2, *halves), bf16),
            *[sem(dp // GROUP)] * 3,
        ],
    )


def run_student(at, cols_t, cols, rows):
    dp = rows.shape[0]
    big, halves = ((dp, cols.shape[1], CAP), (dp, LINES, HALF))
    return call(
        student_body,
        [(big, bf16), (halves, bf16), (halves, bf16)],
        (at, cols_t, cols, rows),
        in_specs=[SMEM, VMEM, VMEM, HBM],
        out_specs=[HBM, HBM, HBM],
        scratch=[
            pltpu.VMEM(rows.shape, bf16),
            pltpu.VMEM(big, bf16),
            pltpu.VMEM((2, *halves), bf16),
            *[sem(dp // GROUP)] * 4,
        ],
    )


def run_columns_grad(expo, raised, scale, got, rows, proto, norm):
    dp, held = (expo.shape[0], pltpu.VMEM(expo.shape, bf16))
    return call(
        columns_grad_body,
        [(proto.shape, f32)],
        (expo, raised, scale, got, rows, proto, norm),
        in_specs=[HBM, HBM, VMEM, HBM, HBM, VMEM, VMEM],
        scratch=[
            held,
            held,
            pltpu.VMEM(proto.shape[::-1], f32),
            pltpu.VMEM((dp, EXTRA, CAP), bf16),
            pltpu.VMEM(rows.shape, bf16),
            *[sem(dp // GROUP)] * 4,
        ],
    )[0]


def exchange(x, axis):
    return lax.all_to_all(x, axis, split_axis=0, concat_axis=0, tiled=True)


def sibling(x):
    peers = lax.axis_size("tensor")
    return lax.ppermute(x, "tensor", [(i, i ^ 1) for i in range(peers)])


def everywhere(part, small):
    got = exchange(part, "tensor")
    (sums,) = call(relay_body, [((small[0], *small), bf16)], (got,))
    return exchange(sums, "dp")


def levels(x, by):
    peers = lax.axis_size("tensor")
    return lax.ppermute(x, "tensor", [(i, i ^ (2 * by)) for i in range(peers)])


def paired(keep, give):
    return (keep.astype(f32) + sibling(give).astype(f32)).astype(bf16)


def slot_sums_body(parts_hbm, out_ref, parts_ref, sems):
    peers = parts_hbm.shape[0]
    load = lambda g: pltpu.make_async_copy(parts_hbm.at[g], parts_ref.at[g], sems.at[g])
    start_all(peers, load)
    load(0).wait()
    acc = parts_ref[0].astype(f32)
    for g in range(1, peers):
        load(g).wait()
        acc = acc + parts_ref[g].astype(f32)
    out_ref[...] = acc.astype(bf16)


def slot_sums(parts):
    out = parts.shape[1:]
    scratch = [pltpu.VMEM(parts.shape, bf16), pltpu.SemaphoreType.DMA((parts.shape[0],))]
    return call(slot_sums_body, [(out, bf16)], (parts,), in_specs=[HBM], scratch=scratch)[0]


def after(x, earlier):
    return lax.optimization_barrier((x, earlier))[0]


def parts_of(tokens, teacher_feats, masks, w_in, w_out, proto_student, proto_teacher):
    dim = tokens.shape[1]
    hid = w_in.shape[1]
    bot, width = proto_student.shape
    dp, tensor = (lax.axis_size("dp"), lax.axis_size("tensor"))
    per = w_in.shape[0]
    half = hid // 2
    share = w_out.shape[0] // 4
    t = lax.axis_index("tensor").astype(jnp.int32)
    g = lax.axis_index("dp").astype(jnp.int32)
    at = jnp.stack([t % 2, t // 2, g // (dp // 2)])

    lines = per + w_out.shape[0] * bot // half
    (w_pack,) = call(weights_body, [((lines, half), bf16)], (at, w_in, w_out), in_specs=[SMEM, VMEM, VMEM])
    w_all = lax.all_gather(w_pack, "dp", axis=0, tiled=True).reshape(dp, lines, half)
    dma = pltpu.SemaphoreType.DMA
    sems = dma((dp,))
    sel, send, member, mine = call(
        select_body,
        [((CAP, tokens.shape[0]), bf16), ((dp, HALF + EXTRA, bot), bf16), ((8, CAP), f32), ((EXTRA, CAP), bf16)],
        (at, masks, teacher_feats),
        in_specs=[SMEM, VMEM, VMEM],
        out_specs=[VMEM, HBM, VMEM, VMEM],
        scratch=[pltpu.VMEM((CAP, bot), bf16), pltpu.VMEM((HALF + EXTRA, bot), bf16), sems],
    )
    packs = exchange(send, "dp")
    others = sibling(packs)
    cols, student_t, teacher_t, norm = call(
        columns_body,
        [((bot, width), bf16), ((width, bot), bf16), ((width, bot), bf16), ((1, width), f32)],
        (proto_student, proto_teacher),
    )
    expo, part, live, _ = run_expo(at, teacher_t, packs, others, tensor)
    loads = dma((dp + 2 * dp,))
    w_held = [pltpu.VMEM((dim, half), bf16), pltpu.VMEM((half, bot), bf16)]
    rows, hidden, slope, feats = call(
        forward_body,
        [((CAP, dim), bf16), ((CAP, half), bf16), ((CAP, half), f32), ((CAP, bot), f32)],
        (at, sel, tokens, after(w_all, part)),
        in_specs=[SMEM, VMEM, HBM, HBM],
        scratch=[pltpu.VMEM(tokens.shape, bf16), *w_held, loads, dma(())],
    )
    unit, inv, student_rows = call(
        unit_body, [((bot, CAP), f32), ((8, CAP), f32), ((CAP, bot), bf16)], (feats, sibling(feats))
    )
    all_rows = lax.all_gather(student_rows, "dp", axis=0, tiled=True).reshape(dp, CAP, bot)
    got = everywhere(part, live.shape)
    part = run_balance(expo, got, live, tensor)
    got = everywhere(part, live.shape)
    keep, give, scale = run_last(at, expo, got, live, cols)
    pull = paired(keep, give)
    pull_got = exchange(pull, "dp")
    all_rows = after(all_rows, pull)
    raised, keep, give = run_student(at, student_t, cols, all_rows)
    push_got = exchange(paired(keep, give), "dp")
    both = jnp.stack([slot_sums(pull_got), slot_sums(push_got)])
    near, far, last = (levels(both, by) for by in (1, 2, 3))
    wide = lambda x: x.astype(f32)
    both = (wide(both) + wide(near)) + (wide(far) + wide(last))
    back_lines = per + share + EXTRA
    send, grad_rows, loss = call(
        backward_body,
        [((dp, back_lines, bot), bf16), ((CAP, dim), bf16), ((8, 128), f32)],
        (at, both, sibling(both), mine, member, unit, inv, rows, hidden, slope, w_all),
        in_specs=[SMEM] + [VMEM] * 9 + [HBM],
        out_specs=[HBM, VMEM, VMEM],
        scratch=[
            *w_held,
            pltpu.VMEM((dp, back_lines, bot), bf16),
            pltpu.VMEM((CAP, half), bf16),
            pltpu.VMEM((half, bot), bf16),
            loads,
            sems,
        ],
    )
    got = exchange(send, "dp")
    pieces = 4
    d_shape = (pieces, tokens.shape[0] // pieces, dim)
    (d_tokens,) = call(
        place_body,
        [(d_shape, bf16)],
        (sel, grad_rows, sibling(grad_rows)),
        out_specs=[HBM],
        scratch=[pltpu.VMEM(d_shape, bf16), dma((pieces,))],
    )
    got, d_tokens = lax.optimization_barrier((got, d_tokens))
    (sent,) = call(gather_grads_body, [((tensor, per + share, bot), bf16)], (got,))
    parts = exchange(sent, "tensor")
    grad_proto = run_columns_grad(expo, raised, scale, got, all_rows, proto_student, norm)
    grad_in, grad_out = call(
        weight_grads_body, [((per, hid), f32), ((w_out.shape[0], bot), f32)], (at, parts), in_specs=[SMEM, VMEM]
    )
    return (d_tokens.reshape(tokens.shape), grad_in, grad_out, grad_proto, loss[: masks.shape[0], 0])


def solution(mesh):
    placed = (
        P("dp", None),
        P("dp", None),
        P("dp", None),
        P("dp", None),
        P("dp", None),
        P(None, ("dp", "tensor")),
        P(None, ("dp", "tensor")),
    )
    return jax.shard_map(
        parts_of,
        mesh=mesh,
        in_specs=placed,
        out_specs=(P("dp", None), P("dp", None), P("dp", None), P(None, ("dp", "tensor")), P("dp")),
        check_vma=False,
    )
```

```python
import jax
import jax.numpy as jnp
from jax import lax
from jax.experimental import pallas as pl
from jax.experimental.pallas import tpu as pltpu
from jax.sharding import PartitionSpec as P

CAP = 256
TEACHER_TEMP = 0.07
STUDENT_TEMP = 0.1
EPS = 1e-06
GRAD_SCALE = 65536.0
INTERPRET = False
f32, bf16 = (jnp.float32, jnp.bfloat16)
VMEM = pl.BlockSpec(memory_space=pltpu.VMEM)
HBM = pl.BlockSpec(memory_space=pltpu.HBM)
ANY = pl.BlockSpec(memory_space=pl.ANY)
SMEM = pl.BlockSpec(memory_space=pltpu.SMEM)
NT = (((1,), (1,)), ((), ()))
TN = (((0,), (0,)), ((), ()))
EXTRA = 16
HALF = CAP // 2
LINES = CAP + EXTRA


def mm(a, b, dims=None):
    if dims is None:
        return jnp.dot(a, b, preferred_element_type=f32)
    return lax.dot_general(a, b, dims, preferred_element_type=f32)


def call(body, outs, ins, out_specs=None, in_specs=None, scratch=()):
    specs = out_specs or [VMEM] * len(outs)
    in_specs = in_specs or [VMEM] * len(ins)
    ins = [pltpu.with_memory_space_constraint(x, pltpu.HBM) if spec is HBM else x for x, spec in zip(ins, in_specs)]
    outs = tuple(pltpu.HBM(*o) if spec is HBM else jax.ShapeDtypeStruct(*o) for o, spec in zip(outs, specs))
    return pl.pallas_call(
        body,
        out_shape=outs,
        in_specs=in_specs,
        out_specs=tuple(specs),
        scratch_shapes=list(scratch),
        interpret=INTERPRET,
        compiler_params=pltpu.CompilerParams(vmem_limit_bytes=48 << 20),
    )(*ins)


def iota(shape, dim):
    return lax.broadcasted_iota(jnp.int32, shape, dim)


def copies(pairs, sems):
    return [pltpu.make_async_copy(a, b, sems.at[i]) for i, (a, b) in enumerate(pairs)]


GROUP = 4
UNROLL = 4


def group(ref, q):
    return ref.at[pl.ds(q * GROUP, GROUP)]


def start_all(number, make):
    def go(i, _):
        make(i).start()
        return 0

    lax.fori_loop(0, number, go, 0)


def wait_all(number, make):
    def go(i, _):
        make(i).wait()
        return 0

    lax.fori_loop(0, number, go, 0)


def over_groups(peers, step, loads=(), stores=(), unroll=1):
    def go(q, _):
        for make in loads:
            make(q).wait()
        lax.fori_loop(0, GROUP, lambda i, _: step(q * GROUP + i), 0, unroll=unroll)
        for make in stores:
            make(q).start()
        return 0

    lax.fori_loop(0, peers // GROUP, go, 0)


def select_body(
    at_ref, mask_ref, feats_ref, sel_ref, send_hbm, member_hbm, mine_hbm, unit_ref, pack_ref, member_ref, mine_ref, sems, late_sems
):
    crops, patches = mask_ref.shape
    mask = mask_ref[...].astype(f32)
    upto = (iota((patches, patches), 0) <= iota((patches, patches), 1)).astype(f32).astype(bf16)
    rank = mm(mask.astype(bf16), upto)
    count = jnp.sum(mask, axis=1, keepdims=True)
    total = jnp.sum(count, axis=0, keepdims=True)
    slot = iota((CAP, patches), 0).astype(f32)
    lane = iota((1, CAP), 1).astype(f32)
    start = jnp.zeros((1, 1), f32)
    weight = jnp.zeros((1, CAP), f32)
    first = iota((CAP, patches), 1) == 0
    member_ref[...] = jnp.zeros_like(member_ref)
    for c in range(crops):
        hit = jnp.where((rank[c : c + 1] + start == slot + 1.0) & (mask[c : c + 1] > 0.0), 1.0, 0.0)
        if c == 0:
            hit = jnp.where(first & (slot >= total), 1.0, hit)
        sel_ref[:, c * patches : (c + 1) * patches] = hit.astype(bf16)
        own = count[c : c + 1]
        inside = jnp.where((lane >= start) & (lane < start + own), 1.0, 0.0)
        part = inside * (1.0 / jnp.maximum(own, 1.0))
        member_ref[c : c + 1, :] = part
        weight = weight + part
        start = start + own
    live = jnp.where(lane < total, 1.0, 0.0)
    picked = mm(sel_ref[...], feats_ref[...])
    scale = lax.rsqrt(jnp.sum(picked * picked, axis=1, keepdims=True) + EPS)
    unit_ref[...] = (picked * scale).astype(bf16)
    at = iota((EXTRA, CAP), 0)
    tail = jnp.where(at == 0, live, jnp.where(at == 1, weight * GRAD_SCALE, 0.0)).astype(bf16)
    mine_ref[...] = tail
    late = copies([(member_ref, member_hbm), (mine_ref, mine_hbm)], late_sems)
    for copy in late:
        copy.start()
    pack_ref[0:HALF, :] = unit_ref[pl.ds(pl.multiple_of(at_ref[0] * HALF, HALF), HALF), :]
    pack_ref[HALF : HALF + EXTRA, :] = tail
    peers = send_hbm.shape[0]
    make = lambda g: pltpu.make_async_copy(pack_ref, send_hbm.at[g], sems.at[g])
    start_all(peers, make)
    for copy in late:
        copy.wait()
    wait_all(peers, make)


def columns_body(
    student_ref, teacher_ref, cols_hbm, student_t_hbm, teacher_t_hbm, norm_hbm, cols_ref, student_t_ref, teacher_t_ref, norm_ref, sems
):
    for part in chunks_of(student_ref.shape[1]):
        wide = student_ref[:, part].astype(f32)
        norm = jnp.sqrt(jnp.sum(wide * wide, axis=0, keepdims=True) + EPS)
        norm_ref[:, part] = norm
        unit = wide / norm
        cols_ref[:, part] = unit.astype(bf16)
        student_t_ref[part, :] = unit.T.astype(bf16)
        wide = teacher_ref[:, part].astype(f32)
        norm = jnp.sqrt(jnp.sum(wide * wide, axis=0, keepdims=True) + EPS)
        teacher_t_ref[part, :] = (wide / norm).T.astype(bf16)
    held = (cols_ref, student_t_ref, teacher_t_ref, norm_ref)
    stores = copies(list(zip(held, (cols_hbm, student_t_hbm, teacher_t_hbm, norm_hbm))), sems)
    for store in stores:
        store.start()
    for store in stores:
        store.wait()


def weights_body(at_ref, w_in_hbm, w_out_hbm, pack_hbm, sems):
    rows, hid = w_in_hbm.shape
    half = hid // 2
    bot = w_out_hbm.shape[1]
    lines = w_out_hbm.shape[0] * bot // half
    column = pl.multiple_of(at_ref[0] * half, half)
    pairs = [(w_in_hbm.at[:, pl.ds(column, half)], pack_hbm.at[0:rows, :])]
    for q in range(half // bot):
        source = w_out_hbm.at[q * lines : (q + 1) * lines, :]
        pairs.append((source, pack_hbm.at[rows : rows + lines, q * bot : (q + 1) * bot]))
    moves = copies(pairs, sems)
    for move in moves:
        move.start()
    for move in moves:
        move.wait()


def weight_loads(at_ref, w_hbm, w_in_ref, w_out_ref, sems):
    peers = w_hbm.shape[0]
    rows = w_in_ref.shape[0] // peers
    lines = w_hbm.shape[1] - rows
    bot = w_out_ref.shape[1]
    quarters = w_hbm.shape[2] // bot
    pairs = [(w_hbm.at[g, 0:rows, :], w_in_ref.at[g * rows : (g + 1) * rows, :]) for g in range(peers)]
    for i in range(peers // 2):
        for q in range(quarters):
            source = w_hbm.at[at_ref[0] * (peers // 2) + i, rows : rows + lines, q * bot : (q + 1) * bot]
            at = (i * quarters + q) * lines
            pairs.append((source, w_out_ref.at[at : at + lines, :]))
    return copies(pairs, sems)


def tokens_body(sel_ref, tokens_hbm, rows_hbm, tokens_ref, rows_ref, sems):
    load = pltpu.make_async_copy(tokens_hbm, tokens_ref, sems.at[0])
    load.start()
    load.wait()
    rows_ref[...] = mm(sel_ref[...], tokens_ref[...]).astype(bf16)
    store = pltpu.make_async_copy(rows_ref, rows_hbm, sems.at[1])
    store.start()
    store.wait()


def forward_body(
    at_ref, rows_hbm, w_hbm, hidden_hbm, slope_hbm, feats_ref,
    rows_ref, hidden_ref, slope_ref, w_in_ref, w_out_ref, sems, own_sems,
):
    first = pltpu.make_async_copy(rows_hbm, rows_ref, own_sems.at[0])
    first.start()
    loads = weight_loads(at_ref, w_hbm, w_in_ref, w_out_ref, sems)
    for load in loads:
        load.start()
    first.wait()
    for load in loads:
        load.wait()
    rows = rows_ref[...]
    feats = jnp.zeros(feats_ref.shape, f32)
    for part in chunks_of(hidden_ref.shape[1]):
        pre = mm(rows, w_in_ref[:, part])
        cdf = 0.5 * (1.0 + lax.erf(pre * 0.7071067811865476))
        slope_ref[:, part] = cdf + pre * (jnp.exp(-0.5 * pre * pre) * 0.3989422804014327)
        hidden = (pre * cdf).astype(bf16)
        hidden_ref[:, part] = hidden
        feats = feats + mm(hidden, w_out_ref[part, :])
    feats_ref[...] = feats
    stores = copies([(hidden_ref, hidden_hbm), (slope_ref, slope_hbm)], own_sems)
    for store in stores:
        store.start()
    for store in stores:
        store.wait()


def unit_of(feats_ref, other_ref):
    feats = feats_ref[...] + other_ref[...]
    inv = lax.rsqrt(jnp.sum(feats * feats, axis=1, keepdims=True) + EPS)
    return (feats * inv, inv)


def unit_body(feats_ref, other_ref, rows_ref):
    rows_ref[...] = unit_of(feats_ref, other_ref)[0].astype(bf16)


def chunks_of(width):
    step = min(256, width)
    return [slice(at, at + step) for at in range(0, width, step)]


def row_of(ref, g):
    return ref[pl.ds(g, 1), :]


def fold(x):
    return x.reshape(x.shape[0] // 8, 8, x.shape[1]).sum(axis=0)


def expo_body(
    at_ref, cols_hbm, own_hbm, other_hbm, expo_hbm, part_ref, live_ref,
    cols_ref, rows_ref, tail_ref, expo_ref, total_ref, sums_ref, sems, own_sems, other_sems, tail_sems,
):
    peers = own_hbm.shape[0]
    width = cols_ref.shape[0]
    core = at_ref[0]
    number = peers // GROUP
    rows_of = lambda ref, q: ref.at[pl.ds(q * GROUP, GROUP), 0:HALF, :]
    rows_at = lambda q, c: rows_ref.at[pl.ds(q * GROUP, GROUP), c]
    load_own = lambda q: pltpu.make_async_copy(rows_of(own_hbm, q), rows_at(q, core), own_sems.at[q])
    load_other = lambda q: pltpu.make_async_copy(rows_of(other_hbm, q), rows_at(q, 1 - core), other_sems.at[q])
    load_tail = pltpu.make_async_copy(own_hbm.at[:, HALF : HALF + EXTRA, :], tail_ref, tail_sems.at[0])
    store = lambda q: pltpu.make_async_copy(group(expo_ref, q), group(expo_hbm, q), sems.at[q])
    load_cols = pltpu.make_async_copy(cols_hbm, cols_ref, tail_sems.at[1])
    load_cols.start()
    load_tail.start()
    start_all(number, load_own)
    start_all(number, load_other)
    total_ref[...] = jnp.zeros_like(total_ref)
    load_tail.wait()
    load_cols.wait()

    def first(g):
        rows = rows_ref[g].reshape(CAP, rows_ref.shape[3])
        tail = tail_ref[g].astype(f32)
        live = tail[0:1]
        live_ref[pl.ds(g, 1), :] = live
        for part in chunks_of(width):
            cos = mm(cols_ref[part, :], rows, NT)
            expo = jnp.exp(cos * (1.0 / TEACHER_TEMP)) * live
            expo_ref[g, part, :] = expo.astype(bf16)
            total_ref[part, :] += expo[:, 0:128] + expo[:, 128:256]
        return 0

    over_groups(peers, first, (load_own, load_other), (store,), UNROLL)
    spread_scale(total_ref)
    row_parts(expo_ref, total_ref, sums_ref, part_ref)
    wait_all(number, store)


def spread_scale(total_ref):
    for part in chunks_of(total_ref.shape[0]):
        sums = jnp.sum(total_ref[part, :], axis=1, keepdims=True)
        total_ref[part, :] = jnp.broadcast_to(1.0 / sums, sums.shape[:1] + (128,))


def scaled(expo, scale):
    return jnp.concatenate([expo[:, 0:128] * scale, expo[:, 128:256] * scale], axis=1)


def row_parts(expo_ref, scale_ref, sums_ref, part_ref):
    def step(g):
        acc = jnp.zeros((8, CAP), f32)
        for part in chunks_of(scale_ref.shape[0]):
            acc = acc + fold(scaled(expo_ref[g, part, :].astype(f32), scale_ref[part, :]))
        sums_ref[pl.ds(g, 1), :] = jnp.sum(acc, axis=0, keepdims=True)
        return 0

    over_groups(expo_ref.shape[0], step, unroll=UNROLL)
    sums = sums_ref[...].astype(bf16)
    for t in range(part_ref.shape[0]):
        part_ref[t] = sums


def relay_body(parts_ref, out_ref):
    sums = parts_ref[0].astype(f32)
    for t in range(1, parts_ref.shape[0]):
        sums = sums + parts_ref[t].astype(f32)
    sums = sums.astype(bf16)
    for g in range(out_ref.shape[0]):
        out_ref[g] = sums


def scales_from(parts_ref, live_ref, scale_ref):
    sums = parts_ref[0].astype(f32)
    for g in range(1, parts_ref.shape[0]):
        sums = sums + parts_ref[g].astype(f32)
    live = live_ref[...]
    scale_ref[...] = live / (sums + 1.0 - live)


def column_sums(load, expo_ref, scale_ref, total_ref):
    total_ref[...] = jnp.zeros_like(total_ref)

    def step(g):
        row = row_of(scale_ref, g)
        for part in chunks_of(total_ref.shape[0]):
            expo = expo_ref[g, part, :].astype(f32)
            total_ref[part, :] += expo[:, 0:128] * row[:, 0:128] + expo[:, 128:256] * row[:, 128:256]
        return 0

    over_groups(expo_ref.shape[0], step, (load,), unroll=UNROLL)
    spread_scale(total_ref)


def balance_body(expo_hbm, parts_ref, live_ref, part_ref, expo_ref, total_ref, sums_ref, scale_ref, sems):
    load = lambda q: pltpu.make_async_copy(group(expo_hbm, q), group(expo_ref, q), sems.at[q])
    start_all(expo_ref.shape[0] // GROUP, load)
    scales_from(parts_ref, live_ref, scale_ref)
    column_sums(load, expo_ref, scale_ref, total_ref)
    row_parts(expo_ref, total_ref, sums_ref, part_ref)


def divide_up(g, acc, pull, halves_ref):
    rows = jnp.sum(acc, axis=0, keepdims=True)
    rows = jnp.where(iota((EXTRA, CAP), 0) == 0, rows, 0.0).astype(bf16)
    pull = pull.astype(bf16)
    for at, block in ((slice(0, CAP), pull), (slice(CAP, LINES), rows)):
        halves_ref[0, g, at, :] = block[:, 0:HALF]
        halves_ref[1, g, at, :] = block[:, HALF:CAP]


def last_body(
    at_ref, expo_hbm, parts_ref, live_ref, cols_ref, keep_hbm, give_hbm, total_hbm,
    expo_ref, total_ref, scale_ref, halves_ref, sems, keep_sems, give_sems,
):
    peers = expo_ref.shape[0]
    core = at_ref[0]
    load = lambda q: pltpu.make_async_copy(group(expo_hbm, q), group(expo_ref, q), sems.at[q])
    half_at = lambda c, q: halves_ref.at[c, pl.ds(q * GROUP, GROUP)]
    keep = lambda q: pltpu.make_async_copy(half_at(core, q), group(keep_hbm, q), keep_sems.at[q])
    give = lambda q: pltpu.make_async_copy(half_at(1 - core, q), group(give_hbm, q), give_sems.at[q])
    number = peers // GROUP
    start_all(number, load)
    scales_from(parts_ref, live_ref, scale_ref)
    column_sums(load, expo_ref, scale_ref, total_ref)

    def step(g):
        acc = jnp.zeros((8, CAP), f32)
        pull = jnp.zeros((cols_ref.shape[0], CAP), f32)
        for part in chunks_of(total_ref.shape[0]):
            balanced = scaled(expo_ref[g, part, :].astype(f32), total_ref[part, :])
            acc = acc + fold(balanced)
            pull = pull + mm(cols_ref[:, part], balanced.astype(bf16))
        divide_up(g, acc, pull, halves_ref)
        return 0

    spare = pltpu.make_async_copy(total_ref, total_hbm, sems.at[0])
    spare.start()
    over_groups(peers, step, (), (give, keep), UNROLL)
    wait_all(number, give)
    wait_all(number, keep)
    spare.wait()


def student_body(
    at_ref, cols_t_ref, cols_ref, rows_hbm, raised_hbm, keep_hbm, give_hbm,
    rows_ref, raised_ref, halves_ref, row_sems, sems, keep_sems, give_sems,
):
    peers = rows_ref.shape[0]
    load = lambda q: pltpu.make_async_copy(group(rows_hbm, q), group(rows_ref, q), row_sems.at[q])
    start_all(peers // GROUP, load)
    core = at_ref[0]
    width = cols_t_ref.shape[0]
    store = lambda q: pltpu.make_async_copy(group(raised_ref, q), group(raised_hbm, q), sems.at[q])
    half_at = lambda c, q: halves_ref.at[c, pl.ds(q * GROUP, GROUP)]
    keep = lambda q: pltpu.make_async_copy(half_at(core, q), group(keep_hbm, q), keep_sems.at[q])
    give = lambda q: pltpu.make_async_copy(half_at(1 - core, q), group(give_hbm, q), give_sems.at[q])
    number = peers // GROUP

    def step(g):
        rows = rows_ref[g]
        acc = jnp.zeros((8, CAP), f32)
        pull = jnp.zeros((cols_ref.shape[0], CAP), f32)
        for part in chunks_of(width):
            raised = jnp.exp(mm(cols_t_ref[part, :], rows, NT) * (1.0 / STUDENT_TEMP))
            acc = acc + fold(raised)
            raised = raised.astype(bf16)
            raised_ref[g, part, :] = raised
            pull = pull + mm(cols_ref[:, part], raised)
        divide_up(g, acc, pull, halves_ref)
        return 0

    over_groups(peers, step, (load,), (store, give, keep), UNROLL)
    for make in (give, keep, store):
        wait_all(number, make)


def columns_grad_body(
    expo_hbm, raised_hbm, scale_hbm, got_hbm, rows_hbm, proto_hbm, norm_hbm,
    grad_ref, scale_ref, proto_ref, norm_ref, expo_ref, raised_ref, acc_ref, tail_ref, rows_ref, esems, rsems, tail_sems, row_sems, late_sems,
):
    peers = expo_ref.shape[0]
    load = lambda q: pltpu.make_async_copy(group(expo_hbm, q), group(expo_ref, q), esems.at[q])
    load_raised = lambda q: pltpu.make_async_copy(group(raised_hbm, q), group(raised_ref, q), rsems.at[q])
    load_rows = lambda q: pltpu.make_async_copy(group(rows_hbm, q), group(rows_ref, q), row_sems.at[q])
    lines = got_hbm.shape[1] - EXTRA
    load_tail = pltpu.make_async_copy(got_hbm.at[:, lines : lines + EXTRA, :], tail_ref, tail_sems.at[0])
    load_scale = pltpu.make_async_copy(scale_hbm, scale_ref, tail_sems.at[1])
    late = copies([(proto_hbm, proto_ref), (norm_hbm, norm_ref)], late_sems)
    load_tail.start()
    load_scale.start()

    def begin(q, _):
        for make in (load_rows, load, load_raised):
            make(q).start()
        return 0

    lax.fori_loop(0, peers // GROUP, begin, 0)
    for copy in late:
        copy.start()
    acc_ref[...] = jnp.zeros_like(acc_ref)
    load_tail.wait()
    load_scale.wait()

    def step(g):
        tail = tail_ref[g].astype(f32)
        alpha = tail[0:1] + tail[1:2]
        beta = tail[2:3] + tail[3:4]
        rows = rows_ref[g]
        for part in chunks_of(acc_ref.shape[0]):
            balanced = scaled(expo_ref[g, part, :].astype(f32), scale_ref[part, :])
            score = raised_ref[g, part, :].astype(f32) * alpha - balanced * beta
            acc_ref[part, :] += mm(score.astype(bf16), rows)
        return 0

    over_groups(peers, step, (load_rows, load, load_raised), (), UNROLL)
    for copy in late:
        copy.wait()
    for part in chunks_of(acc_ref.shape[0]):
        grad = acc_ref[part, :].T
        norm = norm_ref[:, part]
        unit = proto_ref[:, part].astype(f32) / norm
        grad_ref[:, part] = (grad - unit * jnp.sum(unit * grad, axis=0, keepdims=True)) / norm


def join(core, both_ref, other_ref, at):
    own, other = (both_ref[at], other_ref[at])
    low = core == 0
    return jnp.concatenate([jnp.where(low, own, other), jnp.where(low, other, own)], axis=1)


def two_parts(x):
    high = x.astype(bf16)
    return (high.astype(f32), x - high.astype(f32))


def backward_body(
    at_ref, both_ref, other_ref, mine_ref, member_ref, feats_ref, feats_other_ref, rows_ref, hidden_ref, slope_ref, w_hbm,
    send_hbm, grad_rows_hbm, loss_ref, w_in_ref, w_out_ref, send_ref, pre_ref, out_ref, grad_rows_ref, sems, send_sems, rows_sem,
):
    peers = w_hbm.shape[0]
    loads = weight_loads(at_ref, w_hbm, w_in_ref, w_out_ref, sems)
    for load in loads:
        load.start()
    tail = mine_ref[...].astype(f32)
    live, weight = (tail[0:1], tail[1:2] * (1.0 / STUDENT_TEMP))
    pull = join(at_ref[0], both_ref, other_ref, 0)
    push = join(at_ref[0], both_ref, other_ref, 1)
    norm_sum = push[CAP : CAP + 1]
    push = push[0:CAP]
    scale = live / (pull[CAP : CAP + 1] + 1.0 - live)
    pull = pull[0:CAP]
    unit, inv = unit_of(feats_ref, feats_other_ref)
    inv = jnp.broadcast_to(inv, unit.shape).T[0:1]
    unit = unit.T
    cross = jnp.sum(unit.astype(bf16).astype(f32) * pull, axis=0, keepdims=True) * (1.0 / STUDENT_TEMP)
    row_loss = jnp.log(norm_sum) - scale * cross
    loss = jnp.sum(member_ref[...] * row_loss, axis=1, keepdims=True)
    square = (member_ref.shape[0], 128)
    loss = jnp.where(iota(square, 0) == iota(square, 1), loss, 0.0)
    loss_ref[...] = jnp.sum(loss, axis=0, keepdims=True)[:, 0 : loss_ref.shape[1]]
    alpha = weight / norm_sum
    beta = weight * scale
    grad_unit = push * alpha - pull * beta
    inner = jnp.sum(unit * grad_unit, axis=0, keepdims=True)
    grad_feats = (inv * (grad_unit - unit * inner)).T.astype(bf16)
    for load in loads:
        load.wait()
    width = send_ref.shape[2]
    grad_rows = jnp.zeros(grad_rows_ref.shape, f32)
    for part in chunks_of(hidden_ref.shape[1]):
        grad_pre = (mm(grad_feats, w_out_ref[part, :], NT) * slope_ref[:, part]).astype(bf16)
        pre_ref[:, part] = grad_pre
        grad_rows = grad_rows + mm(grad_pre, w_in_ref[:, part], NT)
        out_ref[part, :] = mm(hidden_ref[:, part], grad_feats, TN).astype(bf16)
    grad_rows_ref[...] = grad_rows.astype(bf16)
    rows_out = pltpu.make_async_copy(grad_rows_ref, grad_rows_hbm, rows_sem.at[0])
    rows_out.start()
    core, level = (at_ref[0], at_ref[1])
    own = pre_ref[:, pl.ds(pl.multiple_of(level * width, width), width)]
    grad_in = mm(rows_ref[...], own, TN).astype(bf16)
    per = grad_in.shape[0] // peers
    block = out_ref.shape[0] // (peers // 2)
    share = block // 4
    at = iota((EXTRA, CAP), 0)
    rows = jnp.zeros((EXTRA, CAP), f32)
    for i, x in enumerate(two_parts(alpha) + two_parts(beta)):
        rows = jnp.where(at == i, x, rows)
    rows = rows.astype(bf16)
    store = lambda g: pltpu.make_async_copy(send_ref.at[g], send_hbm.at[g], send_sems.at[g])
    for g in range(peers):
        send_ref[g, 0:per, :] = grad_in[g * per : (g + 1) * per, :]
        start = pl.multiple_of((g % (peers // 2)) * block + level * share, share)
        out = out_ref[pl.ds(start, share), :]
        send_ref[g, per : per + share, :] = jnp.where(core == g // (peers // 2), out, jnp.zeros_like(out))
        send_ref[g, per + share : per + share + EXTRA, :] = rows
        store(g).start()
    rows_out.wait()
    wait_all(peers, store)


def place_body(sel_ref, rows_ref, other_ref, out_hbm, out_ref, sems):
    rows = (rows_ref[...].astype(f32) + other_ref[...].astype(f32)).astype(bf16)
    pieces = out_ref.shape[0]
    size = out_ref.shape[1]
    store = lambda i: pltpu.make_async_copy(out_ref.at[i], out_hbm.at[i], sems.at[i])
    for i in range(pieces):
        out_ref[i] = mm(sel_ref[:, i * size : (i + 1) * size], rows, TN).astype(bf16)
        store(i).start()
    wait_all(pieces, store)


def gather_grads_body(got_hbm, send_hbm, got_ref, sum_ref, load_sems, sems):
    peers = got_hbm.shape[0]
    lines = sum_ref.shape[0]
    load = lambda g: pltpu.make_async_copy(got_hbm.at[g, 0:lines, :], got_ref.at[g], load_sems.at[g])
    start_all(peers, load)
    load(0).wait()
    acc = got_ref[0].astype(f32)
    for g in range(1, peers):
        load(g).wait()
        acc = acc + got_ref[g].astype(f32)
    sum_ref[...] = acc.astype(bf16)
    store = lambda t: pltpu.make_async_copy(sum_ref, send_hbm.at[t], sems.at[t])
    start_all(send_hbm.shape[0], store)
    wait_all(send_hbm.shape[0], store)


def weight_grads_body(at_ref, parts_ref, grad_in_ref, grad_out_ref):
    peers, lines, width = parts_ref.shape
    per = grad_in_ref.shape[0]
    share = lines - per
    for t in range(peers):
        to = ((t % 2) * (peers // 2) + t // 2) * width
        grad_in_ref[:, to : to + width] = parts_ref[t, 0:per, :].astype(f32)
    for z in range(peers // 2):
        grad_out_ref[z * share : (z + 1) * share, :] = parts_ref[2 * z + at_ref[2], per:lines, :].astype(f32)


def sem(number):
    return pltpu.SemaphoreType.DMA((number,))


def run_expo(at, cols_t, own, other, tensor):
    dp, (width, bot) = (own.shape[0], cols_t.shape)
    big, small = ((dp, width, CAP), (dp, CAP))
    return call(
        expo_body,
        [(big, bf16), ((tensor, *small), bf16), (small, f32)],
        (at, cols_t, own, other),
        in_specs=[SMEM, HBM, ANY, ANY],
        out_specs=[HBM, VMEM, VMEM],
        scratch=[
            pltpu.VMEM((width, bot), bf16),
            pltpu.VMEM((dp, 2, HALF, bot), bf16),
            pltpu.VMEM((dp, EXTRA, bot), bf16),
            pltpu.VMEM(big, bf16),
            pltpu.VMEM((width, 128), f32),
            pltpu.VMEM(small, f32),
            *[sem(dp // GROUP)] * 4,
        ],
    )


def run_balance(expo, got, live, tensor):
    dp, width, _ = expo.shape
    small = pltpu.VMEM(live.shape, f32)
    return call(
        balance_body,
        [((tensor, *live.shape), bf16)],
        (expo, got, live),
        in_specs=[HBM, VMEM, VMEM],
        scratch=[pltpu.VMEM(expo.shape, bf16), pltpu.VMEM((width, 128), f32), small, small, sem(dp // GROUP)],
    )[0]


def run_last(at, expo, got, live, cols):
    dp, width, _ = expo.shape
    halves = (dp, LINES, HALF)
    return call(
        last_body,
        [(halves, bf16), (halves, bf16), ((width, 128), f32)],
        (at, expo, got, live, cols),
        in_specs=[SMEM, HBM, VMEM, VMEM, VMEM],
        out_specs=[HBM, HBM, HBM],
        scratch=[
            pltpu.VMEM(expo.shape, bf16),
            pltpu.VMEM((width, 128), f32),
            pltpu.VMEM(live.shape, f32),
            pltpu.VMEM((2, *halves), bf16),
            *[sem(dp // GROUP)] * 3,
        ],
    )


def run_student(at, cols_t, cols, rows):
    dp = rows.shape[0]
    big, halves = ((dp, cols.shape[1], CAP), (dp, LINES, HALF))
    return call(
        student_body,
        [(big, bf16), (halves, bf16), (halves, bf16)],
        (at, cols_t, cols, rows),
        in_specs=[SMEM, VMEM, VMEM, HBM],
        out_specs=[HBM, HBM, HBM],
        scratch=[
            pltpu.VMEM(rows.shape, bf16),
            pltpu.VMEM(big, bf16),
            pltpu.VMEM((2, *halves), bf16),
            *[sem(dp // GROUP)] * 4,
        ],
    )


def run_columns_grad(expo, raised, scale, got, rows, proto, norm):
    dp, held = (expo.shape[0], pltpu.VMEM(expo.shape, bf16))
    return call(
        columns_grad_body,
        [(proto.shape, f32)],
        (expo, raised, scale, got, rows, proto, norm),
        in_specs=[HBM] * 3 + [ANY] + [HBM] * 3,
        scratch=[
            pltpu.VMEM(scale.shape, f32),
            pltpu.VMEM(proto.shape, bf16),
            pltpu.VMEM(norm.shape, f32),
            held,
            held,
            pltpu.VMEM(proto.shape[::-1], f32),
            pltpu.VMEM((dp, EXTRA, CAP), bf16),
            pltpu.VMEM(rows.shape, bf16),
            *[sem(dp // GROUP)] * 4,
            sem(2),
        ],
    )[0]


def exchange(x, axis):
    return lax.all_to_all(x, axis, split_axis=0, concat_axis=0, tiled=True)


def sibling(x):
    peers = lax.axis_size("tensor")
    return lax.ppermute(x, "tensor", [(i, i ^ 1) for i in range(peers)])


def everywhere(part, small):
    got = exchange(part, "tensor")
    (sums,) = call(relay_body, [((small[0], *small), bf16)], (got,))
    return exchange(sums, "dp")


def levels(x, by):
    peers = lax.axis_size("tensor")
    return lax.ppermute(x, "tensor", [(i, i ^ (2 * by)) for i in range(peers)])


def paired(keep, give):
    return (keep.astype(f32) + sibling(give).astype(f32)).astype(bf16)


def slot_sums_body(*refs):
    *earlier, parts_hbm, out_hbm, parts_ref, out_ref, sems, out_sem = refs
    moves = [pltpu.make_async_copy(ref.at[0], out_ref.at[0], out_sem.at[0]) for ref in earlier]
    for move in moves:
        move.start()
    peers = parts_hbm.shape[0]
    load = lambda g: pltpu.make_async_copy(parts_hbm.at[g], parts_ref.at[g], sems.at[g])
    start_all(peers, load)
    load(0).wait()
    acc = parts_ref[0].astype(f32)
    for g in range(1, peers):
        load(g).wait()
        acc = acc + parts_ref[g].astype(f32)
    out_ref[len(earlier)] = acc.astype(bf16)
    for move in moves:
        move.wait()
    store = pltpu.make_async_copy(out_ref, out_hbm, out_sem.at[0])
    store.start()
    store.wait()


def slot_sums(parts, *earlier):
    out = (1 + len(earlier), *parts.shape[1:])
    return call(
        slot_sums_body,
        [(out, bf16)],
        (*earlier, parts),
        in_specs=[HBM] * len(earlier) + [ANY],
        out_specs=[HBM],
        scratch=[pltpu.VMEM(parts.shape, bf16), pltpu.VMEM(out, bf16), sem(parts.shape[0]), sem(1)],
    )[0]


def after(x, earlier):
    return lax.optimization_barrier((x, earlier))[0]


def parts_of(tokens, teacher_feats, masks, w_in, w_out, proto_student, proto_teacher):
    dim = tokens.shape[1]
    hid = w_in.shape[1]
    bot, width = proto_student.shape
    dp, tensor = (lax.axis_size("dp"), lax.axis_size("tensor"))
    per = w_in.shape[0]
    half = hid // 2
    share = w_out.shape[0] // 4
    t = lax.axis_index("tensor").astype(jnp.int32)
    g = lax.axis_index("dp").astype(jnp.int32)
    at = jnp.stack([t % 2, t // 2, g // (dp // 2)])

    lines = per + w_out.shape[0] * bot // half
    (w_pack,) = call(weights_body, [((lines, half), bf16)], (at, w_in, w_out), in_specs=[SMEM, HBM, HBM], out_specs=[HBM], scratch=[sem(1 + half // bot)])
    w_all = lax.all_gather(w_pack, "dp", axis=0, tiled=True).reshape(dp, lines, half)
    dma = pltpu.SemaphoreType.DMA
    sems = dma((dp,))
    sel, send, member, mine = call(
        select_body,
        [((CAP, tokens.shape[0]), bf16), ((dp, HALF + EXTRA, bot), bf16), ((8, CAP), f32), ((EXTRA, CAP), bf16)],
        (at, masks, teacher_feats),
        in_specs=[SMEM, VMEM, VMEM],
        out_specs=[VMEM, HBM, HBM, HBM],
        scratch=[
            pltpu.VMEM((CAP, bot), bf16),
            pltpu.VMEM((HALF + EXTRA, bot), bf16),
            pltpu.VMEM((8, CAP), f32),
            pltpu.VMEM((EXTRA, CAP), bf16),
            sems,
            sem(2),
        ],
    )
    packs = exchange(send, "dp")
    others = sibling(packs)
    cols, student_t, teacher_t, norm = call(
        columns_body,
        [((bot, width), bf16), ((width, bot), bf16), ((width, bot), bf16), ((1, width), f32)],
        (proto_student, proto_teacher),
        out_specs=[HBM] * 4,
        scratch=[
            pltpu.VMEM((bot, width), bf16),
            pltpu.VMEM((width, bot), bf16),
            pltpu.VMEM((width, bot), bf16),
            pltpu.VMEM((1, width), f32),
            sem(4),
        ],
    )
    expo, part, live = run_expo(at, teacher_t, packs, others, tensor)
    loads = dma((dp + 2 * dp,))
    w_held = [pltpu.VMEM((dim, half), bf16), pltpu.VMEM((half, bot), bf16)]
    (rows,) = call(
        tokens_body,
        [((CAP, dim), bf16)],
        (sel, tokens),
        in_specs=[VMEM, HBM],
        out_specs=[HBM],
        scratch=[pltpu.VMEM(tokens.shape, bf16), pltpu.VMEM((CAP, dim), bf16), sem(2)],
    )
    hidden, slope, feats = call(
        forward_body,
        [((CAP, half), bf16), ((CAP, half), f32), ((CAP, bot), f32)],
        (at, rows, after(w_all, part)),
        in_specs=[SMEM, HBM, HBM],
        out_specs=[HBM, HBM, VMEM],
        scratch=[
            pltpu.VMEM((CAP, dim), bf16),
            pltpu.VMEM((CAP, half), bf16),
            pltpu.VMEM((CAP, half), f32),
            *w_held,
            loads,
            sem(2),
        ],
    )
    feats_other = sibling(feats)
    (student_rows,) = call(unit_body, [((CAP, bot), bf16)], (feats, feats_other))
    all_rows = lax.all_gather(student_rows, "dp", axis=0, tiled=True).reshape(dp, CAP, bot)
    got = everywhere(part, live.shape)
    part = run_balance(expo, got, live, tensor)
    got = everywhere(part, live.shape)
    keep, give, scale = run_last(at, expo, got, live, cols)
    pull = paired(keep, give)
    pull_got = exchange(pull, "dp")
    all_rows = after(all_rows, pull)
    raised, keep, give = run_student(at, student_t, cols, all_rows)
    push_got = exchange(paired(keep, give), "dp")
    both = slot_sums(push_got, slot_sums(pull_got))
    near, far, last = (levels(both, by) for by in (1, 2, 3))
    wide = lambda x: x.astype(f32)
    both = (wide(both) + wide(near)) + (wide(far) + wide(last))
    back_lines = per + share + EXTRA
    send, grad_rows, loss = call(
        backward_body,
        [((dp, back_lines, bot), bf16), ((CAP, dim), bf16), ((1, masks.shape[0]), f32)],
        (at, both, sibling(both), mine, member, feats, feats_other, rows, hidden, slope, w_all),
        in_specs=[SMEM] + [VMEM] * 9 + [HBM],
        out_specs=[HBM, HBM, VMEM],
        scratch=[
            *w_held,
            pltpu.VMEM((dp, back_lines, bot), bf16),
            pltpu.VMEM((CAP, half), bf16),
            pltpu.VMEM((half, bot), bf16),
            pltpu.VMEM((CAP, dim), bf16),
            loads,
            sems,
            sem(1),
        ],
    )
    got = exchange(send, "dp")
    pieces = 4
    d_shape = (pieces, tokens.shape[0] // pieces, dim)
    (d_tokens,) = call(
        place_body,
        [(d_shape, bf16)],
        (sel, grad_rows, sibling(grad_rows)),
        out_specs=[HBM],
        scratch=[pltpu.VMEM(d_shape, bf16), dma((pieces,))],
    )
    got, d_tokens = lax.optimization_barrier((got, d_tokens))
    (sent,) = call(
        gather_grads_body,
        [((tensor, per + share, bot), bf16)],
        (got,),
        in_specs=[ANY],
        out_specs=[HBM],
        scratch=[pltpu.VMEM((dp, per + share, bot), bf16), pltpu.VMEM((per + share, bot), bf16), sems, sem(tensor)],
    )
    parts = exchange(sent, "tensor")
    grad_proto = run_columns_grad(expo, raised, scale, got, all_rows, proto_student, norm)
    grad_in, grad_out = call(
        weight_grads_body, [((per, hid), f32), ((w_out.shape[0], bot), f32)], (at, parts), in_specs=[SMEM, VMEM]
    )
    return (d_tokens.reshape(tokens.shape), grad_in, grad_out, grad_proto, loss.reshape(masks.shape[0]))


def solution(mesh):
    placed = (
        P("dp", None),
        P("dp", None),
        P("dp", None),
        P("dp", None),
        P("dp", None),
        P(None, ("dp", "tensor")),
        P(None, ("dp", "tensor")),
    )
    return jax.shard_map(
        parts_of,
        mesh=mesh,
        in_specs=placed,
        out_specs=(P("dp", None), P("dp", None), P("dp", None), P(None, ("dp", "tensor")), P("dp")),
        check_vma=False,
    )
```

```python
import jax
import jax.numpy as jnp
from jax import lax
from jax.experimental import pallas as pl
from jax.experimental.pallas import tpu as pltpu
from jax.sharding import PartitionSpec as P

CAP = 256
TEACHER_TEMP = 0.07
STUDENT_TEMP = 0.1
EPS = 1e-06
GRAD_SCALE = 65536.0
INTERPRET = False
f32, bf16 = (jnp.float32, jnp.bfloat16)
VMEM = pl.BlockSpec(memory_space=pltpu.VMEM)
HBM = pl.BlockSpec(memory_space=pltpu.HBM)
ANY = pl.BlockSpec(memory_space=pl.ANY)
SMEM = pl.BlockSpec(memory_space=pltpu.SMEM)
NT = (((1,), (1,)), ((), ()))
TN = (((0,), (0,)), ((), ()))
EXTRA = 16
HALF = CAP // 2
LINES = CAP + EXTRA


def mm(a, b, dims=None):
    if dims is None:
        return jnp.dot(a, b, preferred_element_type=f32)
    return lax.dot_general(a, b, dims, preferred_element_type=f32)


def call(body, outs, ins, out_specs=None, in_specs=None, scratch=()):
    specs = out_specs or [VMEM] * len(outs)
    in_specs = in_specs or [VMEM] * len(ins)
    ins = [pltpu.with_memory_space_constraint(x, pltpu.HBM) if spec is HBM else x for x, spec in zip(ins, in_specs)]
    outs = tuple(pltpu.HBM(*o) if spec is HBM else jax.ShapeDtypeStruct(*o) for o, spec in zip(outs, specs))
    return pl.pallas_call(
        body,
        out_shape=outs,
        in_specs=in_specs,
        out_specs=tuple(specs),
        scratch_shapes=list(scratch),
        interpret=INTERPRET,
        compiler_params=pltpu.CompilerParams(vmem_limit_bytes=48 << 20),
    )(*ins)


def iota(shape, dim):
    return lax.broadcasted_iota(jnp.int32, shape, dim)


def copies(pairs, sems):
    return [pltpu.make_async_copy(a, b, sems.at[i]) for i, (a, b) in enumerate(pairs)]


GROUP = 4
UNROLL = 4


def group(ref, q):
    return ref.at[pl.ds(q * GROUP, GROUP)]


def start_all(number, make):
    def go(i, _):
        make(i).start()
        return 0

    lax.fori_loop(0, number, go, 0)


def wait_all(number, make):
    def go(i, _):
        make(i).wait()
        return 0

    lax.fori_loop(0, number, go, 0)


def over_groups(peers, step, loads=(), stores=(), unroll=1):
    def go(q, _):
        for make in loads:
            make(q).wait()
        lax.fori_loop(0, GROUP, lambda i, _: step(q * GROUP + i), 0, unroll=unroll)
        for make in stores:
            make(q).start()
        return 0

    lax.fori_loop(0, peers // GROUP, go, 0)


def select_body(
    at_ref, mask_ref, feats_ref, sel_ref, send_hbm, member_hbm, mine_hbm, unit_ref, pack_ref, member_ref, mine_ref, sems, late_sems
):
    crops, patches = mask_ref.shape
    mask = mask_ref[...].astype(f32)
    upto = (iota((patches, patches), 0) <= iota((patches, patches), 1)).astype(f32).astype(bf16)
    rank = mm(mask.astype(bf16), upto)
    count = jnp.sum(mask, axis=1, keepdims=True)
    total = jnp.sum(count, axis=0, keepdims=True)
    slot = iota((CAP, patches), 0).astype(f32)
    lane = iota((1, CAP), 1).astype(f32)
    start = jnp.zeros((1, 1), f32)
    weight = jnp.zeros((1, CAP), f32)
    first = iota((CAP, patches), 1) == 0
    member_ref[...] = jnp.zeros_like(member_ref)
    for c in range(crops):
        hit = jnp.where((rank[c : c + 1] + start == slot + 1.0) & (mask[c : c + 1] > 0.0), 1.0, 0.0)
        if c == 0:
            hit = jnp.where(first & (slot >= total), 1.0, hit)
        sel_ref[:, c * patches : (c + 1) * patches] = hit.astype(bf16)
        own = count[c : c + 1]
        inside = jnp.where((lane >= start) & (lane < start + own), 1.0, 0.0)
        part = inside * (1.0 / jnp.maximum(own, 1.0))
        member_ref[c : c + 1, :] = part
        weight = weight + part
        start = start + own
    live = jnp.where(lane < total, 1.0, 0.0)
    picked = mm(sel_ref[...], feats_ref[...])
    scale = lax.rsqrt(jnp.sum(picked * picked, axis=1, keepdims=True) + EPS)
    unit_ref[...] = (picked * scale).astype(bf16)
    at = iota((EXTRA, CAP), 0)
    tail = jnp.where(at == 0, live, jnp.where(at == 1, weight * GRAD_SCALE, 0.0)).astype(bf16)
    mine_ref[...] = tail
    late = copies([(member_ref, member_hbm), (mine_ref, mine_hbm)], late_sems)
    for copy in late:
        copy.start()
    pack_ref[0:HALF, :] = unit_ref[pl.ds(pl.multiple_of(at_ref[0] * HALF, HALF), HALF), :]
    pack_ref[HALF : HALF + EXTRA, :] = tail
    peers = send_hbm.shape[0]
    make = lambda g: pltpu.make_async_copy(pack_ref, send_hbm.at[g], sems.at[g])
    start_all(peers, make)
    for copy in late:
        copy.wait()
    wait_all(peers, make)


def columns_body(
    student_ref, teacher_ref, cols_hbm, student_t_hbm, teacher_t_hbm, norm_hbm, cols_ref, student_t_ref, teacher_t_ref, norm_ref, sems
):
    for part in chunks_of(student_ref.shape[1]):
        wide = student_ref[:, part].astype(f32)
        norm = jnp.sqrt(jnp.sum(wide * wide, axis=0, keepdims=True) + EPS)
        norm_ref[:, part] = norm
        unit = wide / norm
        cols_ref[:, part] = unit.astype(bf16)
        student_t_ref[part, :] = unit.T.astype(bf16)
        wide = teacher_ref[:, part].astype(f32)
        norm = jnp.sqrt(jnp.sum(wide * wide, axis=0, keepdims=True) + EPS)
        teacher_t_ref[part, :] = (wide / norm).T.astype(bf16)
    held = (cols_ref, student_t_ref, teacher_t_ref, norm_ref)
    stores = copies(list(zip(held, (cols_hbm, student_t_hbm, teacher_t_hbm, norm_hbm))), sems)
    for store in stores:
        store.start()
    for store in stores:
        store.wait()


def weights_body(at_ref, w_in_ref, w_out_ref, pack_hbm, pack_ref, sems):
    rows, hid = w_in_ref.shape
    half = hid // 2
    bot = w_out_ref.shape[1]
    lines = w_out_ref.shape[0] * bot // half
    pack_ref[0:rows, :] = w_in_ref[:, pl.ds(pl.multiple_of(at_ref[0] * half, half), half)]
    for q in range(half // bot):
        pack_ref[rows : rows + lines, q * bot : (q + 1) * bot] = w_out_ref[q * lines : (q + 1) * lines, :]
    store = pltpu.make_async_copy(pack_ref, pack_hbm, sems.at[0])
    store.start()
    store.wait()


def weight_loads(at_ref, w_hbm, w_in_ref, w_out_ref, sems):
    peers = w_hbm.shape[0]
    rows = w_in_ref.shape[0] // peers
    lines = w_hbm.shape[1] - rows
    bot = w_out_ref.shape[1]
    quarters = w_hbm.shape[2] // bot
    pairs = [(w_hbm.at[g, 0:rows, :], w_in_ref.at[g * rows : (g + 1) * rows, :]) for g in range(peers)]
    for i in range(peers // 2):
        for q in range(quarters):
            source = w_hbm.at[at_ref[0] * (peers // 2) + i, rows : rows + lines, q * bot : (q + 1) * bot]
            at = (i * quarters + q) * lines
            pairs.append((source, w_out_ref.at[at : at + lines, :]))
    return copies(pairs, sems)


def tokens_body(sel_ref, tokens_hbm, rows_hbm, tokens_ref, rows_ref, sems):
    load = pltpu.make_async_copy(tokens_hbm, tokens_ref, sems.at[0])
    load.start()
    load.wait()
    rows_ref[...] = mm(sel_ref[...], tokens_ref[...]).astype(bf16)
    store = pltpu.make_async_copy(rows_ref, rows_hbm, sems.at[1])
    store.start()
    store.wait()


def forward_body(
    at_ref, rows_hbm, w_hbm, hidden_hbm, slope_hbm, feats_ref, w_in_hbm, w_out_hbm,
    rows_ref, hidden_ref, slope_ref, w_in_ref, w_out_ref, sems, own_sems,
):
    first = pltpu.make_async_copy(rows_hbm, rows_ref, own_sems.at[0])
    first.start()
    loads = weight_loads(at_ref, w_hbm, w_in_ref, w_out_ref, sems)
    for load in loads:
        load.start()
    first.wait()
    for load in loads:
        load.wait()
    keeps = copies([(w_in_ref, w_in_hbm), (w_out_ref, w_out_hbm)], sems)
    for keep in keeps:
        keep.start()
    rows = rows_ref[...]
    feats = jnp.zeros(feats_ref.shape, f32)
    for part in chunks_of(hidden_ref.shape[1]):
        pre = mm(rows, w_in_ref[:, part])
        cdf = 0.5 * (1.0 + lax.erf(pre * 0.7071067811865476))
        slope_ref[:, part] = cdf + pre * (jnp.exp(-0.5 * pre * pre) * 0.3989422804014327)
        hidden = (pre * cdf).astype(bf16)
        hidden_ref[:, part] = hidden
        feats = feats + mm(hidden, w_out_ref[part, :])
    feats_ref[...] = feats
    stores = copies([(hidden_ref, hidden_hbm), (slope_ref, slope_hbm)], own_sems)
    for store in stores:
        store.start()
    for store in keeps + stores:
        store.wait()


def unit_of(feats_ref, other_ref):
    feats = feats_ref[...] + other_ref[...]
    inv = lax.rsqrt(jnp.sum(feats * feats, axis=1, keepdims=True) + EPS)
    return (feats * inv, inv)


def unit_body(feats_ref, other_ref, rows_ref):
    rows_ref[...] = unit_of(feats_ref, other_ref)[0].astype(bf16)


def chunks_of(width):
    step = min(256, width)
    return [slice(at, at + step) for at in range(0, width, step)]


def row_of(ref, g):
    return ref[pl.ds(g, 1), :]


def fold(x):
    return x.reshape(x.shape[0] // 8, 8, x.shape[1]).sum(axis=0)


def expo_body(
    at_ref, cols_hbm, own_hbm, other_hbm, expo_hbm, part_ref, live_ref,
    cols_ref, rows_ref, tail_ref, expo_ref, total_ref, sums_ref, sems, own_sems, other_sems, tail_sems,
):
    peers = own_hbm.shape[0]
    width = cols_ref.shape[0]
    core = at_ref[0]
    number = peers // GROUP
    rows_of = lambda ref, q: ref.at[pl.ds(q * GROUP, GROUP), 0:HALF, :]
    rows_at = lambda q, c: rows_ref.at[pl.ds(q * GROUP, GROUP), c]
    load_own = lambda q: pltpu.make_async_copy(rows_of(own_hbm, q), rows_at(q, core), own_sems.at[q])
    load_other = lambda q: pltpu.make_async_copy(rows_of(other_hbm, q), rows_at(q, 1 - core), other_sems.at[q])
    load_tail = pltpu.make_async_copy(own_hbm.at[:, HALF : HALF + EXTRA, :], tail_ref, tail_sems.at[0])
    store = lambda q: pltpu.make_async_copy(group(expo_ref, q), group(expo_hbm, q), sems.at[q])
    load_cols = pltpu.make_async_copy(cols_hbm, cols_ref, tail_sems.at[1])
    load_cols.start()
    load_tail.start()
    start_all(number, load_own)
    start_all(number, load_other)
    total_ref[...] = jnp.zeros_like(total_ref)
    load_tail.wait()
    load_cols.wait()

    def first(g):
        rows = rows_ref[g].reshape(CAP, rows_ref.shape[3])
        tail = tail_ref[g].astype(f32)
        live = tail[0:1]
        live_ref[pl.ds(g, 1), :] = live
        for part in chunks_of(width):
            cos = mm(cols_ref[part, :], rows, NT)
            expo = jnp.exp(cos * (1.0 / TEACHER_TEMP)) * live
            expo_ref[g, part, :] = expo.astype(bf16)
            total_ref[part, :] += expo[:, 0:128] + expo[:, 128:256]
        return 0

    over_groups(peers, first, (load_own, load_other), (store,), UNROLL)
    spread_scale(total_ref)
    row_parts(expo_ref, total_ref, sums_ref, part_ref)
    wait_all(number, store)


def spread_scale(total_ref):
    for part in chunks_of(total_ref.shape[0]):
        sums = jnp.sum(total_ref[part, :], axis=1, keepdims=True)
        total_ref[part, :] = jnp.broadcast_to(1.0 / sums, sums.shape[:1] + (128,))


def scaled(expo, scale):
    return jnp.concatenate([expo[:, 0:128] * scale, expo[:, 128:256] * scale], axis=1)


def row_parts(expo_ref, scale_ref, sums_ref, part_ref):
    def step(g):
        acc = jnp.zeros((8, CAP), f32)
        for part in chunks_of(scale_ref.shape[0]):
            acc = acc + fold(scaled(expo_ref[g, part, :].astype(f32), scale_ref[part, :]))
        sums_ref[pl.ds(g, 1), :] = jnp.sum(acc, axis=0, keepdims=True)
        return 0

    over_groups(expo_ref.shape[0], step, unroll=UNROLL)
    sums = sums_ref[...].astype(bf16)
    for t in range(part_ref.shape[0]):
        part_ref[t] = sums


def relay_body(parts_ref, out_ref):
    sums = parts_ref[0].astype(f32)
    for t in range(1, parts_ref.shape[0]):
        sums = sums + parts_ref[t].astype(f32)
    sums = sums.astype(bf16)
    for g in range(out_ref.shape[0]):
        out_ref[g] = sums


def scales_from(parts_ref, live_ref, scale_ref):
    sums = parts_ref[0].astype(f32)
    for g in range(1, parts_ref.shape[0]):
        sums = sums + parts_ref[g].astype(f32)
    live = live_ref[...]
    scale_ref[...] = live / (sums + 1.0 - live)


def column_sums(load, expo_ref, scale_ref, total_ref):
    total_ref[...] = jnp.zeros_like(total_ref)

    def step(g):
        row = row_of(scale_ref, g)
        for part in chunks_of(total_ref.shape[0]):
            expo = expo_ref[g, part, :].astype(f32)
            total_ref[part, :] += expo[:, 0:128] * row[:, 0:128] + expo[:, 128:256] * row[:, 128:256]
        return 0

    over_groups(expo_ref.shape[0], step, (load,), unroll=UNROLL)
    spread_scale(total_ref)


def balance_body(expo_hbm, parts_ref, live_ref, part_ref, expo_ref, total_ref, sums_ref, scale_ref, sems):
    load = lambda q: pltpu.make_async_copy(group(expo_hbm, q), group(expo_ref, q), sems.at[q])
    start_all(expo_ref.shape[0] // GROUP, load)
    scales_from(parts_ref, live_ref, scale_ref)
    column_sums(load, expo_ref, scale_ref, total_ref)
    row_parts(expo_ref, total_ref, sums_ref, part_ref)


def divide_up(g, acc, pull, halves_ref):
    rows = jnp.sum(acc, axis=0, keepdims=True)
    rows = jnp.where(iota((EXTRA, CAP), 0) == 0, rows, 0.0).astype(bf16)
    pull = pull.astype(bf16)
    for at, block in ((slice(0, CAP), pull), (slice(CAP, LINES), rows)):
        halves_ref[0, g, at, :] = block[:, 0:HALF]
        halves_ref[1, g, at, :] = block[:, HALF:CAP]


def last_body(
    at_ref, expo_hbm, parts_ref, live_ref, cols_ref, keep_hbm, give_hbm, total_hbm,
    expo_ref, total_ref, scale_ref, halves_ref, sems, keep_sems, give_sems,
):
    peers = expo_ref.shape[0]
    core = at_ref[0]
    load = lambda q: pltpu.make_async_copy(group(expo_hbm, q), group(expo_ref, q), sems.at[q])
    half_at = lambda c, q: halves_ref.at[c, pl.ds(q * GROUP, GROUP)]
    keep = lambda q: pltpu.make_async_copy(half_at(core, q), group(keep_hbm, q), keep_sems.at[q])
    give = lambda q: pltpu.make_async_copy(half_at(1 - core, q), group(give_hbm, q), give_sems.at[q])
    number = peers // GROUP
    start_all(number, load)
    scales_from(parts_ref, live_ref, scale_ref)
    column_sums(load, expo_ref, scale_ref, total_ref)

    def step(g):
        acc = jnp.zeros((8, CAP), f32)
        pull = jnp.zeros((cols_ref.shape[0], CAP), f32)
        for part in chunks_of(total_ref.shape[0]):
            balanced = scaled(expo_ref[g, part, :].astype(f32), total_ref[part, :])
            acc = acc + fold(balanced)
            pull = pull + mm(cols_ref[:, part], balanced.astype(bf16))
        divide_up(g, acc, pull, halves_ref)
        return 0

    spare = pltpu.make_async_copy(total_ref, total_hbm, sems.at[0])
    spare.start()
    over_groups(peers, step, (), (give, keep), UNROLL)
    wait_all(number, give)
    wait_all(number, keep)
    spare.wait()


def student_body(
    at_ref, cols_t_ref, cols_ref, rows_hbm, raised_hbm, keep_hbm, give_hbm,
    rows_ref, raised_ref, halves_ref, row_sems, sems, keep_sems, give_sems,
):
    peers = rows_ref.shape[0]
    load = lambda q: pltpu.make_async_copy(group(rows_hbm, q), group(rows_ref, q), row_sems.at[q])
    start_all(peers // GROUP, load)
    core = at_ref[0]
    width = cols_t_ref.shape[0]
    store = lambda q: pltpu.make_async_copy(group(raised_ref, q), group(raised_hbm, q), sems.at[q])
    half_at = lambda c, q: halves_ref.at[c, pl.ds(q * GROUP, GROUP)]
    keep = lambda q: pltpu.make_async_copy(half_at(core, q), group(keep_hbm, q), keep_sems.at[q])
    give = lambda q: pltpu.make_async_copy(half_at(1 - core, q), group(give_hbm, q), give_sems.at[q])
    number = peers // GROUP

    def step(g):
        rows = rows_ref[g]
        acc = jnp.zeros((8, CAP), f32)
        pull = jnp.zeros((cols_ref.shape[0], CAP), f32)
        for part in chunks_of(width):
            raised = jnp.exp(mm(cols_t_ref[part, :], rows, NT) * (1.0 / STUDENT_TEMP))
            acc = acc + fold(raised)
            raised = raised.astype(bf16)
            raised_ref[g, part, :] = raised
            pull = pull + mm(cols_ref[:, part], raised)
        divide_up(g, acc, pull, halves_ref)
        return 0

    over_groups(peers, step, (load,), (store, give, keep), UNROLL)
    for make in (give, keep, store):
        wait_all(number, make)


def columns_grad_body(
    expo_hbm, raised_hbm, scale_hbm, got_hbm, rows_hbm, proto_hbm, norm_hbm,
    grad_ref, scale_ref, proto_ref, norm_ref, expo_ref, raised_ref, acc_ref, tail_ref, rows_ref, esems, rsems, tail_sems, row_sems, late_sems,
):
    peers = expo_ref.shape[0]
    load = lambda q: pltpu.make_async_copy(group(expo_hbm, q), group(expo_ref, q), esems.at[q])
    load_raised = lambda q: pltpu.make_async_copy(group(raised_hbm, q), group(raised_ref, q), rsems.at[q])
    load_rows = lambda q: pltpu.make_async_copy(group(rows_hbm, q), group(rows_ref, q), row_sems.at[q])
    lines = got_hbm.shape[1] - EXTRA
    load_tail = pltpu.make_async_copy(got_hbm.at[:, lines : lines + EXTRA, :], tail_ref, tail_sems.at[0])
    load_scale = pltpu.make_async_copy(scale_hbm, scale_ref, tail_sems.at[1])
    late = copies([(proto_hbm, proto_ref), (norm_hbm, norm_ref)], late_sems)
    load_tail.start()
    load_scale.start()

    def begin(q, _):
        for make in (load_rows, load, load_raised):
            make(q).start()
        return 0

    lax.fori_loop(0, peers // GROUP, begin, 0)
    for copy in late:
        copy.start()
    acc_ref[...] = jnp.zeros_like(acc_ref)
    load_tail.wait()
    load_scale.wait()

    def step(g):
        tail = tail_ref[g].astype(f32)
        alpha = tail[0:1] + tail[1:2]
        beta = tail[2:3] + tail[3:4]
        rows = rows_ref[g]
        for part in chunks_of(acc_ref.shape[0]):
            balanced = scaled(expo_ref[g, part, :].astype(f32), scale_ref[part, :])
            score = raised_ref[g, part, :].astype(f32) * alpha - balanced * beta
            acc_ref[part, :] += mm(score.astype(bf16), rows)
        return 0

    over_groups(peers, step, (load_rows, load, load_raised), (), UNROLL)
    for copy in late:
        copy.wait()
    for part in chunks_of(acc_ref.shape[0]):
        grad = acc_ref[part, :].T
        norm = norm_ref[:, part]
        unit = proto_ref[:, part].astype(f32) / norm
        grad_ref[:, part] = (grad - unit * jnp.sum(unit * grad, axis=0, keepdims=True)) / norm


def join(core, both_ref, other_ref, at):
    own, other = (both_ref[at], other_ref[at])
    low = core == 0
    return jnp.concatenate([jnp.where(low, own, other), jnp.where(low, other, own)], axis=1)


def two_parts(x):
    high = x.astype(bf16)
    return (high.astype(f32), x - high.astype(f32))


def backward_body(
    at_ref, both_ref, other_ref, mine_ref, member_ref, feats_ref, feats_other_ref, rows_hbm, slope_hbm, hidden_hbm, w_in_hbm, w_out_hbm,
    send_hbm, grad_rows_hbm, loss_ref, w_out_ref, slope_ref, w_in_ref, hidden_ref, rows_ref, send_ref, pre_ref, out_ref, grad_rows_ref, send_sems, rows_sem, load_sems,
):
    peers = send_ref.shape[0]
    sources = (w_out_hbm, slope_hbm, w_in_hbm, hidden_hbm, rows_hbm)
    loads = copies(list(zip(sources, (w_out_ref, slope_ref, w_in_ref, hidden_ref, rows_ref))), load_sems)
    for load in loads:
        load.start()
    tail = mine_ref[...].astype(f32)
    live, weight = (tail[0:1], tail[1:2] * (1.0 / STUDENT_TEMP))
    pull = join(at_ref[0], both_ref, other_ref, 0)
    push = join(at_ref[0], both_ref, other_ref, 1)
    norm_sum = push[CAP : CAP + 1]
    push = push[0:CAP]
    scale = live / (pull[CAP : CAP + 1] + 1.0 - live)
    pull = pull[0:CAP]
    unit, inv = unit_of(feats_ref, feats_other_ref)
    inv = jnp.broadcast_to(inv, unit.shape).T[0:1]
    unit = unit.T
    cross = jnp.sum(unit.astype(bf16).astype(f32) * pull, axis=0, keepdims=True) * (1.0 / STUDENT_TEMP)
    row_loss = jnp.log(norm_sum) - scale * cross
    loss = jnp.sum(member_ref[...] * row_loss, axis=1, keepdims=True)
    square = (member_ref.shape[0], 128)
    loss = jnp.where(iota(square, 0) == iota(square, 1), loss, 0.0)
    loss_ref[...] = jnp.sum(loss, axis=0, keepdims=True)[:, 0 : loss_ref.shape[1]]
    alpha = weight / norm_sum
    beta = weight * scale
    grad_unit = push * alpha - pull * beta
    inner = jnp.sum(unit * grad_unit, axis=0, keepdims=True)
    grad_feats = (inv * (grad_unit - unit * inner)).T.astype(bf16)
    for load in loads:
        load.wait()
    width = send_ref.shape[2]
    grad_rows = jnp.zeros(grad_rows_ref.shape, f32)
    for part in chunks_of(hidden_ref.shape[1]):
        grad_pre = (mm(grad_feats, w_out_ref[part, :], NT) * slope_ref[:, part]).astype(bf16)
        pre_ref[:, part] = grad_pre
        grad_rows = grad_rows + mm(grad_pre, w_in_ref[:, part], NT)
        out_ref[part, :] = mm(hidden_ref[:, part], grad_feats, TN).astype(bf16)
    grad_rows_ref[...] = grad_rows.astype(bf16)
    rows_out = pltpu.make_async_copy(grad_rows_ref, grad_rows_hbm, rows_sem.at[0])
    rows_out.start()
    core, level = (at_ref[0], at_ref[1])
    own = pre_ref[:, pl.ds(pl.multiple_of(level * width, width), width)]
    grad_in = mm(rows_ref[...], own, TN).astype(bf16)
    per = grad_in.shape[0] // peers
    block = out_ref.shape[0] // (peers // 2)
    share = block // 4
    at = iota((EXTRA, CAP), 0)
    rows = jnp.zeros((EXTRA, CAP), f32)
    for i, x in enumerate(two_parts(alpha) + two_parts(beta)):
        rows = jnp.where(at == i, x, rows)
    rows = rows.astype(bf16)
    store = lambda g: pltpu.make_async_copy(send_ref.at[g], send_hbm.at[g], send_sems.at[g])
    for g in range(peers):
        send_ref[g, 0:per, :] = grad_in[g * per : (g + 1) * per, :]
        start = pl.multiple_of((g % (peers // 2)) * block + level * share, share)
        out = out_ref[pl.ds(start, share), :]
        send_ref[g, per : per + share, :] = jnp.where(core == g // (peers // 2), out, jnp.zeros_like(out))
        send_ref[g, per + share : per + share + EXTRA, :] = rows
        store(g).start()
    rows_out.wait()
    wait_all(peers, store)


def place_body(sel_ref, rows_ref, other_ref, out_hbm, out_ref, sems):
    rows = (rows_ref[...].astype(f32) + other_ref[...].astype(f32)).astype(bf16)
    pieces = out_ref.shape[0]
    size = out_ref.shape[1]
    store = lambda i: pltpu.make_async_copy(out_ref.at[i], out_hbm.at[i], sems.at[i])
    for i in range(pieces):
        out_ref[i] = mm(sel_ref[:, i * size : (i + 1) * size], rows, TN).astype(bf16)
        store(i).start()
    wait_all(pieces, store)


def gather_grads_body(got_hbm, send_hbm, got_ref, sum_ref, load_sems, sems):
    peers = got_hbm.shape[0]
    lines = sum_ref.shape[0]
    source = lambda q: got_hbm.at[pl.ds(q * GROUP, GROUP), 0:lines, :]
    load = lambda q: pltpu.make_async_copy(source(q), group(got_ref, q), load_sems.at[q])
    start_all(peers // GROUP, load)
    acc = jnp.zeros(got_ref.shape[1:], f32)
    for g in range(peers):
        if g % GROUP == 0:
            load(g // GROUP).wait()
        acc = acc + got_ref[g].astype(f32)
    sum_ref[...] = acc.astype(bf16)
    store = lambda t: pltpu.make_async_copy(sum_ref, send_hbm.at[t], sems.at[t])
    start_all(send_hbm.shape[0], store)
    wait_all(send_hbm.shape[0], store)


def weight_grads_body(at_ref, parts_ref, grad_in_ref, grad_out_ref):
    peers, lines, width = parts_ref.shape
    per = grad_in_ref.shape[0]
    share = lines - per
    for t in range(peers):
        to = ((t % 2) * (peers // 2) + t // 2) * width
        grad_in_ref[:, to : to + width] = parts_ref[t, 0:per, :].astype(f32)
    for z in range(peers // 2):
        grad_out_ref[z * share : (z + 1) * share, :] = parts_ref[2 * z + at_ref[2], per:lines, :].astype(f32)


def sem(number):
    return pltpu.SemaphoreType.DMA((number,))


def run_expo(at, cols_t, own, other, tensor):
    dp, (width, bot) = (own.shape[0], cols_t.shape)
    big, small = ((dp, width, CAP), (dp, CAP))
    return call(
        expo_body,
        [(big, bf16), ((tensor, *small), bf16), (small, f32)],
        (at, cols_t, own, other),
        in_specs=[SMEM, HBM, ANY, ANY],
        out_specs=[HBM, VMEM, VMEM],
        scratch=[
            pltpu.VMEM((width, bot), bf16),
            pltpu.VMEM((dp, 2, HALF, bot), bf16),
            pltpu.VMEM((dp, EXTRA, bot), bf16),
            pltpu.VMEM(big, bf16),
            pltpu.VMEM((width, 128), f32),
            pltpu.VMEM(small, f32),
            *[sem(dp // GROUP)] * 4,
        ],
    )


def run_balance(expo, got, live, tensor):
    dp, width, _ = expo.shape
    small = pltpu.VMEM(live.shape, f32)
    return call(
        balance_body,
        [((tensor, *live.shape), bf16)],
        (expo, got, live),
        in_specs=[HBM, VMEM, VMEM],
        scratch=[pltpu.VMEM(expo.shape, bf16), pltpu.VMEM((width, 128), f32), small, small, sem(dp // GROUP)],
    )[0]


def run_last(at, expo, got, live, cols):
    dp, width, _ = expo.shape
    halves = (dp, LINES, HALF)
    return call(
        last_body,
        [(halves, bf16), (halves, bf16), ((width, 128), f32)],
        (at, expo, got, live, cols),
        in_specs=[SMEM, HBM, VMEM, VMEM, VMEM],
        out_specs=[ANY, ANY, HBM],
        scratch=[
            pltpu.VMEM(expo.shape, bf16),
            pltpu.VMEM((width, 128), f32),
            pltpu.VMEM(live.shape, f32),
            pltpu.VMEM((2, *halves), bf16),
            *[sem(dp // GROUP)] * 3,
        ],
    )


def run_student(at, cols_t, cols, rows):
    dp = rows.shape[0]
    big, halves = ((dp, cols.shape[1], CAP), (dp, LINES, HALF))
    return call(
        student_body,
        [(big, bf16), (halves, bf16), (halves, bf16)],
        (at, cols_t, cols, rows),
        in_specs=[SMEM, VMEM, VMEM, HBM],
        out_specs=[HBM, ANY, ANY],
        scratch=[
            pltpu.VMEM(rows.shape, bf16),
            pltpu.VMEM(big, bf16),
            pltpu.VMEM((2, *halves), bf16),
            *[sem(dp // GROUP)] * 4,
        ],
    )


def run_columns_grad(expo, raised, scale, got, rows, proto, norm):
    dp, held = (expo.shape[0], pltpu.VMEM(expo.shape, bf16))
    return call(
        columns_grad_body,
        [(proto.shape, f32)],
        (expo, raised, scale, got, rows, proto, norm),
        in_specs=[HBM] * 3 + [ANY] + [HBM] * 3,
        scratch=[
            pltpu.VMEM(scale.shape, f32),
            pltpu.VMEM(proto.shape, bf16),
            pltpu.VMEM(norm.shape, f32),
            held,
            held,
            pltpu.VMEM(proto.shape[::-1], f32),
            pltpu.VMEM((dp, EXTRA, CAP), bf16),
            pltpu.VMEM(rows.shape, bf16),
            *[sem(dp // GROUP)] * 4,
            sem(2),
        ],
    )[0]


def exchange(x, axis):
    return lax.all_to_all(x, axis, split_axis=0, concat_axis=0, tiled=True)


def sibling(x):
    peers = lax.axis_size("tensor")
    return lax.ppermute(x, "tensor", [(i, i ^ 1) for i in range(peers)])


def everywhere(part, small):
    got = exchange(part, "tensor")
    (sums,) = call(relay_body, [((small[0], *small), bf16)], (got,))
    return exchange(sums, "dp")


def levels(x, by):
    peers = lax.axis_size("tensor")
    return lax.ppermute(x, "tensor", [(i, i ^ (2 * by)) for i in range(peers)])


def paired(keep, give):
    return (keep.astype(f32) + sibling(give).astype(f32)).astype(bf16)


def slot_sums_body(*refs):
    *earlier, parts_hbm, out_hbm, parts_ref, out_ref, sems, out_sem = refs
    moves = [pltpu.make_async_copy(ref.at[0], out_ref.at[0], out_sem.at[0]) for ref in earlier]
    for move in moves:
        move.start()
    peers = parts_hbm.shape[0]
    load = lambda q: pltpu.make_async_copy(group(parts_hbm, q), group(parts_ref, q), sems.at[q])
    start_all(peers // GROUP, load)
    acc = jnp.zeros(parts_ref.shape[1:], f32)
    for g in range(peers):
        if g % GROUP == 0:
            load(g // GROUP).wait()
        acc = acc + parts_ref[g].astype(f32)
    out_ref[len(earlier)] = acc.astype(bf16)
    for move in moves:
        move.wait()
    store = pltpu.make_async_copy(out_ref, out_hbm, out_sem.at[0])
    store.start()
    store.wait()


def slot_sums(parts, *earlier):
    out = (1 + len(earlier), *parts.shape[1:])
    return call(
        slot_sums_body,
        [(out, bf16)],
        (*earlier, parts),
        in_specs=[HBM] * len(earlier) + [ANY],
        out_specs=[HBM],
        scratch=[pltpu.VMEM(parts.shape, bf16), pltpu.VMEM(out, bf16), sem(parts.shape[0] // GROUP), sem(1)],
    )[0]


def after(x, earlier):
    return lax.optimization_barrier((x, earlier))[0]


def parts_of(tokens, teacher_feats, masks, w_in, w_out, proto_student, proto_teacher):
    dim = tokens.shape[1]
    hid = w_in.shape[1]
    bot, width = proto_student.shape
    dp, tensor = (lax.axis_size("dp"), lax.axis_size("tensor"))
    per = w_in.shape[0]
    half = hid // 2
    share = w_out.shape[0] // 4
    t = lax.axis_index("tensor").astype(jnp.int32)
    g = lax.axis_index("dp").astype(jnp.int32)
    at = jnp.stack([t % 2, t // 2, g // (dp // 2)])

    lines = per + w_out.shape[0] * bot // half
    (w_pack,) = call(weights_body, [((lines, half), bf16)], (at, w_in, w_out), in_specs=[SMEM, VMEM, VMEM], out_specs=[HBM], scratch=[pltpu.VMEM((lines, half), bf16), sem(1)])
    w_all = lax.all_gather(w_pack, "dp", axis=0, tiled=True).reshape(dp, lines, half)
    dma = pltpu.SemaphoreType.DMA
    sems = dma((dp,))
    sel, send, member, mine = call(
        select_body,
        [((CAP, tokens.shape[0]), bf16), ((dp, HALF + EXTRA, bot), bf16), ((8, CAP), f32), ((EXTRA, CAP), bf16)],
        (at, masks, teacher_feats),
        in_specs=[SMEM, VMEM, VMEM],
        out_specs=[VMEM, HBM, HBM, HBM],
        scratch=[
            pltpu.VMEM((CAP, bot), bf16),
            pltpu.VMEM((HALF + EXTRA, bot), bf16),
            pltpu.VMEM((8, CAP), f32),
            pltpu.VMEM((EXTRA, CAP), bf16),
            sems,
            sem(2),
        ],
    )
    packs = exchange(send, "dp")
    others = sibling(packs)
    cols, student_t, teacher_t, norm = call(
        columns_body,
        [((bot, width), bf16), ((width, bot), bf16), ((width, bot), bf16), ((1, width), f32)],
        (proto_student, proto_teacher),
        out_specs=[HBM] * 4,
        scratch=[
            pltpu.VMEM((bot, width), bf16),
            pltpu.VMEM((width, bot), bf16),
            pltpu.VMEM((width, bot), bf16),
            pltpu.VMEM((1, width), f32),
            sem(4),
        ],
    )
    expo, part, live = run_expo(at, teacher_t, packs, others, tensor)
    loads = dma((dp + 2 * dp,))
    w_held = [pltpu.VMEM((dim, half), bf16), pltpu.VMEM((half, bot), bf16)]
    (rows,) = call(
        tokens_body,
        [((CAP, dim), bf16)],
        (sel, tokens),
        in_specs=[VMEM, HBM],
        out_specs=[HBM],
        scratch=[pltpu.VMEM(tokens.shape, bf16), pltpu.VMEM((CAP, dim), bf16), sem(2)],
    )
    hidden, slope, feats, w_in_half, w_out_half = call(
        forward_body,
        [((CAP, half), bf16), ((CAP, half), f32), ((CAP, bot), f32), ((dim, half), bf16), ((half, bot), bf16)],
        (at, rows, after(w_all, part)),
        in_specs=[SMEM, HBM, HBM],
        out_specs=[HBM, HBM, VMEM, HBM, HBM],
        scratch=[
            pltpu.VMEM((CAP, dim), bf16),
            pltpu.VMEM((CAP, half), bf16),
            pltpu.VMEM((CAP, half), f32),
            *w_held,
            loads,
            sem(2),
        ],
    )
    feats_other = sibling(feats)
    (student_rows,) = call(unit_body, [((CAP, bot), bf16)], (feats, feats_other))
    all_rows = lax.all_gather(student_rows, "dp", axis=0, tiled=True).reshape(dp, CAP, bot)
    got = everywhere(part, live.shape)
    part = run_balance(expo, got, live, tensor)
    got = everywhere(part, live.shape)
    keep, give, scale = run_last(at, expo, got, live, cols)
    pull = paired(keep, give)
    pull_got = exchange(pull, "dp")
    all_rows = after(all_rows, pull)
    raised, keep, give = run_student(at, student_t, cols, all_rows)
    push_got = exchange(paired(keep, give), "dp")
    both = slot_sums(push_got, slot_sums(pull_got))
    near, far, last = (levels(both, by) for by in (1, 2, 3))
    wide = lambda x: x.astype(f32)
    both = (wide(both) + wide(near)) + (wide(far) + wide(last))
    back_lines = per + share + EXTRA
    send, grad_rows, loss = call(
        backward_body,
        [((dp, back_lines, bot), bf16), ((CAP, dim), bf16), ((1, masks.shape[0]), f32)],
        (at, both, sibling(both), mine, member, feats, feats_other, rows, slope, hidden, w_in_half, w_out_half),
        in_specs=[SMEM] + [VMEM] * 6 + [HBM] * 5,
        out_specs=[HBM, HBM, VMEM],
        scratch=[
            pltpu.VMEM((half, bot), bf16),
            pltpu.VMEM((CAP, half), f32),
            pltpu.VMEM((dim, half), bf16),
            pltpu.VMEM((CAP, half), bf16),
            pltpu.VMEM((CAP, dim), bf16),
            pltpu.VMEM((dp, back_lines, bot), bf16),
            pltpu.VMEM((CAP, half), bf16),
            pltpu.VMEM((half, bot), bf16),
            pltpu.VMEM((CAP, dim), bf16),
            sems,
            sem(1),
            sem(5),
        ],
    )
    got = exchange(send, "dp")
    pieces = 4
    d_shape = (pieces, tokens.shape[0] // pieces, dim)
    (d_tokens,) = call(
        place_body,
        [(d_shape, bf16)],
        (sel, grad_rows, sibling(grad_rows)),
        out_specs=[HBM],
        scratch=[pltpu.VMEM(d_shape, bf16), dma((pieces,))],
    )
    got, d_tokens = lax.optimization_barrier((got, d_tokens))
    (sent,) = call(
        gather_grads_body,
        [((tensor, per + share, bot), bf16)],
        (got,),
        in_specs=[ANY],
        out_specs=[HBM],
        scratch=[pltpu.VMEM((dp, per + share, bot), bf16), pltpu.VMEM((per + share, bot), bf16), sems, sem(tensor)],
    )
    parts = exchange(sent, "tensor")
    grad_proto = run_columns_grad(expo, raised, scale, got, all_rows, proto_student, norm)
    grad_in, grad_out = call(
        weight_grads_body, [((per, hid), f32), ((w_out.shape[0], bot), f32)], (at, parts), in_specs=[SMEM, VMEM]
    )
    return (d_tokens.reshape(tokens.shape), grad_in, grad_out, grad_proto, loss.reshape(masks.shape[0]))


def solution(mesh):
    placed = (
        P("dp", None),
        P("dp", None),
        P("dp", None),
        P("dp", None),
        P("dp", None),
        P(None, ("dp", "tensor")),
        P(None, ("dp", "tensor")),
    )
    return jax.shard_map(
        parts_of,
        mesh=mesh,
        in_specs=placed,
        out_specs=(P("dp", None), P("dp", None), P("dp", None), P(None, ("dp", "tensor")), P("dp")),
        check_vma=False,
    )
```

```python
import jax
import jax.numpy as jnp
from jax import lax
from jax.experimental import pallas as pl
from jax.experimental.pallas import tpu as pltpu
from jax.sharding import PartitionSpec as P

CAP = 256
TEACHER_TEMP = 0.07
STUDENT_TEMP = 0.1
EPS = 1e-06
GRAD_SCALE = 65536.0
INTERPRET = False
f32, bf16 = (jnp.float32, jnp.bfloat16)
VMEM = pl.BlockSpec(memory_space=pltpu.VMEM)
HBM = pl.BlockSpec(memory_space=pltpu.HBM)
ANY = pl.BlockSpec(memory_space=pl.ANY)
SMEM = pl.BlockSpec(memory_space=pltpu.SMEM)
NT = (((1,), (1,)), ((), ()))
TN = (((0,), (0,)), ((), ()))
EXTRA = 16
HALF = CAP // 2
LINES = CAP + EXTRA


def mm(a, b, dims=None):
    if dims is None:
        return jnp.dot(a, b, preferred_element_type=f32)
    return lax.dot_general(a, b, dims, preferred_element_type=f32)


def call(body, outs, ins, out_specs=None, in_specs=None, scratch=()):
    specs = out_specs or [VMEM] * len(outs)
    in_specs = in_specs or [VMEM] * len(ins)
    ins = [pltpu.with_memory_space_constraint(x, pltpu.HBM) if spec is HBM else x for x, spec in zip(ins, in_specs)]
    outs = tuple(pltpu.HBM(*o) if spec is HBM else jax.ShapeDtypeStruct(*o) for o, spec in zip(outs, specs))
    return pl.pallas_call(
        body,
        out_shape=outs,
        in_specs=in_specs,
        out_specs=tuple(specs),
        scratch_shapes=list(scratch),
        interpret=INTERPRET,
        compiler_params=pltpu.CompilerParams(vmem_limit_bytes=48 << 20),
    )(*ins)


def iota(shape, dim):
    return lax.broadcasted_iota(jnp.int32, shape, dim)


def copies(pairs, sems):
    return [pltpu.make_async_copy(a, b, sems.at[i]) for i, (a, b) in enumerate(pairs)]


GROUP = 4
UNROLL = 4


def group(ref, q):
    return ref.at[pl.ds(q * GROUP, GROUP)]


def start_all(number, make):
    def go(i, _):
        make(i).start()
        return 0

    lax.fori_loop(0, number, go, 0)


def wait_all(number, make):
    def go(i, _):
        make(i).wait()
        return 0

    lax.fori_loop(0, number, go, 0)


def over_groups(peers, step, loads=(), stores=(), unroll=1):
    def go(q, _):
        for make in loads:
            make(q).wait()
        lax.fori_loop(0, GROUP, lambda i, _: step(q * GROUP + i), 0, unroll=unroll)
        for make in stores:
            make(q).start()
        return 0

    lax.fori_loop(0, peers // GROUP, go, 0)


def select_body(
    at_ref, mask_ref, feats_ref, sel_ref, send_hbm, member_hbm, mine_hbm, unit_ref, pack_ref, member_ref, mine_ref, sems, late_sems
):
    crops, patches = mask_ref.shape
    mask = mask_ref[...].astype(f32)
    upto = (iota((patches, patches), 0) <= iota((patches, patches), 1)).astype(f32).astype(bf16)
    rank = mm(mask.astype(bf16), upto)
    count = jnp.sum(mask, axis=1, keepdims=True)
    total = jnp.sum(count, axis=0, keepdims=True)
    slot = iota((CAP, patches), 0).astype(f32)
    lane = iota((1, CAP), 1).astype(f32)
    start = jnp.zeros((1, 1), f32)
    weight = jnp.zeros((1, CAP), f32)
    first = iota((CAP, patches), 1) == 0
    member_ref[...] = jnp.zeros_like(member_ref)
    for c in range(crops):
        hit = jnp.where((rank[c : c + 1] + start == slot + 1.0) & (mask[c : c + 1] > 0.0), 1.0, 0.0)
        if c == 0:
            hit = jnp.where(first & (slot >= total), 1.0, hit)
        sel_ref[:, c * patches : (c + 1) * patches] = hit.astype(bf16)
        own = count[c : c + 1]
        inside = jnp.where((lane >= start) & (lane < start + own), 1.0, 0.0)
        part = inside * (1.0 / jnp.maximum(own, 1.0))
        member_ref[c : c + 1, :] = part
        weight = weight + part
        start = start + own
    live = jnp.where(lane < total, 1.0, 0.0)
    picked = mm(sel_ref[...], feats_ref[...])
    scale = lax.rsqrt(jnp.sum(picked * picked, axis=1, keepdims=True) + EPS)
    unit_ref[...] = (picked * scale).astype(bf16)
    at = iota((EXTRA, CAP), 0)
    tail = jnp.where(at == 0, live, jnp.where(at == 1, weight * GRAD_SCALE, 0.0)).astype(bf16)
    mine_ref[...] = tail
    late = copies([(member_ref, member_hbm), (mine_ref, mine_hbm)], late_sems)
    for copy in late:
        copy.start()
    pack_ref[0:HALF, :] = unit_ref[pl.ds(pl.multiple_of(at_ref[0] * HALF, HALF), HALF), :]
    pack_ref[HALF : HALF + EXTRA, :] = tail
    peers = send_hbm.shape[0]
    make = lambda g: pltpu.make_async_copy(pack_ref, send_hbm.at[g], sems.at[g])
    start_all(peers, make)
    for copy in late:
        copy.wait()
    wait_all(peers, make)


def columns_body(
    student_ref, teacher_ref, cols_hbm, student_t_hbm, teacher_t_hbm, norm_hbm, cols_ref, student_t_ref, teacher_t_ref, norm_ref, sems
):
    for part in chunks_of(student_ref.shape[1]):
        wide = student_ref[:, part].astype(f32)
        norm = jnp.sqrt(jnp.sum(wide * wide, axis=0, keepdims=True) + EPS)
        norm_ref[:, part] = norm
        unit = wide / norm
        cols_ref[:, part] = unit.astype(bf16)
        student_t_ref[part, :] = unit.T.astype(bf16)
        wide = teacher_ref[:, part].astype(f32)
        norm = jnp.sqrt(jnp.sum(wide * wide, axis=0, keepdims=True) + EPS)
        teacher_t_ref[part, :] = (wide / norm).T.astype(bf16)
    held = (cols_ref, student_t_ref, teacher_t_ref, norm_ref)
    stores = copies(list(zip(held, (cols_hbm, student_t_hbm, teacher_t_hbm, norm_hbm))), sems)
    for store in stores:
        store.start()
    for store in stores:
        store.wait()


def weights_body(at_ref, w_in_hbm, w_out_hbm, pack_hbm, pack_ref, sems):
    rows, hid = w_in_hbm.shape
    half = hid // 2
    bot = w_out_hbm.shape[1]
    lines = w_out_hbm.shape[0] * bot // half
    column = pl.multiple_of(at_ref[0] * half, half)
    pairs = [(w_in_hbm.at[:, pl.ds(column, half)], pack_ref.at[0:rows, :])]
    for q in range(half // bot):
        source = w_out_hbm.at[q * lines : (q + 1) * lines, :]
        pairs.append((source, pack_ref.at[rows : rows + lines, q * bot : (q + 1) * bot]))
    loads = copies(pairs, sems)
    for load in loads:
        load.start()
    for load in loads:
        load.wait()
    store = pltpu.make_async_copy(pack_ref, pack_hbm, sems.at[0])
    store.start()
    store.wait()


def w_in_loads(w_hbm, w_in_ref, sems):
    peers = w_hbm.shape[0]
    rows = w_in_ref.shape[0] // peers
    return copies([(w_hbm.at[g, 0:rows, :], w_in_ref.at[g * rows : (g + 1) * rows, :]) for g in range(peers)], sems)


def w_out_loads(at_ref, w_hbm, w_out_ref, sems):
    peers = w_hbm.shape[0]
    bot = w_out_ref.shape[1]
    quarters = w_hbm.shape[2] // bot
    lines = w_out_ref.shape[0] // (peers // 2 * quarters)
    rows = w_hbm.shape[1] - lines
    pairs = []
    for i in range(peers // 2):
        for q in range(quarters):
            source = w_hbm.at[at_ref[0] * (peers // 2) + i, rows : rows + lines, q * bot : (q + 1) * bot]
            at = (i * quarters + q) * lines
            pairs.append((source, w_out_ref.at[at : at + lines, :]))
    return copies(pairs, sems)


def tokens_body(sel_ref, tokens_hbm, rows_hbm, tokens_ref, rows_ref, sems):
    load = pltpu.make_async_copy(tokens_hbm, tokens_ref, sems.at[0])
    load.start()
    load.wait()
    rows_ref[...] = mm(sel_ref[...], tokens_ref[...]).astype(bf16)
    store = pltpu.make_async_copy(rows_ref, rows_hbm, sems.at[1])
    store.start()
    store.wait()


def forward_body(
    at_ref, rows_hbm, w_hbm, hidden_hbm, slope_hbm, feats_ref, w_out_hbm,
    rows_ref, hidden_ref, slope_ref, w_in_ref, w_out_ref, sems, out_sems, own_sems,
):
    first = pltpu.make_async_copy(rows_hbm, rows_ref, own_sems.at[0])
    first.start()
    loads = w_in_loads(w_hbm, w_in_ref, sems) + w_out_loads(at_ref, w_hbm, w_out_ref, out_sems)
    for load in loads:
        load.start()
    first.wait()
    for load in loads:
        load.wait()
    keeps = copies([(w_out_ref, w_out_hbm)], sems)
    for keep in keeps:
        keep.start()
    rows = rows_ref[...]
    feats = jnp.zeros(feats_ref.shape, f32)
    for part in chunks_of(hidden_ref.shape[1]):
        pre = mm(rows, w_in_ref[:, part])
        cdf = 0.5 * (1.0 + lax.erf(pre * 0.7071067811865476))
        slope_ref[:, part] = cdf + pre * (jnp.exp(-0.5 * pre * pre) * 0.3989422804014327)
        hidden = (pre * cdf).astype(bf16)
        hidden_ref[:, part] = hidden
        feats = feats + mm(hidden, w_out_ref[part, :])
    feats_ref[...] = feats
    stores = copies([(hidden_ref, hidden_hbm), (slope_ref, slope_hbm)], own_sems)
    for store in stores:
        store.start()
    for store in keeps + stores:
        store.wait()


def unit_of(feats_ref, other_ref):
    feats = feats_ref[...] + other_ref[...]
    inv = lax.rsqrt(jnp.sum(feats * feats, axis=1, keepdims=True) + EPS)
    return (feats * inv, inv)


def unit_body(feats_ref, other_ref, rows_ref):
    rows_ref[...] = unit_of(feats_ref, other_ref)[0].astype(bf16)


def chunks_of(width):
    step = min(256, width)
    return [slice(at, at + step) for at in range(0, width, step)]


def row_of(ref, g):
    return ref[pl.ds(g, 1), :]


def fold(x):
    return x.reshape(x.shape[0] // 8, 8, x.shape[1]).sum(axis=0)


def expo_body(
    at_ref, cols_hbm, own_hbm, other_hbm, expo_hbm, part_ref, live_ref,
    cols_ref, rows_ref, tail_ref, expo_ref, total_ref, sums_ref, sems, own_sems, other_sems, tail_sems,
):
    peers = own_hbm.shape[0]
    width = cols_ref.shape[0]
    core = at_ref[0]
    number = peers // GROUP
    rows_of = lambda ref, q: ref.at[pl.ds(q * GROUP, GROUP), 0:HALF, :]
    rows_at = lambda q, c: rows_ref.at[pl.ds(q * GROUP, GROUP), c]
    load_own = lambda q: pltpu.make_async_copy(rows_of(own_hbm, q), rows_at(q, core), own_sems.at[q])
    load_other = lambda q: pltpu.make_async_copy(rows_of(other_hbm, q), rows_at(q, 1 - core), other_sems.at[q])
    load_tail = pltpu.make_async_copy(own_hbm.at[:, HALF : HALF + EXTRA, :], tail_ref, tail_sems.at[0])
    store = lambda q: pltpu.make_async_copy(group(expo_ref, q), group(expo_hbm, q), sems.at[q])
    load_cols = pltpu.make_async_copy(cols_hbm, cols_ref, tail_sems.at[1])
    load_cols.start()
    load_tail.start()
    start_all(number, load_own)
    start_all(number, load_other)
    total_ref[...] = jnp.zeros_like(total_ref)
    load_tail.wait()
    load_cols.wait()

    def first(g):
        rows = rows_ref[g].reshape(CAP, rows_ref.shape[3])
        tail = tail_ref[g].astype(f32)
        live = tail[0:1]
        live_ref[pl.ds(g, 1), :] = live
        for part in chunks_of(width):
            cos = mm(cols_ref[part, :], rows, NT)
            expo = jnp.exp(cos * (1.0 / TEACHER_TEMP)) * live
            expo_ref[g, part, :] = expo.astype(bf16)
            total_ref[part, :] += expo[:, 0:128] + expo[:, 128:256]
        return 0

    over_groups(peers, first, (load_own, load_other), (store,), UNROLL)
    spread_scale(total_ref)
    row_parts(expo_ref, total_ref, sums_ref, part_ref)
    wait_all(number, store)


def spread_scale(total_ref):
    for part in chunks_of(total_ref.shape[0]):
        sums = jnp.sum(total_ref[part, :], axis=1, keepdims=True)
        total_ref[part, :] = jnp.broadcast_to(1.0 / sums, sums.shape[:1] + (128,))


def scaled(expo, scale):
    return jnp.concatenate([expo[:, 0:128] * scale, expo[:, 128:256] * scale], axis=1)


def row_parts(expo_ref, scale_ref, sums_ref, part_ref):
    def step(g):
        acc = jnp.zeros((8, CAP), f32)
        for part in chunks_of(scale_ref.shape[0]):
            acc = acc + fold(scaled(expo_ref[g, part, :].astype(f32), scale_ref[part, :]))
        sums_ref[pl.ds(g, 1), :] = jnp.sum(acc, axis=0, keepdims=True)
        return 0

    over_groups(expo_ref.shape[0], step, unroll=UNROLL)
    sums = sums_ref[...].astype(bf16)
    for t in range(part_ref.shape[0]):
        part_ref[t] = sums


def relay_body(parts_ref, out_ref):
    sums = parts_ref[0].astype(f32)
    for t in range(1, parts_ref.shape[0]):
        sums = sums + parts_ref[t].astype(f32)
    sums = sums.astype(bf16)
    for g in range(out_ref.shape[0]):
        out_ref[g] = sums


def scales_from(parts_ref, live_ref, scale_ref):
    sums = parts_ref[0].astype(f32)
    for g in range(1, parts_ref.shape[0]):
        sums = sums + parts_ref[g].astype(f32)
    live = live_ref[...]
    scale_ref[...] = live / (sums + 1.0 - live)


def column_sums(load, expo_ref, scale_ref, total_ref):
    total_ref[...] = jnp.zeros_like(total_ref)

    def step(g):
        row = row_of(scale_ref, g)
        for part in chunks_of(total_ref.shape[0]):
            expo = expo_ref[g, part, :].astype(f32)
            total_ref[part, :] += expo[:, 0:128] * row[:, 0:128] + expo[:, 128:256] * row[:, 128:256]
        return 0

    over_groups(expo_ref.shape[0], step, (load,), unroll=UNROLL)
    spread_scale(total_ref)


def balance_body(expo_hbm, parts_ref, live_ref, part_ref, expo_ref, total_ref, sums_ref, scale_ref, sems):
    load = lambda q: pltpu.make_async_copy(group(expo_hbm, q), group(expo_ref, q), sems.at[q])
    start_all(expo_ref.shape[0] // GROUP, load)
    scales_from(parts_ref, live_ref, scale_ref)
    column_sums(load, expo_ref, scale_ref, total_ref)
    row_parts(expo_ref, total_ref, sums_ref, part_ref)


def divide_up(g, acc, pull, halves_ref):
    rows = jnp.sum(acc, axis=0, keepdims=True)
    rows = jnp.where(iota((EXTRA, CAP), 0) == 0, rows, 0.0).astype(bf16)
    pull = pull.astype(bf16)
    for at, block in ((slice(0, CAP), pull), (slice(CAP, LINES), rows)):
        halves_ref[0, g, at, :] = block[:, 0:HALF]
        halves_ref[1, g, at, :] = block[:, HALF:CAP]


def last_body(
    at_ref, expo_hbm, parts_ref, live_ref, cols_ref, keep_hbm, give_hbm, total_hbm,
    expo_ref, total_ref, scale_ref, halves_ref, sems, keep_sems, give_sems,
):
    peers = expo_ref.shape[0]
    core = at_ref[0]
    load = lambda q: pltpu.make_async_copy(group(expo_hbm, q), group(expo_ref, q), sems.at[q])
    half_at = lambda c, q: halves_ref.at[c, pl.ds(q * GROUP, GROUP)]
    keep = lambda q: pltpu.make_async_copy(half_at(core, q), group(keep_hbm, q), keep_sems.at[q])
    give = lambda q: pltpu.make_async_copy(half_at(1 - core, q), group(give_hbm, q), give_sems.at[q])
    number = peers // GROUP
    start_all(number, load)
    scales_from(parts_ref, live_ref, scale_ref)
    column_sums(load, expo_ref, scale_ref, total_ref)

    def step(g):
        acc = jnp.zeros((8, CAP), f32)
        pull = jnp.zeros((cols_ref.shape[0], CAP), f32)
        for part in chunks_of(total_ref.shape[0]):
            balanced = scaled(expo_ref[g, part, :].astype(f32), total_ref[part, :])
            acc = acc + fold(balanced)
            pull = pull + mm(cols_ref[:, part], balanced.astype(bf16))
        divide_up(g, acc, pull, halves_ref)
        return 0

    spare = pltpu.make_async_copy(total_ref, total_hbm, sems.at[0])
    spare.start()
    over_groups(peers, step, (), (give, keep), UNROLL)
    wait_all(number, give)
    wait_all(number, keep)
    spare.wait()


def student_body(
    at_ref, cols_t_ref, cols_ref, rows_hbm, raised_hbm, keep_hbm, give_hbm,
    rows_ref, raised_ref, halves_ref, row_sems, sems, keep_sems, give_sems,
):
    peers = rows_ref.shape[0]
    load = lambda q: pltpu.make_async_copy(group(rows_hbm, q), group(rows_ref, q), row_sems.at[q])
    start_all(peers // GROUP, load)
    core = at_ref[0]
    width = cols_t_ref.shape[0]
    store = lambda q: pltpu.make_async_copy(group(raised_ref, q), group(raised_hbm, q), sems.at[q])
    half_at = lambda c, q: halves_ref.at[c, pl.ds(q * GROUP, GROUP)]
    keep = lambda q: pltpu.make_async_copy(half_at(core, q), group(keep_hbm, q), keep_sems.at[q])
    give = lambda q: pltpu.make_async_copy(half_at(1 - core, q), group(give_hbm, q), give_sems.at[q])
    number = peers // GROUP

    def step(g):
        rows = rows_ref[g]
        acc = jnp.zeros((8, CAP), f32)
        pull = jnp.zeros((cols_ref.shape[0], CAP), f32)
        for part in chunks_of(width):
            raised = jnp.exp(mm(cols_t_ref[part, :], rows, NT) * (1.0 / STUDENT_TEMP))
            acc = acc + fold(raised)
            raised = raised.astype(bf16)
            raised_ref[g, part, :] = raised
            pull = pull + mm(cols_ref[:, part], raised)
        divide_up(g, acc, pull, halves_ref)
        return 0

    over_groups(peers, step, (load,), (store, give, keep), UNROLL)
    for make in (give, keep, store):
        wait_all(number, make)


def columns_grad_body(
    expo_hbm, raised_hbm, scale_hbm, got_hbm, rows_hbm, proto_hbm, norm_hbm,
    grad_ref, scale_ref, proto_ref, norm_ref, expo_ref, raised_ref, acc_ref, tail_ref, rows_ref, esems, rsems, tail_sems, row_sems, late_sems,
):
    peers = expo_ref.shape[0]
    load = lambda q: pltpu.make_async_copy(group(expo_hbm, q), group(expo_ref, q), esems.at[q])
    load_raised = lambda q: pltpu.make_async_copy(group(raised_hbm, q), group(raised_ref, q), rsems.at[q])
    load_rows = lambda q: pltpu.make_async_copy(group(rows_hbm, q), group(rows_ref, q), row_sems.at[q])
    lines = got_hbm.shape[1] - EXTRA
    load_tail = pltpu.make_async_copy(got_hbm.at[:, lines : lines + EXTRA, :], tail_ref, tail_sems.at[0])
    load_scale = pltpu.make_async_copy(scale_hbm, scale_ref, tail_sems.at[1])
    late = copies([(proto_hbm, proto_ref), (norm_hbm, norm_ref)], late_sems)
    load_tail.start()
    load_scale.start()

    def begin(q, _):
        for make in (load_rows, load, load_raised):
            make(q).start()
        return 0

    lax.fori_loop(0, peers // GROUP, begin, 0)
    for copy in late:
        copy.start()
    acc_ref[...] = jnp.zeros_like(acc_ref)
    load_tail.wait()
    load_scale.wait()

    def step(g):
        tail = tail_ref[g].astype(f32)
        alpha = tail[0:1] + tail[1:2]
        beta = tail[2:3] + tail[3:4]
        rows = rows_ref[g]
        for part in chunks_of(acc_ref.shape[0]):
            balanced = scaled(expo_ref[g, part, :].astype(f32), scale_ref[part, :])
            score = raised_ref[g, part, :].astype(f32) * alpha - balanced * beta
            acc_ref[part, :] += mm(score.astype(bf16), rows)
        return 0

    over_groups(peers, step, (load_rows, load, load_raised), (), UNROLL)
    for copy in late:
        copy.wait()
    for part in chunks_of(acc_ref.shape[0]):
        grad = acc_ref[part, :].T
        norm = norm_ref[:, part]
        unit = proto_ref[:, part].astype(f32) / norm
        grad_ref[:, part] = (grad - unit * jnp.sum(unit * grad, axis=0, keepdims=True)) / norm


def join(core, own_ref, other_ref):
    own, other = (own_ref[0], other_ref[0])
    low = core == 0
    return jnp.concatenate([jnp.where(low, own, other), jnp.where(low, other, own)], axis=1)


def two_parts(x):
    high = x.astype(bf16)
    return (high.astype(f32), x - high.astype(f32))


def backward_body(
    at_ref, pull_ref, pull_other_ref, push_ref, push_other_ref, mine_ref, member_ref, feats_ref, feats_other_ref,
    rows_hbm, slope_hbm, hidden_hbm, w_out_hbm,
    send_hbm, pre_hbm, loss_ref, w_out_ref, slope_ref, hidden_ref, rows_ref, send_ref, pre_ref, out_ref, send_sems, pre_sem, load_sems,
):
    peers = send_ref.shape[0]
    sources = (w_out_hbm, slope_hbm, rows_hbm, hidden_hbm)
    loads = copies(list(zip(sources, (w_out_ref, slope_ref, rows_ref, hidden_ref))), load_sems)
    for load in loads:
        load.start()
    tail = mine_ref[...].astype(f32)
    live, weight = (tail[0:1], tail[1:2] * (1.0 / STUDENT_TEMP))
    pull = join(at_ref[0], pull_ref, pull_other_ref)
    push = join(at_ref[0], push_ref, push_other_ref)
    norm_sum = push[CAP : CAP + 1]
    push = push[0:CAP]
    scale = live / (pull[CAP : CAP + 1] + 1.0 - live)
    pull = pull[0:CAP]
    unit, inv = unit_of(feats_ref, feats_other_ref)
    inv = jnp.broadcast_to(inv, unit.shape).T[0:1]
    unit = unit.T
    cross = jnp.sum(unit.astype(bf16).astype(f32) * pull, axis=0, keepdims=True) * (1.0 / STUDENT_TEMP)
    row_loss = jnp.log(norm_sum) - scale * cross
    loss = jnp.sum(member_ref[...] * row_loss, axis=1, keepdims=True)
    square = (member_ref.shape[0], 128)
    loss = jnp.where(iota(square, 0) == iota(square, 1), loss, 0.0)
    loss_ref[...] = jnp.sum(loss, axis=0, keepdims=True)[:, 0 : loss_ref.shape[1]]
    alpha = weight / norm_sum
    beta = weight * scale
    grad_unit = push * alpha - pull * beta
    inner = jnp.sum(unit * grad_unit, axis=0, keepdims=True)
    grad_feats = (inv * (grad_unit - unit * inner)).T.astype(bf16)
    width = send_ref.shape[2]
    loads[0].wait()
    loads[1].wait()
    for part in chunks_of(hidden_ref.shape[1]):
        pre_ref[:, part] = (mm(grad_feats, w_out_ref[part, :], NT) * slope_ref[:, part]).astype(bf16)
    pre_out = pltpu.make_async_copy(pre_ref, pre_hbm, pre_sem.at[0])
    pre_out.start()
    loads[2].wait()
    loads[3].wait()
    for part in chunks_of(hidden_ref.shape[1]):
        out_ref[part, :] = mm(hidden_ref[:, part], grad_feats, TN).astype(bf16)
    core, level = (at_ref[0], at_ref[1])
    own = pre_ref[:, pl.ds(pl.multiple_of(level * width, width), width)]
    grad_in = mm(rows_ref[...], own, TN).astype(bf16)
    per = grad_in.shape[0] // peers
    block = out_ref.shape[0] // (peers // 2)
    share = block // 4
    at = iota((EXTRA, CAP), 0)
    rows = jnp.zeros((EXTRA, CAP), f32)
    for i, x in enumerate(two_parts(alpha) + two_parts(beta)):
        rows = jnp.where(at == i, x, rows)
    rows = rows.astype(bf16)
    store = lambda g: pltpu.make_async_copy(send_ref.at[g], send_hbm.at[g], send_sems.at[g])
    for g in range(peers):
        send_ref[g, 0:per, :] = grad_in[g * per : (g + 1) * per, :]
        start = pl.multiple_of((g % (peers // 2)) * block + level * share, share)
        out = out_ref[pl.ds(start, share), :]
        send_ref[g, per : per + share, :] = jnp.where(core == g // (peers // 2), out, jnp.zeros_like(out))
        send_ref[g, per + share : per + share + EXTRA, :] = rows
        store(g).start()
    pre_out.wait()
    wait_all(peers, store)


def backward_rows_body(pre_ref, w_hbm, out_hbm, w_in_ref, out_ref, sems, out_sem):
    loads = w_in_loads(w_hbm, w_in_ref, sems)
    for load in loads:
        load.start()
    for load in loads:
        load.wait()
    out_ref[...] = mm(pre_ref[...], w_in_ref[...], NT).astype(bf16)
    store = pltpu.make_async_copy(out_ref, out_hbm, out_sem.at[0])
    store.start()
    store.wait()


def place_body(sel_ref, rows_ref, other_ref, out_hbm, out_ref, sems):
    rows = (rows_ref[...].astype(f32) + other_ref[...].astype(f32)).astype(bf16)
    pieces = out_ref.shape[0]
    size = out_ref.shape[1]
    store = lambda i: pltpu.make_async_copy(out_ref.at[i], out_hbm.at[i], sems.at[i])
    for i in range(pieces):
        out_ref[i] = mm(sel_ref[:, i * size : (i + 1) * size], rows, TN).astype(bf16)
        store(i).start()
    wait_all(pieces, store)


def gather_grads_body(got_hbm, send_hbm, got_ref, sum_ref, load_sems, sems):
    peers = got_hbm.shape[0]
    lines = sum_ref.shape[0]
    source = lambda q: got_hbm.at[pl.ds(q * GROUP, GROUP), 0:lines, :]
    load = lambda q: pltpu.make_async_copy(source(q), group(got_ref, q), load_sems.at[q])
    start_all(peers // GROUP, load)
    acc = jnp.zeros(got_ref.shape[1:], f32)
    for g in range(peers):
        if g % GROUP == 0:
            load(g // GROUP).wait()
        acc = acc + got_ref[g].astype(f32)
    sum_ref[...] = acc.astype(bf16)
    store = lambda t: pltpu.make_async_copy(sum_ref, send_hbm.at[t], sems.at[t])
    start_all(send_hbm.shape[0], store)
    wait_all(send_hbm.shape[0], store)


def weight_grads_body(at_ref, parts_ref, grad_in_ref, grad_out_ref):
    peers, lines, width = parts_ref.shape
    per = grad_in_ref.shape[0]
    share = lines - per
    for t in range(peers):
        to = ((t % 2) * (peers // 2) + t // 2) * width
        grad_in_ref[:, to : to + width] = parts_ref[t, 0:per, :].astype(f32)
    for z in range(peers // 2):
        grad_out_ref[z * share : (z + 1) * share, :] = parts_ref[2 * z + at_ref[2], per:lines, :].astype(f32)


def sem(number):
    return pltpu.SemaphoreType.DMA((number,))


def run_expo(at, cols_t, own, other, tensor):
    dp, (width, bot) = (own.shape[0], cols_t.shape)
    big, small = ((dp, width, CAP), (dp, CAP))
    return call(
        expo_body,
        [(big, bf16), ((tensor, *small), bf16), (small, f32)],
        (at, cols_t, own, other),
        in_specs=[SMEM, HBM, ANY, ANY],
        out_specs=[HBM, VMEM, VMEM],
        scratch=[
            pltpu.VMEM((width, bot), bf16),
            pltpu.VMEM((dp, 2, HALF, bot), bf16),
            pltpu.VMEM((dp, EXTRA, bot), bf16),
            pltpu.VMEM(big, bf16),
            pltpu.VMEM((width, 128), f32),
            pltpu.VMEM(small, f32),
            *[sem(dp // GROUP)] * 4,
        ],
    )


def run_balance(expo, got, live, tensor):
    dp, width, _ = expo.shape
    small = pltpu.VMEM(live.shape, f32)
    return call(
        balance_body,
        [((tensor, *live.shape), bf16)],
        (expo, got, live),
        in_specs=[HBM, VMEM, VMEM],
        scratch=[pltpu.VMEM(expo.shape, bf16), pltpu.VMEM((width, 128), f32), small, small, sem(dp // GROUP)],
    )[0]


def run_last(at, expo, got, live, cols):
    dp, width, _ = expo.shape
    halves = (dp, LINES, HALF)
    return call(
        last_body,
        [(halves, bf16), (halves, bf16), ((width, 128), f32)],
        (at, expo, got, live, cols),
        in_specs=[SMEM, HBM, VMEM, VMEM, VMEM],
        out_specs=[ANY, ANY, HBM],
        scratch=[
            pltpu.VMEM(expo.shape, bf16),
            pltpu.VMEM((width, 128), f32),
            pltpu.VMEM(live.shape, f32),
            pltpu.VMEM((2, *halves), bf16),
            *[sem(dp // GROUP)] * 3,
        ],
    )


def run_student(at, cols_t, cols, rows):
    dp = rows.shape[0]
    big, halves = ((dp, cols.shape[1], CAP), (dp, LINES, HALF))
    return call(
        student_body,
        [(big, bf16), (halves, bf16), (halves, bf16)],
        (at, cols_t, cols, rows),
        in_specs=[SMEM, VMEM, VMEM, HBM],
        out_specs=[HBM, ANY, ANY],
        scratch=[
            pltpu.VMEM(rows.shape, bf16),
            pltpu.VMEM(big, bf16),
            pltpu.VMEM((2, *halves), bf16),
            *[sem(dp // GROUP)] * 4,
        ],
    )


def run_columns_grad(expo, raised, scale, got, rows, proto, norm):
    dp, held = (expo.shape[0], pltpu.VMEM(expo.shape, bf16))
    return call(
        columns_grad_body,
        [(proto.shape, f32)],
        (expo, raised, scale, got, rows, proto, norm),
        in_specs=[HBM] * 3 + [ANY] + [HBM] * 3,
        scratch=[
            pltpu.VMEM(scale.shape, f32),
            pltpu.VMEM(proto.shape, bf16),
            pltpu.VMEM(norm.shape, f32),
            held,
            held,
            pltpu.VMEM(proto.shape[::-1], f32),
            pltpu.VMEM((dp, EXTRA, CAP), bf16),
            pltpu.VMEM(rows.shape, bf16),
            *[sem(dp // GROUP)] * 4,
            sem(2),
        ],
    )[0]


def exchange(x, axis):
    return lax.all_to_all(x, axis, split_axis=0, concat_axis=0, tiled=True)


def sibling(x):
    peers = lax.axis_size("tensor")
    return lax.ppermute(x, "tensor", [(i, i ^ 1) for i in range(peers)])


def everywhere(part, small):
    got = exchange(part, "tensor")
    (sums,) = call(relay_body, [((small[0], *small), bf16)], (got,))
    return exchange(sums, "dp")


def levels(x, by):
    peers = lax.axis_size("tensor")
    return lax.ppermute(x, "tensor", [(i, i ^ (2 * by)) for i in range(peers)])


def level_sums(x):
    near, far, last = (levels(x, by) for by in (1, 2, 3))
    wide = lambda y: y.astype(f32)
    return (wide(x) + wide(near)) + (wide(far) + wide(last))


def paired(keep, give):
    return (keep.astype(f32) + sibling(give).astype(f32)).astype(bf16)


def slot_sums_body(parts_hbm, out_hbm, parts_ref, out_ref, sems, out_sem):
    peers = parts_hbm.shape[0]
    load = lambda q: pltpu.make_async_copy(group(parts_hbm, q), group(parts_ref, q), sems.at[q])
    start_all(peers // GROUP, load)
    acc = jnp.zeros(parts_ref.shape[1:], f32)
    for g in range(peers):
        if g % GROUP == 0:
            load(g // GROUP).wait()
        acc = acc + parts_ref[g].astype(f32)
    out_ref[0] = acc.astype(bf16)
    store = pltpu.make_async_copy(out_ref, out_hbm, out_sem.at[0])
    store.start()
    store.wait()


def slot_sums(parts):
    out = (1, *parts.shape[1:])
    return call(
        slot_sums_body,
        [(out, bf16)],
        (parts,),
        in_specs=[ANY],
        out_specs=[HBM],
        scratch=[pltpu.VMEM(parts.shape, bf16), pltpu.VMEM(out, bf16), sem(parts.shape[0] // GROUP), sem(1)],
    )[0]


def after(x, earlier):
    return lax.optimization_barrier((x, earlier))[0]


def parts_of(tokens, teacher_feats, masks, w_in, w_out, proto_student, proto_teacher):
    dim = tokens.shape[1]
    hid = w_in.shape[1]
    bot, width = proto_student.shape
    dp, tensor = (lax.axis_size("dp"), lax.axis_size("tensor"))
    per = w_in.shape[0]
    half = hid // 2
    share = w_out.shape[0] // 4
    t = lax.axis_index("tensor").astype(jnp.int32)
    g = lax.axis_index("dp").astype(jnp.int32)
    at = jnp.stack([t % 2, t // 2, g // (dp // 2)])

    lines = per + w_out.shape[0] * bot // half
    (w_pack,) = call(weights_body, [((lines, half), bf16)], (at, w_in, w_out), in_specs=[SMEM, HBM, HBM], out_specs=[HBM], scratch=[pltpu.VMEM((lines, half), bf16), sem(1 + half // bot)])
    w_all = lax.all_gather(w_pack, "dp", axis=0, tiled=True).reshape(dp, lines, half)
    dma = pltpu.SemaphoreType.DMA
    sems = dma((dp,))
    sel, send, member, mine = call(
        select_body,
        [((CAP, tokens.shape[0]), bf16), ((dp, HALF + EXTRA, bot), bf16), ((8, CAP), f32), ((EXTRA, CAP), bf16)],
        (at, masks, teacher_feats),
        in_specs=[SMEM, VMEM, VMEM],
        out_specs=[VMEM, HBM, HBM, HBM],
        scratch=[
            pltpu.VMEM((CAP, bot), bf16),
            pltpu.VMEM((HALF + EXTRA, bot), bf16),
            pltpu.VMEM((8, CAP), f32),
            pltpu.VMEM((EXTRA, CAP), bf16),
            sems,
            sem(2),
        ],
    )
    packs = exchange(send, "dp")
    others = sibling(packs)
    cols, student_t, teacher_t, norm = call(
        columns_body,
        [((bot, width), bf16), ((width, bot), bf16), ((width, bot), bf16), ((1, width), f32)],
        (proto_student, proto_teacher),
        out_specs=[HBM] * 4,
        scratch=[
            pltpu.VMEM((bot, width), bf16),
            pltpu.VMEM((width, bot), bf16),
            pltpu.VMEM((width, bot), bf16),
            pltpu.VMEM((1, width), f32),
            sem(4),
        ],
    )
    expo, part, live = run_expo(at, teacher_t, packs, others, tensor)
    w_held = [pltpu.VMEM((dim, half), bf16), pltpu.VMEM((half, bot), bf16)]
    (rows,) = call(
        tokens_body,
        [((CAP, dim), bf16)],
        (sel, tokens),
        in_specs=[VMEM, HBM],
        out_specs=[HBM],
        scratch=[pltpu.VMEM(tokens.shape, bf16), pltpu.VMEM((CAP, dim), bf16), sem(2)],
    )
    hidden, slope, feats, w_out_half = call(
        forward_body,
        [((CAP, half), bf16), ((CAP, half), f32), ((CAP, bot), f32), ((half, bot), bf16)],
        (at, rows, after(w_all, part)),
        in_specs=[SMEM, HBM, HBM],
        out_specs=[HBM, HBM, VMEM, HBM],
        scratch=[
            pltpu.VMEM((CAP, dim), bf16),
            pltpu.VMEM((CAP, half), bf16),
            pltpu.VMEM((CAP, half), f32),
            *w_held,
            sems,
            sem(2 * dp),
            sem(2),
        ],
    )
    feats_other = sibling(feats)
    (student_rows,) = call(unit_body, [((CAP, bot), bf16)], (feats, feats_other))
    all_rows = lax.all_gather(student_rows, "dp", axis=0, tiled=True).reshape(dp, CAP, bot)
    got = everywhere(part, live.shape)
    part = run_balance(expo, got, live, tensor)
    got = everywhere(part, live.shape)
    keep, give, scale = run_last(at, expo, got, live, cols)
    pull = paired(keep, give)
    pull_got = exchange(pull, "dp")
    all_rows = after(all_rows, pull)
    raised, keep, give = run_student(at, student_t, cols, all_rows)
    push_got = exchange(paired(keep, give), "dp")
    pull = level_sums(slot_sums(pull_got))
    pull_other = sibling(pull)
    push = level_sums(slot_sums(push_got))
    push_other = sibling(push)
    back_lines = per + share + EXTRA
    send, grad_pre, loss = call(
        backward_body,
        [((dp, back_lines, bot), bf16), ((CAP, half), bf16), ((1, masks.shape[0]), f32)],
        (at, pull, pull_other, push, push_other, mine, member, feats, feats_other, rows, slope, hidden, w_out_half),
        in_specs=[SMEM] + [VMEM] * 8 + [HBM] * 4,
        out_specs=[HBM, HBM, VMEM],
        scratch=[
            pltpu.VMEM((half, bot), bf16),
            pltpu.VMEM((CAP, half), f32),
            pltpu.VMEM((CAP, half), bf16),
            pltpu.VMEM((CAP, dim), bf16),
            pltpu.VMEM((dp, back_lines, bot), bf16),
            pltpu.VMEM((CAP, half), bf16),
            pltpu.VMEM((half, bot), bf16),
            sems,
            sem(1),
            sem(4),
        ],
    )
    got = exchange(send, "dp")
    (grad_rows,) = call(
        backward_rows_body,
        [((CAP, dim), bf16)],
        (grad_pre, w_all),
        in_specs=[VMEM, HBM],
        out_specs=[HBM],
        scratch=[pltpu.VMEM((dim, half), bf16), pltpu.VMEM((CAP, dim), bf16), sems, sem(1)],
    )
    pieces = 4
    d_shape = (pieces, tokens.shape[0] // pieces, dim)
    (d_tokens,) = call(
        place_body,
        [(d_shape, bf16)],
        (sel, grad_rows, sibling(grad_rows)),
        out_specs=[HBM],
        scratch=[pltpu.VMEM(d_shape, bf16), dma((pieces,))],
    )
    got, d_tokens = lax.optimization_barrier((got, d_tokens))
    (sent,) = call(
        gather_grads_body,
        [((tensor, per + share, bot), bf16)],
        (got,),
        in_specs=[ANY],
        out_specs=[HBM],
        scratch=[pltpu.VMEM((dp, per + share, bot), bf16), pltpu.VMEM((per + share, bot), bf16), sems, sem(tensor)],
    )
    parts = exchange(sent, "tensor")
    grad_proto = run_columns_grad(expo, raised, scale, got, all_rows, proto_student, norm)
    grad_in, grad_out = call(
        weight_grads_body, [((per, hid), f32), ((w_out.shape[0], bot), f32)], (at, parts), in_specs=[SMEM, VMEM]
    )
    return (d_tokens.reshape(tokens.shape), grad_in, grad_out, grad_proto, loss.reshape(masks.shape[0]))


def solution(mesh):
    placed = (
        P("dp", None),
        P("dp", None),
        P("dp", None),
        P("dp", None),
        P("dp", None),
        P(None, ("dp", "tensor")),
        P(None, ("dp", "tensor")),
    )
    return jax.shard_map(
        parts_of,
        mesh=mesh,
        in_specs=placed,
        out_specs=(P("dp", None), P("dp", None), P("dp", None), P(None, ("dp", "tensor")), P("dp")),
        check_vma=False,
    )
```

```python
import jax
import jax.numpy as jnp
from jax import lax
from jax.experimental import pallas as pl
from jax.experimental.pallas import tpu as pltpu
from jax.sharding import PartitionSpec as P

CAP = 256
TEACHER_TEMP = 0.07
STUDENT_TEMP = 0.1
EPS = 1e-06
GRAD_SCALE = 65536.0
INTERPRET = False
f32, bf16 = (jnp.float32, jnp.bfloat16)
VMEM = pl.BlockSpec(memory_space=pltpu.VMEM)
HBM = pl.BlockSpec(memory_space=pltpu.HBM)
ANY = pl.BlockSpec(memory_space=pl.ANY)
SMEM = pl.BlockSpec(memory_space=pltpu.SMEM)
NT = (((1,), (1,)), ((), ()))
TN = (((0,), (0,)), ((), ()))
EXTRA = 16
HALF = CAP // 2
LINES = CAP + EXTRA


def mm(a, b, dims=None):
    if dims is None:
        return jnp.dot(a, b, preferred_element_type=f32)
    return lax.dot_general(a, b, dims, preferred_element_type=f32)


def call(body, outs, ins, out_specs=None, in_specs=None, scratch=()):
    specs = out_specs or [VMEM] * len(outs)
    in_specs = in_specs or [VMEM] * len(ins)
    ins = [pltpu.with_memory_space_constraint(x, pltpu.HBM) if spec is HBM else x for x, spec in zip(ins, in_specs)]
    outs = tuple(pltpu.HBM(*o) if spec is HBM else jax.ShapeDtypeStruct(*o) for o, spec in zip(outs, specs))
    return pl.pallas_call(
        body,
        out_shape=outs,
        in_specs=in_specs,
        out_specs=tuple(specs),
        scratch_shapes=list(scratch),
        interpret=INTERPRET,
        compiler_params=pltpu.CompilerParams(vmem_limit_bytes=48 << 20),
    )(*ins)


def iota(shape, dim):
    return lax.broadcasted_iota(jnp.int32, shape, dim)


def copies(pairs, sems):
    return [pltpu.make_async_copy(a, b, sems.at[i]) for i, (a, b) in enumerate(pairs)]


GROUP = 4
UNROLL = 4


def group(ref, q):
    return ref.at[pl.ds(q * GROUP, GROUP)]


def start_all(number, make):
    def go(i, _):
        make(i).start()
        return 0

    lax.fori_loop(0, number, go, 0)


def wait_all(number, make):
    def go(i, _):
        make(i).wait()
        return 0

    lax.fori_loop(0, number, go, 0)


def over_groups(peers, step, loads=(), stores=(), unroll=1):
    def go(q, _):
        for make in loads:
            make(q).wait()
        lax.fori_loop(0, GROUP, lambda i, _: step(q * GROUP + i), 0, unroll=unroll)
        for make in stores:
            make(q).start()
        return 0

    lax.fori_loop(0, peers // GROUP, go, 0)


def select_body(
    at_ref, mask_ref, feats_ref, sel_ref, send_hbm, member_hbm, mine_hbm, unit_ref, pack_ref, member_ref, mine_ref, sems, late_sems
):
    crops, patches = mask_ref.shape
    mask = mask_ref[...].astype(f32)
    upto = (iota((patches, patches), 0) <= iota((patches, patches), 1)).astype(f32).astype(bf16)
    rank = mm(mask.astype(bf16), upto)
    count = jnp.sum(mask, axis=1, keepdims=True)
    total = jnp.sum(count, axis=0, keepdims=True)
    slot = iota((CAP, patches), 0).astype(f32)
    lane = iota((1, CAP), 1).astype(f32)
    start = jnp.zeros((1, 1), f32)
    weight = jnp.zeros((1, CAP), f32)
    first = iota((CAP, patches), 1) == 0
    member_ref[...] = jnp.zeros_like(member_ref)
    for c in range(crops):
        hit = jnp.where((rank[c : c + 1] + start == slot + 1.0) & (mask[c : c + 1] > 0.0), 1.0, 0.0)
        if c == 0:
            hit = jnp.where(first & (slot >= total), 1.0, hit)
        sel_ref[:, c * patches : (c + 1) * patches] = hit.astype(bf16)
        own = count[c : c + 1]
        inside = jnp.where((lane >= start) & (lane < start + own), 1.0, 0.0)
        part = inside * (1.0 / jnp.maximum(own, 1.0))
        member_ref[c : c + 1, :] = part
        weight = weight + part
        start = start + own
    live = jnp.where(lane < total, 1.0, 0.0)
    picked = mm(sel_ref[...], feats_ref[...])
    scale = lax.rsqrt(jnp.sum(picked * picked, axis=1, keepdims=True) + EPS)
    unit_ref[...] = (picked * scale).astype(bf16)
    at = iota((EXTRA, CAP), 0)
    tail = jnp.where(at == 0, live, jnp.where(at == 1, weight * GRAD_SCALE, 0.0)).astype(bf16)
    mine_ref[...] = tail
    late = copies([(member_ref, member_hbm), (mine_ref, mine_hbm)], late_sems)
    for copy in late:
        copy.start()
    pack_ref[0:HALF, :] = unit_ref[pl.ds(pl.multiple_of(at_ref[0] * HALF, HALF), HALF), :]
    pack_ref[HALF : HALF + EXTRA, :] = tail
    peers = send_hbm.shape[0]
    make = lambda g: pltpu.make_async_copy(pack_ref, send_hbm.at[g], sems.at[g])
    start_all(peers, make)
    for copy in late:
        copy.wait()
    wait_all(peers, make)


def columns_body(
    student_ref, teacher_ref, cols_hbm, student_t_hbm, teacher_t_hbm, norm_hbm, cols_ref, student_t_ref, teacher_t_ref, norm_ref, sems
):
    for part in chunks_of(student_ref.shape[1]):
        wide = student_ref[:, part].astype(f32)
        norm = jnp.sqrt(jnp.sum(wide * wide, axis=0, keepdims=True) + EPS)
        norm_ref[:, part] = norm
        unit = wide / norm
        cols_ref[:, part] = unit.astype(bf16)
        student_t_ref[part, :] = unit.T.astype(bf16)
        wide = teacher_ref[:, part].astype(f32)
        norm = jnp.sqrt(jnp.sum(wide * wide, axis=0, keepdims=True) + EPS)
        teacher_t_ref[part, :] = (wide / norm).T.astype(bf16)
    held = (cols_ref, student_t_ref, teacher_t_ref, norm_ref)
    stores = copies(list(zip(held, (cols_hbm, student_t_hbm, teacher_t_hbm, norm_hbm))), sems)
    for store in stores:
        store.start()
    for store in stores:
        store.wait()


def weights_body(at_ref, w_in_hbm, w_out_hbm, pack_hbm, pack_ref, sems):
    rows, hid = w_in_hbm.shape
    half = hid // 2
    bot = w_out_hbm.shape[1]
    lines = w_out_hbm.shape[0] * bot // half
    column = pl.multiple_of(at_ref[0] * half, half)
    pairs = [(w_in_hbm.at[:, pl.ds(column, half)], pack_ref.at[0:rows, :])]
    for q in range(half // bot):
        source = w_out_hbm.at[q * lines : (q + 1) * lines, :]
        pairs.append((source, pack_ref.at[rows : rows + lines, q * bot : (q + 1) * bot]))
    loads = copies(pairs, sems)
    for load in loads:
        load.start()
    for load in loads:
        load.wait()
    store = pltpu.make_async_copy(pack_ref, pack_hbm, sems.at[0])
    store.start()
    store.wait()


def w_in_loads(w_hbm, w_in_ref, sems):
    peers = w_hbm.shape[0]
    rows = w_in_ref.shape[0] // peers
    return copies([(w_hbm.at[g, 0:rows, :], w_in_ref.at[g * rows : (g + 1) * rows, :]) for g in range(peers)], sems)


def w_out_loads(at_ref, w_hbm, w_out_ref, sems):
    peers = w_hbm.shape[0]
    bot = w_out_ref.shape[1]
    quarters = w_hbm.shape[2] // bot
    lines = w_out_ref.shape[0] // (peers // 2 * quarters)
    rows = w_hbm.shape[1] - lines
    pairs = []
    for i in range(peers // 2):
        for q in range(quarters):
            source = w_hbm.at[at_ref[0] * (peers // 2) + i, rows : rows + lines, q * bot : (q + 1) * bot]
            at = (i * quarters + q) * lines
            pairs.append((source, w_out_ref.at[at : at + lines, :]))
    return copies(pairs, sems)


def tokens_body(sel_ref, tokens_hbm, rows_hbm, tokens_ref, rows_ref, sems):
    load = pltpu.make_async_copy(tokens_hbm, tokens_ref, sems.at[0])
    load.start()
    load.wait()
    rows_ref[...] = mm(sel_ref[...], tokens_ref[...]).astype(bf16)
    store = pltpu.make_async_copy(rows_ref, rows_hbm, sems.at[1])
    store.start()
    store.wait()


def forward_body(
    at_ref, rows_hbm, w_hbm, hidden_hbm, slope_hbm, feats_ref, w_out_hbm,
    rows_ref, hidden_ref, slope_ref, w_in_ref, w_out_ref, sems, out_sems, own_sems,
):
    first = pltpu.make_async_copy(rows_hbm, rows_ref, own_sems.at[0])
    first.start()
    loads = w_in_loads(w_hbm, w_in_ref, sems) + w_out_loads(at_ref, w_hbm, w_out_ref, out_sems)
    for load in loads:
        load.start()
    first.wait()
    for load in loads:
        load.wait()
    keeps = copies([(w_out_ref, w_out_hbm)], sems)
    for keep in keeps:
        keep.start()
    rows = rows_ref[...]
    feats = jnp.zeros(feats_ref.shape, f32)
    for part in chunks_of(hidden_ref.shape[1]):
        pre = mm(rows, w_in_ref[:, part])
        cdf = 0.5 * (1.0 + lax.erf(pre * 0.7071067811865476))
        slope_ref[:, part] = cdf + pre * (jnp.exp(-0.5 * pre * pre) * 0.3989422804014327)
        hidden = (pre * cdf).astype(bf16)
        hidden_ref[:, part] = hidden
        feats = feats + mm(hidden, w_out_ref[part, :])
    feats_ref[...] = feats
    stores = copies([(hidden_ref, hidden_hbm), (slope_ref, slope_hbm)], own_sems)
    for store in stores:
        store.start()
    for store in keeps + stores:
        store.wait()


def unit_of(feats_ref, other_ref):
    feats = feats_ref[...] + other_ref[...]
    inv = lax.rsqrt(jnp.sum(feats * feats, axis=1, keepdims=True) + EPS)
    return (feats * inv, inv)


def unit_body(feats_ref, other_ref, rows_ref):
    rows_ref[...] = unit_of(feats_ref, other_ref)[0].astype(bf16)


def chunks_of(width):
    step = min(256, width)
    return [slice(at, at + step) for at in range(0, width, step)]


def row_of(ref, g):
    return ref[pl.ds(g, 1), :]


def fold(x):
    return x.reshape(x.shape[0] // 8, 8, x.shape[1]).sum(axis=0)


def expo_body(
    at_ref, cols_hbm, own_hbm, other_hbm, expo_hbm, part_ref, live_ref,
    cols_ref, rows_ref, tail_ref, expo_ref, total_ref, sems, own_sems, other_sems, tail_sems,
):
    peers = own_hbm.shape[0]
    width = cols_ref.shape[0]
    core = at_ref[0]
    number = peers // GROUP
    rows_of = lambda ref, q: ref.at[pl.ds(q * GROUP, GROUP), 0:HALF, :]
    rows_at = lambda q, c: rows_ref.at[pl.ds(q * GROUP, GROUP), c]
    load_own = lambda q: pltpu.make_async_copy(rows_of(own_hbm, q), rows_at(q, core), own_sems.at[q])
    load_other = lambda q: pltpu.make_async_copy(rows_of(other_hbm, q), rows_at(q, 1 - core), other_sems.at[q])
    load_tail = pltpu.make_async_copy(own_hbm.at[:, HALF : HALF + EXTRA, :], tail_ref, tail_sems.at[0])
    store = lambda q: pltpu.make_async_copy(group(expo_ref, q), group(expo_hbm, q), sems.at[q])
    load_cols = pltpu.make_async_copy(cols_hbm, cols_ref, tail_sems.at[1])
    load_cols.start()
    load_tail.start()
    start_all(number, load_own)
    start_all(number, load_other)
    total_ref[...] = jnp.zeros_like(total_ref)
    load_tail.wait()
    load_cols.wait()

    def first(g):
        rows = rows_ref[g].reshape(CAP, rows_ref.shape[3])
        tail = tail_ref[g].astype(f32)
        live = tail[0:1]
        live_ref[pl.ds(g, 1), :] = live
        for part in chunks_of(width):
            cos = mm(cols_ref[part, :], rows, NT)
            expo = jnp.exp(cos * (1.0 / TEACHER_TEMP)) * live
            expo_ref[g, part, :] = expo.astype(bf16)
            total_ref[part, :] += expo[:, 0:128] + expo[:, 128:256]
        return 0

    over_groups(peers, first, (load_own, load_other), (store,), UNROLL)
    spread_scale(total_ref)
    row_parts(expo_ref, total_ref, part_ref)
    wait_all(number, store)


def spread_scale(total_ref):
    for part in chunks_of(total_ref.shape[0]):
        sums = jnp.sum(total_ref[part, :], axis=1, keepdims=True)
        total_ref[part, :] = jnp.broadcast_to(1.0 / sums, sums.shape[:1] + (128,))


def scaled(expo, scale):
    return jnp.concatenate([expo[:, 0:128] * scale, expo[:, 128:256] * scale], axis=1)


def row_parts(expo_ref, scale_ref, part_ref):
    def step(g):
        acc = jnp.zeros((8, CAP), f32)
        for part in chunks_of(scale_ref.shape[0]):
            acc = acc + fold(scaled(expo_ref[g, part, :].astype(f32), scale_ref[part, :]))
        part_ref[pl.ds(g, 1), :] = jnp.sum(acc, axis=0, keepdims=True)
        return 0

    over_groups(expo_ref.shape[0], step, unroll=UNROLL)


def relay_body(own_ref, near_ref, far_ref, last_ref, out_ref):
    sums = (own_ref[...] + near_ref[...]) + (far_ref[...] + last_ref[...])
    sums = sums.astype(bf16)
    for g in range(out_ref.shape[0]):
        out_ref[g] = sums


def scales_from(parts_ref, live_ref, scale_ref):
    sums = parts_ref[0].astype(f32)
    for g in range(1, parts_ref.shape[0]):
        sums = sums + parts_ref[g].astype(f32)
    live = live_ref[...]
    scale_ref[...] = live / (sums + 1.0 - live)


def column_sums(load, expo_ref, scale_ref, total_ref):
    total_ref[...] = jnp.zeros_like(total_ref)

    def step(g):
        row = row_of(scale_ref, g)
        for part in chunks_of(total_ref.shape[0]):
            expo = expo_ref[g, part, :].astype(f32)
            total_ref[part, :] += expo[:, 0:128] * row[:, 0:128] + expo[:, 128:256] * row[:, 128:256]
        return 0

    over_groups(expo_ref.shape[0], step, (load,), unroll=UNROLL)
    spread_scale(total_ref)


def balance_body(expo_hbm, parts_ref, live_ref, part_ref, expo_ref, total_ref, scale_ref, sems):
    load = lambda q: pltpu.make_async_copy(group(expo_hbm, q), group(expo_ref, q), sems.at[q])
    start_all(expo_ref.shape[0] // GROUP, load)
    scales_from(parts_ref, live_ref, scale_ref)
    column_sums(load, expo_ref, scale_ref, total_ref)
    row_parts(expo_ref, total_ref, part_ref)


def divide_up(g, acc, pull, halves_ref):
    rows = jnp.sum(acc, axis=0, keepdims=True)
    rows = jnp.where(iota((EXTRA, CAP), 0) == 0, rows, 0.0).astype(bf16)
    pull = pull.astype(bf16)
    for at, block in ((slice(0, CAP), pull), (slice(CAP, LINES), rows)):
        halves_ref[0, g, at, :] = block[:, 0:HALF]
        halves_ref[1, g, at, :] = block[:, HALF:CAP]


def last_body(
    at_ref, expo_hbm, parts_ref, live_ref, cols_ref, keep_hbm, give_hbm, total_hbm,
    expo_ref, total_ref, scale_ref, halves_ref, sems, keep_sems, give_sems,
):
    peers = expo_ref.shape[0]
    core = at_ref[0]
    load = lambda q: pltpu.make_async_copy(group(expo_hbm, q), group(expo_ref, q), sems.at[q])
    half_at = lambda c, q: halves_ref.at[c, pl.ds(q * GROUP, GROUP)]
    keep = lambda q: pltpu.make_async_copy(half_at(core, q), group(keep_hbm, q), keep_sems.at[q])
    give = lambda q: pltpu.make_async_copy(half_at(1 - core, q), group(give_hbm, q), give_sems.at[q])
    number = peers // GROUP
    start_all(number, load)
    scales_from(parts_ref, live_ref, scale_ref)
    column_sums(load, expo_ref, scale_ref, total_ref)

    def step(g):
        acc = jnp.zeros((8, CAP), f32)
        pull = jnp.zeros((cols_ref.shape[0], CAP), f32)
        for part in chunks_of(total_ref.shape[0]):
            balanced = scaled(expo_ref[g, part, :].astype(f32), total_ref[part, :])
            acc = acc + fold(balanced)
            pull = pull + mm(cols_ref[:, part], balanced.astype(bf16))
        divide_up(g, acc, pull, halves_ref)
        return 0

    spare = pltpu.make_async_copy(total_ref, total_hbm, sems.at[0])
    spare.start()
    over_groups(peers, step, (), (give, keep), UNROLL)
    wait_all(number, give)
    wait_all(number, keep)
    spare.wait()


def student_body(
    at_ref, cols_t_ref, cols_ref, rows_hbm, raised_hbm, keep_hbm, give_hbm,
    rows_ref, raised_ref, halves_ref, row_sems, sems, keep_sems, give_sems,
):
    peers = rows_ref.shape[0]
    load = lambda q: pltpu.make_async_copy(group(rows_hbm, q), group(rows_ref, q), row_sems.at[q])
    start_all(peers // GROUP, load)
    core = at_ref[0]
    width = cols_t_ref.shape[0]
    store = lambda q: pltpu.make_async_copy(group(raised_ref, q), group(raised_hbm, q), sems.at[q])
    half_at = lambda c, q: halves_ref.at[c, pl.ds(q * GROUP, GROUP)]
    keep = lambda q: pltpu.make_async_copy(half_at(core, q), group(keep_hbm, q), keep_sems.at[q])
    give = lambda q: pltpu.make_async_copy(half_at(1 - core, q), group(give_hbm, q), give_sems.at[q])
    number = peers // GROUP

    def step(g):
        rows = rows_ref[g]
        acc = jnp.zeros((8, CAP), f32)
        pull = jnp.zeros((cols_ref.shape[0], CAP), f32)
        for part in chunks_of(width):
            raised = jnp.exp(mm(cols_t_ref[part, :], rows, NT) * (1.0 / STUDENT_TEMP))
            acc = acc + fold(raised)
            raised = raised.astype(bf16)
            raised_ref[g, part, :] = raised
            pull = pull + mm(cols_ref[:, part], raised)
        divide_up(g, acc, pull, halves_ref)
        return 0

    over_groups(peers, step, (load,), (store, give, keep), UNROLL)
    for make in (give, keep, store):
        wait_all(number, make)


def columns_grad_body(
    expo_hbm, raised_hbm, scale_hbm, got_hbm, rows_hbm, proto_hbm, norm_hbm,
    grad_ref, scale_ref, proto_ref, norm_ref, expo_ref, raised_ref, acc_ref, tail_ref, rows_ref, esems, rsems, tail_sems, row_sems, late_sems,
):
    peers = expo_ref.shape[0]
    load = lambda q: pltpu.make_async_copy(group(expo_hbm, q), group(expo_ref, q), esems.at[q])
    load_raised = lambda q: pltpu.make_async_copy(group(raised_hbm, q), group(raised_ref, q), rsems.at[q])
    load_rows = lambda q: pltpu.make_async_copy(group(rows_hbm, q), group(rows_ref, q), row_sems.at[q])
    lines = got_hbm.shape[1] - EXTRA
    load_tail = pltpu.make_async_copy(got_hbm.at[:, lines : lines + EXTRA, :], tail_ref, tail_sems.at[0])
    load_scale = pltpu.make_async_copy(scale_hbm, scale_ref, tail_sems.at[1])
    late = copies([(proto_hbm, proto_ref), (norm_hbm, norm_ref)], late_sems)
    load_tail.start()
    load_scale.start()

    def begin(q, _):
        for make in (load_rows, load, load_raised):
            make(q).start()
        return 0

    lax.fori_loop(0, peers // GROUP, begin, 0)
    for copy in late:
        copy.start()
    acc_ref[...] = jnp.zeros_like(acc_ref)
    load_tail.wait()
    load_scale.wait()

    def step(g):
        tail = tail_ref[g].astype(f32)
        alpha = tail[0:1] + tail[1:2]
        beta = tail[2:3] + tail[3:4]
        rows = rows_ref[g]
        for part in chunks_of(acc_ref.shape[0]):
            balanced = scaled(expo_ref[g, part, :].astype(f32), scale_ref[part, :])
            score = raised_ref[g, part, :].astype(f32) * alpha - balanced * beta
            acc_ref[part, :] += mm(score.astype(bf16), rows)
        return 0

    over_groups(peers, step, (load_rows, load, load_raised), (), UNROLL)
    for copy in late:
        copy.wait()
    for part in chunks_of(acc_ref.shape[0]):
        grad = acc_ref[part, :].T
        norm = norm_ref[:, part]
        unit = proto_ref[:, part].astype(f32) / norm
        grad_ref[:, part] = (grad - unit * jnp.sum(unit * grad, axis=0, keepdims=True)) / norm


def join(core, own_ref, other_ref):
    own, other = (own_ref[0], other_ref[0])
    low = core == 0
    return jnp.concatenate([jnp.where(low, own, other), jnp.where(low, other, own)], axis=1)


def two_parts(x):
    high = x.astype(bf16)
    return (high.astype(f32), x - high.astype(f32))


def backward_body(
    at_ref, pull_ref, pull_other_ref, push_ref, push_other_ref, mine_ref, member_ref, feats_ref, feats_other_ref,
    rows_hbm, slope_hbm, hidden_hbm, w_out_hbm,
    send_hbm, pre_hbm, loss_ref, w_out_ref, slope_ref, hidden_ref, rows_ref, send_ref, pre_ref, out_ref, send_sems, pre_sem, load_sems,
):
    peers = send_ref.shape[0]
    sources = (w_out_hbm, slope_hbm, rows_hbm, hidden_hbm)
    loads = copies(list(zip(sources, (w_out_ref, slope_ref, rows_ref, hidden_ref))), load_sems)
    for load in loads:
        load.start()
    tail = mine_ref[...].astype(f32)
    live, weight = (tail[0:1], tail[1:2] * (1.0 / STUDENT_TEMP))
    pull = join(at_ref[0], pull_ref, pull_other_ref)
    push = join(at_ref[0], push_ref, push_other_ref)
    norm_sum = push[CAP : CAP + 1]
    push = push[0:CAP]
    scale = live / (pull[CAP : CAP + 1] + 1.0 - live)
    pull = pull[0:CAP]
    unit, inv = unit_of(feats_ref, feats_other_ref)
    inv = jnp.broadcast_to(inv, unit.shape).T[0:1]
    unit = unit.T
    cross = jnp.sum(unit.astype(bf16).astype(f32) * pull, axis=0, keepdims=True) * (1.0 / STUDENT_TEMP)
    row_loss = jnp.log(norm_sum) - scale * cross
    loss = jnp.sum(member_ref[...] * row_loss, axis=1, keepdims=True)
    square = (member_ref.shape[0], 128)
    loss = jnp.where(iota(square, 0) == iota(square, 1), loss, 0.0)
    loss_ref[...] = jnp.sum(loss, axis=0, keepdims=True)[:, 0 : loss_ref.shape[1]]
    alpha = weight / norm_sum
    beta = weight * scale
    grad_unit = push * alpha - pull * beta
    inner = jnp.sum(unit * grad_unit, axis=0, keepdims=True)
    grad_feats = (inv * (grad_unit - unit * inner)).T.astype(bf16)
    width = send_ref.shape[2]
    loads[0].wait()
    loads[1].wait()
    for part in chunks_of(hidden_ref.shape[1]):
        pre_ref[:, part] = (mm(grad_feats, w_out_ref[part, :], NT) * slope_ref[:, part]).astype(bf16)
    pre_out = pltpu.make_async_copy(pre_ref, pre_hbm, pre_sem.at[0])
    pre_out.start()
    loads[2].wait()
    loads[3].wait()
    for part in chunks_of(hidden_ref.shape[1]):
        out_ref[part, :] = mm(hidden_ref[:, part], grad_feats, TN).astype(bf16)
    core, level = (at_ref[0], at_ref[1])
    own = pre_ref[:, pl.ds(pl.multiple_of(level * width, width), width)]
    grad_in = mm(rows_ref[...], own, TN).astype(bf16)
    per = grad_in.shape[0] // peers
    block = out_ref.shape[0] // (peers // 2)
    share = block // 4
    at = iota((EXTRA, CAP), 0)
    rows = jnp.zeros((EXTRA, CAP), f32)
    for i, x in enumerate(two_parts(alpha) + two_parts(beta)):
        rows = jnp.where(at == i, x, rows)
    rows = rows.astype(bf16)
    store = lambda g: pltpu.make_async_copy(send_ref.at[g], send_hbm.at[g], send_sems.at[g])
    for g in range(peers):
        send_ref[g, 0:per, :] = grad_in[g * per : (g + 1) * per, :]
        start = pl.multiple_of((g % (peers // 2)) * block + level * share, share)
        out = out_ref[pl.ds(start, share), :]
        send_ref[g, per : per + share, :] = jnp.where(core == g // (peers // 2), out, jnp.zeros_like(out))
        send_ref[g, per + share : per + share + EXTRA, :] = rows
        store(g).start()
    pre_out.wait()
    wait_all(peers, store)


def backward_rows_body(pre_ref, w_hbm, out_hbm, w_in_ref, out_ref, sems, out_sem):
    loads = w_in_loads(w_hbm, w_in_ref, sems)
    for load in loads:
        load.start()
    for load in loads:
        load.wait()
    out_ref[...] = mm(pre_ref[...], w_in_ref[...], NT).astype(bf16)
    store = pltpu.make_async_copy(out_ref, out_hbm, out_sem.at[0])
    store.start()
    store.wait()


def place_body(sel_ref, rows_ref, other_ref, out_hbm, out_ref, sems):
    rows = (rows_ref[...].astype(f32) + other_ref[...].astype(f32)).astype(bf16)
    pieces = out_ref.shape[0]
    size = out_ref.shape[1]
    store = lambda i: pltpu.make_async_copy(out_ref.at[i], out_hbm.at[i], sems.at[i])
    for i in range(pieces):
        out_ref[i] = mm(sel_ref[:, i * size : (i + 1) * size], rows, TN).astype(bf16)
        store(i).start()
    wait_all(pieces, store)


def gather_grads_body(got_hbm, send_hbm, got_ref, sum_ref, load_sems, sems):
    peers = got_hbm.shape[0]
    lines = sum_ref.shape[0]
    source = lambda q: got_hbm.at[pl.ds(q * GROUP, GROUP), 0:lines, :]
    load = lambda q: pltpu.make_async_copy(source(q), group(got_ref, q), load_sems.at[q])
    start_all(peers // GROUP, load)
    acc = jnp.zeros(got_ref.shape[1:], f32)
    for g in range(peers):
        if g % GROUP == 0:
            load(g // GROUP).wait()
        acc = acc + got_ref[g].astype(f32)
    sum_ref[...] = acc.astype(bf16)
    store = lambda t: pltpu.make_async_copy(sum_ref, send_hbm.at[t], sems.at[t])
    start_all(send_hbm.shape[0], store)
    wait_all(send_hbm.shape[0], store)


def weight_grads_body(at_ref, parts_ref, grad_in_ref, grad_out_ref):
    peers, lines, width = parts_ref.shape
    per = grad_in_ref.shape[0]
    share = lines - per
    for t in range(peers):
        to = ((t % 2) * (peers // 2) + t // 2) * width
        grad_in_ref[:, to : to + width] = parts_ref[t, 0:per, :].astype(f32)
    for z in range(peers // 2):
        grad_out_ref[z * share : (z + 1) * share, :] = parts_ref[2 * z + at_ref[2], per:lines, :].astype(f32)


def sem(number):
    return pltpu.SemaphoreType.DMA((number,))


def run_expo(at, cols_t, own, other):
    dp, (width, bot) = (own.shape[0], cols_t.shape)
    big, small = ((dp, width, CAP), (dp, CAP))
    return call(
        expo_body,
        [(big, bf16), (small, f32), (small, f32)],
        (at, cols_t, own, other),
        in_specs=[SMEM, HBM, ANY, ANY],
        out_specs=[HBM, VMEM, VMEM],
        scratch=[
            pltpu.VMEM((width, bot), bf16),
            pltpu.VMEM((dp, 2, HALF, bot), bf16),
            pltpu.VMEM((dp, EXTRA, bot), bf16),
            pltpu.VMEM(big, bf16),
            pltpu.VMEM((width, 128), f32),
            *[sem(dp // GROUP)] * 4,
        ],
    )


def run_balance(expo, got, live):
    dp, width, _ = expo.shape
    small = pltpu.VMEM(live.shape, f32)
    return call(
        balance_body,
        [(live.shape, f32)],
        (expo, got, live),
        in_specs=[HBM, VMEM, VMEM],
        scratch=[pltpu.VMEM(expo.shape, bf16), pltpu.VMEM((width, 128), f32), small, sem(dp // GROUP)],
    )[0]


def run_last(at, expo, got, live, cols):
    dp, width, _ = expo.shape
    halves = (dp, LINES, HALF)
    return call(
        last_body,
        [(halves, bf16), (halves, bf16), ((width, 128), f32)],
        (at, expo, got, live, cols),
        in_specs=[SMEM, HBM, VMEM, VMEM, VMEM],
        out_specs=[ANY, ANY, HBM],
        scratch=[
            pltpu.VMEM(expo.shape, bf16),
            pltpu.VMEM((width, 128), f32),
            pltpu.VMEM(live.shape, f32),
            pltpu.VMEM((2, *halves), bf16),
            *[sem(dp // GROUP)] * 3,
        ],
    )


def run_student(at, cols_t, cols, rows):
    dp = rows.shape[0]
    big, halves = ((dp, cols.shape[1], CAP), (dp, LINES, HALF))
    return call(
        student_body,
        [(big, bf16), (halves, bf16), (halves, bf16)],
        (at, cols_t, cols, rows),
        in_specs=[SMEM, VMEM, VMEM, HBM],
        out_specs=[HBM, ANY, ANY],
        scratch=[
            pltpu.VMEM(rows.shape, bf16),
            pltpu.VMEM(big, bf16),
            pltpu.VMEM((2, *halves), bf16),
            *[sem(dp // GROUP)] * 4,
        ],
    )


def run_columns_grad(expo, raised, scale, got, rows, proto, norm):
    dp, held = (expo.shape[0], pltpu.VMEM(expo.shape, bf16))
    return call(
        columns_grad_body,
        [(proto.shape, f32)],
        (expo, raised, scale, got, rows, proto, norm),
        in_specs=[HBM] * 3 + [ANY] + [HBM] * 3,
        scratch=[
            pltpu.VMEM(scale.shape, f32),
            pltpu.VMEM(proto.shape, bf16),
            pltpu.VMEM(norm.shape, f32),
            held,
            held,
            pltpu.VMEM(proto.shape[::-1], f32),
            pltpu.VMEM((dp, EXTRA, CAP), bf16),
            pltpu.VMEM(rows.shape, bf16),
            *[sem(dp // GROUP)] * 4,
            sem(2),
        ],
    )[0]


def exchange(x, axis):
    return lax.all_to_all(x, axis, split_axis=0, concat_axis=0, tiled=True)


def sibling(x):
    peers = lax.axis_size("tensor")
    return lax.ppermute(x, "tensor", [(i, i ^ 1) for i in range(peers)])


def everywhere(part):
    both = part + sibling(part)
    near, far, last = (levels(both, by) for by in (1, 2, 3))
    (sums,) = call(relay_body, [((part.shape[0], *part.shape), bf16)], (both, near, far, last))
    return exchange(sums, "dp")


def levels(x, by):
    peers = lax.axis_size("tensor")
    return lax.ppermute(x, "tensor", [(i, i ^ (2 * by)) for i in range(peers)])


def level_sums(x):
    near, far, last = (levels(x, by) for by in (1, 2, 3))
    wide = lambda y: y.astype(f32)
    return (wide(x) + wide(near)) + (wide(far) + wide(last))


def paired(keep, give):
    return (keep.astype(f32) + sibling(give).astype(f32)).astype(bf16)


def slot_sums_body(parts_hbm, out_hbm, parts_ref, out_ref, sems, out_sem):
    peers = parts_hbm.shape[0]
    load = lambda q: pltpu.make_async_copy(group(parts_hbm, q), group(parts_ref, q), sems.at[q])
    start_all(peers // GROUP, load)
    acc = jnp.zeros(parts_ref.shape[1:], f32)
    for g in range(peers):
        if g % GROUP == 0:
            load(g // GROUP).wait()
        acc = acc + parts_ref[g].astype(f32)
    out_ref[0] = acc.astype(bf16)
    store = pltpu.make_async_copy(out_ref, out_hbm, out_sem.at[0])
    store.start()
    store.wait()


def slot_sums(parts):
    out = (1, *parts.shape[1:])
    return call(
        slot_sums_body,
        [(out, bf16)],
        (parts,),
        in_specs=[ANY],
        out_specs=[HBM],
        scratch=[pltpu.VMEM(parts.shape, bf16), pltpu.VMEM(out, bf16), sem(parts.shape[0] // GROUP), sem(1)],
    )[0]


def after(x, earlier):
    return lax.optimization_barrier((x, earlier))[0]


def parts_of(tokens, teacher_feats, masks, w_in, w_out, proto_student, proto_teacher):
    dim = tokens.shape[1]
    hid = w_in.shape[1]
    bot, width = proto_student.shape
    dp, tensor = (lax.axis_size("dp"), lax.axis_size("tensor"))
    per = w_in.shape[0]
    half = hid // 2
    share = w_out.shape[0] // 4
    t = lax.axis_index("tensor").astype(jnp.int32)
    g = lax.axis_index("dp").astype(jnp.int32)
    at = jnp.stack([t % 2, t // 2, g // (dp // 2)])

    lines = per + w_out.shape[0] * bot // half
    (w_pack,) = call(weights_body, [((lines, half), bf16)], (at, w_in, w_out), in_specs=[SMEM, HBM, HBM], out_specs=[HBM], scratch=[pltpu.VMEM((lines, half), bf16), sem(1 + half // bot)])
    w_all = lax.all_gather(w_pack, "dp", axis=0, tiled=True).reshape(dp, lines, half)
    dma = pltpu.SemaphoreType.DMA
    sems = dma((dp,))
    sel, send, member, mine = call(
        select_body,
        [((CAP, tokens.shape[0]), bf16), ((dp, HALF + EXTRA, bot), bf16), ((8, CAP), f32), ((EXTRA, CAP), bf16)],
        (at, masks, teacher_feats),
        in_specs=[SMEM, VMEM, VMEM],
        out_specs=[VMEM, HBM, HBM, HBM],
        scratch=[
            pltpu.VMEM((CAP, bot), bf16),
            pltpu.VMEM((HALF + EXTRA, bot), bf16),
            pltpu.VMEM((8, CAP), f32),
            pltpu.VMEM((EXTRA, CAP), bf16),
            sems,
            sem(2),
        ],
    )
    packs = exchange(send, "dp")
    others = sibling(packs)
    cols, student_t, teacher_t, norm = call(
        columns_body,
        [((bot, width), bf16), ((width, bot), bf16), ((width, bot), bf16), ((1, width), f32)],
        (proto_student, proto_teacher),
        out_specs=[HBM] * 4,
        scratch=[
            pltpu.VMEM((bot, width), bf16),
            pltpu.VMEM((width, bot), bf16),
            pltpu.VMEM((width, bot), bf16),
            pltpu.VMEM((1, width), f32),
            sem(4),
        ],
    )
    expo, part, live = run_expo(at, teacher_t, packs, others)
    w_held = [pltpu.VMEM((dim, half), bf16), pltpu.VMEM((half, bot), bf16)]
    (rows,) = call(
        tokens_body,
        [((CAP, dim), bf16)],
        (sel, tokens),
        in_specs=[VMEM, HBM],
        out_specs=[HBM],
        scratch=[pltpu.VMEM(tokens.shape, bf16), pltpu.VMEM((CAP, dim), bf16), sem(2)],
    )
    hidden, slope, feats, w_out_half = call(
        forward_body,
        [((CAP, half), bf16), ((CAP, half), f32), ((CAP, bot), f32), ((half, bot), bf16)],
        (at, rows, after(w_all, part)),
        in_specs=[SMEM, HBM, HBM],
        out_specs=[HBM, HBM, VMEM, HBM],
        scratch=[
            pltpu.VMEM((CAP, dim), bf16),
            pltpu.VMEM((CAP, half), bf16),
            pltpu.VMEM((CAP, half), f32),
            *w_held,
            sems,
            sem(2 * dp),
            sem(2),
        ],
    )
    feats_other = sibling(feats)
    (student_rows,) = call(unit_body, [((CAP, bot), bf16)], (feats, feats_other))
    all_rows = lax.all_gather(student_rows, "dp", axis=0, tiled=True).reshape(dp, CAP, bot)
    got = everywhere(part)
    part = run_balance(expo, got, live)
    got = everywhere(part)
    keep, give, scale = run_last(at, expo, got, live, cols)
    pull = paired(keep, give)
    pull_got = exchange(pull, "dp")
    all_rows = after(all_rows, pull)
    raised, keep, give = run_student(at, student_t, cols, all_rows)
    push_got = exchange(paired(keep, give), "dp")
    pull = level_sums(slot_sums(pull_got))
    pull_other = sibling(pull)
    push = level_sums(slot_sums(push_got))
    push_other = sibling(push)
    back_lines = per + share + EXTRA
    send, grad_pre, loss = call(
        backward_body,
        [((dp, back_lines, bot), bf16), ((CAP, half), bf16), ((1, masks.shape[0]), f32)],
        (at, pull, pull_other, push, push_other, mine, member, feats, feats_other, rows, slope, hidden, w_out_half),
        in_specs=[SMEM] + [VMEM] * 8 + [HBM] * 4,
        out_specs=[HBM, HBM, VMEM],
        scratch=[
            pltpu.VMEM((half, bot), bf16),
            pltpu.VMEM((CAP, half), f32),
            pltpu.VMEM((CAP, half), bf16),
            pltpu.VMEM((CAP, dim), bf16),
            pltpu.VMEM((dp, back_lines, bot), bf16),
            pltpu.VMEM((CAP, half), bf16),
            pltpu.VMEM((half, bot), bf16),
            sems,
            sem(1),
            sem(4),
        ],
    )
    got = exchange(send, "dp")
    (grad_rows,) = call(
        backward_rows_body,
        [((CAP, dim), bf16)],
        (grad_pre, w_all),
        in_specs=[VMEM, HBM],
        out_specs=[HBM],
        scratch=[pltpu.VMEM((dim, half), bf16), pltpu.VMEM((CAP, dim), bf16), sems, sem(1)],
    )
    pieces = 4
    d_shape = (pieces, tokens.shape[0] // pieces, dim)
    (d_tokens,) = call(
        place_body,
        [(d_shape, bf16)],
        (sel, grad_rows, sibling(grad_rows)),
        out_specs=[HBM],
        scratch=[pltpu.VMEM(d_shape, bf16), dma((pieces,))],
    )
    got, d_tokens = lax.optimization_barrier((got, d_tokens))
    (sent,) = call(
        gather_grads_body,
        [((tensor, per + share, bot), bf16)],
        (got,),
        in_specs=[ANY],
        out_specs=[HBM],
        scratch=[pltpu.VMEM((dp, per + share, bot), bf16), pltpu.VMEM((per + share, bot), bf16), sems, sem(tensor)],
    )
    parts = exchange(sent, "tensor")
    grad_proto = run_columns_grad(expo, raised, scale, got, all_rows, proto_student, norm)
    grad_in, grad_out = call(
        weight_grads_body, [((per, hid), f32), ((w_out.shape[0], bot), f32)], (at, parts), in_specs=[SMEM, VMEM]
    )
    return (d_tokens.reshape(tokens.shape), grad_in, grad_out, grad_proto, loss.reshape(masks.shape[0]))


def solution(mesh):
    placed = (
        P("dp", None),
        P("dp", None),
        P("dp", None),
        P("dp", None),
        P("dp", None),
        P(None, ("dp", "tensor")),
        P(None, ("dp", "tensor")),
    )
    return jax.shard_map(
        parts_of,
        mesh=mesh,
        in_specs=placed,
        out_specs=(P("dp", None), P("dp", None), P("dp", None), P(None, ("dp", "tensor")), P("dp")),
        check_vma=False,
    )
```

```python
import jax
import jax.numpy as jnp
from jax import lax
from jax.experimental import pallas as pl
from jax.experimental.pallas import tpu as pltpu
from jax.sharding import PartitionSpec as P

CAP = 256
TEACHER_TEMP = 0.07
STUDENT_TEMP = 0.1
EPS = 1e-06
GRAD_SCALE = 65536.0
INTERPRET = False
f32, bf16 = (jnp.float32, jnp.bfloat16)
VMEM = pl.BlockSpec(memory_space=pltpu.VMEM)
HBM = pl.BlockSpec(memory_space=pltpu.HBM)
ANY = pl.BlockSpec(memory_space=pl.ANY)
SMEM = pl.BlockSpec(memory_space=pltpu.SMEM)
NT = (((1,), (1,)), ((), ()))
TN = (((0,), (0,)), ((), ()))
EXTRA = 16
HALF = CAP // 2
LINES = CAP + EXTRA


def mm(a, b, dims=None):
    if dims is None:
        return jnp.dot(a, b, preferred_element_type=f32)
    return lax.dot_general(a, b, dims, preferred_element_type=f32)


def call(body, outs, ins, out_specs=None, in_specs=None, scratch=()):
    specs = out_specs or [VMEM] * len(outs)
    in_specs = in_specs or [VMEM] * len(ins)
    ins = [pltpu.with_memory_space_constraint(x, pltpu.HBM) if spec is HBM else x for x, spec in zip(ins, in_specs)]
    outs = tuple(pltpu.HBM(*o) if spec is HBM else jax.ShapeDtypeStruct(*o) for o, spec in zip(outs, specs))
    return pl.pallas_call(
        body,
        out_shape=outs,
        in_specs=in_specs,
        out_specs=tuple(specs),
        scratch_shapes=list(scratch),
        interpret=INTERPRET,
        compiler_params=pltpu.CompilerParams(vmem_limit_bytes=48 << 20),
    )(*ins)


def iota(shape, dim):
    return lax.broadcasted_iota(jnp.int32, shape, dim)


def copies(pairs, sems):
    return [pltpu.make_async_copy(a, b, sems.at[i]) for i, (a, b) in enumerate(pairs)]


GROUP = 4
UNROLL = 4


def group(ref, q):
    return ref.at[pl.ds(q * GROUP, GROUP)]


def start_all(number, make):
    def go(i, _):
        make(i).start()
        return 0

    lax.fori_loop(0, number, go, 0)


def wait_all(number, make):
    def go(i, _):
        make(i).wait()
        return 0

    lax.fori_loop(0, number, go, 0)


def over_groups(peers, step, loads=(), stores=(), unroll=1):
    def go(q, _):
        for make in loads:
            make(q).wait()
        lax.fori_loop(0, GROUP, lambda i, _: step(q * GROUP + i), 0, unroll=unroll)
        for make in stores:
            make(q).start()
        return 0

    lax.fori_loop(0, peers // GROUP, go, 0)


def select_body(
    at_ref, mask_ref, feats_ref, sel_ref, send_hbm, member_hbm, mine_hbm, unit_ref, pack_ref, member_ref, mine_ref, sems, late_sems
):
    crops, patches = mask_ref.shape
    mask = mask_ref[...].astype(f32)
    upto = (iota((patches, patches), 0) <= iota((patches, patches), 1)).astype(f32).astype(bf16)
    rank = mm(mask.astype(bf16), upto)
    count = jnp.sum(mask, axis=1, keepdims=True)
    total = jnp.sum(count, axis=0, keepdims=True)
    slot = iota((CAP, patches), 0).astype(f32)
    lane = iota((1, CAP), 1).astype(f32)
    start = jnp.zeros((1, 1), f32)
    weight = jnp.zeros((1, CAP), f32)
    first = iota((CAP, patches), 1) == 0
    member_ref[...] = jnp.zeros_like(member_ref)
    for c in range(crops):
        hit = jnp.where((rank[c : c + 1] + start == slot + 1.0) & (mask[c : c + 1] > 0.0), 1.0, 0.0)
        if c == 0:
            hit = jnp.where(first & (slot >= total), 1.0, hit)
        sel_ref[:, c * patches : (c + 1) * patches] = hit.astype(bf16)
        own = count[c : c + 1]
        inside = jnp.where((lane >= start) & (lane < start + own), 1.0, 0.0)
        part = inside * (1.0 / jnp.maximum(own, 1.0))
        member_ref[c : c + 1, :] = part
        weight = weight + part
        start = start + own
    live = jnp.where(lane < total, 1.0, 0.0)
    picked = mm(sel_ref[...], feats_ref[...])
    scale = lax.rsqrt(jnp.sum(picked * picked, axis=1, keepdims=True) + EPS)
    unit_ref[...] = (picked * scale).astype(bf16)
    at = iota((EXTRA, CAP), 0)
    tail = jnp.where(at == 0, live, jnp.where(at == 1, weight * GRAD_SCALE, 0.0)).astype(bf16)
    mine_ref[...] = tail
    late = copies([(member_ref, member_hbm), (mine_ref, mine_hbm)], late_sems)
    for copy in late:
        copy.start()
    pack_ref[0:HALF, :] = unit_ref[pl.ds(pl.multiple_of(at_ref[0] * HALF, HALF), HALF), :]
    pack_ref[HALF : HALF + EXTRA, :] = tail
    peers = send_hbm.shape[0]
    make = lambda g: pltpu.make_async_copy(pack_ref, send_hbm.at[g], sems.at[g])
    start_all(peers, make)
    for copy in late:
        copy.wait()
    wait_all(peers, make)


def columns_body(
    student_ref, teacher_ref, cols_hbm, student_t_hbm, teacher_t_hbm, norm_hbm, cols_ref, student_t_ref, teacher_t_ref, norm_ref, sems
):
    for part in chunks_of(student_ref.shape[1]):
        wide = student_ref[:, part].astype(f32)
        norm = jnp.sqrt(jnp.sum(wide * wide, axis=0, keepdims=True) + EPS)
        norm_ref[:, part] = norm
        unit = wide / norm
        cols_ref[:, part] = unit.astype(bf16)
        student_t_ref[part, :] = unit.T.astype(bf16)
        wide = teacher_ref[:, part].astype(f32)
        norm = jnp.sqrt(jnp.sum(wide * wide, axis=0, keepdims=True) + EPS)
        teacher_t_ref[part, :] = (wide / norm).T.astype(bf16)
    held = (cols_ref, student_t_ref, teacher_t_ref, norm_ref)
    stores = copies(list(zip(held, (cols_hbm, student_t_hbm, teacher_t_hbm, norm_hbm))), sems)
    for store in stores:
        store.start()
    for store in stores:
        store.wait()


def weights_body(at_ref, w_in_hbm, w_out_hbm, pack_hbm, w_in_ref, w_out_ref, pack_ref, sems):
    rows, hid = w_in_hbm.shape
    block, bot = w_out_hbm.shape
    half = block // 2
    loads = copies([(w_in_hbm, w_in_ref), (w_out_hbm, w_out_ref)], sems)
    for load in loads:
        load.start()
    core = at_ref[0]
    row = iota((2 * block, block), 0)
    col = iota((2 * block, block), 1)
    pick = (row == (col // half) * block + core * half + col % half).astype(f32).astype(bf16)
    for load in loads:
        load.wait()
    for p in range(hid // (2 * block)):
        two = w_in_ref[:, p * 2 * block : (p + 1) * 2 * block]
        pack_ref[0:rows, p * block : (p + 1) * block] = mm(two, pick).astype(bf16)
    lines = pack_ref.shape[0] - rows
    for q in range(half // lines):
        at = pl.multiple_of(core * half + q * lines, lines)
        pack_ref[rows : rows + lines, q * bot : (q + 1) * bot] = w_out_ref[pl.ds(at, lines), :]
    store = pltpu.make_async_copy(pack_ref, pack_hbm, sems.at[0])
    store.start()
    store.wait()


def w_in_load(w_hbm, w_in_ref, at):
    return pltpu.make_async_copy(w_hbm.at[:, 0 : w_in_ref.shape[1], :], w_in_ref, at)


def w_in_of(w_in_ref, part):
    peers, rows, _ = w_in_ref.shape
    return w_in_ref[:, :, part].reshape(peers * rows, part.stop - part.start)


def tokens_body(sel_ref, tokens_hbm, rows_hbm, tokens_ref, rows_ref, sems):
    load = pltpu.make_async_copy(tokens_hbm, tokens_ref, sems.at[0])
    load.start()
    load.wait()
    rows_ref[...] = mm(sel_ref[...], tokens_ref[...]).astype(bf16)
    store = pltpu.make_async_copy(rows_ref, rows_hbm, sems.at[1])
    store.start()
    store.wait()


def forward_body(
    rows_hbm, w_hbm, hidden_hbm, slope_hbm, feats_ref, w_out_hbm,
    rows_ref, hidden_ref, slope_ref, w_in_ref, lines_ref, w_out_ref, own_sems,
):
    first = pltpu.make_async_copy(rows_hbm, rows_ref, own_sems.at[0])
    first.start()
    per, lines = (w_in_ref.shape[1], lines_ref.shape[1])
    loads = [
        pltpu.make_async_copy(w_hbm.at[:, per : per + lines, :], lines_ref, own_sems.at[1]),
        w_in_load(w_hbm, w_in_ref, own_sems.at[2]),
    ]
    for load in loads:
        load.start()
    first.wait()
    loads[0].wait()
    bot = w_out_ref.shape[1]
    quarters = lines_ref.shape[2] // bot
    for g in range(lines_ref.shape[0]):
        for q in range(quarters):
            at = (g * quarters + q) * lines
            w_out_ref[at : at + lines, :] = lines_ref[g, :, q * bot : (q + 1) * bot]
    loads[1].wait()
    keeps = [pltpu.make_async_copy(w_out_ref, w_out_hbm, own_sems.at[2])]
    for keep in keeps:
        keep.start()
    rows = rows_ref[...]
    feats = jnp.zeros(feats_ref.shape, f32)
    for part in chunks_of(hidden_ref.shape[1]):
        pre = mm(rows, w_in_of(w_in_ref, part))
        cdf = 0.5 * (1.0 + lax.erf(pre * 0.7071067811865476))
        slope_ref[:, part] = cdf + pre * (jnp.exp(-0.5 * pre * pre) * 0.3989422804014327)
        hidden = (pre * cdf).astype(bf16)
        hidden_ref[:, part] = hidden
        feats = feats + mm(hidden, w_out_ref[part, :])
    feats_ref[...] = feats
    stores = copies([(hidden_ref, hidden_hbm), (slope_ref, slope_hbm)], own_sems)
    for store in stores:
        store.start()
    for store in keeps + stores:
        store.wait()


def unit_of(feats_ref, other_ref):
    feats = feats_ref[...] + other_ref[...]
    inv = lax.rsqrt(jnp.sum(feats * feats, axis=1, keepdims=True) + EPS)
    return (feats * inv, inv)


def unit_body(feats_ref, other_ref, rows_ref):
    rows_ref[...] = unit_of(feats_ref, other_ref)[0].astype(bf16)


def chunks_of(width):
    step = min(256, width)
    return [slice(at, at + step) for at in range(0, width, step)]


def row_of(ref, g):
    return ref[pl.ds(g, 1), :]


def fold(x):
    return x.reshape(x.shape[0] // 8, 8, x.shape[1]).sum(axis=0)


def expo_body(
    at_ref, cols_hbm, own_hbm, other_hbm, expo_hbm, part_ref, live_ref,
    cols_ref, rows_ref, tail_ref, expo_ref, total_ref, sems, own_sems, other_sems, tail_sems,
):
    peers = own_hbm.shape[0]
    width = cols_ref.shape[0]
    core = at_ref[0]
    number = peers // GROUP
    rows_of = lambda ref, q: ref.at[pl.ds(q * GROUP, GROUP), 0:HALF, :]
    rows_at = lambda q, c: rows_ref.at[pl.ds(q * GROUP, GROUP), c]
    load_own = lambda q: pltpu.make_async_copy(rows_of(own_hbm, q), rows_at(q, core), own_sems.at[q])
    load_other = lambda q: pltpu.make_async_copy(rows_of(other_hbm, q), rows_at(q, 1 - core), other_sems.at[q])
    load_tail = pltpu.make_async_copy(own_hbm.at[:, HALF : HALF + EXTRA, :], tail_ref, tail_sems.at[0])
    store = lambda q: pltpu.make_async_copy(group(expo_ref, q), group(expo_hbm, q), sems.at[q])
    load_cols = pltpu.make_async_copy(cols_hbm, cols_ref, tail_sems.at[1])
    load_cols.start()
    load_tail.start()
    start_all(number, load_own)
    start_all(number, load_other)
    total_ref[...] = jnp.zeros_like(total_ref)
    load_tail.wait()
    load_cols.wait()

    def first(g):
        rows = rows_ref[g].reshape(CAP, rows_ref.shape[3])
        tail = tail_ref[g].astype(f32)
        live = tail[0:1]
        live_ref[pl.ds(g, 1), :] = live
        for part in chunks_of(width):
            cos = mm(cols_ref[part, :], rows, NT)
            expo = jnp.exp(cos * (1.0 / TEACHER_TEMP)) * live
            expo_ref[g, part, :] = expo.astype(bf16)
            total_ref[part, :] += expo[:, 0:128] + expo[:, 128:256]
        return 0

    over_groups(peers, first, (load_own, load_other), (store,), UNROLL)
    spread_scale(total_ref)
    row_parts(expo_ref, total_ref, part_ref)
    wait_all(number, store)


def spread_scale(total_ref):
    for part in chunks_of(total_ref.shape[0]):
        sums = jnp.sum(total_ref[part, :], axis=1, keepdims=True)
        total_ref[part, :] = jnp.broadcast_to(1.0 / sums, sums.shape[:1] + (128,))


def scaled(expo, scale):
    return jnp.concatenate([expo[:, 0:128] * scale, expo[:, 128:256] * scale], axis=1)


def row_parts(expo_ref, scale_ref, part_ref):
    def step(g):
        acc = jnp.zeros((8, CAP), f32)
        for part in chunks_of(scale_ref.shape[0]):
            acc = acc + fold(scaled(expo_ref[g, part, :].astype(f32), scale_ref[part, :]))
        part_ref[pl.ds(g, 1), :] = jnp.sum(acc, axis=0, keepdims=True)
        return 0

    over_groups(expo_ref.shape[0], step, unroll=UNROLL)


def relay_body(own_ref, near_ref, far_ref, last_ref, out_ref):
    sums = (own_ref[...] + near_ref[...]) + (far_ref[...] + last_ref[...])
    sums = sums.astype(bf16)
    for g in range(out_ref.shape[0]):
        out_ref[g] = sums


def scales_from(parts_ref, live_ref, scale_ref):
    sums = parts_ref[0].astype(f32)
    for g in range(1, parts_ref.shape[0]):
        sums = sums + parts_ref[g].astype(f32)
    live = live_ref[...]
    scale_ref[...] = live / (sums + 1.0 - live)


def column_sums(load, expo_ref, scale_ref, total_ref):
    total_ref[...] = jnp.zeros_like(total_ref)

    def step(g):
        row = row_of(scale_ref, g)
        for part in chunks_of(total_ref.shape[0]):
            expo = expo_ref[g, part, :].astype(f32)
            total_ref[part, :] += expo[:, 0:128] * row[:, 0:128] + expo[:, 128:256] * row[:, 128:256]
        return 0

    over_groups(expo_ref.shape[0], step, (load,), unroll=UNROLL)
    spread_scale(total_ref)


def balance_body(expo_hbm, parts_ref, live_ref, part_ref, expo_ref, total_ref, scale_ref, sems):
    load = lambda q: pltpu.make_async_copy(group(expo_hbm, q), group(expo_ref, q), sems.at[q])
    start_all(expo_ref.shape[0] // GROUP, load)
    scales_from(parts_ref, live_ref, scale_ref)
    column_sums(load, expo_ref, scale_ref, total_ref)
    row_parts(expo_ref, total_ref, part_ref)


def divide_up(g, acc, pull, halves_ref):
    rows = jnp.sum(acc, axis=0, keepdims=True)
    rows = jnp.where(iota((EXTRA, CAP), 0) == 0, rows, 0.0).astype(bf16)
    pull = pull.astype(bf16)
    for at, block in ((slice(0, CAP), pull), (slice(CAP, LINES), rows)):
        halves_ref[0, g, at, :] = block[:, 0:HALF]
        halves_ref[1, g, at, :] = block[:, HALF:CAP]


def last_body(
    at_ref, expo_hbm, parts_ref, live_ref, cols_ref, keep_hbm, give_hbm, total_hbm,
    expo_ref, total_ref, scale_ref, halves_ref, sems, keep_sems, give_sems,
):
    peers = expo_ref.shape[0]
    core = at_ref[0]
    load = lambda q: pltpu.make_async_copy(group(expo_hbm, q), group(expo_ref, q), sems.at[q])
    half_at = lambda c, q: halves_ref.at[c, pl.ds(q * GROUP, GROUP)]
    keep = lambda q: pltpu.make_async_copy(half_at(core, q), group(keep_hbm, q), keep_sems.at[q])
    give = lambda q: pltpu.make_async_copy(half_at(1 - core, q), group(give_hbm, q), give_sems.at[q])
    number = peers // GROUP
    start_all(number, load)
    scales_from(parts_ref, live_ref, scale_ref)
    column_sums(load, expo_ref, scale_ref, total_ref)

    def step(g):
        acc = jnp.zeros((8, CAP), f32)
        pull = jnp.zeros((cols_ref.shape[0], CAP), f32)
        for part in chunks_of(total_ref.shape[0]):
            balanced = scaled(expo_ref[g, part, :].astype(f32), total_ref[part, :])
            acc = acc + fold(balanced)
            pull = pull + mm(cols_ref[:, part], balanced.astype(bf16))
        divide_up(g, acc, pull, halves_ref)
        return 0

    spare = pltpu.make_async_copy(total_ref, total_hbm, sems.at[0])
    spare.start()
    over_groups(peers, step, (), (give, keep), UNROLL)
    wait_all(number, give)
    wait_all(number, keep)
    spare.wait()


def student_body(
    at_ref, cols_t_ref, cols_ref, rows_hbm, raised_hbm, keep_hbm, give_hbm,
    rows_ref, raised_ref, halves_ref, row_sems, sems, keep_sems, give_sems,
):
    peers = rows_ref.shape[0]
    load = lambda q: pltpu.make_async_copy(group(rows_hbm, q), group(rows_ref, q), row_sems.at[q])
    start_all(peers // GROUP, load)
    core = at_ref[0]
    width = cols_t_ref.shape[0]
    store = lambda q: pltpu.make_async_copy(group(raised_ref, q), group(raised_hbm, q), sems.at[q])
    half_at = lambda c, q: halves_ref.at[c, pl.ds(q * GROUP, GROUP)]
    keep = lambda q: pltpu.make_async_copy(half_at(core, q), group(keep_hbm, q), keep_sems.at[q])
    give = lambda q: pltpu.make_async_copy(half_at(1 - core, q), group(give_hbm, q), give_sems.at[q])
    number = peers // GROUP

    def step(g):
        rows = rows_ref[g]
        acc = jnp.zeros((8, CAP), f32)
        pull = jnp.zeros((cols_ref.shape[0], CAP), f32)
        for part in chunks_of(width):
            raised = jnp.exp(mm(cols_t_ref[part, :], rows, NT) * (1.0 / STUDENT_TEMP))
            acc = acc + fold(raised)
            raised = raised.astype(bf16)
            raised_ref[g, part, :] = raised
            pull = pull + mm(cols_ref[:, part], raised)
        divide_up(g, acc, pull, halves_ref)
        return 0

    over_groups(peers, step, (load,), (store, give, keep), UNROLL)
    for make in (give, keep, store):
        wait_all(number, make)


def columns_grad_body(
    expo_hbm, raised_hbm, scale_hbm, got_hbm, rows_hbm, proto_hbm, norm_hbm,
    grad_ref, scale_ref, proto_ref, norm_ref, expo_ref, raised_ref, acc_ref, tail_ref, rows_ref, esems, rsems, tail_sems, row_sems, late_sems,
):
    peers = expo_ref.shape[0]
    load = lambda q: pltpu.make_async_copy(group(expo_hbm, q), group(expo_ref, q), esems.at[q])
    load_raised = lambda q: pltpu.make_async_copy(group(raised_hbm, q), group(raised_ref, q), rsems.at[q])
    load_rows = lambda q: pltpu.make_async_copy(group(rows_hbm, q), group(rows_ref, q), row_sems.at[q])
    lines = got_hbm.shape[1] - EXTRA
    load_tail = pltpu.make_async_copy(got_hbm.at[:, lines : lines + EXTRA, :], tail_ref, tail_sems.at[0])
    load_scale = pltpu.make_async_copy(scale_hbm, scale_ref, tail_sems.at[1])
    late = copies([(proto_hbm, proto_ref), (norm_hbm, norm_ref)], late_sems)
    load_tail.start()
    load_scale.start()

    def begin(q, _):
        for make in (load_rows, load, load_raised):
            make(q).start()
        return 0

    lax.fori_loop(0, peers // GROUP, begin, 0)
    for copy in late:
        copy.start()
    acc_ref[...] = jnp.zeros_like(acc_ref)
    load_tail.wait()
    load_scale.wait()

    def step(g):
        tail = tail_ref[g].astype(f32)
        alpha = tail[0:1] + tail[1:2]
        beta = tail[2:3] + tail[3:4]
        rows = rows_ref[g]
        for part in chunks_of(acc_ref.shape[0]):
            balanced = scaled(expo_ref[g, part, :].astype(f32), scale_ref[part, :])
            score = raised_ref[g, part, :].astype(f32) * alpha - balanced * beta
            acc_ref[part, :] += mm(score.astype(bf16), rows)
        return 0

    over_groups(peers, step, (load_rows, load, load_raised), (), UNROLL)
    for copy in late:
        copy.wait()
    for part in chunks_of(acc_ref.shape[0]):
        grad = acc_ref[part, :].T
        norm = norm_ref[:, part]
        unit = proto_ref[:, part].astype(f32) / norm
        grad_ref[:, part] = (grad - unit * jnp.sum(unit * grad, axis=0, keepdims=True)) / norm


def join(core, own_ref, other_ref):
    own, other = (own_ref[0], other_ref[0])
    low = core == 0
    return jnp.concatenate([jnp.where(low, own, other), jnp.where(low, other, own)], axis=1)


def two_parts(x):
    high = x.astype(bf16)
    return (high.astype(f32), x - high.astype(f32))


def backward_body(
    at_ref, pull_ref, pull_other_ref, push_ref, push_other_ref, mine_ref, member_ref, feats_ref, feats_other_ref,
    rows_hbm, slope_hbm, hidden_hbm, w_out_hbm,
    send_hbm, pre_hbm, loss_ref, w_out_ref, slope_ref, hidden_ref, rows_ref, send_ref, pre_ref, out_ref, send_sems, pre_sem, load_sems,
):
    peers = send_ref.shape[0]
    sources = (w_out_hbm, slope_hbm, rows_hbm, hidden_hbm)
    loads = copies(list(zip(sources, (w_out_ref, slope_ref, rows_ref, hidden_ref))), load_sems)
    for load in loads:
        load.start()
    tail = mine_ref[...].astype(f32)
    live, weight = (tail[0:1], tail[1:2] * (1.0 / STUDENT_TEMP))
    pull = join(at_ref[0], pull_ref, pull_other_ref)
    push = join(at_ref[0], push_ref, push_other_ref)
    norm_sum = push[CAP : CAP + 1]
    push = push[0:CAP]
    scale = live / (pull[CAP : CAP + 1] + 1.0 - live)
    pull = pull[0:CAP]
    unit, inv = unit_of(feats_ref, feats_other_ref)
    inv = jnp.broadcast_to(inv, unit.shape).T[0:1]
    unit = unit.T
    cross = jnp.sum(unit.astype(bf16).astype(f32) * pull, axis=0, keepdims=True) * (1.0 / STUDENT_TEMP)
    row_loss = jnp.log(norm_sum) - scale * cross
    loss = jnp.sum(member_ref[...] * row_loss, axis=1, keepdims=True)
    square = (member_ref.shape[0], 128)
    loss = jnp.where(iota(square, 0) == iota(square, 1), loss, 0.0)
    loss_ref[...] = jnp.sum(loss, axis=0, keepdims=True)[:, 0 : loss_ref.shape[1]]
    alpha = weight / norm_sum
    beta = weight * scale
    grad_unit = push * alpha - pull * beta
    inner = jnp.sum(unit * grad_unit, axis=0, keepdims=True)
    grad_feats = (inv * (grad_unit - unit * inner)).T.astype(bf16)
    width = send_ref.shape[2]
    loads[0].wait()
    loads[1].wait()
    for part in chunks_of(hidden_ref.shape[1]):
        pre_ref[:, part] = (mm(grad_feats, w_out_ref[part, :], NT) * slope_ref[:, part]).astype(bf16)
    pre_out = pltpu.make_async_copy(pre_ref, pre_hbm, pre_sem.at[0])
    pre_out.start()
    loads[2].wait()
    loads[3].wait()
    for part in chunks_of(hidden_ref.shape[1]):
        out_ref[part, :] = mm(hidden_ref[:, part], grad_feats, TN).astype(bf16)
    level = at_ref[1]
    own = pre_ref[:, pl.ds(pl.multiple_of(level * width, width), width)]
    grad_in = mm(rows_ref[...], own, TN).astype(bf16)
    per = grad_in.shape[0] // peers
    block = out_ref.shape[0] // peers
    share = block // 4
    at = iota((EXTRA, CAP), 0)
    rows = jnp.zeros((EXTRA, CAP), f32)
    for i, x in enumerate(two_parts(alpha) + two_parts(beta)):
        rows = jnp.where(at == i, x, rows)
    rows = rows.astype(bf16)
    store = lambda g: pltpu.make_async_copy(send_ref.at[g], send_hbm.at[g], send_sems.at[g])
    for g in range(peers):
        send_ref[g, 0:per, :] = grad_in[g * per : (g + 1) * per, :]
        start = pl.multiple_of(g * block + level * share, share)
        send_ref[g, per : per + share, :] = out_ref[pl.ds(start, share), :]
        send_ref[g, per + share : per + share + EXTRA, :] = rows
        store(g).start()
    pre_out.wait()
    wait_all(peers, store)


def backward_rows_body(pre_ref, w_hbm, out_hbm, w_in_ref, out_ref, sem, out_sem):
    load = w_in_load(w_hbm, w_in_ref, sem.at[0])
    load.start()
    load.wait()
    w_in = w_in_of(w_in_ref, slice(0, w_in_ref.shape[2]))
    out_ref[...] = mm(pre_ref[...], w_in, NT).astype(bf16)
    store = pltpu.make_async_copy(out_ref, out_hbm, out_sem.at[0])
    store.start()
    store.wait()


def place_body(sel_ref, rows_ref, other_ref, out_hbm, out_ref, sems):
    rows = (rows_ref[...].astype(f32) + other_ref[...].astype(f32)).astype(bf16)
    pieces = out_ref.shape[0]
    size = out_ref.shape[1]
    store = lambda i: pltpu.make_async_copy(out_ref.at[i], out_hbm.at[i], sems.at[i])
    for i in range(pieces):
        out_ref[i] = mm(sel_ref[:, i * size : (i + 1) * size], rows, TN).astype(bf16)
        store(i).start()
    wait_all(pieces, store)


def gather_grads_body(got_hbm, send_hbm, got_ref, sum_ref, load_sems, sems):
    peers = got_hbm.shape[0]
    lines = sum_ref.shape[0]
    source = lambda q: got_hbm.at[pl.ds(q * GROUP, GROUP), 0:lines, :]
    load = lambda q: pltpu.make_async_copy(source(q), group(got_ref, q), load_sems.at[q])
    start_all(peers // GROUP, load)
    acc = jnp.zeros(got_ref.shape[1:], f32)
    for g in range(peers):
        if g % GROUP == 0:
            load(g // GROUP).wait()
        acc = acc + got_ref[g].astype(f32)
    sum_ref[...] = acc.astype(bf16)
    store = lambda t: pltpu.make_async_copy(sum_ref, send_hbm.at[t], sems.at[t])
    start_all(send_hbm.shape[0], store)
    wait_all(send_hbm.shape[0], store)


def weight_grads_body(parts_ref, grad_in_ref, grad_out_ref):
    peers, lines, width = parts_ref.shape
    per = grad_in_ref.shape[0]
    share = lines - per
    block = 2 * (width // 4)
    row = iota((2 * width, 2 * width), 0)
    col = iota((2 * width, 2 * width), 1)
    half = block // 2
    from_row = ((col % block) // half) * width + (col // block) * half + col % half
    order = (row == from_row).astype(f32).astype(bf16)
    for z in range(peers // 2):
        both = jnp.concatenate([parts_ref[2 * z, 0:per, :], parts_ref[2 * z + 1, 0:per, :]], axis=1)
        grad_in_ref[:, z * 2 * width : (z + 1) * 2 * width] = mm(both, order)
        for c in range(2):
            at = c * half + z * share
            grad_out_ref[at : at + share, :] = parts_ref[2 * z + c, per:lines, :].astype(f32)


def sem(number):
    return pltpu.SemaphoreType.DMA((number,))


def run_expo(at, cols_t, own, other):
    dp, (width, bot) = (own.shape[0], cols_t.shape)
    big, small = ((dp, width, CAP), (dp, CAP))
    return call(
        expo_body,
        [(big, bf16), (small, f32), (small, f32)],
        (at, cols_t, own, other),
        in_specs=[SMEM, HBM, ANY, ANY],
        out_specs=[HBM, VMEM, VMEM],
        scratch=[
            pltpu.VMEM((width, bot), bf16),
            pltpu.VMEM((dp, 2, HALF, bot), bf16),
            pltpu.VMEM((dp, EXTRA, bot), bf16),
            pltpu.VMEM(big, bf16),
            pltpu.VMEM((width, 128), f32),
            *[sem(dp // GROUP)] * 4,
        ],
    )


def run_balance(expo, got, live):
    dp, width, _ = expo.shape
    small = pltpu.VMEM(live.shape, f32)
    return call(
        balance_body,
        [(live.shape, f32)],
        (expo, got, live),
        in_specs=[HBM, VMEM, VMEM],
        scratch=[pltpu.VMEM(expo.shape, bf16), pltpu.VMEM((width, 128), f32), small, sem(dp // GROUP)],
    )[0]


def run_last(at, expo, got, live, cols):
    dp, width, _ = expo.shape
    halves = (dp, LINES, HALF)
    return call(
        last_body,
        [(halves, bf16), (halves, bf16), ((width, 128), f32)],
        (at, expo, got, live, cols),
        in_specs=[SMEM, HBM, VMEM, VMEM, VMEM],
        out_specs=[ANY, ANY, HBM],
        scratch=[
            pltpu.VMEM(expo.shape, bf16),
            pltpu.VMEM((width, 128), f32),
            pltpu.VMEM(live.shape, f32),
            pltpu.VMEM((2, *halves), bf16),
            *[sem(dp // GROUP)] * 3,
        ],
    )


def run_student(at, cols_t, cols, rows):
    dp = rows.shape[0]
    big, halves = ((dp, cols.shape[1], CAP), (dp, LINES, HALF))
    return call(
        student_body,
        [(big, bf16), (halves, bf16), (halves, bf16)],
        (at, cols_t, cols, rows),
        in_specs=[SMEM, VMEM, VMEM, HBM],
        out_specs=[HBM, ANY, ANY],
        scratch=[
            pltpu.VMEM(rows.shape, bf16),
            pltpu.VMEM(big, bf16),
            pltpu.VMEM((2, *halves), bf16),
            *[sem(dp // GROUP)] * 4,
        ],
    )


def run_columns_grad(expo, raised, scale, got, rows, proto, norm):
    dp, held = (expo.shape[0], pltpu.VMEM(expo.shape, bf16))
    return call(
        columns_grad_body,
        [(proto.shape, f32)],
        (expo, raised, scale, got, rows, proto, norm),
        in_specs=[HBM] * 3 + [ANY] + [HBM] * 3,
        scratch=[
            pltpu.VMEM(scale.shape, f32),
            pltpu.VMEM(proto.shape, bf16),
            pltpu.VMEM(norm.shape, f32),
            held,
            held,
            pltpu.VMEM(proto.shape[::-1], f32),
            pltpu.VMEM((dp, EXTRA, CAP), bf16),
            pltpu.VMEM(rows.shape, bf16),
            *[sem(dp // GROUP)] * 4,
            sem(2),
        ],
    )[0]


def exchange(x, axis):
    return lax.all_to_all(x, axis, split_axis=0, concat_axis=0, tiled=True)


def sibling(x):
    peers = lax.axis_size("tensor")
    return lax.ppermute(x, "tensor", [(i, i ^ 1) for i in range(peers)])


def everywhere(part):
    both = part + sibling(part)
    near, far, last = (levels(both, by) for by in (1, 2, 3))
    (sums,) = call(relay_body, [((part.shape[0], *part.shape), bf16)], (both, near, far, last))
    return exchange(sums, "dp")


def levels(x, by):
    peers = lax.axis_size("tensor")
    return lax.ppermute(x, "tensor", [(i, i ^ (2 * by)) for i in range(peers)])


def level_sums(x):
    near, far, last = (levels(x, by) for by in (1, 2, 3))
    wide = lambda y: y.astype(f32)
    return (wide(x) + wide(near)) + (wide(far) + wide(last))


def paired(keep, give):
    return (keep.astype(f32) + sibling(give).astype(f32)).astype(bf16)


def slot_sums_body(parts_hbm, out_hbm, parts_ref, out_ref, sems, out_sem):
    peers = parts_hbm.shape[0]
    load = lambda q: pltpu.make_async_copy(group(parts_hbm, q), group(parts_ref, q), sems.at[q])
    start_all(peers // GROUP, load)
    acc = jnp.zeros(parts_ref.shape[1:], f32)
    for g in range(peers):
        if g % GROUP == 0:
            load(g // GROUP).wait()
        acc = acc + parts_ref[g].astype(f32)
    out_ref[0] = acc.astype(bf16)
    store = pltpu.make_async_copy(out_ref, out_hbm, out_sem.at[0])
    store.start()
    store.wait()


def slot_sums(parts):
    out = (1, *parts.shape[1:])
    return call(
        slot_sums_body,
        [(out, bf16)],
        (parts,),
        in_specs=[ANY],
        out_specs=[HBM],
        scratch=[pltpu.VMEM(parts.shape, bf16), pltpu.VMEM(out, bf16), sem(parts.shape[0] // GROUP), sem(1)],
    )[0]


def after(x, earlier):
    return lax.optimization_barrier((x, earlier))[0]


def parts_of(tokens, teacher_feats, masks, w_in, w_out, proto_student, proto_teacher):
    dim = tokens.shape[1]
    hid = w_in.shape[1]
    bot, width = proto_student.shape
    dp, tensor = (lax.axis_size("dp"), lax.axis_size("tensor"))
    per = w_in.shape[0]
    half = hid // 2
    share = w_out.shape[0] // 8
    t = lax.axis_index("tensor").astype(jnp.int32)
    at = jnp.stack([t % 2, t // 2])

    lines = per + w_out.shape[0] // 2 * bot // half
    (w_pack,) = call(
        weights_body,
        [((lines, half), bf16)],
        (at, w_in, w_out),
        in_specs=[SMEM, HBM, HBM],
        out_specs=[HBM],
        scratch=[pltpu.VMEM(w_in.shape, bf16), pltpu.VMEM(w_out.shape, bf16), pltpu.VMEM((lines, half), bf16), sem(2)],
    )
    w_all = lax.all_gather(w_pack, "dp", axis=0, tiled=True).reshape(dp, lines, half)
    dma = pltpu.SemaphoreType.DMA
    sems = dma((dp,))
    sel, send, member, mine = call(
        select_body,
        [((CAP, tokens.shape[0]), bf16), ((dp, HALF + EXTRA, bot), bf16), ((8, CAP), f32), ((EXTRA, CAP), bf16)],
        (at, masks, teacher_feats),
        in_specs=[SMEM, VMEM, VMEM],
        out_specs=[VMEM, HBM, HBM, HBM],
        scratch=[
            pltpu.VMEM((CAP, bot), bf16),
            pltpu.VMEM((HALF + EXTRA, bot), bf16),
            pltpu.VMEM((8, CAP), f32),
            pltpu.VMEM((EXTRA, CAP), bf16),
            sems,
            sem(2),
        ],
    )
    packs = exchange(send, "dp")
    others = sibling(packs)
    cols, student_t, teacher_t, norm = call(
        columns_body,
        [((bot, width), bf16), ((width, bot), bf16), ((width, bot), bf16), ((1, width), f32)],
        (proto_student, proto_teacher),
        out_specs=[HBM] * 4,
        scratch=[
            pltpu.VMEM((bot, width), bf16),
            pltpu.VMEM((width, bot), bf16),
            pltpu.VMEM((width, bot), bf16),
            pltpu.VMEM((1, width), f32),
            sem(4),
        ],
    )
    expo, part, live = run_expo(at, teacher_t, packs, others)
    (rows,) = call(
        tokens_body,
        [((CAP, dim), bf16)],
        (sel, tokens),
        in_specs=[VMEM, HBM],
        out_specs=[HBM],
        scratch=[pltpu.VMEM(tokens.shape, bf16), pltpu.VMEM((CAP, dim), bf16), sem(2)],
    )
    hidden, slope, feats, w_out_half = call(
        forward_body,
        [((CAP, half), bf16), ((CAP, half), f32), ((CAP, bot), f32), ((half, bot), bf16)],
        (rows, after(w_all, part)),
        in_specs=[HBM, HBM],
        out_specs=[HBM, HBM, VMEM, HBM],
        scratch=[
            pltpu.VMEM((CAP, dim), bf16),
            pltpu.VMEM((CAP, half), bf16),
            pltpu.VMEM((CAP, half), f32),
            pltpu.VMEM((dp, per, half), bf16),
            pltpu.VMEM((dp, share, half), bf16),
            pltpu.VMEM((half, bot), bf16),
            sem(3),
        ],
    )
    feats_other = sibling(feats)
    (student_rows,) = call(unit_body, [((CAP, bot), bf16)], (feats, feats_other))
    all_rows = lax.all_gather(student_rows, "dp", axis=0, tiled=True).reshape(dp, CAP, bot)
    got = everywhere(part)
    part = run_balance(expo, got, live)
    got = everywhere(part)
    keep, give, scale = run_last(at, expo, got, live, cols)
    pull = paired(keep, give)
    pull_got = exchange(pull, "dp")
    all_rows = after(all_rows, pull)
    raised, keep, give = run_student(at, student_t, cols, all_rows)
    push_got = exchange(paired(keep, give), "dp")
    pull = level_sums(slot_sums(pull_got))
    pull_other = sibling(pull)
    push = level_sums(slot_sums(push_got))
    push_other = sibling(push)
    back_lines = per + share + EXTRA
    send, grad_pre, loss = call(
        backward_body,
        [((dp, back_lines, bot), bf16), ((CAP, half), bf16), ((1, masks.shape[0]), f32)],
        (at, pull, pull_other, push, push_other, mine, member, feats, feats_other, rows, slope, hidden, w_out_half),
        in_specs=[SMEM] + [VMEM] * 8 + [HBM] * 4,
        out_specs=[HBM, HBM, VMEM],
        scratch=[
            pltpu.VMEM((half, bot), bf16),
            pltpu.VMEM((CAP, half), f32),
            pltpu.VMEM((CAP, half), bf16),
            pltpu.VMEM((CAP, dim), bf16),
            pltpu.VMEM((dp, back_lines, bot), bf16),
            pltpu.VMEM((CAP, half), bf16),
            pltpu.VMEM((half, bot), bf16),
            sems,
            sem(1),
            sem(4),
        ],
    )
    got = exchange(send, "dp")
    (grad_rows,) = call(
        backward_rows_body,
        [((CAP, dim), bf16)],
        (grad_pre, w_all),
        in_specs=[VMEM, HBM],
        out_specs=[HBM],
        scratch=[pltpu.VMEM((dp, per, half), bf16), pltpu.VMEM((CAP, dim), bf16), sem(1), sem(1)],
    )
    pieces = 4
    d_shape = (pieces, tokens.shape[0] // pieces, dim)
    (d_tokens,) = call(
        place_body,
        [(d_shape, bf16)],
        (sel, grad_rows, sibling(grad_rows)),
        out_specs=[HBM],
        scratch=[pltpu.VMEM(d_shape, bf16), dma((pieces,))],
    )
    got, d_tokens = lax.optimization_barrier((got, d_tokens))
    (sent,) = call(
        gather_grads_body,
        [((tensor, per + share, bot), bf16)],
        (got,),
        in_specs=[ANY],
        out_specs=[HBM],
        scratch=[pltpu.VMEM((dp, per + share, bot), bf16), pltpu.VMEM((per + share, bot), bf16), sems, sem(tensor)],
    )
    parts = exchange(sent, "tensor")
    grad_proto = run_columns_grad(expo, raised, scale, got, all_rows, proto_student, norm)
    grad_in, grad_out = call(weight_grads_body, [((per, hid), f32), ((w_out.shape[0], bot), f32)], (parts,))
    return (d_tokens.reshape(tokens.shape), grad_in, grad_out, grad_proto, loss.reshape(masks.shape[0]))


def solution(mesh):
    placed = (
        P("dp", None),
        P("dp", None),
        P("dp", None),
        P("dp", None),
        P("dp", None),
        P(None, ("dp", "tensor")),
        P(None, ("dp", "tensor")),
    )
    return jax.shard_map(
        parts_of,
        mesh=mesh,
        in_specs=placed,
        out_specs=(P("dp", None), P("dp", None), P("dp", None), P(None, ("dp", "tensor")), P("dp")),
        check_vma=False,
    )
```

```python
import jax
import jax.numpy as jnp
from jax import lax
from jax.experimental import pallas as pl
from jax.experimental.pallas import tpu as pltpu
from jax.sharding import PartitionSpec as P

CAP = 256
TEACHER_TEMP = 0.07
STUDENT_TEMP = 0.1
EPS = 1e-06
GRAD_SCALE = 65536.0
INTERPRET = False
f32, bf16 = (jnp.float32, jnp.bfloat16)
VMEM = pl.BlockSpec(memory_space=pltpu.VMEM)
HBM = pl.BlockSpec(memory_space=pltpu.HBM)
ANY = pl.BlockSpec(memory_space=pl.ANY)
SMEM = pl.BlockSpec(memory_space=pltpu.SMEM)
NT = (((1,), (1,)), ((), ()))
TN = (((0,), (0,)), ((), ()))
EXTRA = 16
HALF = CAP // 2
LINES = CAP + EXTRA
DEAD = 2.0
LOG2E = 1.4426950408889634


def mm(a, b, dims=None):
    if dims is None:
        return jnp.dot(a, b, preferred_element_type=f32)
    return lax.dot_general(a, b, dims, preferred_element_type=f32)


def call(body, outs, ins, out_specs=None, in_specs=None, scratch=()):
    specs = out_specs or [VMEM] * len(outs)
    in_specs = in_specs or [VMEM] * len(ins)
    ins = [pltpu.with_memory_space_constraint(x, pltpu.HBM) if spec is HBM else x for x, spec in zip(ins, in_specs)]
    outs = tuple(pltpu.HBM(*o) if spec is HBM else jax.ShapeDtypeStruct(*o) for o, spec in zip(outs, specs))
    return pl.pallas_call(
        body,
        out_shape=outs,
        in_specs=in_specs,
        out_specs=tuple(specs),
        scratch_shapes=list(scratch),
        interpret=INTERPRET,
        compiler_params=pltpu.CompilerParams(vmem_limit_bytes=48 << 20),
    )(*ins)


def iota(shape, dim):
    return lax.broadcasted_iota(jnp.int32, shape, dim)


def copies(pairs, sems):
    return [pltpu.make_async_copy(a, b, sems.at[i]) for i, (a, b) in enumerate(pairs)]


GROUP = 4
UNROLL = 4


def group(ref, q):
    return ref.at[pl.ds(q * GROUP, GROUP)]


def start_all(number, make):
    def go(i, _):
        make(i).start()
        return 0

    lax.fori_loop(0, number, go, 0)


def wait_all(number, make):
    def go(i, _):
        make(i).wait()
        return 0

    lax.fori_loop(0, number, go, 0)


def over_groups(peers, step, loads=(), stores=(), unroll=1):
    def go(q, _):
        for make in loads:
            make(q).wait()
        lax.fori_loop(0, GROUP, lambda i, _: step(q * GROUP + i), 0, unroll=unroll)
        for make in stores:
            make(q).start()
        return 0

    lax.fori_loop(0, peers // GROUP, go, 0)


def select_body(
    at_ref, mask_ref, feats_ref, sel_ref, send_hbm, member_hbm, mine_hbm, unit_ref, pack_ref, member_ref, mine_ref, sems, late_sems
):
    crops, patches = mask_ref.shape
    mask = mask_ref[...].astype(f32)
    upto = (iota((patches, patches), 0) <= iota((patches, patches), 1)).astype(f32).astype(bf16)
    rank = mm(mask.astype(bf16), upto)
    count = jnp.sum(mask, axis=1, keepdims=True)
    total = jnp.sum(count, axis=0, keepdims=True)
    slot = iota((CAP, patches), 0).astype(f32)
    lane = iota((1, CAP), 1).astype(f32)
    start = jnp.zeros((1, 1), f32)
    weight = jnp.zeros((1, CAP), f32)
    first = iota((CAP, patches), 1) == 0
    member_ref[...] = jnp.zeros_like(member_ref)
    for c in range(crops):
        hit = jnp.where((rank[c : c + 1] + start == slot + 1.0) & (mask[c : c + 1] > 0.0), 1.0, 0.0)
        if c == 0:
            hit = jnp.where(first & (slot >= total), 1.0, hit)
        sel_ref[:, c * patches : (c + 1) * patches] = hit.astype(bf16)
        own = count[c : c + 1]
        inside = jnp.where((lane >= start) & (lane < start + own), 1.0, 0.0)
        part = inside * (1.0 / jnp.maximum(own, 1.0))
        member_ref[c : c + 1, :] = part
        weight = weight + part
        start = start + own
    live = jnp.where(lane < total, 1.0, 0.0)
    picked = mm(sel_ref[...], feats_ref[...])
    scale = lax.rsqrt(jnp.sum(picked * picked, axis=1, keepdims=True) + EPS)
    dead = iota(picked.shape, 0).astype(f32) >= total
    mark = jnp.where(iota(picked.shape, 1) == 0, DEAD, 0.0)
    unit_ref[...] = jnp.where(dead, mark, picked * scale).astype(bf16)
    at = iota((EXTRA, CAP), 0)
    tail = jnp.where(at == 0, live, jnp.where(at == 1, weight * GRAD_SCALE, 0.0)).astype(bf16)
    mine_ref[...] = tail
    late = copies([(member_ref, member_hbm), (mine_ref, mine_hbm)], late_sems)
    for copy in late:
        copy.start()
    pack_ref[...] = unit_ref[pl.ds(pl.multiple_of(at_ref[0] * HALF, HALF), HALF), :]
    peers = send_hbm.shape[0]
    make = lambda g: pltpu.make_async_copy(pack_ref, send_hbm.at[g], sems.at[g])
    start_all(peers, make)
    for copy in late:
        copy.wait()
    wait_all(peers, make)


def columns_body(
    student_ref, teacher_ref, cols_hbm, student_t_hbm, teacher_t_hbm, norm_hbm, cols_ref, student_t_ref, teacher_t_ref, norm_ref, sems
):
    for part in chunks_of(student_ref.shape[1]):
        wide = student_ref[:, part].astype(f32)
        norm = jnp.sqrt(jnp.sum(wide * wide, axis=0, keepdims=True) + EPS)
        norm_ref[:, part] = norm
        unit = wide / norm
        cols_ref[:, part] = unit.astype(bf16)
        student_t_ref[part, :] = unit.T.astype(bf16)
        wide = teacher_ref[:, part].astype(f32)
        norm = jnp.sqrt(jnp.sum(wide * wide, axis=0, keepdims=True) + EPS)
        teacher_t_ref[part, :] = (wide / norm).T.astype(bf16)
    held = (cols_ref, student_t_ref, teacher_t_ref, norm_ref)
    stores = copies(list(zip(held, (cols_hbm, student_t_hbm, teacher_t_hbm, norm_hbm))), sems)
    for store in stores:
        store.start()
    for store in stores:
        store.wait()


def weights_body(at_ref, w_in_hbm, w_out_hbm, pack_hbm, w_in_ref, w_out_ref, pack_ref, sems):
    rows, hid = w_in_hbm.shape
    block, bot = w_out_hbm.shape
    half = block // 2
    loads = copies([(w_in_hbm, w_in_ref), (w_out_hbm, w_out_ref)], sems)
    for load in loads:
        load.start()
    core = at_ref[0]
    row = iota((2 * block, block), 0)
    col = iota((2 * block, block), 1)
    pick = (row == (col // half) * block + core * half + col % half).astype(f32).astype(bf16)
    for load in loads:
        load.wait()
    for p in range(hid // (2 * block)):
        two = w_in_ref[:, p * 2 * block : (p + 1) * 2 * block]
        pack_ref[0:rows, p * block : (p + 1) * block] = mm(two, pick).astype(bf16)
    lines = pack_ref.shape[0] - rows
    for q in range(half // lines):
        at = pl.multiple_of(core * half + q * lines, lines)
        pack_ref[rows : rows + lines, q * bot : (q + 1) * bot] = w_out_ref[pl.ds(at, lines), :]
    store = pltpu.make_async_copy(pack_ref, pack_hbm, sems.at[0])
    store.start()
    store.wait()


def w_in_load(w_hbm, w_in_ref, at):
    return pltpu.make_async_copy(w_hbm.at[:, 0 : w_in_ref.shape[1], :], w_in_ref, at)


def w_in_of(w_in_ref, part):
    peers, rows, _ = w_in_ref.shape
    return w_in_ref[:, :, part].reshape(peers * rows, part.stop - part.start)


def tokens_body(sel_ref, tokens_hbm, rows_hbm, tokens_ref, rows_ref, sems):
    load = pltpu.make_async_copy(tokens_hbm, tokens_ref, sems.at[0])
    load.start()
    load.wait()
    rows_ref[...] = mm(sel_ref[...], tokens_ref[...]).astype(bf16)
    store = pltpu.make_async_copy(rows_ref, rows_hbm, sems.at[1])
    store.start()
    store.wait()


def forward_body(
    rows_hbm, w_hbm, hidden_hbm, slope_hbm, feats_ref, w_out_hbm,
    rows_ref, hidden_ref, slope_ref, w_in_ref, lines_ref, w_out_ref, own_sems,
):
    first = pltpu.make_async_copy(rows_hbm, rows_ref, own_sems.at[0])
    first.start()
    per, lines = (w_in_ref.shape[1], lines_ref.shape[1])
    loads = [
        pltpu.make_async_copy(w_hbm.at[:, per : per + lines, :], lines_ref, own_sems.at[1]),
    ]
    parts = chunks_of(hidden_ref.shape[1])
    for i, part in enumerate(parts):
        source = w_hbm.at[:, 0:per, part]
        loads.append(pltpu.make_async_copy(source, w_in_ref.at[:, :, part], own_sems.at[2 + i]))
    for load in loads:
        load.start()
    first.wait()
    loads[0].wait()
    bot = w_out_ref.shape[1]
    quarters = lines_ref.shape[2] // bot
    for g in range(lines_ref.shape[0]):
        for q in range(quarters):
            at = (g * quarters + q) * lines
            w_out_ref[at : at + lines, :] = lines_ref[g, :, q * bot : (q + 1) * bot]
    keeps = [pltpu.make_async_copy(w_out_ref, w_out_hbm, own_sems.at[0])]
    for keep in keeps:
        keep.start()
    rows = rows_ref[...]
    feats = jnp.zeros(feats_ref.shape, f32)
    for load, part in zip(loads[1:], parts):
        load.wait()
        pre = mm(rows, w_in_of(w_in_ref, part))
        cdf = 0.5 * (1.0 + lax.erf(pre * 0.7071067811865476))
        slope_ref[:, part] = cdf + pre * (jnp.exp(-0.5 * pre * pre) * 0.3989422804014327)
        hidden = (pre * cdf).astype(bf16)
        hidden_ref[:, part] = hidden
        feats = feats + mm(hidden, w_out_ref[part, :])
    feats_ref[...] = feats
    pairs = [(hidden_ref, hidden_hbm), (slope_ref, slope_hbm)]
    stores = [pltpu.make_async_copy(a, b, own_sems.at[1 + i]) for i, (a, b) in enumerate(pairs)]
    for store in stores:
        store.start()
    for store in keeps + stores:
        store.wait()


def unit_of(feats_ref, other_ref):
    feats = feats_ref[...] + other_ref[...]
    inv = lax.rsqrt(jnp.sum(feats * feats, axis=1, keepdims=True) + EPS)
    return (feats * inv, inv)


def unit_body(feats_ref, other_ref, rows_ref):
    rows_ref[...] = unit_of(feats_ref, other_ref)[0].astype(bf16)


def chunks_of(width):
    step = min(256, width)
    return [slice(at, at + step) for at in range(0, width, step)]


def row_of(ref, g):
    return ref[pl.ds(g, 1), :]


def fold(x):
    return x.reshape(x.shape[0] // 8, 8, x.shape[1]).sum(axis=0)


def expo_body(
    at_ref, cols_hbm, own_hbm, other_hbm, expo_hbm, part_ref, live_ref,
    cols_ref, rows_ref, expo_ref, total_ref, sems, own_sems, other_sems, cols_sem,
):
    peers = own_hbm.shape[0]
    width = cols_ref.shape[0]
    core = at_ref[0]
    number = peers // GROUP
    rows_at = lambda q, c: rows_ref.at[pl.ds(q * GROUP, GROUP), c]
    load_own = lambda q: pltpu.make_async_copy(group(own_hbm, q), rows_at(q, core), own_sems.at[q])
    load_other = lambda q: pltpu.make_async_copy(group(other_hbm, q), rows_at(q, 1 - core), other_sems.at[q])
    store = lambda q: pltpu.make_async_copy(group(expo_ref, q), group(expo_hbm, q), sems.at[q])
    load_cols = pltpu.make_async_copy(cols_hbm, cols_ref, cols_sem.at[0])
    load_cols.start()
    start_all(number, load_own)
    start_all(number, load_other)
    total_ref[...] = jnp.zeros_like(total_ref)
    lead = ((iota((EXTRA, cols_ref.shape[1]), 0) == 0) & (iota((EXTRA, cols_ref.shape[1]), 1) == 0)).astype(f32).astype(bf16)
    load_cols.wait()

    def first(g):
        rows = rows_ref[g].reshape(CAP, rows_ref.shape[3])
        live = jnp.where(mm(lead, rows, NT)[0:1] < 0.75 * DEAD, 1.0, 0.0)
        live_ref[pl.ds(g, 1), :] = live
        for part in chunks_of(width):
            cos = mm(cols_ref[part, :], rows, NT)
            expo = jnp.exp2(cos * (LOG2E / TEACHER_TEMP)) * live
            expo_ref[g, part, :] = expo.astype(bf16)
            total_ref[part, :] += expo[:, 0:128] + expo[:, 128:256]
        return 0

    over_groups(peers, first, (load_own, load_other), (store,), UNROLL)
    spread_scale(total_ref)
    row_parts(expo_ref, total_ref, part_ref)
    wait_all(number, store)


def spread_scale(total_ref):
    for part in chunks_of(total_ref.shape[0]):
        sums = jnp.sum(total_ref[part, :], axis=1, keepdims=True)
        total_ref[part, :] = jnp.broadcast_to(1.0 / sums, sums.shape[:1] + (128,))


def scaled(expo, scale):
    return jnp.concatenate([expo[:, 0:128] * scale, expo[:, 128:256] * scale], axis=1)


def row_parts(expo_ref, scale_ref, part_ref):
    def step(g):
        acc = jnp.zeros((8, CAP), f32)
        for part in chunks_of(scale_ref.shape[0]):
            acc = acc + fold(scaled(expo_ref[g, part, :].astype(f32), scale_ref[part, :]))
        part_ref[pl.ds(g, 1), :] = jnp.sum(acc, axis=0, keepdims=True)
        return 0

    over_groups(expo_ref.shape[0], step, unroll=UNROLL)


def relay_body(own_ref, near_ref, far_ref, last_ref, out_ref):
    sums = (own_ref[...] + near_ref[...]) + (far_ref[...] + last_ref[...])
    sums = sums.astype(bf16)
    for g in range(out_ref.shape[0]):
        out_ref[g] = sums


def scales_from(parts_ref, live_ref, scale_ref):
    sums = parts_ref[0].astype(f32)
    for g in range(1, parts_ref.shape[0]):
        sums = sums + parts_ref[g].astype(f32)
    live = live_ref[...]
    scale_ref[...] = live / (sums + 1.0 - live)


def column_sums(load, expo_ref, scale_ref, total_ref):
    total_ref[...] = jnp.zeros_like(total_ref)

    def step(g):
        row = row_of(scale_ref, g)
        for part in chunks_of(total_ref.shape[0]):
            expo = expo_ref[g, part, :].astype(f32)
            total_ref[part, :] += expo[:, 0:128] * row[:, 0:128] + expo[:, 128:256] * row[:, 128:256]
        return 0

    over_groups(expo_ref.shape[0], step, (load,), unroll=UNROLL)
    spread_scale(total_ref)


def balance_body(expo_hbm, parts_ref, live_ref, part_ref, expo_ref, total_ref, scale_ref, sems):
    load = lambda q: pltpu.make_async_copy(group(expo_hbm, q), group(expo_ref, q), sems.at[q])
    start_all(expo_ref.shape[0] // GROUP, load)
    scales_from(parts_ref, live_ref, scale_ref)
    column_sums(load, expo_ref, scale_ref, total_ref)
    row_parts(expo_ref, total_ref, part_ref)


def divide_up(g, acc, pull, halves_ref):
    rows = jnp.sum(acc, axis=0, keepdims=True)
    rows = jnp.where(iota((EXTRA, CAP), 0) == 0, rows, 0.0).astype(bf16)
    pull = pull.astype(bf16)
    for at, block in ((slice(0, CAP), pull), (slice(CAP, LINES), rows)):
        halves_ref[0, g, at, :] = block[:, 0:HALF]
        halves_ref[1, g, at, :] = block[:, HALF:CAP]


def last_body(
    at_ref, expo_hbm, parts_ref, live_ref, cols_ref, keep_hbm, give_hbm, total_hbm,
    expo_ref, total_ref, scale_ref, halves_ref, sems, keep_sems, give_sems,
):
    peers = expo_ref.shape[0]
    core = at_ref[0]
    load = lambda q: pltpu.make_async_copy(group(expo_hbm, q), group(expo_ref, q), sems.at[q])
    half_at = lambda c, q: halves_ref.at[c, pl.ds(q * GROUP, GROUP)]
    keep = lambda q: pltpu.make_async_copy(half_at(core, q), group(keep_hbm, q), keep_sems.at[q])
    give = lambda q: pltpu.make_async_copy(half_at(1 - core, q), group(give_hbm, q), give_sems.at[q])
    number = peers // GROUP
    start_all(number, load)
    scales_from(parts_ref, live_ref, scale_ref)
    column_sums(load, expo_ref, scale_ref, total_ref)

    def step(g):
        acc = jnp.zeros((8, CAP), f32)
        pull = jnp.zeros((cols_ref.shape[0], CAP), f32)
        for part in chunks_of(total_ref.shape[0]):
            balanced = scaled(expo_ref[g, part, :].astype(f32), total_ref[part, :])
            acc = acc + fold(balanced)
            pull = pull + mm(cols_ref[:, part], balanced.astype(bf16))
        divide_up(g, acc, pull, halves_ref)
        return 0

    spare = pltpu.make_async_copy(total_ref, total_hbm, sems.at[0])
    spare.start()
    over_groups(peers, step, (), (give, keep), UNROLL)
    wait_all(number, give)
    wait_all(number, keep)
    spare.wait()


def student_body(
    at_ref, cols_t_ref, cols_ref, rows_hbm, raised_hbm, keep_hbm, give_hbm,
    rows_ref, raised_ref, halves_ref, row_sems, sems, keep_sems, give_sems,
):
    peers = rows_ref.shape[0]
    load = lambda q: pltpu.make_async_copy(group(rows_hbm, q), group(rows_ref, q), row_sems.at[q])
    start_all(peers // GROUP, load)
    core = at_ref[0]
    width = cols_t_ref.shape[0]
    store = lambda q: pltpu.make_async_copy(group(raised_ref, q), group(raised_hbm, q), sems.at[q])
    half_at = lambda c, q: halves_ref.at[c, pl.ds(q * GROUP, GROUP)]
    keep = lambda q: pltpu.make_async_copy(half_at(core, q), group(keep_hbm, q), keep_sems.at[q])
    give = lambda q: pltpu.make_async_copy(half_at(1 - core, q), group(give_hbm, q), give_sems.at[q])
    number = peers // GROUP

    def step(g):
        rows = rows_ref[g]
        acc = jnp.zeros((8, CAP), f32)
        pull = jnp.zeros((cols_ref.shape[0], CAP), f32)
        for part in chunks_of(width):
            raised = jnp.exp2(mm(cols_t_ref[part, :], rows, NT) * (LOG2E / STUDENT_TEMP))
            acc = acc + fold(raised)
            raised = raised.astype(bf16)
            raised_ref[g, part, :] = raised
            pull = pull + mm(cols_ref[:, part], raised)
        divide_up(g, acc, pull, halves_ref)
        return 0

    over_groups(peers, step, (load,), (store, give, keep), UNROLL)
    for make in (give, keep, store):
        wait_all(number, make)


def columns_grad_body(
    expo_hbm, raised_hbm, scale_hbm, got_hbm, rows_hbm, proto_hbm, norm_hbm,
    grad_ref, scale_ref, proto_ref, norm_ref, expo_ref, raised_ref, acc_ref, tail_ref, rows_ref, esems, rsems, tail_sems, row_sems, late_sems,
):
    peers = expo_ref.shape[0]
    load = lambda q: pltpu.make_async_copy(group(expo_hbm, q), group(expo_ref, q), esems.at[q])
    load_raised = lambda q: pltpu.make_async_copy(group(raised_hbm, q), group(raised_ref, q), rsems.at[q])
    load_rows = lambda q: pltpu.make_async_copy(group(rows_hbm, q), group(rows_ref, q), row_sems.at[q])
    lines = got_hbm.shape[1] - EXTRA
    load_tail = pltpu.make_async_copy(got_hbm.at[:, lines : lines + EXTRA, :], tail_ref, tail_sems.at[0])
    load_scale = pltpu.make_async_copy(scale_hbm, scale_ref, tail_sems.at[1])
    late = copies([(proto_hbm, proto_ref), (norm_hbm, norm_ref)], late_sems)
    load_tail.start()
    load_scale.start()

    def begin(q, _):
        for make in (load_rows, load, load_raised):
            make(q).start()
        return 0

    lax.fori_loop(0, peers // GROUP, begin, 0)
    for copy in late:
        copy.start()
    acc_ref[...] = jnp.zeros_like(acc_ref)
    load_tail.wait()
    load_scale.wait()

    def step(g):
        tail = tail_ref[g].astype(f32)
        alpha = tail[0:1] + tail[1:2]
        beta = tail[2:3] + tail[3:4]
        rows = rows_ref[g]
        for part in chunks_of(acc_ref.shape[0]):
            balanced = scaled(expo_ref[g, part, :].astype(f32), scale_ref[part, :])
            score = raised_ref[g, part, :].astype(f32) * alpha - balanced * beta
            acc_ref[part, :] += mm(score.astype(bf16), rows)
        return 0

    over_groups(peers, step, (load_rows, load, load_raised), (), UNROLL)
    for copy in late:
        copy.wait()
    for part in chunks_of(acc_ref.shape[0]):
        grad = acc_ref[part, :].T
        norm = norm_ref[:, part]
        unit = proto_ref[:, part].astype(f32) / norm
        grad_ref[:, part] = (grad - unit * jnp.sum(unit * grad, axis=0, keepdims=True)) / norm


def join(core, own_ref, other_ref):
    own, other = (own_ref[0], other_ref[0])
    low = core == 0
    return jnp.concatenate([jnp.where(low, own, other), jnp.where(low, other, own)], axis=1)


def two_parts(x):
    high = x.astype(bf16)
    return (high.astype(f32), x - high.astype(f32))


def backward_body(
    at_ref, pull_ref, pull_other_ref, push_ref, push_other_ref, mine_ref, member_ref, feats_ref, feats_other_ref,
    rows_hbm, slope_hbm, hidden_hbm, w_out_hbm,
    send_hbm, pre_hbm, loss_ref, w_out_ref, slope_ref, hidden_ref, rows_ref, send_ref, pre_ref, out_ref, send_sems, pre_sem, load_sems,
):
    peers = send_ref.shape[0]
    sources = (w_out_hbm, slope_hbm, rows_hbm, hidden_hbm)
    loads = copies(list(zip(sources, (w_out_ref, slope_ref, rows_ref, hidden_ref))), load_sems)
    for load in loads:
        load.start()
    tail = mine_ref[...].astype(f32)
    live, weight = (tail[0:1], tail[1:2] * (1.0 / STUDENT_TEMP))
    pull = join(at_ref[0], pull_ref, pull_other_ref)
    push = join(at_ref[0], push_ref, push_other_ref)
    norm_sum = push[CAP : CAP + 1]
    push = push[0:CAP]
    scale = live / (pull[CAP : CAP + 1] + 1.0 - live)
    pull = pull[0:CAP]
    unit, inv = unit_of(feats_ref, feats_other_ref)
    inv = jnp.broadcast_to(inv, unit.shape).T[0:1]
    unit = unit.T
    cross = jnp.sum(unit.astype(bf16).astype(f32) * pull, axis=0, keepdims=True) * (1.0 / STUDENT_TEMP)
    row_loss = jnp.log(norm_sum) - scale * cross
    loss = jnp.sum(member_ref[...] * row_loss, axis=1, keepdims=True)
    square = (member_ref.shape[0], 128)
    loss = jnp.where(iota(square, 0) == iota(square, 1), loss, 0.0)
    loss_ref[...] = jnp.sum(loss, axis=0, keepdims=True)[:, 0 : loss_ref.shape[1]]
    alpha = weight / norm_sum
    beta = weight * scale
    grad_unit = push * alpha - pull * beta
    inner = jnp.sum(unit * grad_unit, axis=0, keepdims=True)
    grad_feats = (inv * (grad_unit - unit * inner)).T.astype(bf16)
    width = send_ref.shape[2]
    loads[0].wait()
    loads[1].wait()
    for part in chunks_of(hidden_ref.shape[1]):
        pre_ref[:, part] = (mm(grad_feats, w_out_ref[part, :], NT) * slope_ref[:, part]).astype(bf16)
    pre_out = pltpu.make_async_copy(pre_ref, pre_hbm, pre_sem.at[0])
    pre_out.start()
    loads[2].wait()
    loads[3].wait()
    for part in chunks_of(hidden_ref.shape[1]):
        out_ref[part, :] = mm(hidden_ref[:, part], grad_feats, TN).astype(bf16)
    level = at_ref[1]
    own = pre_ref[:, pl.ds(pl.multiple_of(level * width, width), width)]
    grad_in = mm(rows_ref[...], own, TN).astype(bf16)
    per = grad_in.shape[0] // peers
    block = out_ref.shape[0] // peers
    share = block // 4
    at = iota((EXTRA, CAP), 0)
    rows = jnp.zeros((EXTRA, CAP), f32)
    for i, x in enumerate(two_parts(alpha) + two_parts(beta)):
        rows = jnp.where(at == i, x, rows)
    rows = rows.astype(bf16)
    store = lambda g: pltpu.make_async_copy(send_ref.at[g], send_hbm.at[g], send_sems.at[g])
    for g in range(peers):
        send_ref[g, 0:per, :] = grad_in[g * per : (g + 1) * per, :]
        start = pl.multiple_of(g * block + level * share, share)
        send_ref[g, per : per + share, :] = out_ref[pl.ds(start, share), :]
        send_ref[g, per + share : per + share + EXTRA, :] = rows
        store(g).start()
    pre_out.wait()
    wait_all(peers, store)


def backward_rows_body(pre_ref, w_hbm, out_hbm, w_in_ref, out_ref, sem, out_sem):
    load = w_in_load(w_hbm, w_in_ref, sem.at[0])
    load.start()
    load.wait()
    w_in = w_in_of(w_in_ref, slice(0, w_in_ref.shape[2]))
    out_ref[...] = mm(pre_ref[...], w_in, NT).astype(bf16)
    store = pltpu.make_async_copy(out_ref, out_hbm, out_sem.at[0])
    store.start()
    store.wait()


def place_body(sel_ref, rows_ref, other_ref, out_hbm, out_ref, sems):
    rows = (rows_ref[...].astype(f32) + other_ref[...].astype(f32)).astype(bf16)
    pieces = out_ref.shape[0]
    size = out_ref.shape[1]
    store = lambda i: pltpu.make_async_copy(out_ref.at[i], out_hbm.at[i], sems.at[i])
    for i in range(pieces):
        out_ref[i] = mm(sel_ref[:, i * size : (i + 1) * size], rows, TN).astype(bf16)
        store(i).start()
    wait_all(pieces, store)


def gather_grads_body(got_hbm, send_hbm, got_ref, sum_ref, load_sems, sems):
    peers = got_hbm.shape[0]
    lines = sum_ref.shape[0]
    source = lambda q: got_hbm.at[pl.ds(q * GROUP, GROUP), 0:lines, :]
    load = lambda q: pltpu.make_async_copy(source(q), group(got_ref, q), load_sems.at[q])
    start_all(peers // GROUP, load)
    acc = jnp.zeros(got_ref.shape[1:], f32)
    for g in range(peers):
        if g % GROUP == 0:
            load(g // GROUP).wait()
        acc = acc + got_ref[g].astype(f32)
    sum_ref[...] = acc.astype(bf16)
    store = lambda t: pltpu.make_async_copy(sum_ref, send_hbm.at[t], sems.at[t])
    start_all(send_hbm.shape[0], store)
    wait_all(send_hbm.shape[0], store)


def weight_grads_body(parts_ref, grad_in_ref, grad_out_ref):
    peers, lines, width = parts_ref.shape
    per = grad_in_ref.shape[0]
    share = lines - per
    block = 2 * (width // 4)
    row = iota((2 * width, 2 * width), 0)
    col = iota((2 * width, 2 * width), 1)
    half = block // 2
    from_row = ((col % block) // half) * width + (col // block) * half + col % half
    order = (row == from_row).astype(f32).astype(bf16)
    for z in range(peers // 2):
        both = jnp.concatenate([parts_ref[2 * z, 0:per, :], parts_ref[2 * z + 1, 0:per, :]], axis=1)
        grad_in_ref[:, z * 2 * width : (z + 1) * 2 * width] = mm(both, order)
        for c in range(2):
            at = c * half + z * share
            grad_out_ref[at : at + share, :] = parts_ref[2 * z + c, per:lines, :].astype(f32)


def sem(number):
    return pltpu.SemaphoreType.DMA((number,))


def run_expo(at, cols_t, own, other):
    dp, (width, bot) = (own.shape[0], cols_t.shape)
    big, small = ((dp, width, CAP), (dp, CAP))
    return call(
        expo_body,
        [(big, bf16), (small, f32), (small, f32)],
        (at, cols_t, own, other),
        in_specs=[SMEM, HBM, ANY, ANY],
        out_specs=[HBM, VMEM, VMEM],
        scratch=[
            pltpu.VMEM((width, bot), bf16),
            pltpu.VMEM((dp, 2, HALF, bot), bf16),
            pltpu.VMEM(big, bf16),
            pltpu.VMEM((width, 128), f32),
            *[sem(dp // GROUP)] * 4,
        ],
    )


def run_balance(expo, got, live):
    dp, width, _ = expo.shape
    small = pltpu.VMEM(live.shape, f32)
    return call(
        balance_body,
        [(live.shape, f32)],
        (expo, got, live),
        in_specs=[HBM, VMEM, VMEM],
        scratch=[pltpu.VMEM(expo.shape, bf16), pltpu.VMEM((width, 128), f32), small, sem(dp // GROUP)],
    )[0]


def run_last(at, expo, got, live, cols):
    dp, width, _ = expo.shape
    halves = (dp, LINES, HALF)
    return call(
        last_body,
        [(halves, bf16), (halves, bf16), ((width, 128), f32)],
        (at, expo, got, live, cols),
        in_specs=[SMEM, HBM, VMEM, VMEM, VMEM],
        out_specs=[ANY, ANY, HBM],
        scratch=[
            pltpu.VMEM(expo.shape, bf16),
            pltpu.VMEM((width, 128), f32),
            pltpu.VMEM(live.shape, f32),
            pltpu.VMEM((2, *halves), bf16),
            *[sem(dp // GROUP)] * 3,
        ],
    )


def run_student(at, cols_t, cols, rows):
    dp = rows.shape[0]
    big, halves = ((dp, cols.shape[1], CAP), (dp, LINES, HALF))
    return call(
        student_body,
        [(big, bf16), (halves, bf16), (halves, bf16)],
        (at, cols_t, cols, rows),
        in_specs=[SMEM, VMEM, VMEM, HBM],
        out_specs=[HBM, ANY, ANY],
        scratch=[
            pltpu.VMEM(rows.shape, bf16),
            pltpu.VMEM(big, bf16),
            pltpu.VMEM((2, *halves), bf16),
            *[sem(dp // GROUP)] * 4,
        ],
    )


def run_columns_grad(expo, raised, scale, got, rows, proto, norm):
    dp, held = (expo.shape[0], pltpu.VMEM(expo.shape, bf16))
    return call(
        columns_grad_body,
        [(proto.shape, f32)],
        (expo, raised, scale, got, rows, proto, norm),
        in_specs=[HBM] * 3 + [ANY] + [HBM] * 3,
        scratch=[
            pltpu.VMEM(scale.shape, f32),
            pltpu.VMEM(proto.shape, bf16),
            pltpu.VMEM(norm.shape, f32),
            held,
            held,
            pltpu.VMEM(proto.shape[::-1], f32),
            pltpu.VMEM((dp, EXTRA, CAP), bf16),
            pltpu.VMEM(rows.shape, bf16),
            *[sem(dp // GROUP)] * 4,
            sem(2),
        ],
    )[0]


def exchange(x, axis):
    return lax.all_to_all(x, axis, split_axis=0, concat_axis=0, tiled=True)


def sibling(x):
    peers = lax.axis_size("tensor")
    return lax.ppermute(x, "tensor", [(i, i ^ 1) for i in range(peers)])


def everywhere(part):
    both = part + sibling(part)
    near, far, last = (levels(both, by) for by in (1, 2, 3))
    (sums,) = call(relay_body, [((part.shape[0], *part.shape), bf16)], (both, near, far, last))
    return exchange(sums, "dp")


def levels(x, by):
    peers = lax.axis_size("tensor")
    return lax.ppermute(x, "tensor", [(i, i ^ (2 * by)) for i in range(peers)])


def level_sums(x):
    near, far, last = (levels(x, by) for by in (1, 2, 3))
    wide = lambda y: y.astype(f32)
    return (wide(x) + wide(near)) + (wide(far) + wide(last))


def paired(keep, give):
    return (keep.astype(f32) + sibling(give).astype(f32)).astype(bf16)


def slot_sums_body(parts_hbm, out_hbm, parts_ref, out_ref, sems, out_sem):
    peers = parts_hbm.shape[0]
    load = lambda q: pltpu.make_async_copy(group(parts_hbm, q), group(parts_ref, q), sems.at[q])
    start_all(peers // GROUP, load)
    acc = jnp.zeros(parts_ref.shape[1:], f32)
    for g in range(peers):
        if g % GROUP == 0:
            load(g // GROUP).wait()
        acc = acc + parts_ref[g].astype(f32)
    out_ref[0] = acc.astype(bf16)
    store = pltpu.make_async_copy(out_ref, out_hbm, out_sem.at[0])
    store.start()
    store.wait()


def slot_sums(parts):
    out = (1, *parts.shape[1:])
    return call(
        slot_sums_body,
        [(out, bf16)],
        (parts,),
        in_specs=[ANY],
        out_specs=[HBM],
        scratch=[pltpu.VMEM(parts.shape, bf16), pltpu.VMEM(out, bf16), sem(parts.shape[0] // GROUP), sem(1)],
    )[0]


def after(x, earlier):
    return lax.optimization_barrier((x, earlier))[0]


def parts_of(tokens, teacher_feats, masks, w_in, w_out, proto_student, proto_teacher):
    dim = tokens.shape[1]
    hid = w_in.shape[1]
    bot, width = proto_student.shape
    dp, tensor = (lax.axis_size("dp"), lax.axis_size("tensor"))
    per = w_in.shape[0]
    half = hid // 2
    share = w_out.shape[0] // 8
    t = lax.axis_index("tensor").astype(jnp.int32)
    at = jnp.stack([t % 2, t // 2])

    lines = per + w_out.shape[0] // 2 * bot // half
    (w_pack,) = call(
        weights_body,
        [((lines, half), bf16)],
        (at, w_in, w_out),
        in_specs=[SMEM, HBM, HBM],
        out_specs=[HBM],
        scratch=[pltpu.VMEM(w_in.shape, bf16), pltpu.VMEM(w_out.shape, bf16), pltpu.VMEM((lines, half), bf16), sem(2)],
    )
    w_all = lax.all_gather(w_pack, "dp", axis=0, tiled=True).reshape(dp, lines, half)
    dma = pltpu.SemaphoreType.DMA
    sems = dma((dp,))
    sel, send, member, mine = call(
        select_body,
        [((CAP, tokens.shape[0]), bf16), ((dp, HALF, bot), bf16), ((8, CAP), f32), ((EXTRA, CAP), bf16)],
        (at, masks, teacher_feats),
        in_specs=[SMEM, VMEM, VMEM],
        out_specs=[VMEM, HBM, HBM, HBM],
        scratch=[
            pltpu.VMEM((CAP, bot), bf16),
            pltpu.VMEM((HALF, bot), bf16),
            pltpu.VMEM((8, CAP), f32),
            pltpu.VMEM((EXTRA, CAP), bf16),
            sems,
            sem(2),
        ],
    )
    packs = exchange(send, "dp")
    others = sibling(packs)
    cols, student_t, teacher_t, norm = call(
        columns_body,
        [((bot, width), bf16), ((width, bot), bf16), ((width, bot), bf16), ((1, width), f32)],
        (proto_student, proto_teacher),
        out_specs=[HBM] * 4,
        scratch=[
            pltpu.VMEM((bot, width), bf16),
            pltpu.VMEM((width, bot), bf16),
            pltpu.VMEM((width, bot), bf16),
            pltpu.VMEM((1, width), f32),
            sem(4),
        ],
    )
    expo, part, live = run_expo(at, teacher_t, packs, others)
    (rows,) = call(
        tokens_body,
        [((CAP, dim), bf16)],
        (sel, tokens),
        in_specs=[VMEM, HBM],
        out_specs=[HBM],
        scratch=[pltpu.VMEM(tokens.shape, bf16), pltpu.VMEM((CAP, dim), bf16), sem(2)],
    )
    hidden, slope, feats, w_out_half = call(
        forward_body,
        [((CAP, half), bf16), ((CAP, half), f32), ((CAP, bot), f32), ((half, bot), bf16)],
        (rows, after(w_all, part)),
        in_specs=[HBM, HBM],
        out_specs=[HBM, HBM, VMEM, HBM],
        scratch=[
            pltpu.VMEM((CAP, dim), bf16),
            pltpu.VMEM((CAP, half), bf16),
            pltpu.VMEM((CAP, half), f32),
            pltpu.VMEM((dp, per, half), bf16),
            pltpu.VMEM((dp, share, half), bf16),
            pltpu.VMEM((half, bot), bf16),
            sem(2 + len(chunks_of(half))),
        ],
    )
    feats_other = sibling(feats)
    (student_rows,) = call(unit_body, [((CAP, bot), bf16)], (feats, feats_other))
    all_rows = lax.all_gather(student_rows, "dp", axis=0, tiled=True).reshape(dp, CAP, bot)
    got = everywhere(part)
    part = run_balance(expo, got, live)
    got = everywhere(part)
    keep, give, scale = run_last(at, expo, got, live, cols)
    pull = paired(keep, give)
    pull_got = exchange(pull, "dp")
    all_rows = after(all_rows, pull)
    raised, keep, give = run_student(at, student_t, cols, all_rows)
    push_got = exchange(paired(keep, give), "dp")
    pull = level_sums(slot_sums(pull_got))
    pull_other = sibling(pull)
    push = level_sums(slot_sums(push_got))
    push_other = sibling(push)
    back_lines = per + share + EXTRA
    send, grad_pre, loss = call(
        backward_body,
        [((dp, back_lines, bot), bf16), ((CAP, half), bf16), ((1, masks.shape[0]), f32)],
        (at, pull, pull_other, push, push_other, mine, member, feats, feats_other, rows, slope, hidden, w_out_half),
        in_specs=[SMEM] + [VMEM] * 8 + [HBM] * 4,
        out_specs=[HBM, HBM, VMEM],
        scratch=[
            pltpu.VMEM((half, bot), bf16),
            pltpu.VMEM((CAP, half), f32),
            pltpu.VMEM((CAP, half), bf16),
            pltpu.VMEM((CAP, dim), bf16),
            pltpu.VMEM((dp, back_lines, bot), bf16),
            pltpu.VMEM((CAP, half), bf16),
            pltpu.VMEM((half, bot), bf16),
            sems,
            sem(1),
            sem(4),
        ],
    )
    got = exchange(send, "dp")
    (grad_rows,) = call(
        backward_rows_body,
        [((CAP, dim), bf16)],
        (grad_pre, w_all),
        in_specs=[VMEM, HBM],
        out_specs=[HBM],
        scratch=[pltpu.VMEM((dp, per, half), bf16), pltpu.VMEM((CAP, dim), bf16), sem(1), sem(1)],
    )
    pieces = 4
    d_shape = (pieces, tokens.shape[0] // pieces, dim)
    (d_tokens,) = call(
        place_body,
        [(d_shape, bf16)],
        (sel, grad_rows, sibling(grad_rows)),
        out_specs=[HBM],
        scratch=[pltpu.VMEM(d_shape, bf16), dma((pieces,))],
    )
    got, d_tokens = lax.optimization_barrier((got, d_tokens))
    (sent,) = call(
        gather_grads_body,
        [((tensor, per + share, bot), bf16)],
        (got,),
        in_specs=[ANY],
        out_specs=[HBM],
        scratch=[pltpu.VMEM((dp, per + share, bot), bf16), pltpu.VMEM((per + share, bot), bf16), sems, sem(tensor)],
    )
    parts = exchange(sent, "tensor")
    grad_proto = run_columns_grad(expo, raised, scale, got, all_rows, proto_student, norm)
    grad_in, grad_out = call(weight_grads_body, [((per, hid), f32), ((w_out.shape[0], bot), f32)], (parts,))
    return (d_tokens.reshape(tokens.shape), grad_in, grad_out, grad_proto, loss.reshape(masks.shape[0]))


def solution(mesh):
    placed = (
        P("dp", None),
        P("dp", None),
        P("dp", None),
        P("dp", None),
        P("dp", None),
        P(None, ("dp", "tensor")),
        P(None, ("dp", "tensor")),
    )
    return jax.shard_map(
        parts_of,
        mesh=mesh,
        in_specs=placed,
        out_specs=(P("dp", None), P("dp", None), P("dp", None), P(None, ("dp", "tensor")), P("dp")),
        check_vma=False,
    )
```

```python
import jax
import jax.numpy as jnp
from jax import lax
from jax.experimental import pallas as pl
from jax.experimental.pallas import tpu as pltpu
from jax.sharding import PartitionSpec as P

CAP = 256
TEACHER_TEMP = 0.07
STUDENT_TEMP = 0.1
EPS = 1e-06
GRAD_SCALE = 65536.0
INTERPRET = False
f32, bf16 = (jnp.float32, jnp.bfloat16)
VMEM = pl.BlockSpec(memory_space=pltpu.VMEM)
HBM = pl.BlockSpec(memory_space=pltpu.HBM)
ANY = pl.BlockSpec(memory_space=pl.ANY)
SMEM = pl.BlockSpec(memory_space=pltpu.SMEM)
NT = (((1,), (1,)), ((), ()))
TN = (((0,), (0,)), ((), ()))
EXTRA = 16
HALF = CAP // 2
LINES = CAP + EXTRA
DEAD = 2.0
LOG2E = 1.4426950408889634


def mm(a, b, dims=None):
    if dims is None:
        return jnp.dot(a, b, preferred_element_type=f32)
    return lax.dot_general(a, b, dims, preferred_element_type=f32)


def call(body, outs, ins, out_specs=None, in_specs=None, scratch=()):
    specs = out_specs or [VMEM] * len(outs)
    in_specs = in_specs or [VMEM] * len(ins)
    ins = [pltpu.with_memory_space_constraint(x, pltpu.HBM) if spec is HBM else x for x, spec in zip(ins, in_specs)]
    outs = tuple(pltpu.HBM(*o) if spec is HBM else jax.ShapeDtypeStruct(*o) for o, spec in zip(outs, specs))
    return pl.pallas_call(
        body,
        out_shape=outs,
        in_specs=in_specs,
        out_specs=tuple(specs),
        scratch_shapes=list(scratch),
        interpret=INTERPRET,
        compiler_params=pltpu.CompilerParams(vmem_limit_bytes=48 << 20),
    )(*ins)


def iota(shape, dim):
    return lax.broadcasted_iota(jnp.int32, shape, dim)


def copies(pairs, sems):
    return [pltpu.make_async_copy(a, b, sems.at[i]) for i, (a, b) in enumerate(pairs)]


GROUP = 4
UNROLL = 4


def group(ref, q):
    return ref.at[pl.ds(q * GROUP, GROUP)]


def start_all(number, make):
    def go(i, _):
        make(i).start()
        return 0

    lax.fori_loop(0, number, go, 0)


def wait_all(number, make):
    def go(i, _):
        make(i).wait()
        return 0

    lax.fori_loop(0, number, go, 0)


def over_groups(peers, step, loads=(), stores=(), unroll=1):
    def go(q, _):
        for make in loads:
            make(q).wait()
        lax.fori_loop(0, GROUP, lambda i, _: step(q * GROUP + i), 0, unroll=unroll)
        for make in stores:
            make(q).start()
        return 0

    lax.fori_loop(0, peers // GROUP, go, 0)


def select_body(
    at_ref, mask_ref, feats_ref, sel_ref, send_hbm, member_hbm, mine_hbm, unit_ref, pack_ref, member_ref, mine_ref, sems, late_sems
):
    crops, patches = mask_ref.shape
    mask = mask_ref[...].astype(f32)
    upto = (iota((patches, patches), 0) <= iota((patches, patches), 1)).astype(f32).astype(bf16)
    rank = mm(mask.astype(bf16), upto)
    count = jnp.sum(mask, axis=1, keepdims=True)
    total = jnp.sum(count, axis=0, keepdims=True)
    slot = iota((CAP, patches), 0).astype(f32)
    lane = iota((1, CAP), 1).astype(f32)
    start = jnp.zeros((1, 1), f32)
    weight = jnp.zeros((1, CAP), f32)
    first = iota((CAP, patches), 1) == 0
    member_ref[...] = jnp.zeros_like(member_ref)
    for c in range(crops):
        hit = jnp.where((rank[c : c + 1] + start == slot + 1.0) & (mask[c : c + 1] > 0.0), 1.0, 0.0)
        if c == 0:
            hit = jnp.where(first & (slot >= total), 1.0, hit)
        sel_ref[:, c * patches : (c + 1) * patches] = hit.astype(bf16)
        own = count[c : c + 1]
        inside = jnp.where((lane >= start) & (lane < start + own), 1.0, 0.0)
        part = inside * (1.0 / jnp.maximum(own, 1.0))
        member_ref[c : c + 1, :] = part
        weight = weight + part
        start = start + own
    live = jnp.where(lane < total, 1.0, 0.0)
    picked = mm(sel_ref[...], feats_ref[...])
    scale = lax.rsqrt(jnp.sum(picked * picked, axis=1, keepdims=True) + EPS)
    dead = iota(picked.shape, 0).astype(f32) >= total
    mark = jnp.where(iota(picked.shape, 1) == 0, DEAD, 0.0)
    unit_ref[...] = jnp.where(dead, mark, picked * scale).astype(bf16)
    at = iota((EXTRA, CAP), 0)
    tail = jnp.where(at == 0, live, jnp.where(at == 1, weight * GRAD_SCALE, 0.0)).astype(bf16)
    mine_ref[...] = tail
    late = copies([(member_ref, member_hbm), (mine_ref, mine_hbm)], late_sems)
    for copy in late:
        copy.start()
    pack_ref[...] = unit_ref[pl.ds(pl.multiple_of(at_ref[0] * HALF, HALF), HALF), :]
    peers = send_hbm.shape[0]
    make = lambda g: pltpu.make_async_copy(pack_ref, send_hbm.at[g], sems.at[g])
    start_all(peers, make)
    for copy in late:
        copy.wait()
    wait_all(peers, make)


def columns_body(
    student_ref, teacher_ref, cols_hbm, student_t_hbm, teacher_t_hbm, norm_hbm, cols_ref, student_t_ref, teacher_t_ref, norm_ref, sems
):
    for part in chunks_of(student_ref.shape[1]):
        wide = student_ref[:, part].astype(f32)
        norm = jnp.sqrt(jnp.sum(wide * wide, axis=0, keepdims=True) + EPS)
        norm_ref[:, part] = norm
        unit = wide / norm
        cols_ref[:, part] = unit.astype(bf16)
        student_t_ref[part, :] = unit.T.astype(bf16)
        wide = teacher_ref[:, part].astype(f32)
        norm = jnp.sqrt(jnp.sum(wide * wide, axis=0, keepdims=True) + EPS)
        teacher_t_ref[part, :] = (wide / norm).T.astype(bf16)
    held = (cols_ref, student_t_ref, teacher_t_ref, norm_ref)
    stores = copies(list(zip(held, (cols_hbm, student_t_hbm, teacher_t_hbm, norm_hbm))), sems)
    for store in stores:
        store.start()
    for store in stores:
        store.wait()


def weights_body(at_ref, w_in_hbm, w_out_hbm, pack_hbm, w_in_ref, w_out_ref, pack_ref, sems):
    rows, hid = w_in_hbm.shape
    block, bot = w_out_hbm.shape
    half = block // 2
    parts = [slice(0, hid // 2), slice(hid // 2, hid)]
    pairs = [(w_out_hbm, w_out_ref)] + [(w_in_hbm.at[:, part], w_in_ref.at[:, part]) for part in parts]
    loads = copies(pairs, sems)
    for load in loads:
        load.start()
    core = at_ref[0]
    row = iota((2 * block, block), 0)
    col = iota((2 * block, block), 1)
    pick = (row == (col // half) * block + core * half + col % half).astype(f32).astype(bf16)
    loads[0].wait()
    lines = pack_ref.shape[0] - rows
    for q in range(half // lines):
        at = pl.multiple_of(core * half + q * lines, lines)
        pack_ref[rows : rows + lines, q * bot : (q + 1) * bot] = w_out_ref[pl.ds(at, lines), :]
    count = hid // (4 * block)
    stores = []
    for i in range(2):
        loads[1 + i].wait()
        for p in range(i * count, (i + 1) * count):
            two = w_in_ref[:, p * 2 * block : (p + 1) * 2 * block]
            pack_ref[0:rows, p * block : (p + 1) * block] = mm(two, pick).astype(bf16)
        done = slice(i * count * block, (i + 1) * count * block)
        store = pltpu.make_async_copy(pack_ref.at[:, done], pack_hbm.at[:, done], sems.at[3 + i])
        store.start()
        stores.append(store)
    for store in stores:
        store.wait()


def w_in_load(w_hbm, w_in_ref, at):
    return pltpu.make_async_copy(w_hbm.at[:, 0 : w_in_ref.shape[1], :], w_in_ref, at)


def w_in_of(w_in_ref, part):
    peers, rows, _ = w_in_ref.shape
    return w_in_ref[:, :, part].reshape(peers * rows, part.stop - part.start)


def tokens_body(sel_ref, tokens_hbm, rows_hbm, tokens_ref, rows_ref, sems):
    load = pltpu.make_async_copy(tokens_hbm, tokens_ref, sems.at[0])
    load.start()
    load.wait()
    rows_ref[...] = mm(sel_ref[...], tokens_ref[...]).astype(bf16)
    store = pltpu.make_async_copy(rows_ref, rows_hbm, sems.at[1])
    store.start()
    store.wait()


def forward_body(
    rows_hbm, w_hbm, hidden_hbm, slope_hbm, feats_ref, w_out_hbm,
    rows_ref, hidden_ref, slope_ref, w_in_ref, lines_ref, w_out_ref, own_sems,
):
    first = pltpu.make_async_copy(rows_hbm, rows_ref, own_sems.at[0])
    first.start()
    per, lines = (w_in_ref.shape[1], lines_ref.shape[1])
    loads = [
        pltpu.make_async_copy(w_hbm.at[:, per : per + lines, :], lines_ref, own_sems.at[1]),
    ]
    parts = chunks_of(hidden_ref.shape[1])
    for i, part in enumerate(parts):
        source = w_hbm.at[:, 0:per, part]
        loads.append(pltpu.make_async_copy(source, w_in_ref.at[:, :, part], own_sems.at[2 + i]))
    for load in loads:
        load.start()
    first.wait()
    loads[0].wait()
    bot = w_out_ref.shape[1]
    quarters = lines_ref.shape[2] // bot
    for g in range(lines_ref.shape[0]):
        for q in range(quarters):
            at = (g * quarters + q) * lines
            w_out_ref[at : at + lines, :] = lines_ref[g, :, q * bot : (q + 1) * bot]
    keeps = [pltpu.make_async_copy(w_out_ref, w_out_hbm, own_sems.at[0])]
    for keep in keeps:
        keep.start()
    rows = rows_ref[...]
    feats = jnp.zeros(feats_ref.shape, f32)
    for load, part in zip(loads[1:], parts):
        load.wait()
        pre = mm(rows, w_in_of(w_in_ref, part))
        cdf = 0.5 * (1.0 + lax.erf(pre * 0.7071067811865476))
        slope_ref[:, part] = cdf + pre * (jnp.exp(-0.5 * pre * pre) * 0.3989422804014327)
        hidden = (pre * cdf).astype(bf16)
        hidden_ref[:, part] = hidden
        feats = feats + mm(hidden, w_out_ref[part, :])
    feats_ref[...] = feats
    pairs = [(hidden_ref, hidden_hbm), (slope_ref, slope_hbm)]
    stores = [pltpu.make_async_copy(a, b, own_sems.at[1 + i]) for i, (a, b) in enumerate(pairs)]
    for store in stores:
        store.start()
    for store in keeps + stores:
        store.wait()


def unit_of(feats_ref, other_ref):
    feats = feats_ref[...] + other_ref[...]
    inv = lax.rsqrt(jnp.sum(feats * feats, axis=1, keepdims=True) + EPS)
    return (feats * inv, inv)


def unit_body(feats_ref, other_ref, rows_ref):
    rows_ref[...] = unit_of(feats_ref, other_ref)[0].astype(bf16)


def chunks_of(width):
    step = min(256, width)
    return [slice(at, at + step) for at in range(0, width, step)]


def row_of(ref, g):
    return ref[pl.ds(g, 1), :]


def fold(x):
    return x.reshape(x.shape[0] // 8, 8, x.shape[1]).sum(axis=0)


def expo_body(
    at_ref, cols_hbm, own_hbm, other_hbm, expo_hbm, part_ref, live_ref,
    cols_ref, rows_ref, expo_ref, total_ref, sems, own_sems, other_sems, cols_sem,
):
    peers = own_hbm.shape[0]
    width = cols_ref.shape[0]
    core = at_ref[0]
    number = peers // GROUP
    rows_at = lambda q, c: rows_ref.at[pl.ds(q * GROUP, GROUP), c]
    load_own = lambda q: pltpu.make_async_copy(group(own_hbm, q), rows_at(q, core), own_sems.at[q])
    load_other = lambda q: pltpu.make_async_copy(group(other_hbm, q), rows_at(q, 1 - core), other_sems.at[q])
    store = lambda q: pltpu.make_async_copy(group(expo_ref, q), group(expo_hbm, q), sems.at[q])
    load_cols = pltpu.make_async_copy(cols_hbm, cols_ref, cols_sem.at[0])
    load_cols.start()
    start_all(number, load_own)
    start_all(number, load_other)
    total_ref[...] = jnp.zeros_like(total_ref)
    lead = ((iota((EXTRA, cols_ref.shape[1]), 0) == 0) & (iota((EXTRA, cols_ref.shape[1]), 1) == 0)).astype(f32).astype(bf16)
    load_cols.wait()

    def first(g):
        rows = rows_ref[g].reshape(CAP, rows_ref.shape[3])
        live = jnp.where(mm(lead, rows, NT)[0:1] < 0.75 * DEAD, 1.0, 0.0)
        live_ref[pl.ds(g, 1), :] = live
        for part in chunks_of(width):
            cos = mm(cols_ref[part, :], rows, NT)
            expo = jnp.exp2(cos * (LOG2E / TEACHER_TEMP)) * live
            expo_ref[g, part, :] = expo.astype(bf16)
            total_ref[part, :] += expo[:, 0:128] + expo[:, 128:256]
        return 0

    over_groups(peers, first, (load_own, load_other), (store,), UNROLL)
    spread_scale(total_ref)
    row_parts(expo_ref, total_ref, part_ref)
    wait_all(number, store)


def spread_scale(total_ref):
    for part in chunks_of(total_ref.shape[0]):
        sums = jnp.sum(total_ref[part, :], axis=1, keepdims=True)
        total_ref[part, :] = jnp.broadcast_to(1.0 / sums, sums.shape[:1] + (128,))


def scaled(expo, scale):
    return jnp.concatenate([expo[:, 0:128] * scale, expo[:, 128:256] * scale], axis=1)


def row_parts(expo_ref, scale_ref, part_ref):
    def step(g):
        acc = jnp.zeros((8, CAP), f32)
        for part in chunks_of(scale_ref.shape[0]):
            acc = acc + fold(scaled(expo_ref[g, part, :].astype(f32), scale_ref[part, :]))
        part_ref[pl.ds(g, 1), :] = jnp.sum(acc, axis=0, keepdims=True)
        return 0

    over_groups(expo_ref.shape[0], step, unroll=UNROLL)


def relay_body(own_ref, near_ref, far_ref, last_ref, out_ref):
    sums = (own_ref[...] + near_ref[...]) + (far_ref[...] + last_ref[...])
    sums = sums.astype(bf16)
    for g in range(out_ref.shape[0]):
        out_ref[g] = sums


def scales_from(parts_ref, live_ref, scale_ref):
    sums = parts_ref[0].astype(f32)
    for g in range(1, parts_ref.shape[0]):
        sums = sums + parts_ref[g].astype(f32)
    live = live_ref[...]
    scale_ref[...] = live / (sums + 1.0 - live)


def column_sums(load, expo_ref, scale_ref, total_ref):
    total_ref[...] = jnp.zeros_like(total_ref)

    def step(g):
        row = row_of(scale_ref, g)
        for part in chunks_of(total_ref.shape[0]):
            expo = expo_ref[g, part, :].astype(f32)
            total_ref[part, :] += expo[:, 0:128] * row[:, 0:128] + expo[:, 128:256] * row[:, 128:256]
        return 0

    over_groups(expo_ref.shape[0], step, (load,), unroll=UNROLL)
    spread_scale(total_ref)


def balance_body(expo_hbm, parts_ref, live_ref, part_ref, expo_ref, total_ref, scale_ref, sems):
    load = lambda q: pltpu.make_async_copy(group(expo_hbm, q), group(expo_ref, q), sems.at[q])
    start_all(expo_ref.shape[0] // GROUP, load)
    scales_from(parts_ref, live_ref, scale_ref)
    column_sums(load, expo_ref, scale_ref, total_ref)
    row_parts(expo_ref, total_ref, part_ref)


def divide_up(g, acc, pull, halves_ref):
    rows = jnp.sum(acc, axis=0, keepdims=True)
    rows = jnp.where(iota((EXTRA, CAP), 0) == 0, rows, 0.0).astype(bf16)
    pull = pull.astype(bf16)
    for at, block in ((slice(0, CAP), pull), (slice(CAP, LINES), rows)):
        halves_ref[0, g, at, :] = block[:, 0:HALF]
        halves_ref[1, g, at, :] = block[:, HALF:CAP]


def last_body(
    at_ref, expo_hbm, parts_ref, live_ref, cols_ref, keep_hbm, give_hbm, total_hbm,
    expo_ref, total_ref, scale_ref, halves_ref, sems, keep_sems, give_sems,
):
    peers = expo_ref.shape[0]
    core = at_ref[0]
    load = lambda q: pltpu.make_async_copy(group(expo_hbm, q), group(expo_ref, q), sems.at[q])
    half_at = lambda c, q: halves_ref.at[c, pl.ds(q * GROUP, GROUP)]
    keep = lambda q: pltpu.make_async_copy(half_at(core, q), group(keep_hbm, q), keep_sems.at[q])
    give = lambda q: pltpu.make_async_copy(half_at(1 - core, q), group(give_hbm, q), give_sems.at[q])
    number = peers // GROUP
    start_all(number, load)
    scales_from(parts_ref, live_ref, scale_ref)
    column_sums(load, expo_ref, scale_ref, total_ref)

    def step(g):
        acc = jnp.zeros((8, CAP), f32)
        pull = jnp.zeros((cols_ref.shape[0], CAP), f32)
        for part in chunks_of(total_ref.shape[0]):
            balanced = scaled(expo_ref[g, part, :].astype(f32), total_ref[part, :])
            acc = acc + fold(balanced)
            pull = pull + mm(cols_ref[:, part], balanced.astype(bf16))
        divide_up(g, acc, pull, halves_ref)
        return 0

    spare = pltpu.make_async_copy(total_ref, total_hbm, sems.at[0])
    spare.start()
    over_groups(peers, step, (), (give, keep), UNROLL)
    wait_all(number, give)
    wait_all(number, keep)
    spare.wait()


def student_body(
    at_ref, cols_t_ref, cols_ref, rows_hbm, raised_hbm, keep_hbm, give_hbm,
    rows_ref, raised_ref, halves_ref, row_sems, sems, keep_sems, give_sems,
):
    peers = rows_ref.shape[0]
    load = lambda q: pltpu.make_async_copy(group(rows_hbm, q), group(rows_ref, q), row_sems.at[q])
    start_all(peers // GROUP, load)
    core = at_ref[0]
    width = cols_t_ref.shape[0]
    store = lambda q: pltpu.make_async_copy(group(raised_ref, q), group(raised_hbm, q), sems.at[q])
    half_at = lambda c, q: halves_ref.at[c, pl.ds(q * GROUP, GROUP)]
    keep = lambda q: pltpu.make_async_copy(half_at(core, q), group(keep_hbm, q), keep_sems.at[q])
    give = lambda q: pltpu.make_async_copy(half_at(1 - core, q), group(give_hbm, q), give_sems.at[q])
    number = peers // GROUP

    def step(g):
        rows = rows_ref[g]
        acc = jnp.zeros((8, CAP), f32)
        pull = jnp.zeros((cols_ref.shape[0], CAP), f32)
        for part in chunks_of(width):
            raised = jnp.exp2(mm(cols_t_ref[part, :], rows, NT) * (LOG2E / STUDENT_TEMP))
            acc = acc + fold(raised)
            raised = raised.astype(bf16)
            raised_ref[g, part, :] = raised
            pull = pull + mm(cols_ref[:, part], raised)
        divide_up(g, acc, pull, halves_ref)
        return 0

    over_groups(peers, step, (load,), (store, give, keep), UNROLL)
    for make in (give, keep, store):
        wait_all(number, make)


def columns_grad_body(
    expo_hbm, raised_hbm, scale_hbm, got_hbm, rows_hbm, proto_hbm, norm_hbm,
    grad_ref, scale_ref, proto_ref, norm_ref, expo_ref, raised_ref, acc_ref, tail_ref, rows_ref, esems, rsems, tail_sems, row_sems, late_sems,
):
    peers = expo_ref.shape[0]
    load = lambda q: pltpu.make_async_copy(group(expo_hbm, q), group(expo_ref, q), esems.at[q])
    load_raised = lambda q: pltpu.make_async_copy(group(raised_hbm, q), group(raised_ref, q), rsems.at[q])
    load_rows = lambda q: pltpu.make_async_copy(group(rows_hbm, q), group(rows_ref, q), row_sems.at[q])
    lines = got_hbm.shape[1] - EXTRA
    load_tail = pltpu.make_async_copy(got_hbm.at[:, lines : lines + EXTRA, :], tail_ref, tail_sems.at[0])
    load_scale = pltpu.make_async_copy(scale_hbm, scale_ref, tail_sems.at[1])
    late = copies([(proto_hbm, proto_ref), (norm_hbm, norm_ref)], late_sems)
    load_tail.start()
    load_scale.start()

    def begin(q, _):
        for make in (load_rows, load, load_raised):
            make(q).start()
        return 0

    lax.fori_loop(0, peers // GROUP, begin, 0)
    for copy in late:
        copy.start()
    acc_ref[...] = jnp.zeros_like(acc_ref)
    load_tail.wait()
    load_scale.wait()

    def step(g):
        tail = tail_ref[g].astype(f32)
        alpha = tail[0:1] + tail[1:2]
        beta = tail[2:3] + tail[3:4]
        rows = rows_ref[g]
        for part in chunks_of(acc_ref.shape[0]):
            balanced = scaled(expo_ref[g, part, :].astype(f32), scale_ref[part, :])
            score = raised_ref[g, part, :].astype(f32) * alpha - balanced * beta
            acc_ref[part, :] += mm(score.astype(bf16), rows)
        return 0

    over_groups(peers, step, (load_rows, load, load_raised), (), UNROLL)
    for copy in late:
        copy.wait()
    for part in chunks_of(acc_ref.shape[0]):
        grad = acc_ref[part, :].T
        norm = norm_ref[:, part]
        unit = proto_ref[:, part].astype(f32) / norm
        grad_ref[:, part] = (grad - unit * jnp.sum(unit * grad, axis=0, keepdims=True)) / norm


def join(core, own_ref, other_ref):
    own, other = (own_ref[0], other_ref[0])
    low = core == 0
    return jnp.concatenate([jnp.where(low, own, other), jnp.where(low, other, own)], axis=1)


def two_parts(x):
    high = x.astype(bf16)
    return (high.astype(f32), x - high.astype(f32))


def backward_body(
    at_ref, pull_ref, pull_other_ref, push_ref, push_other_ref, mine_ref, member_ref, feats_ref, feats_other_ref,
    rows_hbm, slope_hbm, hidden_hbm, w_out_hbm,
    send_hbm, pre_hbm, loss_ref, w_out_ref, slope_ref, hidden_ref, rows_ref, send_ref, pre_ref, out_ref, send_sems, pre_sem, load_sems,
):
    peers = send_ref.shape[0]
    sources = (w_out_hbm, slope_hbm, rows_hbm, hidden_hbm)
    loads = copies(list(zip(sources, (w_out_ref, slope_ref, rows_ref, hidden_ref))), load_sems)
    for load in loads:
        load.start()
    tail = mine_ref[...].astype(f32)
    live, weight = (tail[0:1], tail[1:2] * (1.0 / STUDENT_TEMP))
    pull = join(at_ref[0], pull_ref, pull_other_ref)
    push = join(at_ref[0], push_ref, push_other_ref)
    norm_sum = push[CAP : CAP + 1]
    push = push[0:CAP]
    scale = live / (pull[CAP : CAP + 1] + 1.0 - live)
    pull = pull[0:CAP]
    unit, inv = unit_of(feats_ref, feats_other_ref)
    inv = jnp.broadcast_to(inv, unit.shape).T[0:1]
    unit = unit.T
    cross = jnp.sum(unit.astype(bf16).astype(f32) * pull, axis=0, keepdims=True) * (1.0 / STUDENT_TEMP)
    row_loss = jnp.log(norm_sum) - scale * cross
    loss = jnp.sum(member_ref[...] * row_loss, axis=1, keepdims=True)
    square = (member_ref.shape[0], 128)
    loss = jnp.where(iota(square, 0) == iota(square, 1), loss, 0.0)
    loss_ref[...] = jnp.sum(loss, axis=0, keepdims=True)[:, 0 : loss_ref.shape[1]]
    alpha = weight / norm_sum
    beta = weight * scale
    grad_unit = push * alpha - pull * beta
    inner = jnp.sum(unit * grad_unit, axis=0, keepdims=True)
    grad_feats = (inv * (grad_unit - unit * inner)).T.astype(bf16)
    width = send_ref.shape[2]
    loads[0].wait()
    loads[1].wait()
    for part in chunks_of(hidden_ref.shape[1]):
        pre_ref[:, part] = (mm(grad_feats, w_out_ref[part, :], NT) * slope_ref[:, part]).astype(bf16)
    pre_out = pltpu.make_async_copy(pre_ref, pre_hbm, pre_sem.at[0])
    pre_out.start()
    loads[2].wait()
    loads[3].wait()
    for part in chunks_of(hidden_ref.shape[1]):
        out_ref[part, :] = mm(hidden_ref[:, part], grad_feats, TN).astype(bf16)
    level = at_ref[1]
    own = pre_ref[:, pl.ds(pl.multiple_of(level * width, width), width)]
    grad_in = mm(rows_ref[...], own, TN).astype(bf16)
    per = grad_in.shape[0] // peers
    block = out_ref.shape[0] // peers
    share = block // 4
    at = iota((EXTRA, CAP), 0)
    rows = jnp.zeros((EXTRA, CAP), f32)
    for i, x in enumerate(two_parts(alpha) + two_parts(beta)):
        rows = jnp.where(at == i, x, rows)
    rows = rows.astype(bf16)
    store = lambda g: pltpu.make_async_copy(send_ref.at[g], send_hbm.at[g], send_sems.at[g])
    for g in range(peers):
        send_ref[g, 0:per, :] = grad_in[g * per : (g + 1) * per, :]
        start = pl.multiple_of(g * block + level * share, share)
        send_ref[g, per : per + share, :] = out_ref[pl.ds(start, share), :]
        send_ref[g, per + share : per + share + EXTRA, :] = rows
        store(g).start()
    pre_out.wait()
    wait_all(peers, store)


def backward_rows_body(pre_ref, w_hbm, out_hbm, w_in_ref, out_ref, sem, out_sem):
    load = w_in_load(w_hbm, w_in_ref, sem.at[0])
    load.start()
    load.wait()
    w_in = w_in_of(w_in_ref, slice(0, w_in_ref.shape[2]))
    out_ref[...] = mm(pre_ref[...], w_in, NT).astype(bf16)
    store = pltpu.make_async_copy(out_ref, out_hbm, out_sem.at[0])
    store.start()
    store.wait()


def place_body(sel_ref, rows_ref, other_ref, out_hbm, out_ref, sems):
    rows = (rows_ref[...].astype(f32) + other_ref[...].astype(f32)).astype(bf16)
    pieces = out_ref.shape[0]
    size = out_ref.shape[1]
    store = lambda i: pltpu.make_async_copy(out_ref.at[i], out_hbm.at[i], sems.at[i])
    for i in range(pieces):
        out_ref[i] = mm(sel_ref[:, i * size : (i + 1) * size], rows, TN).astype(bf16)
        store(i).start()
    wait_all(pieces, store)


def gather_grads_body(got_hbm, send_hbm, got_ref, sum_ref, load_sems, sems):
    peers = got_hbm.shape[0]
    lines = sum_ref.shape[0]
    source = lambda q: got_hbm.at[pl.ds(q * GROUP, GROUP), 0:lines, :]
    load = lambda q: pltpu.make_async_copy(source(q), group(got_ref, q), load_sems.at[q])
    start_all(peers // GROUP, load)
    acc = jnp.zeros(got_ref.shape[1:], f32)
    for g in range(peers):
        if g % GROUP == 0:
            load(g // GROUP).wait()
        acc = acc + got_ref[g].astype(f32)
    sum_ref[...] = acc.astype(bf16)
    store = lambda t: pltpu.make_async_copy(sum_ref, send_hbm.at[t], sems.at[t])
    start_all(send_hbm.shape[0], store)
    wait_all(send_hbm.shape[0], store)


def weight_grads_body(parts_ref, grad_in_ref, grad_out_ref):
    peers, lines, width = parts_ref.shape
    per = grad_in_ref.shape[0]
    share = lines - per
    block = 2 * (width // 4)
    row = iota((2 * width, 2 * width), 0)
    col = iota((2 * width, 2 * width), 1)
    half = block // 2
    from_row = ((col % block) // half) * width + (col // block) * half + col % half
    order = (row == from_row).astype(f32).astype(bf16)
    for z in range(peers // 2):
        both = jnp.concatenate([parts_ref[2 * z, 0:per, :], parts_ref[2 * z + 1, 0:per, :]], axis=1)
        grad_in_ref[:, z * 2 * width : (z + 1) * 2 * width] = mm(both, order)
        for c in range(2):
            at = c * half + z * share
            grad_out_ref[at : at + share, :] = parts_ref[2 * z + c, per:lines, :].astype(f32)


def sem(number):
    return pltpu.SemaphoreType.DMA((number,))


def run_expo(at, cols_t, own, other):
    dp, (width, bot) = (own.shape[0], cols_t.shape)
    big, small = ((dp, width, CAP), (dp, CAP))
    return call(
        expo_body,
        [(big, bf16), (small, f32), (small, f32)],
        (at, cols_t, own, other),
        in_specs=[SMEM, HBM, ANY, ANY],
        out_specs=[HBM, VMEM, VMEM],
        scratch=[
            pltpu.VMEM((width, bot), bf16),
            pltpu.VMEM((dp, 2, HALF, bot), bf16),
            pltpu.VMEM(big, bf16),
            pltpu.VMEM((width, 128), f32),
            *[sem(dp // GROUP)] * 4,
        ],
    )


def run_balance(expo, got, live):
    dp, width, _ = expo.shape
    small = pltpu.VMEM(live.shape, f32)
    return call(
        balance_body,
        [(live.shape, f32)],
        (expo, got, live),
        in_specs=[HBM, VMEM, VMEM],
        scratch=[pltpu.VMEM(expo.shape, bf16), pltpu.VMEM((width, 128), f32), small, sem(dp // GROUP)],
    )[0]


def run_last(at, expo, got, live, cols):
    dp, width, _ = expo.shape
    halves = (dp, LINES, HALF)
    return call(
        last_body,
        [(halves, bf16), (halves, bf16), ((width, 128), f32)],
        (at, expo, got, live, cols),
        in_specs=[SMEM, HBM, VMEM, VMEM, VMEM],
        out_specs=[ANY, ANY, HBM],
        scratch=[
            pltpu.VMEM(expo.shape, bf16),
            pltpu.VMEM((width, 128), f32),
            pltpu.VMEM(live.shape, f32),
            pltpu.VMEM((2, *halves), bf16),
            *[sem(dp // GROUP)] * 3,
        ],
    )


def run_student(at, cols_t, cols, rows):
    dp = rows.shape[0]
    big, halves = ((dp, cols.shape[1], CAP), (dp, LINES, HALF))
    return call(
        student_body,
        [(big, bf16), (halves, bf16), (halves, bf16)],
        (at, cols_t, cols, rows),
        in_specs=[SMEM, VMEM, VMEM, HBM],
        out_specs=[HBM, ANY, ANY],
        scratch=[
            pltpu.VMEM(rows.shape, bf16),
            pltpu.VMEM(big, bf16),
            pltpu.VMEM((2, *halves), bf16),
            *[sem(dp // GROUP)] * 4,
        ],
    )


def run_columns_grad(expo, raised, scale, got, rows, proto, norm):
    dp, held = (expo.shape[0], pltpu.VMEM(expo.shape, bf16))
    return call(
        columns_grad_body,
        [(proto.shape, f32)],
        (expo, raised, scale, got, rows, proto, norm),
        in_specs=[HBM] * 3 + [ANY] + [HBM] * 3,
        scratch=[
            pltpu.VMEM(scale.shape, f32),
            pltpu.VMEM(proto.shape, bf16),
            pltpu.VMEM(norm.shape, f32),
            held,
            held,
            pltpu.VMEM(proto.shape[::-1], f32),
            pltpu.VMEM((dp, EXTRA, CAP), bf16),
            pltpu.VMEM(rows.shape, bf16),
            *[sem(dp // GROUP)] * 4,
            sem(2),
        ],
    )[0]


def exchange(x, axis):
    return lax.all_to_all(x, axis, split_axis=0, concat_axis=0, tiled=True)


def sibling(x):
    peers = lax.axis_size("tensor")
    return lax.ppermute(x, "tensor", [(i, i ^ 1) for i in range(peers)])


def everywhere(part):
    both = part + sibling(part)
    near, far, last = (levels(both, by) for by in (1, 2, 3))
    (sums,) = call(relay_body, [((part.shape[0], *part.shape), bf16)], (both, near, far, last))
    return exchange(sums, "dp")


def levels(x, by):
    peers = lax.axis_size("tensor")
    return lax.ppermute(x, "tensor", [(i, i ^ (2 * by)) for i in range(peers)])


def level_sums(x):
    near, far, last = (levels(x, by) for by in (1, 2, 3))
    wide = lambda y: y.astype(f32)
    return (wide(x) + wide(near)) + (wide(far) + wide(last))


def paired(keep, give):
    return (keep.astype(f32) + sibling(give).astype(f32)).astype(bf16)


def slot_sums_body(parts_hbm, out_hbm, parts_ref, out_ref, sems, out_sem):
    peers = parts_hbm.shape[0]
    load = lambda q: pltpu.make_async_copy(group(parts_hbm, q), group(parts_ref, q), sems.at[q])
    start_all(peers // GROUP, load)
    acc = jnp.zeros(parts_ref.shape[1:], f32)
    for g in range(peers):
        if g % GROUP == 0:
            load(g // GROUP).wait()
        acc = acc + parts_ref[g].astype(f32)
    out_ref[0] = acc.astype(bf16)
    store = pltpu.make_async_copy(out_ref, out_hbm, out_sem.at[0])
    store.start()
    store.wait()


def slot_sums(parts):
    out = (1, *parts.shape[1:])
    return call(
        slot_sums_body,
        [(out, bf16)],
        (parts,),
        in_specs=[ANY],
        out_specs=[HBM],
        scratch=[pltpu.VMEM(parts.shape, bf16), pltpu.VMEM(out, bf16), sem(parts.shape[0] // GROUP), sem(1)],
    )[0]


def after(x, earlier):
    return lax.optimization_barrier((x, earlier))[0]


def parts_of(tokens, teacher_feats, masks, w_in, w_out, proto_student, proto_teacher):
    dim = tokens.shape[1]
    hid = w_in.shape[1]
    bot, width = proto_student.shape
    dp, tensor = (lax.axis_size("dp"), lax.axis_size("tensor"))
    per = w_in.shape[0]
    half = hid // 2
    share = w_out.shape[0] // 8
    t = lax.axis_index("tensor").astype(jnp.int32)
    at = jnp.stack([t % 2, t // 2])

    lines = per + w_out.shape[0] // 2 * bot // half
    (w_pack,) = call(
        weights_body,
        [((lines, half), bf16)],
        (at, w_in, w_out),
        in_specs=[SMEM, HBM, HBM],
        out_specs=[HBM],
        scratch=[pltpu.VMEM(w_in.shape, bf16), pltpu.VMEM(w_out.shape, bf16), pltpu.VMEM((lines, half), bf16), sem(5)],
    )
    w_all = lax.all_gather(w_pack, "dp", axis=0, tiled=True).reshape(dp, lines, half)
    dma = pltpu.SemaphoreType.DMA
    sems = dma((dp,))
    sel, send, member, mine = call(
        select_body,
        [((CAP, tokens.shape[0]), bf16), ((dp, HALF, bot), bf16), ((8, CAP), f32), ((EXTRA, CAP), bf16)],
        (at, masks, teacher_feats),
        in_specs=[SMEM, VMEM, VMEM],
        out_specs=[VMEM, HBM, HBM, HBM],
        scratch=[
            pltpu.VMEM((CAP, bot), bf16),
            pltpu.VMEM((HALF, bot), bf16),
            pltpu.VMEM((8, CAP), f32),
            pltpu.VMEM((EXTRA, CAP), bf16),
            sems,
            sem(2),
        ],
    )
    packs = exchange(send, "dp")
    others = sibling(packs)
    cols, student_t, teacher_t, norm = call(
        columns_body,
        [((bot, width), bf16), ((width, bot), bf16), ((width, bot), bf16), ((1, width), f32)],
        (proto_student, proto_teacher),
        out_specs=[HBM] * 4,
        scratch=[
            pltpu.VMEM((bot, width), bf16),
            pltpu.VMEM((width, bot), bf16),
            pltpu.VMEM((width, bot), bf16),
            pltpu.VMEM((1, width), f32),
            sem(4),
        ],
    )
    expo, part, live = run_expo(at, teacher_t, packs, others)
    (rows,) = call(
        tokens_body,
        [((CAP, dim), bf16)],
        (sel, tokens),
        in_specs=[VMEM, HBM],
        out_specs=[HBM],
        scratch=[pltpu.VMEM(tokens.shape, bf16), pltpu.VMEM((CAP, dim), bf16), sem(2)],
    )
    hidden, slope, feats, w_out_half = call(
        forward_body,
        [((CAP, half), bf16), ((CAP, half), f32), ((CAP, bot), f32), ((half, bot), bf16)],
        (rows, after(w_all, part)),
        in_specs=[HBM, HBM],
        out_specs=[HBM, HBM, VMEM, HBM],
        scratch=[
            pltpu.VMEM((CAP, dim), bf16),
            pltpu.VMEM((CAP, half), bf16),
            pltpu.VMEM((CAP, half), f32),
            pltpu.VMEM((dp, per, half), bf16),
            pltpu.VMEM((dp, share, half), bf16),
            pltpu.VMEM((half, bot), bf16),
            sem(2 + len(chunks_of(half))),
        ],
    )
    feats_other = sibling(feats)
    (student_rows,) = call(unit_body, [((CAP, bot), bf16)], (feats, feats_other))
    all_rows = lax.all_gather(student_rows, "dp", axis=0, tiled=True).reshape(dp, CAP, bot)
    got = everywhere(part)
    part = run_balance(expo, got, live)
    got = everywhere(part)
    keep, give, scale = run_last(at, expo, got, live, cols)
    pull = paired(keep, give)
    pull_got = exchange(pull, "dp")
    all_rows = after(all_rows, pull)
    raised, keep, give = run_student(at, student_t, cols, all_rows)
    push_got = exchange(paired(keep, give), "dp")
    pull = level_sums(slot_sums(pull_got))
    pull_other = sibling(pull)
    push = level_sums(slot_sums(push_got))
    push_other = sibling(push)
    back_lines = per + share + EXTRA
    send, grad_pre, loss = call(
        backward_body,
        [((dp, back_lines, bot), bf16), ((CAP, half), bf16), ((1, masks.shape[0]), f32)],
        (at, pull, pull_other, push, push_other, mine, member, feats, feats_other, rows, slope, hidden, w_out_half),
        in_specs=[SMEM] + [VMEM] * 8 + [HBM] * 4,
        out_specs=[HBM, HBM, VMEM],
        scratch=[
            pltpu.VMEM((half, bot), bf16),
            pltpu.VMEM((CAP, half), f32),
            pltpu.VMEM((CAP, half), bf16),
            pltpu.VMEM((CAP, dim), bf16),
            pltpu.VMEM((dp, back_lines, bot), bf16),
            pltpu.VMEM((CAP, half), bf16),
            pltpu.VMEM((half, bot), bf16),
            sems,
            sem(1),
            sem(4),
        ],
    )
    got = exchange(send, "dp")
    (grad_rows,) = call(
        backward_rows_body,
        [((CAP, dim), bf16)],
        (grad_pre, w_all),
        in_specs=[VMEM, HBM],
        out_specs=[HBM],
        scratch=[pltpu.VMEM((dp, per, half), bf16), pltpu.VMEM((CAP, dim), bf16), sem(1), sem(1)],
    )
    pieces = 4
    d_shape = (pieces, tokens.shape[0] // pieces, dim)
    (d_tokens,) = call(
        place_body,
        [(d_shape, bf16)],
        (sel, grad_rows, sibling(grad_rows)),
        out_specs=[HBM],
        scratch=[pltpu.VMEM(d_shape, bf16), dma((pieces,))],
    )
    got, d_tokens = lax.optimization_barrier((got, d_tokens))
    (sent,) = call(
        gather_grads_body,
        [((tensor, per + share, bot), bf16)],
        (got,),
        in_specs=[ANY],
        out_specs=[HBM],
        scratch=[pltpu.VMEM((dp, per + share, bot), bf16), pltpu.VMEM((per + share, bot), bf16), sems, sem(tensor)],
    )
    parts = exchange(sent, "tensor")
    grad_proto = run_columns_grad(expo, raised, scale, got, all_rows, proto_student, norm)
    grad_in, grad_out = call(weight_grads_body, [((per, hid), f32), ((w_out.shape[0], bot), f32)], (parts,))
    return (d_tokens.reshape(tokens.shape), grad_in, grad_out, grad_proto, loss.reshape(masks.shape[0]))


def solution(mesh):
    placed = (
        P("dp", None),
        P("dp", None),
        P("dp", None),
        P("dp", None),
        P("dp", None),
        P(None, ("dp", "tensor")),
        P(None, ("dp", "tensor")),
    )
    return jax.shard_map(
        parts_of,
        mesh=mesh,
        in_specs=placed,
        out_specs=(P("dp", None), P("dp", None), P("dp", None), P(None, ("dp", "tensor")), P("dp")),
        check_vma=False,
    )
```
